32 devices in a mesh: dp: 16 (over z, y, core), mp: 2 (over x).
Axes of the slice: x: 2, y: 2, z: 4, core: 2. Of those that a mesh axis runs over, the one named last changes fastest.
Arguments:
- patch_counts: int32 [128], P('dp'), may hold values from 100 to 240, as said below
- tokens: bfloat16 [128, 280, 768], P('dp'), may hold values from -6 to 6
- cotangent: bfloat16 [128, 280, 768], P('dp'), may hold values from -6 to 6
- attn_gain: float32 [768], P('dp'), may hold values from 0.1 to 1.9
- attn_shift: float32 [768], P('dp'), may hold values from -1.75 to 1.75
- w_qkv: float32 [768, 3, 768], P('dp', None, 'mp'), may hold values from -0.21875 to 0.21875
- b_qv: float32 [2, 768], P(None, 'mp'), may hold values from -3 to 3
- w_proj: float32 [768, 768], P('mp', 'dp'), may hold values from -0.875 to 0.875
- b_proj: float32 [768], P('dp'), may hold values from -3 to 3
- ffn_gain: float32 [768], P('dp'), may hold values from 0.1 to 1.9
- ffn_shift: float32 [768], P('dp'), may hold values from -1.75 to 1.75
- w_up: float32 [768, 3072], P('dp', 'mp'), may hold values from -0.21875 to 0.21875
- b_up: float32 [3072], P('mp'), may hold values from -3 to 3
- w_down: float32 [3072, 768], P('mp', 'dp'), may hold values from -0.109375 to 0.109375
- b_down: float32 [768], P('dp'), may hold values from -3 to 3
Outputs:
- block_out: bfloat16 [128, 280, 768], P('dp')
- tokens_grad: bfloat16 [128, 280, 768], P('dp')
- attn_gain_grad: float32 [768], P('dp')
- attn_shift_grad: float32 [768], P('dp')
- w_qkv_grad: float32 [768, 3, 768], P('dp', None, 'mp')
- b_qv_grad: float32 [2, 768], P(None, 'mp')
- w_proj_grad: float32 [768, 768], P('mp', 'dp')
- b_proj_grad: float32 [768], P('dp')
- ffn_gain_grad: float32 [768], P('dp')
- ffn_shift_grad: float32 [768], P('dp')
- w_up_grad: float32 [768, 3072], P('dp', 'mp')
- b_up_grad: float32 [3072], P('mp')
- w_down_grad: float32 [3072, 768], P('mp', 'dp')
- b_down_grad: float32 [768], P('dp')
The draws below stay inside these ranges and needn't reach their ends.
Inputs may be any that keep to these rules, and one draw needn't show every extreme that they name: `patch_counts`: patch count of each pair; in every draw some pair has exactly 240 patches and some exactly 100.
All inputs are finite; a program needn't handle non-finite values.
Results may differ from the reference program's by a relative error of at most 0.022.
Values may be sent and summed in bfloat16 or wider, within the bound.
A program may use at most 192 MiB of HBM per device.

```python
import jax
import jax.numpy as jnp
from jax import lax

D = 768
HEADS = 12
HEAD_DIM = 64
FF = 3072
TEXT = 40
PATCH_MIN = 100
PATCH_MAX = 240
PAIRS_DEV = 8
SEQ = 280
PAIRS = 128
N_DP = 16
N_MP = 2


def draw_patch_counts(key, part):
    base = jax.random.fold_in(key, 7)
    first, second, third = jax.random.split(base, 3)
    counts = jax.random.randint(first, (PAIRS,), PATCH_MIN, PATCH_MAX + 1, dtype=jnp.int32)
    widest = jax.random.randint(second, (), 0, PAIRS, dtype=jnp.int32)
    offset = jax.random.randint(third, (), 1, PAIRS, dtype=jnp.int32)
    narrowest = (widest + offset) % PAIRS
    places = jnp.arange(PAIRS, dtype=jnp.int32)
    counts = jnp.where(places == widest, PATCH_MAX, counts)
    counts = jnp.where(places == narrowest, PATCH_MIN, counts)
    return counts.astype(jnp.int32)


def spiked(values, rng, source, target, parts, factor):
    owner, partner = [(jnp.arange(values.shape[position]) // (values.shape[position] // parts)).reshape([-1 if axis == position else 1 for axis in range(values.ndim)]) for position in (source, target)]
    chosen = jax.random.permutation(rng, parts)[partner]
    strong = (owner == chosen) | (owner == (partner + parts // 2) % parts)
    return jnp.where(strong, factor * values, values)


def levels(rng, dims, shards, low, largest):
    factor_of = 1.0
    for axis_at, parts in shards:
        draws = jax.random.uniform(jax.random.fold_in(jax.random.fold_in(rng, 6), axis_at), (parts,), jnp.float32, low / len(shards), largest / len(shards))
        factor_of = factor_of * jnp.repeat(jnp.exp(draws), dims[axis_at] // parts).reshape((-1,) + (1,) * (len(dims) - 1 - axis_at))
    return factor_of


def centred(key, extent, scale, limit, shards=(), kind=jnp.bfloat16):
    level = levels(key, extent, shards, -0.22, 0.18) if shards else 1.0
    drawn = jax.random.normal(key, extent, jnp.float32) * scale * level
    return jnp.minimum(jnp.maximum(drawn, -limit), limit).astype(kind)


def heavy_noise(key, shape, width, reach, pieces, heavy, kind=jnp.bfloat16):
    array = width * jax.random.normal(key, shape, jnp.float32)
    if pieces:
        array = array * levels(key, shape, pieces, -0.22, 0.18)
    return jnp.clip(spiked(array, jax.random.fold_in(key, 3), *heavy), -reach, reach).astype(kind)


def setup_inputs(seed: int = 0) -> dict:
    splits = jax.random.split(jax.random.key(seed), 16)
    return {
        "patch_counts": draw_patch_counts(jax.random.fold_in(splits[15], 71), 0),
        "tokens": heavy_noise(splits[1], (PAIRS, SEQ, D), 1.0, 6.0, ((0, 16),), (0, 2, 16, 2.0)),
        "cotangent": heavy_noise(splits[2], (PAIRS, SEQ, D), 1.0, 6.0, ((0, 16),), (0, 2, 16, 2.0)),
        "attn_gain": jnp.clip(1.0 + 0.18 * jax.random.normal(splits[3], (D,), jnp.float32), 0.1, 1.9),
        "attn_shift": centred(splits[4], (D,), 0.3, 1.75, ((0, 16),), jnp.float32),
        "w_qkv": centred(splits[5], (D, 3, D), D ** -0.5, 0.21875, ((0, 16), (2, 2)), jnp.float32),
        "b_qv": centred(splits[6], (2, D), 0.5, 3.0, ((1, 2),), jnp.float32),
        "w_proj": centred(splits[7], (D, D), (D // 16) ** -0.5, 0.875, ((0, 2), (1, 16)), jnp.float32),
        "b_proj": centred(splits[8], (D,), 0.5, 3.0, ((0, 16),), jnp.float32),
        "ffn_gain": jnp.clip(1.0 + 0.18 * jax.random.normal(splits[9], (D,), jnp.float32), 0.1, 1.9),
        "ffn_shift": centred(splits[10], (D,), 0.3, 1.75, ((0, 16),), jnp.float32),
        "w_up": centred(splits[11], (D, FF), D ** -0.5, 0.21875, ((0, 16), (1, 2)), jnp.float32),
        "b_up": centred(splits[12], (FF,), 0.5, 3.0, ((0, 2),), jnp.float32),
        "w_down": centred(splits[13], (FF, D), FF ** -0.5, 0.109375, ((0, 2), (1, 16)), jnp.float32),
        "b_down": centred(splits[14], (D,), 0.5, 3.0, ((0, 16),), jnp.float32),
    }


@jax.custom_vjp
def low(v):
    return lax.optimization_barrier(v.astype(jnp.bfloat16)).astype(jnp.float32)

@jax.custom_vjp
def low_back(v):
    return v

def low_keep(v):
    return (low(v), None)

def low_pass(kept, grad):
    return (grad,)

def back_keep(v):
    return (v, None)

def back_low(kept, grad):
    return (low(grad),)
low.defvjp(low_keep, low_pass)
low_back.defvjp(back_keep, back_low)

def normalize(values, gain, shift):
    center = values - lax.optimization_barrier(jnp.mean(values, axis=-1, keepdims=True))
    spread = lax.optimization_barrier(jnp.mean(center * center, axis=-1, keepdims=True))
    return center * lax.rsqrt(spread + 1e-06) * gain + shift

def rounded(value):
    return low(low_back(value))

def product(formula, left_op, right_op):
    return jnp.einsum(formula, left_op, right_op, precision=lax.Precision.HIGHEST)

def forward(inputs, params, row_valid):
    attn_gain, attn_shift, w_qkv, b_qv, w_proj, b_proj, ffn_gain, ffn_shift, w_up, b_up, w_down, b_down = params
    group_pairs = inputs.shape[0]
    local_width = D // N_MP
    head_count = HEADS // N_MP
    unit_count = FF // N_MP
    score_scale = HEAD_DIM ** (-0.5)
    qkv_copy = low(w_qkv)
    proj_copy = low(w_proj)
    up_copy = low(w_up)
    down_copy = low(w_down)
    bias_copy = low(b_qv)
    up_bias = low(b_up)
    keep_keys = row_valid[:, None, None, :] > 0
    normed_one = low(normalize(inputs, low(attn_gain), low(attn_shift)))
    attn_total = jnp.zeros_like(inputs)
    for group_index in range(N_MP):
        first_col = group_index * local_width
        entry_one = low_back(normed_one)
        qkv = product('gsd,dtc->gstc', entry_one, qkv_copy[:, :, first_col:first_col + local_width])
        queries = rounded(qkv[:, :, 0] + bias_copy[0, first_col:first_col + local_width])
        key_rows = rounded(qkv[:, :, 1])
        values = rounded(qkv[:, :, 2] + bias_copy[1, first_col:first_col + local_width])
        queries = queries.reshape(group_pairs, SEQ, head_count, HEAD_DIM)
        key_rows = key_rows.reshape(group_pairs, SEQ, head_count, HEAD_DIM)
        values = values.reshape(group_pairs, SEQ, head_count, HEAD_DIM)
        scores = low_back(score_scale * product('gqhe,gkhe->ghqk', queries, key_rows))
        scores = jnp.where(keep_keys, scores, -1e+30)
        probs_low = low(jax.nn.softmax(scores, axis=-1))
        attended = rounded(product('ghqk,gkhe->gqhe', probs_low, values)).reshape(group_pairs, SEQ, local_width)
        attn_total = attn_total + rounded(product('gsc,cd->gsd', attended, proj_copy[first_col:first_col + local_width, :]))
    hidden = inputs + attn_total + low(b_proj)
    normed_two = low(normalize(hidden, low(ffn_gain), low(ffn_shift)))
    mlp_total = jnp.zeros_like(inputs)
    for group_index in range(N_MP):
        first_unit = group_index * unit_count
        entry_two = low_back(normed_two)
        pre_act = low_back(product('gsd,df->gsf', entry_two, up_copy[:, first_unit:first_unit + unit_count]) + up_bias[first_unit:first_unit + unit_count])
        active = low(jax.nn.gelu(pre_act, approximate=False))
        mlp_total = mlp_total + rounded(product('gsf,fd->gsd', active, down_copy[first_unit:first_unit + unit_count, :]))
    return (hidden + mlp_total + low(b_down)) * row_valid[:, :, None]

def reference(patch_counts, tokens, cotangent, attn_gain, attn_shift, w_qkv, b_qv, w_proj, b_proj, ffn_gain, ffn_shift, w_up, b_up, w_down, b_down):
    params = (attn_gain, attn_shift, w_qkv, b_qv, w_proj, b_proj, ffn_gain, ffn_shift, w_up, b_up, w_down, b_down)
    params = tuple((member.astype(jnp.float32) for member in params))
    grouped_tokens = tokens.reshape(N_DP, PAIRS_DEV, SEQ, D)
    grouped_cot = cotangent.reshape(N_DP, PAIRS_DEV, SEQ, D)
    grouped_len = (TEXT + patch_counts).astype(jnp.int32).reshape(N_DP, PAIRS_DEV)

    def visit(totals, slices):
        group_tokens, group_cot, group_len = slices
        row_valid = (jnp.arange(SEQ, dtype=jnp.int32)[None, :] < group_len[:, None]).astype(jnp.float32)
        result, pullback = jax.vjp(lambda inputs_here, params_here: forward(inputs_here, params_here, row_valid), group_tokens.astype(jnp.float32), params)
        d_tokens, d_params = pullback(group_cot.astype(jnp.float32))
        totals = jax.tree.map(lambda first, second: first + second, totals, d_params)
        return (totals, (result.astype(jnp.bfloat16), d_tokens.astype(jnp.bfloat16)))
    zeros = jax.tree.map(jnp.zeros_like, params)
    totals, (outputs, input_grads) = lax.scan(visit, zeros, (grouped_tokens, grouped_cot, grouped_len))
    g_attn_gain, g_attn_shift, g_qkv, g_bqv, g_proj, g_bproj, g_ffn_gain, g_ffn_shift, g_up, g_bup, g_down, g_bdown = totals
    return (outputs.reshape(PAIRS, SEQ, D), input_grads.reshape(PAIRS, SEQ, D), g_attn_gain, g_attn_shift, g_qkv, g_bqv, g_proj, g_bproj, g_ffn_gain, g_ffn_shift, g_up, g_bup, g_down, g_bdown)
```

```python
import jax
import jax.numpy as jnp
from jax import lax
from jax.sharding import PartitionSpec as P

HEADS = 12
HEAD_DIM = 64
TEXT = 40
LOW = jnp.bfloat16
F32 = jnp.float32


def normalize(values, gain, shift):
    center = values - jnp.mean(values, axis=-1, keepdims=True)
    spread = jnp.mean(center * center, axis=-1, keepdims=True)
    return center * lax.rsqrt(spread + 1e-06) * gain + shift


def norm_back(values, gain, incoming):
    center = values - jnp.mean(values, axis=-1, keepdims=True)
    spread = jnp.mean(center * center, axis=-1, keepdims=True)
    r = lax.rsqrt(spread + 1e-06)
    xhat = center * r
    dg = incoming * gain
    d_values = r * (
        dg - jnp.mean(dg, axis=-1, keepdims=True) - xhat * jnp.mean(dg * xhat, axis=-1, keepdims=True)
    )
    axes = tuple(range(values.ndim - 1))
    return d_values, jnp.sum(incoming * xhat, axis=axes), jnp.sum(incoming, axis=axes)


def per_device(
    patch_counts, tokens, cotangent, attn_gain, attn_shift, w_qkv, b_qv, w_proj, b_proj,
    ffn_gain, ffn_shift, w_up, b_up, w_down, b_down,
):
    pairs_all, rows, width = tokens.shape
    n_mp = lax.axis_size("mp")
    n_dp = lax.axis_size("dp")
    pairs = pairs_all // n_mp
    part = w_qkv.shape[0]
    lw = w_qkv.shape[2]
    fw = w_up.shape[1]
    mine = lax.axis_index("mp")
    scale = HEAD_DIM ** (-0.5)
    tokens_here = lax.dynamic_slice_in_dim(tokens, mine * pairs, pairs, 0)
    cot_here = lax.dynamic_slice_in_dim(cotangent, mine * pairs, pairs, 0)
    counts = lax.dynamic_slice_in_dim(patch_counts, mine * pairs, pairs, 0)

    first = jnp.concatenate([w_qkv.astype(LOW).reshape(part, 3 * lw), w_proj.astype(LOW).T], axis=1)
    second = jnp.concatenate([w_up.astype(LOW), w_down.astype(LOW).T], axis=1)
    vectors = jnp.stack([attn_gain, attn_shift, b_proj, ffn_gain, ffn_shift, b_down]).astype(LOW)
    vec_full = lax.all_gather(vectors, "dp", axis=1, tiled=True).astype(F32)
    bias_mine = jnp.concatenate([b_qv.reshape(-1), b_up]).astype(LOW)
    bias_all = lax.all_gather(bias_mine, "mp", axis=0).astype(F32)
    full_one = lax.all_gather(first, ("mp", "dp"), axis=0, tiled=True).reshape(n_mp, width, 4 * lw)
    full_two = lax.all_gather(second, ("mp", "dp"), axis=0, tiled=True).reshape(n_mp, width, 2 * fw)
    qkv_full = full_one[:, :, : 3 * lw].reshape(n_mp, width, 3, lw)
    proj_t = full_one[:, :, 3 * lw :]
    up_full = full_two[:, :, :fw]
    down_t = full_two[:, :, fw:]
    gain_one, shift_one, proj_bias, gain_two, shift_two, down_bias = [vec_full[i] for i in range(6)]
    bias_q = bias_all[:, :lw]
    bias_v = bias_all[:, lw : 2 * lw]
    up_bias = bias_all[:, 2 * lw :]

    valid = (jnp.arange(rows, dtype=jnp.int32)[None, :] < (TEXT + counts)[:, None]).astype(F32)
    inputs = tokens_here.astype(F32)
    n_one = normalize(inputs, gain_one, shift_one).astype(LOW)
    qkv = jnp.einsum("psd,mdtc->tpsmc", n_one, qkv_full, preferred_element_type=F32)
    heads = HEADS // n_mp

    def split(a):
        return a.reshape(pairs, rows, n_mp * heads, HEAD_DIM)

    q = split((qkv[0] + bias_q).astype(LOW))
    k = split(qkv[1].astype(LOW))
    v = split((qkv[2] + bias_v).astype(LOW))
    s = jnp.einsum("bqhe,bkhe->bhqk", q, k, preferred_element_type=F32) * scale
    s = jnp.where(valid[:, None, None, :] > 0, s, -1e30)
    prob = jax.nn.softmax(s, axis=-1)
    prob_low = prob.astype(LOW)
    att = jnp.einsum("bhqk,bkhe->bqhe", prob_low, v, preferred_element_type=F32).astype(LOW)
    att = att.reshape(pairs, rows, n_mp, lw)
    proj = jnp.einsum("psmc,mdc->psd", att, proj_t, preferred_element_type=F32)
    hidden = inputs + proj + proj_bias
    n_two = normalize(hidden, gain_two, shift_two).astype(LOW)
    pre = jnp.einsum("psd,mdf->psmf", n_two, up_full, preferred_element_type=F32) + up_bias
    cdf = 0.5 * (1.0 + lax.erf(pre * (2.0 ** -0.5)))
    act = (pre * cdf).astype(LOW)
    slope = cdf + pre * jnp.exp(-0.5 * pre * pre) * 0.3989422804014327
    down = jnp.einsum("psmf,mdf->psd", act, down_t, preferred_element_type=F32)
    out_here = ((hidden + down + down_bias) * valid[:, :, None]).astype(LOW)

    up_stream = cot_here.astype(F32) * valid[:, :, None]
    up_low = up_stream.astype(LOW)
    g_b_down = jnp.sum(up_stream, axis=(0, 1))
    g_down_t = jnp.einsum("psd,psmf->mdf", up_low, act, preferred_element_type=F32)
    d_act = jnp.einsum("psd,mdf->psmf", up_low, down_t, preferred_element_type=F32)
    d_pre = (slope * d_act).astype(LOW)
    g_b_up = jnp.sum(d_pre.astype(F32), axis=(0, 1))
    g_up = jnp.einsum("psd,psmf->mdf", n_two, d_pre, preferred_element_type=F32)
    d_two = jnp.einsum("psmf,mdf->psd", d_pre, up_full, preferred_element_type=F32)
    d_norm, g_gain_two, g_shift_two = norm_back(hidden, gain_two, d_two)
    d_hidden = up_stream + d_norm
    g_b_proj = jnp.sum(d_hidden, axis=(0, 1))
    d_low = d_hidden.astype(LOW)
    g_proj_t = jnp.einsum("psd,psmc->mdc", d_low, att, preferred_element_type=F32)
    d_att = split(jnp.einsum("psd,mdc->psmc", d_low, proj_t, preferred_element_type=F32).astype(LOW))
    d_prob = jnp.einsum("bqhe,bkhe->bhqk", d_att, v, preferred_element_type=F32)
    d_v = jnp.einsum("bhqk,bqhe->bkhe", prob_low, d_att, preferred_element_type=F32)
    inner = jnp.sum(prob * d_prob, axis=-1, keepdims=True)
    d_s = (prob * (d_prob - inner)).astype(LOW)
    d_q = scale * jnp.einsum("bhqk,bkhe->bqhe", d_s, k, preferred_element_type=F32)
    d_k = scale * jnp.einsum("bhqk,bqhe->bkhe", d_s, q, preferred_element_type=F32)

    def join(a):
        return a.astype(LOW).reshape(pairs, rows, n_mp, lw)

    d_qkv = jnp.stack([join(d_q), join(d_k), join(d_v)], axis=3)
    g_b_q = jnp.sum(d_qkv[:, :, :, 0].astype(F32), axis=(0, 1))
    g_b_v = jnp.sum(d_qkv[:, :, :, 2].astype(F32), axis=(0, 1))
    g_qkv = jnp.einsum("psd,psmtc->mdtc", n_one, d_qkv, preferred_element_type=F32)
    d_one = jnp.einsum("psmtc,mdtc->psd", d_qkv, qkv_full, preferred_element_type=F32)
    d_in, g_gain_one, g_shift_one = norm_back(inputs, gain_one, d_one)
    tok_here = (d_hidden + d_in).astype(LOW)

    def both(array):
        other = lax.ppermute(array, "mp", [(0, 1), (1, 0)])
        return jnp.where(mine == 0, jnp.concatenate([array, other]), jnp.concatenate([other, array]))

    block_out = both(out_here)
    tokens_grad = both(tok_here)
    grads_two = jnp.concatenate([g_up, g_down_t], axis=2).reshape(n_mp * width, 2 * fw)
    grads_one = jnp.concatenate([g_qkv.reshape(n_mp, width, 3 * lw), g_proj_t], axis=2).reshape(n_mp * width, 4 * lw)
    red_two = lax.psum_scatter(grads_two, ("mp", "dp"), scatter_dimension=0, tiled=True)
    red_one = lax.psum_scatter(grads_one, ("mp", "dp"), scatter_dimension=0, tiled=True)
    small = jnp.concatenate([
        g_gain_one, g_shift_one, g_b_proj, g_gain_two, g_shift_two, g_b_down,
        g_b_q.reshape(-1), g_b_v.reshape(-1), g_b_up.reshape(-1)])
    small = lax.psum(small, ("mp", "dp"))
    place = lax.axis_index("dp") * part

    def piece(i):
        return lax.dynamic_slice_in_dim(small, i * width + place, part, 0)

    rest = small[6 * width :]
    o_b_q = lax.dynamic_slice_in_dim(rest, mine * lw, lw, 0)
    o_b_v = lax.dynamic_slice_in_dim(rest, (n_mp + mine) * lw, lw, 0)
    o_b_up = lax.dynamic_slice_in_dim(rest, 2 * n_mp * lw + mine * fw, fw, 0)
    return (
        block_out, tokens_grad, piece(0), piece(1),
        red_one[:, : 3 * lw].reshape(part, 3, lw), jnp.stack([o_b_q, o_b_v]),
        red_one[:, 3 * lw :].T, piece(2), piece(3), piece(4), red_two[:, :fw], o_b_up,
        red_two[:, fw:].T, piece(5),
    )


def solution(mesh):
    vec, mat = P("dp"), P("dp", "mp")
    tok = P("dp", None, None)
    in_specs = (
        vec, tok, tok, vec, vec, P("dp", None, "mp"), P(None, "mp"), P("mp", "dp"), vec, vec, vec,
        mat, P("mp"), P("mp", "dp"), vec,
    )
    out_specs = (
        tok, tok, vec, vec, P("dp", None, "mp"), P(None, "mp"), P("mp", "dp"), vec, vec, vec,
        mat, P("mp"), P("mp", "dp"), vec,
    )
    return jax.shard_map(per_device, mesh=mesh, in_specs=in_specs, out_specs=out_specs, check_vma=False)
```

```python
import functools

import jax
import jax.numpy as jnp
from jax import lax
from jax.experimental import pallas as pl
from jax.experimental.pallas import tpu as pltpu
from jax.sharding import PartitionSpec as P

HEADS = 12
HEAD_DIM = 64
TEXT = 40
LOW = jnp.bfloat16
F32 = jnp.float32
EXTRA = 128
NT = (((1,), (1,)), ((), ()))
NN = (((1,), (0,)), ((), ()))


def dot(a, b, dims=NN):
    return lax.dot_general(a, b, dims, preferred_element_type=F32)


def moments(v):
    center = v - jnp.mean(v, axis=-1, keepdims=True)
    spread = jnp.mean(center * center, axis=-1, keepdims=True)
    r = lax.rsqrt(spread + 1e-06)
    return center * r, r


def row_ids(rows):
    return lax.broadcasted_iota(jnp.int32, (rows, 1), 0)


def attn_kernel(lens, off, x_ref, w_ref, bias_ref, qkv_ref, att_ref, prob_ref, hid_ref, n1_ref, n2_ref, vec_ref):
    p = pl.program_id(0)
    rows, width = x_ref.shape[1], x_ref.shape[2]
    groups = w_ref.shape[0]
    lw = width // groups
    tiles = lw // 128

    @pl.when(p == 0)
    def _():
        vec_ref[...] = w_ref[0, :, 4 * lw :].astype(F32).T[:8]

    x = x_ref[0].astype(F32)
    xhat, _ = moments(x)
    n1 = (xhat * vec_ref[0:1] + vec_ref[1:2]).astype(LOW)
    n1_ref[0] = n1
    for m in range(groups):
        y = dot(n1, w_ref[m, :, : 3 * lw])
        base = m * 3 * lw
        qkv_ref[0, :, base : base + lw] = (y[:, :lw] + bias_ref[m, 0:1, :lw]).astype(LOW)
        qkv_ref[0, :, base + lw : base + 2 * lw] = y[:, lw : 2 * lw].astype(LOW)
        qkv_ref[0, :, base + 2 * lw : base + 3 * lw] = (
            y[:, 2 * lw :] + bias_ref[m, 0:1, lw : 2 * lw]
        ).astype(LOW)
    count = lens[p]
    keep = row_ids(rows) < count
    first = lax.broadcasted_iota(jnp.int32, (1, 128), 1) < HEAD_DIM

    def pair(hp, carry):
        base = (hp // tiles) * 3 * lw + (hp % tiles) * 128

        def cols(t):
            return pl.ds(pl.multiple_of(base + t * lw, 128), 128)

        q2 = qkv_ref[0, :, cols(0)] * 0.125
        k2 = qkv_ref[0, :, cols(1)]
        v2t = qkv_ref[0, :, cols(2)].T
        outs = []
        for h in range(2):
            qh = jnp.where(first if h == 0 else ~first, q2, 0)
            st = dot(k2, qh, NT)
            st = jnp.where(keep, st, -1e30)
            e = jnp.exp(st - jnp.max(st, axis=0, keepdims=True))
            pt = (e * (1.0 / jnp.sum(e, axis=0, keepdims=True))).astype(LOW)
            prob_ref[0, hp * 2 + h] = pt
            outs.append(dot(v2t[h * HEAD_DIM : (h + 1) * HEAD_DIM], pt))
        att_ref[0, :, pl.ds(pl.multiple_of(hp * 128, 128), 128)] = jnp.concatenate(outs, axis=0).T.astype(LOW)
        return carry

    lax.fori_loop(0, groups * tiles, pair, 0)
    proj = sum(dot(att_ref[0, :, m * lw : (m + 1) * lw], w_ref[m, :, 3 * lw : 4 * lw], NT) for m in range(groups))
    hid = x + proj + vec_ref[2:3]
    hid_ref[0] = hid
    xhat2, _ = moments(hid)
    n2_ref[0] = (xhat2 * vec_ref[3:4] + vec_ref[4:5]).astype(LOW)


def const_spec(shape):
    return pl.BlockSpec(shape, lambda *_: (0,) * len(shape), pipeline_mode=pl.Buffered(1))


def pair_spec(*shape):
    return pl.BlockSpec((1,) + shape, lambda p, *_: (p,) + (0,) * len(shape))


def attention_forward(lens, off, tokens, w_one, bias):
    pairs = lens.shape[0]
    _, rows, width = tokens.shape
    out = lambda dt, *s: jax.ShapeDtypeStruct((pairs,) + s, dt)
    return pl.pallas_call(
        attn_kernel,
        grid_spec=pltpu.PrefetchScalarGridSpec(
            num_scalar_prefetch=2,
            grid=(pairs,),
            in_specs=[
                pl.BlockSpec((1, rows, width), lambda p, lens, off: (off[0] + p, 0, 0)),
                const_spec(w_one.shape),
                const_spec(bias.shape),
            ],
            out_specs=[
                pair_spec(rows, 3 * width), pair_spec(rows, width), pair_spec(HEADS, rows, rows),
                pair_spec(rows, width), pair_spec(rows, width), pair_spec(rows, width),
                pl.BlockSpec((8, width), lambda *_: (0, 0)),
            ],
        ),
        out_shape=[
            out(LOW, rows, 3 * width), out(LOW, rows, width), out(LOW, HEADS, rows, rows),
            out(F32, rows, width), out(LOW, rows, width), out(LOW, rows, width),
            jax.ShapeDtypeStruct((8, width), F32),
        ],
        compiler_params=pltpu.CompilerParams(vmem_limit_bytes=60 * 2**20),
        name="attention_forward",
    )(lens, off, tokens, w_one, bias)


def ffn_kernel(lens, off, n2_ref, hid_ref, cot_ref, w_ref, bias_ref, vec_ref,
               out_ref, act_ref, dpre_ref, dhid_ref, dlow_ref, upl_ref, sums_ref, bsum_ref):
    p = pl.program_id(0)
    rows, width = n2_ref.shape[1], n2_ref.shape[2]
    groups = w_ref.shape[0]
    fw = w_ref.shape[2] // 2
    lw = width // groups
    step = 512
    keep = row_ids(rows) < lens[p]
    n2 = n2_ref[0]
    upl = jnp.where(keep, cot_ref[0], 0)
    upl_ref[0] = upl

    @pl.when(p == 0)
    def _():
        sums_ref[...] = jnp.zeros_like(sums_ref)
        bsum_ref[...] = jnp.zeros_like(bsum_ref)

    for m in range(groups):
        for c in range(0, fw, step):
            pre = dot(n2, w_ref[m, :, c : c + step]) + bias_ref[m, 0:1, 2 * lw + c : 2 * lw + c + step]
            cdf = 0.5 * (1.0 + lax.erf(pre * (2.0 ** -0.5)))
            at = m * fw + c
            act_ref[0, :, at : at + step] = (pre * cdf).astype(LOW)
            slope = cdf + pre * (0.3989422804014327 * jnp.exp(-0.5 * pre * pre))
            dpre = slope * dot(upl, w_ref[m, :, fw + c : fw + c + step])
            dpre_ref[0, :, at : at + step] = dpre.astype(LOW)
            bsum_ref[0:1, at : at + step] += jnp.sum(dpre, axis=0, keepdims=True)
    hid = hid_ref[0]
    down = sum(dot(act_ref[0, :, m * fw : (m + 1) * fw], w_ref[m, :, fw:], NT) for m in range(groups))
    out_ref[0] = jnp.where(keep, hid + down + vec_ref[5:6], 0.0).astype(LOW)
    dtwo = sum(dot(dpre_ref[0, :, m * fw : (m + 1) * fw], w_ref[m, :, :fw], NT) for m in range(groups))
    xhat, r = moments(hid)
    dg = dtwo * vec_ref[3:4]
    dn = r * (dg - jnp.mean(dg, axis=-1, keepdims=True) - xhat * jnp.mean(dg * xhat, axis=-1, keepdims=True))
    upf = upl.astype(F32)
    dhid = upf + dn
    dhid_ref[0] = dhid
    dlow_ref[0] = dhid.astype(LOW)
    sums_ref[0:1] += jnp.sum(dtwo * xhat, axis=0, keepdims=True)
    sums_ref[1:2] += jnp.sum(dtwo, axis=0, keepdims=True)
    sums_ref[2:3] += jnp.sum(dhid, axis=0, keepdims=True)
    sums_ref[3:4] += jnp.sum(upf, axis=0, keepdims=True)


def ffn(lens, off, n2, hid, cotangent, w_two, bias, vec):
    pairs, rows, width = n2.shape
    ff = w_two.shape[0] * w_two.shape[2] // 2
    out = lambda dt, *s: jax.ShapeDtypeStruct((pairs,) + s, dt)
    return pl.pallas_call(
        ffn_kernel,
        grid_spec=pltpu.PrefetchScalarGridSpec(
            num_scalar_prefetch=2,
            grid=(pairs,),
            in_specs=[
                pair_spec(rows, width), pair_spec(rows, width),
                pl.BlockSpec((1, rows, width), lambda p, lens, off: (off[0] + p, 0, 0)),
                const_spec(w_two.shape), const_spec(bias.shape), const_spec(vec.shape),
            ],
            out_specs=[
                pair_spec(rows, width), pair_spec(rows, ff), pair_spec(rows, ff), pair_spec(rows, width),
                pair_spec(rows, width), pair_spec(rows, width),
                pl.BlockSpec((8, width), lambda *_: (0, 0)), pl.BlockSpec((8, ff), lambda *_: (0, 0)),
            ],
        ),
        out_shape=[
            out(LOW, rows, width), out(LOW, rows, ff), out(LOW, rows, ff), out(F32, rows, width),
            out(LOW, rows, width), out(LOW, rows, width),
            jax.ShapeDtypeStruct((8, width), F32), jax.ShapeDtypeStruct((8, ff), F32),
        ],
        compiler_params=pltpu.CompilerParams(vmem_limit_bytes=60 * 2**20),
        name="feed_forward",
    )(lens, off, n2, hid, cotangent, w_two, bias, vec)


def back_kernel(lens, off, x_ref, dhid_ref, qkv_ref, prob_ref, w_ref, vec_ref,
                tok_ref, dqkv_ref, sums_ref, bsum_ref, do_ref):
    p = pl.program_id(0)
    rows, width = x_ref.shape[1], x_ref.shape[2]
    groups = w_ref.shape[0]
    lw = width // groups
    tiles = lw // 128

    @pl.when(p == 0)
    def _():
        sums_ref[...] = jnp.zeros_like(sums_ref)
        bsum_ref[...] = jnp.zeros_like(bsum_ref)

    dhid = dhid_ref[0]
    dlow = dhid.astype(LOW)
    for m in range(groups):
        do_ref[:, m * lw : (m + 1) * lw] = dot(dlow, w_ref[m, :, 3 * lw : 4 * lw]).astype(LOW)
    first = lax.broadcasted_iota(jnp.int32, (1, 128), 1) < HEAD_DIM

    def pair(hp, carry):
        base = (hp // tiles) * 3 * lw + (hp % tiles) * 128

        def cols(t):
            return pl.ds(pl.multiple_of(base + t * lw, 128), 128)

        q2 = qkv_ref[0, :, cols(0)] * 0.125
        k2t = qkv_ref[0, :, cols(1)].T
        v2 = qkv_ref[0, :, cols(2)]
        do2 = do_ref[:, pl.ds(pl.multiple_of(hp * 128, 128), 128)]
        dq_t = []
        dk = dv = 0.0
        for h in range(2):
            mine = first if h == 0 else ~first
            doh = jnp.where(mine, do2, 0)
            qh = jnp.where(mine, q2, 0)
            dpt = dot(v2, doh, NT)
            plow = prob_ref[0, hp * 2 + h]
            pt = plow.astype(F32)
            inner = jnp.sum(pt * dpt, axis=0, keepdims=True)
            dst = (pt * (dpt - inner)).astype(LOW)
            dv = dv + dot(plow, doh)
            dk = dk + dot(dst, qh)
            dq_t.append(dot(k2t[h * HEAD_DIM : (h + 1) * HEAD_DIM], dst))
        dq = (jnp.concatenate(dq_t, axis=0) * 0.125).T
        dqkv_ref[0, :, cols(0)] = dq.astype(LOW)
        dqkv_ref[0, :, cols(1)] = dk.astype(LOW)
        dqkv_ref[0, :, cols(2)] = dv.astype(LOW)
        bsum_ref[0:1, cols(0)] += jnp.sum(dq, axis=0, keepdims=True)
        bsum_ref[0:1, cols(2)] += jnp.sum(dv, axis=0, keepdims=True)
        return carry

    lax.fori_loop(0, groups * tiles, pair, 0)
    done = sum(dot(dqkv_ref[0, :, m * 3 * lw : (m + 1) * 3 * lw], w_ref[m, :, : 3 * lw], NT) for m in range(groups))
    xhat, r = moments(x_ref[0].astype(F32))
    dg = done * vec_ref[0:1]
    dn = r * (dg - jnp.mean(dg, axis=-1, keepdims=True) - xhat * jnp.mean(dg * xhat, axis=-1, keepdims=True))
    tok_ref[0] = (dhid + dn).astype(LOW)
    sums_ref[0:1] += jnp.sum(done * xhat, axis=0, keepdims=True)
    sums_ref[1:2] += jnp.sum(done, axis=0, keepdims=True)


def attention_backward(lens, off, tokens, dhid, qkv, prob, w_one, vec):
    pairs, rows, width = dhid.shape
    out = lambda dt, *s: jax.ShapeDtypeStruct((pairs,) + s, dt)
    return pl.pallas_call(
        back_kernel,
        grid_spec=pltpu.PrefetchScalarGridSpec(
            num_scalar_prefetch=2,
            grid=(pairs,),
            in_specs=[
                pl.BlockSpec((1, rows, width), lambda p, lens, off: (off[0] + p, 0, 0)),
                pair_spec(rows, width), pair_spec(rows, 3 * width), pair_spec(HEADS, rows, rows),
                const_spec(w_one.shape), const_spec(vec.shape),
            ],
            out_specs=[
                pair_spec(rows, width), pair_spec(rows, 3 * width),
                pl.BlockSpec((8, width), lambda *_: (0, 0)), pl.BlockSpec((8, 3 * width), lambda *_: (0, 0)),
            ],
            scratch_shapes=[pltpu.VMEM((rows, width), LOW)],
        ),
        out_shape=[
            out(LOW, rows, width), out(LOW, rows, 3 * width),
            jax.ShapeDtypeStruct((8, width), F32), jax.ShapeDtypeStruct((8, 3 * width), F32),
        ],
        compiler_params=pltpu.CompilerParams(vmem_limit_bytes=60 * 2**20),
        name="attention_backward",
    )(lens, off, tokens, dhid, qkv, prob, w_one, vec)
MESH_ID = pl.DeviceIdType.MESH
Z, Y, C = 4, 2, 2


def place():
    dp = lax.axis_index("dp")
    m = lax.axis_index("mp")
    c = lax.rem(dp, 2)
    y = lax.rem(dp // 2, 2)
    z = dp // 4
    return z, y, c, m


def index(z, y, c):
    return (z * Y + y) * C + c


def flips(y, c, m):
    one = (y + c * (1 - 2 * y), m + (1 - c) * (1 - 2 * m))
    two = (y + (1 - c) * (1 - 2 * y), m + c * (1 - 2 * m))
    return one, two


def greet(z, y, c, m):
    barrier = pltpu.get_barrier_semaphore()
    (y1, m1), (y2, m2) = flips(y, c, m)
    peers = [(index(lax.rem(z + k, Z), y, c), m) for k in (1, 2, 3)]
    peers += [(index(z, y1, c), m1), (index(z, y2, c), m2), (index(z, y, 1 - c), m)]
    for dp, mp in peers:
        pl.semaphore_signal(barrier, inc=1, device_id={"dp": dp, "mp": mp}, device_id_type=MESH_ID)
    pl.semaphore_wait(barrier, len(peers))
    return peers


def gather_kernel(s0, s1, s2, b_in, w_one, w_two, b_out, send, recv, bsem, local):
    z, y, c, m = place()
    (y1, m1), (y2, m2) = flips(y, c, m)
    part, cols = s1.shape
    peers = greet(z, y, c, m)
    pz, one, two, sib = peers[:3], peers[3], peers[4], peers[5]
    shards = (s0, s1, s2)

    def spot(g, dp, mp):
        rows = pl.ds(pl.multiple_of(dp * part, part), part)
        if g == 0:
            return w_one.at[mp, rows]
        return w_two.at[mp, rows, (g - 1) * cols : g * cols]

    started = []
    count = [0, 0, 0]

    def push(g, src, dp, mp, to):
        copy = pltpu.make_async_remote_copy(
            src_ref=src, dst_ref=spot(g, dp, mp), send_sem=send.at[g, count[g]],
            recv_sem=recv.at[g, mp * (Z * Y * C) + dp],
            device_id={"dp": to[0], "mp": to[1]}, device_id_type=MESH_ID,
        )
        count[g] += 1
        copy.start()
        started.append(copy)

    def arrived(g, dp, mp):
        at = spot(g, dp, mp)
        pltpu.make_async_remote_copy(
            src_ref=at, dst_ref=at, send_sem=send.at[g, 0], recv_sem=recv.at[g, mp * (Z * Y * C) + dp],
            device_id={"dp": sib[0], "mp": sib[1]}, device_id_type=MESH_ID,
        ).wait_recv()
        return at

    me = index(z, y, c)
    bias_copy = pltpu.make_async_remote_copy(
        src_ref=b_in, dst_ref=b_out.at[m], send_sem=bsem.at[0], recv_sem=bsem.at[1],
        device_id={"dp": me, "mp": 1 - m}, device_id_type=MESH_ID,
    )
    bias_copy.start()
    locals_ = [pltpu.make_async_copy(b_in, b_out.at[m], local.at[3])]
    for g in range(3):
        for to in pz + [one, two, sib]:
            push(g, shards[g], me, m, to)
        locals_.append(pltpu.make_async_copy(shards[g], spot(g, me, m), local.at[g]))
    for copy in locals_:
        copy.start()

    def stage_z(g):
        for k in (1, 3, 2):
            dp = index(lax.rem(z + k, Z), y, c)
            at = arrived(g, dp, m)
            for to in (one, two, sib):
                push(g, at, dp, m, to)

    def stage_one(g):
        for k in (0, 1, 3, 2):
            dp = index(lax.rem(z + k, Z), y1, c)
            at = arrived(g, dp, m1)
            for to in (two, sib):
                push(g, at, dp, m1, to)

    def stage_two(g):
        for k in (0, 1, 3, 2):
            for yy, mm in ((y2, m2), (1 - y, 1 - m)):
                dp = index(lax.rem(z + k, Z), yy, c)
                push(g, arrived(g, dp, mm), dp, mm, sib)

    def stage_core(g):
        for k in range(Z):
            for yy in range(Y):
                for mm in range(2):
                    arrived(g, index(k, yy, 1 - c), mm)

    stage_z(0)
    stage_one(0)
    stage_z(1)
    stage_two(0)
    stage_one(1)
    stage_z(2)
    stage_two(1)
    stage_one(2)
    stage_two(2)
    for g in range(3):
        stage_core(g)
    bias_copy.wait()
    for copy in locals_:
        copy.wait()
    for copy in started:
        copy.wait_send()


def gather_weights(first, second_a, second_b, bias):
    part, cols = second_a.shape
    vm = pl.BlockSpec(memory_space=pltpu.VMEM)
    hbm = pl.BlockSpec(memory_space=pl.ANY)
    total = Z * Y * C
    return pl.pallas_call(
        gather_kernel,
        in_specs=[vm] * 4,
        out_specs=[hbm] * 3,
        out_shape=[
            jax.ShapeDtypeStruct((2, total * part, first.shape[1]), LOW),
            jax.ShapeDtypeStruct((2, total * part, 2 * cols), LOW),
            jax.ShapeDtypeStruct((2,) + bias.shape, F32),
        ],
        scratch_shapes=[
            pltpu.SemaphoreType.DMA((3, 31)), pltpu.SemaphoreType.DMA((3, 32)),
            pltpu.SemaphoreType.DMA((2,)), pltpu.SemaphoreType.DMA((4,)),
        ],
        compiler_params=pltpu.CompilerParams(collective_id=0, has_side_effects=True, vmem_limit_bytes=32 * 2**20),
        name="gather_weights",
    )(first, second_a, second_b, bias)


def reduce_kernel(groups, with_small, *refs):
    grads = refs[:groups]
    pos = groups
    small = None
    if with_small:
        small = refs[pos]
        pos += 1
    outs = refs[pos : pos + groups]
    pos += groups
    if with_small:
        small_out = refs[pos]
        pos += 1
    per = [refs[pos + 7 * g : pos + 7 * (g + 1)] for g in range(groups)]
    pos += 7 * groups
    send, recv = refs[pos], refs[pos + 1]
    pos += 2
    z, y, c, m = place()
    (y1, m1), (y2, m2) = flips(y, c, m)
    part = outs[0].shape[0]
    peers = greet(z, y, c, m)
    pz, one, two, sib = peers[:3], peers[3], peers[4], peers[5]
    started = []
    count = [0] * groups

    def push(g, src, dst, sem, to):
        copy = pltpu.make_async_remote_copy(
            src_ref=src, dst_ref=dst, send_sem=send.at[g, count[g]], recv_sem=recv.at[g, sem],
            device_id={"dp": to[0], "mp": to[1]}, device_id_type=MESH_ID,
        )
        count[g] += 1
        copy.start()
        started.append(copy)

    def arrived(g, dst, sem):
        pltpu.make_async_remote_copy(
            src_ref=dst, dst_ref=dst, send_sem=send.at[g, 0], recv_sem=recv.at[g, sem],
            device_id={"dp": sib[0], "mp": sib[1]}, device_id_type=MESH_ID,
        ).wait_recv()

    def grad(g, zz, yy, cc, mm):
        return grads[g].at[mm, pl.ds(pl.multiple_of(index(zz, yy, cc) * part, part), part)]

    if with_small:
        sbuf, ssem = refs[pos], refs[pos + 1]

        def small_push(slot, src, to, sems):
            copy = pltpu.make_async_remote_copy(
                src_ref=src, dst_ref=sbuf.at[slot], send_sem=ssem.at[0, sems], recv_sem=ssem.at[1, sems],
                device_id={"dp": to[0], "mp": to[1]}, device_id_type=MESH_ID,
            )
            copy.start()
            return copy

        copies = [small_push(0, small, sib, 0)]

    (a1, b1), (a2, b2) = flips(y, 1 - c, m)
    order = [(3, 1 - y, 1 - m), (2, a2, b2), (1, a1, b1), (0, y, m)]
    turns = (1, 2, 3, 0)
    for slot, yy, mm in order:
        for k in turns:
            for g in range(groups):
                push(g, grad(g, lax.rem(z + k, Z), yy, 1 - c, mm), per[g][0].at[slot * Z + k], slot * Z + k, sib)

    def base(g, slot, k, yy, mm):
        arrived(g, per[g][0].at[slot * Z + k], slot * Z + k)
        return grad(g, lax.rem(z + k, Z), yy, c, mm)[...].astype(F32) + per[g][0][slot * Z + k].astype(F32)

    for slot, yy, mm in ((3, 1 - y, 1 - m), (2, y2, m2)):
        for k in turns:
            for g in range(groups):
                at = (slot - 2) * Z + k
                per[g][1][at] = base(g, slot, k, yy, mm).astype(LOW)
                push(g, per[g][1].at[at], per[g][2].at[at], 16 + at, two)
    if with_small:
        copies[0].wait()
        sbuf[6] = small[...] + sbuf[0]
        copies.append(small_push(1, sbuf.at[6], one, 1))

    def second(g, slot, k, yy, mm):
        value = base(g, slot, k, yy, mm)
        at = slot * Z + k
        arrived(g, per[g][2].at[at], 16 + at)
        return value + per[g][2][at].astype(F32)

    for k in turns:
        for g in range(groups):
            per[g][3][k] = second(g, 1, k, y1, m1).astype(LOW)
            push(g, per[g][3].at[k], per[g][4].at[k], 24 + k, one)
    if with_small:
        copies[1].wait()
        sbuf[7] = sbuf[6] + sbuf[1]
        copies.append(small_push(2, sbuf.at[7], two, 2))

    def third(g, k):
        value = second(g, 0, k, y, m)
        arrived(g, per[g][4].at[k], 24 + k)
        return value + per[g][4][k].astype(F32)

    for k in (1, 2, 3):
        for g in range(groups):
            per[g][5][k] = third(g, k).astype(LOW)
            push(g, per[g][5].at[k], per[g][6].at[k], 28 + k - 1, pz[k - 1])
    if with_small:
        copies[2].wait()
        sbuf[8] = sbuf[7] + sbuf[2]
        for k in (1, 2, 3):
            copies.append(small_push(2 + k, sbuf.at[8], pz[k - 1], 2 + k))
    for g in range(groups):
        total = third(g, 0)
        for k in (1, 2, 3):
            arrived(g, per[g][6].at[k], 28 + k - 1)
            total = total + per[g][6][k].astype(F32)
        outs[g][...] = total
    if with_small:
        for copy in copies[3:]:
            copy.wait()
        small_out[...] = sbuf[8] + sbuf[3] + sbuf[4] + sbuf[5]
    for copy in started:
        copy.wait_send()


def reduce_grads(grads, small, ident):
    groups = len(grads)
    vm = pl.BlockSpec(memory_space=pltpu.VMEM)
    total = Z * Y * C
    part = grads[0].shape[1] // total
    scratch = []
    for g in grads:
        cols = g.shape[2]
        scratch += [pltpu.VMEM((n, part, cols), LOW) for n in (16, 8, 8, 4, 4, 4, 4)]
    scratch += [pltpu.SemaphoreType.DMA((groups, 31)), pltpu.SemaphoreType.DMA((groups, 31))]
    ins = list(grads)
    out_shape = [jax.ShapeDtypeStruct((part, g.shape[2]), F32) for g in grads]
    if small is not None:
        ins.append(small)
        out_shape.append(jax.ShapeDtypeStruct(small.shape, F32))
        scratch += [pltpu.VMEM((9,) + small.shape, F32), pltpu.SemaphoreType.DMA((2, 6))]
    return pl.pallas_call(
        functools.partial(reduce_kernel, groups, small is not None),
        in_specs=[vm] * len(ins),
        out_specs=[vm] * len(out_shape),
        out_shape=out_shape,
        scratch_shapes=scratch,
        compiler_params=pltpu.CompilerParams(collective_id=ident, has_side_effects=True, vmem_limit_bytes=60 * 2**20),
        name=f"reduce_grads_{ident}",
    )(*ins)


def per_device(
    patch_counts, tokens, cotangent, attn_gain, attn_shift, w_qkv, b_qv, w_proj, b_proj,
    ffn_gain, ffn_shift, w_up, b_up, w_down, b_down,
):
    pairs_all, rows, width = tokens.shape
    n_mp = lax.axis_size("mp")
    n_dp = lax.axis_size("dp")
    direct = n_dp == Z * Y * C and n_mp == 2
    pairs = pairs_all // n_mp
    part = w_qkv.shape[0]
    lw = w_qkv.shape[2]
    fw = w_up.shape[1]
    mine = lax.axis_index("mp")
    off = jnp.reshape(mine * pairs, (1,)).astype(jnp.int32)
    lens = TEXT + lax.dynamic_slice_in_dim(patch_counts, mine * pairs, pairs, 0)

    vectors = jnp.stack([attn_gain, attn_shift, b_proj, ffn_gain, ffn_shift, b_down], axis=1)
    first = jnp.concatenate(
        [w_qkv.reshape(part, 3 * lw), w_proj.T, vectors, jnp.zeros((part, EXTRA - 6), F32)], axis=1
    ).astype(LOW)
    second_a = w_up.astype(LOW)
    second_b = w_down.T.astype(LOW)
    bias = jnp.concatenate([b_qv.reshape(-1), b_up]).astype(LOW).astype(F32)
    bias = jnp.broadcast_to(bias, (8,) + bias.shape)
    if direct:
        w_one, w_two, bias = gather_weights(first, second_a, second_b, bias)
    else:
        both_axes = ("mp", "dp")
        w_one = lax.all_gather(first, both_axes, axis=0, tiled=True).reshape(n_mp, width, -1)
        second = jnp.concatenate([second_a, second_b], axis=1)
        w_two = lax.all_gather(second, both_axes, axis=0, tiled=True).reshape(n_mp, width, -1)
        bias = lax.all_gather(bias, "mp", axis=0)

    qkv, att, prob, hid, n1, n2, vec = attention_forward(lens, off, tokens, w_one, bias)
    out_here, act, dpre, dhid, dlow, upl, sums_two, bsum_up = ffn(lens, off, n2, hid, cotangent, w_two, bias, vec)

    def grad(left, right):
        cols = right.shape[2] // n_mp
        return jnp.einsum(
            "rd,rmf->mdf", left.reshape(pairs * rows, width), right.reshape(pairs * rows, n_mp, cols),
            preferred_element_type=F32,
        )

    def reduce(grads, small, ident):
        if direct:
            return reduce_grads([g.astype(LOW) for g in grads], small, ident)
        axes = ("mp", "dp")
        done = [
            lax.psum_scatter(g.reshape(n_mp * width, -1), axes, scatter_dimension=0, tiled=True) for g in grads
        ]
        if small is not None:
            done.append(lax.psum(small, axes))
        return done

    def both(array):
        other = lax.ppermute(array, "mp", [(0, 1), (1, 0)])
        return jnp.where(mine == 0, jnp.concatenate([array, other]), jnp.concatenate([other, array]))

    r_up, r_down, r_proj = reduce([grad(n2, dpre), grad(upl, act), grad(dlow, att)], None, 1)
    tok_here, dqkv, sums_one, bsum_qkv = attention_backward(lens, off, tokens, dhid, qkv, prob, w_one, vec)
    block_out = both(out_here)
    tokens_grad = both(tok_here)
    flat = bsum_qkv[0].reshape(n_mp, 3, lw)
    small = jnp.concatenate([
        sums_one[0], sums_one[1], sums_two[2], sums_two[0], sums_two[1], sums_two[3],
        flat[:, 0].reshape(-1), flat[:, 2].reshape(-1), bsum_up[0]])
    r_qkv, small = reduce([grad(n1, dqkv)], small.reshape(8, -1), 2)
    small = small.reshape(-1)
    place_dp = lax.axis_index("dp") * part

    def piece(i):
        return lax.dynamic_slice_in_dim(small, i * width + place_dp, part, 0)

    rest = small[6 * width :]
    o_b_q = lax.dynamic_slice_in_dim(rest, mine * lw, lw, 0)
    o_b_v = lax.dynamic_slice_in_dim(rest, (n_mp + mine) * lw, lw, 0)
    o_b_up = lax.dynamic_slice_in_dim(rest, 2 * n_mp * lw + mine * fw, fw, 0)
    return (
        block_out, tokens_grad, piece(0), piece(1),
        r_qkv.reshape(part, 3, lw), jnp.stack([o_b_q, o_b_v]),
        r_proj.T, piece(2), piece(3), piece(4), r_up, o_b_up, r_down.T, piece(5),
    )


def solution(mesh):
    vec, mat = P("dp"), P("dp", "mp")
    tok = P("dp", None, None)
    in_specs = (
        vec, tok, tok, vec, vec, P("dp", None, "mp"), P(None, "mp"), P("mp", "dp"), vec, vec, vec,
        mat, P("mp"), P("mp", "dp"), vec,
    )
    out_specs = (
        tok, tok, vec, vec, P("dp", None, "mp"), P(None, "mp"), P("mp", "dp"), vec, vec, vec,
        mat, P("mp"), P("mp", "dp"), vec,
    )
    return jax.shard_map(per_device, mesh=mesh, in_specs=in_specs, out_specs=out_specs, check_vma=False)
```

```python
import functools

import jax
import jax.numpy as jnp
from jax import lax
from jax.experimental import pallas as pl
from jax.experimental.pallas import tpu as pltpu
from jax.sharding import PartitionSpec as P

HEADS = 12
HEAD_DIM = 64
TEXT = 40
LOW = jnp.bfloat16
F32 = jnp.float32
EXTRA = 128
NT = (((1,), (1,)), ((), ()))
NN = (((1,), (0,)), ((), ()))


def dot(a, b, dims=NN):
    return lax.dot_general(a, b, dims, preferred_element_type=F32)


def moments(v):
    center = v - jnp.mean(v, axis=-1, keepdims=True)
    spread = jnp.mean(center * center, axis=-1, keepdims=True)
    r = lax.rsqrt(spread + 1e-06)
    return center * r, r


def row_ids(rows):
    return lax.broadcasted_iota(jnp.int32, (rows, 1), 0)


def attn_kernel(lens, off, x_ref, w_ref, bias_ref, qkv_ref, att_ref, prob_ref, hid_ref, n1_ref, n2_ref, vec_ref):
    p = pl.program_id(0)
    rows, width = x_ref.shape[1], x_ref.shape[2]
    groups = w_ref.shape[0]
    lw = width // groups
    tiles = lw // 128

    @pl.when(p == 0)
    def _():
        vec_ref[...] = w_ref[0, :, 4 * lw :].astype(F32).T[:8]

    x = x_ref[0].astype(F32)
    xhat, _ = moments(x)
    n1 = (xhat * vec_ref[0:1] + vec_ref[1:2]).astype(LOW)
    n1_ref[0] = n1
    for m in range(groups):
        y = dot(n1, w_ref[m, :, : 3 * lw])
        base = m * 3 * lw
        qkv_ref[0, :, base : base + lw] = (y[:, :lw] + bias_ref[m, 0:1, :lw]).astype(LOW)
        qkv_ref[0, :, base + lw : base + 2 * lw] = y[:, lw : 2 * lw].astype(LOW)
        qkv_ref[0, :, base + 2 * lw : base + 3 * lw] = (
            y[:, 2 * lw :] + bias_ref[m, 0:1, lw : 2 * lw]
        ).astype(LOW)
    count = lens[p]
    keep = row_ids(rows) < count
    first = lax.broadcasted_iota(jnp.int32, (1, 128), 1) < HEAD_DIM

    def pair(hp, carry):
        base = (hp // tiles) * 3 * lw + (hp % tiles) * 128

        def cols(t):
            return pl.ds(pl.multiple_of(base + t * lw, 128), 128)

        q2 = qkv_ref[0, :, cols(0)] * 0.125
        k2 = qkv_ref[0, :, cols(1)]
        v2t = qkv_ref[0, :, cols(2)].T
        outs = []
        for h in range(2):
            qh = jnp.where(first if h == 0 else ~first, q2, 0)
            st = dot(k2, qh, NT)
            st = jnp.where(keep, st, -1e30)
            e = jnp.exp(st - jnp.max(st, axis=0, keepdims=True))
            pt = (e * (1.0 / jnp.sum(e, axis=0, keepdims=True))).astype(LOW)
            prob_ref[0, hp * 2 + h] = pt
            outs.append(dot(v2t[h * HEAD_DIM : (h + 1) * HEAD_DIM], pt))
        att_ref[0, :, pl.ds(pl.multiple_of(hp * 128, 128), 128)] = jnp.concatenate(outs, axis=0).T.astype(LOW)
        return carry

    lax.fori_loop(0, groups * tiles, pair, 0)
    proj = sum(dot(att_ref[0, :, m * lw : (m + 1) * lw], w_ref[m, :, 3 * lw : 4 * lw], NT) for m in range(groups))
    hid = x + proj + vec_ref[2:3]
    hid_ref[0] = hid
    xhat2, _ = moments(hid)
    n2_ref[0] = (xhat2 * vec_ref[3:4] + vec_ref[4:5]).astype(LOW)


def const_spec(shape):
    return pl.BlockSpec(shape, lambda *_: (0,) * len(shape), pipeline_mode=pl.Buffered(1))


def pair_spec(*shape):
    return pl.BlockSpec((1,) + shape, lambda p, *_: (p,) + (0,) * len(shape))


def attention_forward(lens, off, tokens, w_one, bias):
    pairs = lens.shape[0]
    _, rows, width = tokens.shape
    out = lambda dt, *s: jax.ShapeDtypeStruct((pairs,) + s, dt)
    return pl.pallas_call(
        attn_kernel,
        grid_spec=pltpu.PrefetchScalarGridSpec(
            num_scalar_prefetch=2,
            grid=(pairs,),
            in_specs=[
                pl.BlockSpec((1, rows, width), lambda p, lens, off: (off[0] + p, 0, 0)),
                const_spec(w_one.shape),
                const_spec(bias.shape),
            ],
            out_specs=[
                pair_spec(rows, 3 * width), pair_spec(rows, width), pair_spec(HEADS, rows, rows),
                pair_spec(rows, width), pair_spec(rows, width), pair_spec(rows, width),
                pl.BlockSpec((8, width), lambda *_: (0, 0)),
            ],
        ),
        out_shape=[
            out(LOW, rows, 3 * width), out(LOW, rows, width), out(LOW, HEADS, rows, rows),
            out(F32, rows, width), out(LOW, rows, width), out(LOW, rows, width),
            jax.ShapeDtypeStruct((8, width), F32),
        ],
        compiler_params=pltpu.CompilerParams(vmem_limit_bytes=60 * 2**20),
        name="attention_forward",
    )(lens, off, tokens, w_one, bias)


def ffn_kernel(lens, off, n2_ref, hid_ref, cot_ref, w_ref, bias_ref, vec_ref,
               out_ref, act_ref, dpre_ref, dhid_ref, dlow_ref, upl_ref, sums_ref, bsum_ref):
    p = pl.program_id(0)
    rows, width = n2_ref.shape[1], n2_ref.shape[2]
    groups = w_ref.shape[0]
    fw = w_ref.shape[2] // 2
    lw = width // groups
    step = 512
    keep = row_ids(rows) < lens[p]
    n2 = n2_ref[0]
    upl = jnp.where(keep, cot_ref[0], 0)
    upl_ref[0] = upl

    @pl.when(p == 0)
    def _():
        sums_ref[...] = jnp.zeros_like(sums_ref)
        bsum_ref[...] = jnp.zeros_like(bsum_ref)

    for m in range(groups):
        for c in range(0, fw, step):
            pre = dot(n2, w_ref[m, :, c : c + step]) + bias_ref[m, 0:1, 2 * lw + c : 2 * lw + c + step]
            cdf = 0.5 * (1.0 + lax.erf(pre * (2.0 ** -0.5)))
            at = m * fw + c
            act_ref[0, :, at : at + step] = (pre * cdf).astype(LOW)
            slope = cdf + pre * (0.3989422804014327 * jnp.exp(-0.5 * pre * pre))
            dpre = slope * dot(upl, w_ref[m, :, fw + c : fw + c + step])
            dpre_ref[0, :, at : at + step] = dpre.astype(LOW)
            bsum_ref[0:1, at : at + step] += jnp.sum(dpre, axis=0, keepdims=True)
    hid = hid_ref[0]
    down = sum(dot(act_ref[0, :, m * fw : (m + 1) * fw], w_ref[m, :, fw:], NT) for m in range(groups))
    out_ref[0] = jnp.where(keep, hid + down + vec_ref[5:6], 0.0).astype(LOW)
    dtwo = sum(dot(dpre_ref[0, :, m * fw : (m + 1) * fw], w_ref[m, :, :fw], NT) for m in range(groups))
    xhat, r = moments(hid)
    dg = dtwo * vec_ref[3:4]
    dn = r * (dg - jnp.mean(dg, axis=-1, keepdims=True) - xhat * jnp.mean(dg * xhat, axis=-1, keepdims=True))
    upf = upl.astype(F32)
    dhid = upf + dn
    dhid_ref[0] = dhid
    dlow_ref[0] = dhid.astype(LOW)
    sums_ref[0:1] += jnp.sum(dtwo * xhat, axis=0, keepdims=True)
    sums_ref[1:2] += jnp.sum(dtwo, axis=0, keepdims=True)
    sums_ref[2:3] += jnp.sum(dhid, axis=0, keepdims=True)
    sums_ref[3:4] += jnp.sum(upf, axis=0, keepdims=True)


def ffn(lens, off, n2, hid, cotangent, w_two, bias, vec):
    pairs, rows, width = n2.shape
    ff = w_two.shape[0] * w_two.shape[2] // 2
    out = lambda dt, *s: jax.ShapeDtypeStruct((pairs,) + s, dt)
    return pl.pallas_call(
        ffn_kernel,
        grid_spec=pltpu.PrefetchScalarGridSpec(
            num_scalar_prefetch=2,
            grid=(pairs,),
            in_specs=[
                pair_spec(rows, width), pair_spec(rows, width),
                pl.BlockSpec((1, rows, width), lambda p, lens, off: (off[0] + p, 0, 0)),
                const_spec(w_two.shape), const_spec(bias.shape), const_spec(vec.shape),
            ],
            out_specs=[
                pair_spec(rows, width), pair_spec(rows, ff), pair_spec(rows, ff), pair_spec(rows, width),
                pair_spec(rows, width), pair_spec(rows, width),
                pl.BlockSpec((8, width), lambda *_: (0, 0)), pl.BlockSpec((8, ff), lambda *_: (0, 0)),
            ],
        ),
        out_shape=[
            out(LOW, rows, width), out(LOW, rows, ff), out(LOW, rows, ff), out(F32, rows, width),
            out(LOW, rows, width), out(LOW, rows, width),
            jax.ShapeDtypeStruct((8, width), F32), jax.ShapeDtypeStruct((8, ff), F32),
        ],
        compiler_params=pltpu.CompilerParams(vmem_limit_bytes=60 * 2**20),
        name="feed_forward",
    )(lens, off, n2, hid, cotangent, w_two, bias, vec)


def plain_back_kernel(lens, off, x_ref, dhid_ref, qkv_ref, prob_ref, w_ref, vec_ref,
                tok_ref, dqkv_ref, sums_ref, bsum_ref, do_ref):
    p = pl.program_id(0)
    rows, width = x_ref.shape[1], x_ref.shape[2]
    groups = w_ref.shape[0]
    lw = width // groups
    tiles = lw // 128

    @pl.when(p == 0)
    def _():
        sums_ref[...] = jnp.zeros_like(sums_ref)
        bsum_ref[...] = jnp.zeros_like(bsum_ref)

    dhid = dhid_ref[0]
    dlow = dhid.astype(LOW)
    for m in range(groups):
        do_ref[:, m * lw : (m + 1) * lw] = dot(dlow, w_ref[m, :, 3 * lw : 4 * lw]).astype(LOW)
    first = lax.broadcasted_iota(jnp.int32, (1, 128), 1) < HEAD_DIM

    def pair(hp, carry):
        base = (hp // tiles) * 3 * lw + (hp % tiles) * 128

        def cols(t):
            return pl.ds(pl.multiple_of(base + t * lw, 128), 128)

        q2 = qkv_ref[0, :, cols(0)] * 0.125
        k2t = qkv_ref[0, :, cols(1)].T
        v2 = qkv_ref[0, :, cols(2)]
        do2 = do_ref[:, pl.ds(pl.multiple_of(hp * 128, 128), 128)]
        dq_t = []
        dk = dv = 0.0
        for h in range(2):
            mine = first if h == 0 else ~first
            doh = jnp.where(mine, do2, 0)
            qh = jnp.where(mine, q2, 0)
            dpt = dot(v2, doh, NT)
            plow = prob_ref[0, hp * 2 + h]
            pt = plow.astype(F32)
            inner = jnp.sum(pt * dpt, axis=0, keepdims=True)
            dst = (pt * (dpt - inner)).astype(LOW)
            dv = dv + dot(plow, doh)
            dk = dk + dot(dst, qh)
            dq_t.append(dot(k2t[h * HEAD_DIM : (h + 1) * HEAD_DIM], dst))
        dq = (jnp.concatenate(dq_t, axis=0) * 0.125).T
        dqkv_ref[0, :, cols(0)] = dq.astype(LOW)
        dqkv_ref[0, :, cols(1)] = dk.astype(LOW)
        dqkv_ref[0, :, cols(2)] = dv.astype(LOW)
        bsum_ref[0:1, cols(0)] += jnp.sum(dq, axis=0, keepdims=True)
        bsum_ref[0:1, cols(2)] += jnp.sum(dv, axis=0, keepdims=True)
        return carry

    lax.fori_loop(0, groups * tiles, pair, 0)
    done = sum(dot(dqkv_ref[0, :, m * 3 * lw : (m + 1) * 3 * lw], w_ref[m, :, : 3 * lw], NT) for m in range(groups))
    xhat, r = moments(x_ref[0].astype(F32))
    dg = done * vec_ref[0:1]
    dn = r * (dg - jnp.mean(dg, axis=-1, keepdims=True) - xhat * jnp.mean(dg * xhat, axis=-1, keepdims=True))
    tok_ref[0] = (dhid + dn).astype(LOW)
    sums_ref[0:1] += jnp.sum(done * xhat, axis=0, keepdims=True)
    sums_ref[1:2] += jnp.sum(done, axis=0, keepdims=True)


def attention_backward(lens, off, tokens, dhid, qkv, prob, w_one, vec):
    pairs, rows, width = dhid.shape
    out = lambda dt, *s: jax.ShapeDtypeStruct((pairs,) + s, dt)
    return pl.pallas_call(
        plain_back_kernel,
        grid_spec=pltpu.PrefetchScalarGridSpec(
            num_scalar_prefetch=2,
            grid=(pairs,),
            in_specs=[
                pl.BlockSpec((1, rows, width), lambda p, lens, off: (off[0] + p, 0, 0)),
                pair_spec(rows, width), pair_spec(rows, 3 * width), pair_spec(HEADS, rows, rows),
                const_spec(w_one.shape), const_spec(vec.shape),
            ],
            out_specs=[
                pair_spec(rows, width), pair_spec(rows, 3 * width),
                pl.BlockSpec((8, width), lambda *_: (0, 0)), pl.BlockSpec((8, 3 * width), lambda *_: (0, 0)),
            ],
            scratch_shapes=[pltpu.VMEM((rows, width), LOW)],
        ),
        out_shape=[
            out(LOW, rows, width), out(LOW, rows, 3 * width),
            jax.ShapeDtypeStruct((8, width), F32), jax.ShapeDtypeStruct((8, 3 * width), F32),
        ],
        compiler_params=pltpu.CompilerParams(vmem_limit_bytes=60 * 2**20),
        name="attention_backward",
    )(lens, off, tokens, dhid, qkv, prob, w_one, vec)
MESH_ID = pl.DeviceIdType.MESH
Z, Y, C = 4, 2, 2


def place():
    dp = lax.axis_index("dp")
    m = lax.axis_index("mp")
    c = lax.rem(dp, 2)
    y = lax.rem(dp // 2, 2)
    z = dp // 4
    return z, y, c, m


def index(z, y, c):
    return (z * Y + y) * C + c


def flips(y, c, m):
    one = (y + c * (1 - 2 * y), m + (1 - c) * (1 - 2 * m))
    two = (y + (1 - c) * (1 - 2 * y), m + c * (1 - 2 * m))
    return one, two


def greet(z, y, c, m):
    barrier = pltpu.get_barrier_semaphore()
    (y1, m1), (y2, m2) = flips(y, c, m)
    peers = [(index(lax.rem(z + k, Z), y, c), m) for k in (1, 2, 3)]
    peers += [(index(z, y1, c), m1), (index(z, y2, c), m2), (index(z, y, 1 - c), m)]
    for dp, mp in peers:
        pl.semaphore_signal(barrier, inc=1, device_id={"dp": dp, "mp": mp}, device_id_type=MESH_ID)
    pl.semaphore_wait(barrier, len(peers))
    return peers


def gather_kernel(s0, s1, s2, b_in, w_one, w_two, b_out, send, recv, bsem, local):
    z, y, c, m = place()
    (y1, m1), (y2, m2) = flips(y, c, m)
    part, cols = s1.shape
    peers = greet(z, y, c, m)
    pz, one, two, sib = peers[:3], peers[3], peers[4], peers[5]
    shards = (s0, s1, s2)

    def spot(g, dp, mp):
        rows = pl.ds(pl.multiple_of(dp * part, part), part)
        if g == 0:
            return w_one.at[mp, rows]
        return w_two.at[mp, rows, (g - 1) * cols : g * cols]

    started = []
    count = [0, 0, 0]

    def push(g, src, dp, mp, to):
        copy = pltpu.make_async_remote_copy(
            src_ref=src, dst_ref=spot(g, dp, mp), send_sem=send.at[g, count[g]],
            recv_sem=recv.at[g, mp * (Z * Y * C) + dp],
            device_id={"dp": to[0], "mp": to[1]}, device_id_type=MESH_ID,
        )
        count[g] += 1
        copy.start()
        started.append(copy)

    def arrived(g, dp, mp):
        at = spot(g, dp, mp)
        pltpu.make_async_remote_copy(
            src_ref=at, dst_ref=at, send_sem=send.at[g, 0], recv_sem=recv.at[g, mp * (Z * Y * C) + dp],
            device_id={"dp": sib[0], "mp": sib[1]}, device_id_type=MESH_ID,
        ).wait_recv()
        return at

    me = index(z, y, c)
    bias_copy = pltpu.make_async_remote_copy(
        src_ref=b_in, dst_ref=b_out.at[m], send_sem=bsem.at[0], recv_sem=bsem.at[1],
        device_id={"dp": me, "mp": 1 - m}, device_id_type=MESH_ID,
    )
    bias_copy.start()
    locals_ = [pltpu.make_async_copy(b_in, b_out.at[m], local.at[3])]
    for g in range(3):
        for to in pz + [one, two, sib]:
            push(g, shards[g], me, m, to)
        locals_.append(pltpu.make_async_copy(shards[g], spot(g, me, m), local.at[g]))
    for copy in locals_:
        copy.start()

    def stage_z(g):
        for k in (1, 3, 2):
            dp = index(lax.rem(z + k, Z), y, c)
            at = arrived(g, dp, m)
            for to in (one, two, sib):
                push(g, at, dp, m, to)

    def stage_one(g):
        for k in (0, 1, 3, 2):
            dp = index(lax.rem(z + k, Z), y1, c)
            at = arrived(g, dp, m1)
            for to in (two, sib):
                push(g, at, dp, m1, to)

    def stage_two(g):
        for k in (0, 1, 3, 2):
            for yy, mm in ((y2, m2), (1 - y, 1 - m)):
                dp = index(lax.rem(z + k, Z), yy, c)
                push(g, arrived(g, dp, mm), dp, mm, sib)

    def stage_core(g):
        for k in range(Z):
            for yy in range(Y):
                for mm in range(2):
                    arrived(g, index(k, yy, 1 - c), mm)

    stage_z(0)
    stage_one(0)
    stage_z(1)
    stage_two(0)
    stage_one(1)
    stage_z(2)
    stage_two(1)
    stage_one(2)
    stage_two(2)
    for g in range(3):
        stage_core(g)
    bias_copy.wait()
    for copy in locals_:
        copy.wait()
    for copy in started:
        copy.wait_send()


def gather_weights(first, second_a, second_b, bias):
    part, cols = second_a.shape
    vm = pl.BlockSpec(memory_space=pltpu.VMEM)
    hbm = pl.BlockSpec(memory_space=pl.ANY)
    total = Z * Y * C
    return pl.pallas_call(
        gather_kernel,
        in_specs=[vm] * 4,
        out_specs=[hbm] * 3,
        out_shape=[
            jax.ShapeDtypeStruct((2, total * part, first.shape[1]), LOW),
            jax.ShapeDtypeStruct((2, total * part, 2 * cols), LOW),
            jax.ShapeDtypeStruct((2,) + bias.shape, F32),
        ],
        scratch_shapes=[
            pltpu.SemaphoreType.DMA((3, 31)), pltpu.SemaphoreType.DMA((3, 32)),
            pltpu.SemaphoreType.DMA((2,)), pltpu.SemaphoreType.DMA((4,)),
        ],
        compiler_params=pltpu.CompilerParams(collective_id=0, has_side_effects=True, vmem_limit_bytes=32 * 2**20),
        name="gather_weights",
    )(first, second_a, second_b, bias)


BLOCKS = 31


def back_kernel(tok_all, dhid_ref, qkv_ref, prob_ref, n1_ref, w_ref, vec_ref, g_up, g_down, g_proj, sums_two, bsum_up,
                tok_ref, tok_other, r_up, r_down, r_proj, r_qkv, small_out,
                do_ref, xbuf, tokbuf, n1t, dq_all, gq, sums, bsum,
                own_up, own_down, own_proj, rc0, rs0, rz0, rx0, rc1, rs1, rz1, rx1, rc2, rs2, rz2, rx2,
                rc3, rs3, rz3, rx3, sbuf, send, recv, local, tsem, ssem):
    p = pl.program_id(0)
    pairs, rows, width = xbuf.shape
    groups = w_ref.shape[0]
    lw = width // groups
    tiles = lw // 128
    z, y, c, m = place()
    outs = (r_up, r_down, r_proj, r_qkv)
    grads = (g_up, g_down, g_proj, gq)
    owns = (own_up, own_down, own_proj)
    rcs, rss, rzs, rxs = (rc0, rc1, rc2, rc3), (rs0, rs1, rs2, rs3), (rz0, rz1, rz2, rz3), (rx0, rx1, rx2, rx3)
    part = r_up.shape[0]
    me = index(z, y, c)
    sib = (index(z, y, 1 - c), m)

    def beside(k):
        return (index(lax.rem(z + k, Z), y, c), m)

    def x_first(g, cc):
        return cc if g == 0 else 0

    def target(g, cc, ra, rb):
        fx = x_first(g, cc)
        dy = fx * rb + (1 - fx) * ra
        dm = fx * ra + (1 - fx) * rb
        return y + dy * (1 - 2 * y), m + dm * (1 - 2 * m)

    def chip(g, ra, rb):
        yy, mm = target(g, c, ra, rb)
        return (index(z, yy, c), mm)

    def column(g, mm):
        cols = outs[g].shape[1]
        return pl.ds(pl.multiple_of(mm * cols, 128), cols)

    def copy_of(g, src, dst, out_sem, in_sem, to):
        return pltpu.make_async_remote_copy(
            src_ref=src, dst_ref=dst, send_sem=send.at[g, out_sem], recv_sem=recv.at[g, in_sem],
            device_id={"dp": to[0], "mp": to[1]}, device_id_type=MESH_ID,
        )

    def to_sibling(g):
        def one(i, carry):
            slot = 15 - i
            ra, rb, k = slot // 8, lax.rem(slot // 4, 2), lax.rem(slot, 4)
            yy, mm = target(g, 1 - c, ra, rb)
            src = grads[g].at[lax.rem(z + k, Z) * Y + yy, 1 - c, :, column(g, mm)]
            copy_of(g, src, rcs[g].at[slot], slot, slot, sib).start()
            return carry

        lax.fori_loop(0, 16, one, 0)

    def arrived(g, ref, sem):
        copy_of(g, ref, ref, 0, sem, sib).wait_recv()

    def base(g, ra, rb, k):
        slot = (ra * 2 + rb) * 4 + k
        arrived(g, rcs[g].at[slot], slot)
        yy, mm = target(g, c, ra, rb)
        row = lax.rem(z + k, Z) * Y + yy
        mine = owns[g][row, :, column(g, mm)] if g < 3 else gq[row, c, :, column(g, mm)]
        return mine.astype(F32) + rcs[g][slot].astype(F32)

    def level(g, rb, k):
        value = base(g, 0, rb, k)
        at = rb * 4 + k
        arrived(g, rss[g].at[at], 16 + at)
        return value + rss[g][at].astype(F32)

    def lined(g, rb):
        value = level(g, rb, 0)
        for k in (1, 2, 3):
            at = (k - 1) * 2 + rb
            arrived(g, rzs[g].at[at], 24 + at)
            value = value + rzs[g][at].astype(F32)
        return value

    def event_s(g, r):
        rb, k = 1 - r // 4, lax.rem(r + 1, 4)
        slot = (2 + rb) * 4 + k
        at = rb * 4 + k
        rcs[g][slot] = base(g, 1, rb, k).astype(LOW)
        copy_of(g, rcs[g].at[slot], rss[g].at[at], 16 + at, 16 + at, chip(g, 1, 0)).start()

    def event_z(g, r):
        rb, k = 1 - lax.rem(r, 2), 1 + r // 2
        slot = rb * 4 + k
        at = (k - 1) * 2 + rb
        rcs[g][slot] = level(g, rb, k).astype(LOW)
        copy_of(g, rcs[g].at[slot], rzs[g].at[at], 24 + at, 24 + at, beside(k)).start()

    def event_x(g):
        rcs[g][4] = lined(g, 1).astype(LOW)
        copy_of(g, rcs[g].at[4], rxs[g].at[0], 30, 30, chip(g, 0, 1)).start()

    def final(g):
        value = lined(g, 0)
        arrived(g, rxs[g].at[0], 30)
        outs[g][...] = value + rxs[g][0].astype(F32)

        def one(i, carry):
            copy_of(g, rcs[g].at[0], rcs[g].at[0], i, 0, sib).wait_send()
            return carry

        lax.fori_loop(0, BLOCKS, one, 0)

    def tok_copy(i):
        return pltpu.make_async_remote_copy(
            src_ref=tokbuf.at[i], dst_ref=tok_other.at[i], send_sem=tsem.at[0, i], recv_sem=tsem.at[1, i],
            device_id={"dp": me, "mp": 1 - m}, device_id_type=MESH_ID,
        )

    def own_copy(g):
        return pltpu.make_async_copy(grads[g].at[:, c], owns[g], local.at[g])

    x_copy = pltpu.make_async_copy(tok_all.at[pl.ds(m * pairs, pairs)], xbuf, local.at[3])

    @pl.when(p == 0)
    def _():
        for g in range(3):
            own_copy(g).start()
        x_copy.start()
        greet(z, y, c, m)
        for g in range(3):
            to_sibling(g)
        sums[...] = jnp.zeros_like(sums)
        bsum[...] = jnp.zeros_like(bsum)
        for g in range(3):
            own_copy(g).wait()
        x_copy.wait()

    dhid = dhid_ref[0]
    dlow = dhid.astype(LOW)
    for mm in range(groups):
        do_ref[:, mm * lw : (mm + 1) * lw] = dot(dlow, w_ref[mm, :, 3 * lw : 4 * lw]).astype(LOW)
    n1t[p] = n1_ref[0].T
    first = lax.broadcasted_iota(jnp.int32, (1, 128), 1) < HEAD_DIM

    def pair(hp, carry):
        lane = (hp // tiles) * 3 * lw + lax.rem(hp, tiles) * 128

        def cols(t):
            return pl.ds(pl.multiple_of(lane + t * lw, 128), 128)

        q2 = qkv_ref[0, :, cols(0)] * 0.125
        k2t = qkv_ref[0, :, cols(1)].T
        v2 = qkv_ref[0, :, cols(2)]
        do2 = do_ref[:, pl.ds(pl.multiple_of(hp * 128, 128), 128)]
        dq_t = []
        dk = dv = 0.0
        for h in range(2):
            mine = first if h == 0 else ~first
            doh = jnp.where(mine, do2, 0)
            qh = jnp.where(mine, q2, 0)
            dpt = dot(v2, doh, NT)
            plow = prob_ref[0, hp * 2 + h]
            pt = plow.astype(F32)
            inner = jnp.sum(pt * dpt, axis=0, keepdims=True)
            dst = (pt * (dpt - inner)).astype(LOW)
            dv = dv + dot(plow, doh)
            dk = dk + dot(dst, qh)
            dq_t.append(dot(k2t[h * HEAD_DIM : (h + 1) * HEAD_DIM], dst))
        dq = (jnp.concatenate(dq_t, axis=0) * 0.125).T
        dq_all[p, :, cols(0)] = dq.astype(LOW)
        dq_all[p, :, cols(1)] = dk.astype(LOW)
        dq_all[p, :, cols(2)] = dv.astype(LOW)
        bsum[0:1, cols(0)] += jnp.sum(dq, axis=0, keepdims=True)
        bsum[0:1, cols(2)] += jnp.sum(dv, axis=0, keepdims=True)

        step = p * (groups * tiles) + hp
        for g in range(3):

            @pl.when((step >= 4 * g) & (step < 4 * g + 4))
            def _():
                event_s(g, 2 * step - 8 * g)
                event_s(g, 2 * step - 8 * g + 1)

        @pl.when((step >= 17) & (step < 23))
        def _():
            event_z(0, step - 17)

        return carry

    lax.fori_loop(0, groups * tiles, pair, 0)
    done = sum(dot(dq_all[p, :, mm * 3 * lw : (mm + 1) * 3 * lw], w_ref[mm, :, : 3 * lw], NT) for mm in range(groups))
    xhat, r = moments(xbuf[p].astype(F32))
    dg = done * vec_ref[0:1]
    dn = r * (dg - jnp.mean(dg, axis=-1, keepdims=True) - xhat * jnp.mean(dg * xhat, axis=-1, keepdims=True))
    tok = (dhid + dn).astype(LOW)
    tok_ref[0] = tok
    tokbuf[p] = tok
    tok_copy(p).start()
    sums[0:1] += jnp.sum(done * xhat, axis=0, keepdims=True)
    sums[1:2] += jnp.sum(done, axis=0, keepdims=True)

    def small_copy(slot, src, to, sem):
        return pltpu.make_async_remote_copy(
            src_ref=sbuf.at[src], dst_ref=sbuf.at[slot], send_sem=ssem.at[0, sem], recv_sem=ssem.at[1, sem],
            device_id={"dp": to[0], "mp": to[1]}, device_id_type=MESH_ID,
        )

    @pl.when(p == pairs - 1)
    def _():
        sbuf[6] = jnp.zeros_like(sbuf[6])
        sbuf[6, 0:1] = bsum_up[0:1]
        sbuf[6, 1:2, : 3 * width] = bsum[0:1]
        sbuf[6, 2:3, :width] = sums[0:1]
        sbuf[6, 2:3, width : 2 * width] = sums[1:2]
        sbuf[6, 2:3, 2 * width : 3 * width] = sums_two[2:3]
        sbuf[6, 2:3, 3 * width :] = sums_two[0:1]
        sbuf[6, 3:4, :width] = sums_two[1:2]
        sbuf[6, 3:4, width : 2 * width] = sums_two[3:4]
        s0 = small_copy(0, 6, sib, 0)
        s0.start()

        def chunk(i, carry):
            at = pl.ds(pl.multiple_of(i * lw, 128), lw)
            acc = dot(n1t[0], dq_all[0, :, at])
            for q in range(1, pairs):
                acc = acc + dot(n1t[q], dq_all[q, :, at])
            gq[:, :, :, at] = acc.astype(LOW).reshape(Z * Y, C, part, lw)
            event_z(1, i)
            return carry

        lax.fori_loop(0, 3 * groups, chunk, 0)
        to_sibling(3)
        s0.wait()
        sbuf[7] = sbuf[6] + sbuf[0]
        s1 = small_copy(1, 7, chip(1, 1, 0), 1)
        s1.start()

        def loop(n, event, g):
            def one(i, carry):
                event(g, i)
                return carry

            lax.fori_loop(0, n, one, 0)

        loop(8, event_s, 3)
        s1.wait()
        sbuf[8] = sbuf[7] + sbuf[1]
        s2 = small_copy(2, 8, chip(1, 0, 1), 2)
        s2.start()
        event_x(0)
        loop(6, event_z, 2)
        s2.wait()
        sbuf[9] = sbuf[8] + sbuf[2]
        zs = [small_copy(2 + k, 9, beside(k), 2 + k) for k in (1, 2, 3)]
        for copy in zs:
            copy.start()
        event_x(1)
        loop(6, event_z, 3)
        final(0)
        event_x(2)
        for copy in zs:
            copy.wait()
        small_out[...] = (sbuf[9] + sbuf[3] + sbuf[4] + sbuf[5])[:4]
        final(1)
        event_x(3)
        final(2)
        final(3)

        def finish(i, carry):
            tok_copy(i).wait()
            return carry

        lax.fori_loop(0, pairs, finish, 0)


def backward_reduce(tokens, dhid, qkv, prob, n1, w_one, vec, grads, sums_two, bsum_up):
    pairs, rows, width = dhid.shape
    total = Z * Y * C
    part = grads[0].shape[0] // total
    grads = [g.reshape(Z * Y, C, part, g.shape[1]) for g in grads]
    widths = [g.shape[3] // 2 for g in grads] + [3 * width // 2]
    hbm = pl.BlockSpec(memory_space=pl.ANY)
    scratch = [
        pltpu.VMEM((rows, width), LOW), pltpu.VMEM((pairs, rows, width), LOW), pltpu.VMEM((pairs, rows, width), LOW),
        pltpu.VMEM((pairs, width, rows), LOW), pltpu.VMEM((pairs, rows, 3 * width), LOW),
        pltpu.VMEM((Z * Y, C, part, 3 * width), LOW), pltpu.VMEM((8, width), F32), pltpu.VMEM((8, 3 * width), F32),
    ]
    scratch += [pltpu.VMEM((Z * Y, part, 2 * w), LOW) for w in widths[:3]]
    for w in widths:
        scratch += [pltpu.VMEM((n, part, w), LOW) for n in (16, 8, 6, 1)]
    scratch += [
        pltpu.VMEM((10, 8, bsum_up.shape[1]), F32),
        pltpu.SemaphoreType.DMA((4, BLOCKS)), pltpu.SemaphoreType.DMA((4, BLOCKS)), pltpu.SemaphoreType.DMA((4,)),
        pltpu.SemaphoreType.DMA((2, pairs)), pltpu.SemaphoreType.DMA((2, 6)),
    ]
    whole = lambda *s: pl.BlockSpec(s, lambda p: (0,) * len(s))
    return pl.pallas_call(
        back_kernel,
        grid=(pairs,),
        in_specs=[
            hbm, pair_spec(rows, width), pair_spec(rows, 3 * width), pair_spec(HEADS, rows, rows),
            pair_spec(rows, width), const_spec(w_one.shape), const_spec(vec.shape), hbm, hbm, hbm,
            const_spec(sums_two.shape), const_spec(bsum_up.shape),
        ],
        out_specs=[pair_spec(rows, width), hbm] + [whole(part, w) for w in widths] + [whole(4, bsum_up.shape[1])],
        out_shape=[
            jax.ShapeDtypeStruct((pairs, rows, width), LOW), jax.ShapeDtypeStruct((pairs, rows, width), LOW),
        ]
        + [jax.ShapeDtypeStruct((part, w), F32) for w in widths]
        + [jax.ShapeDtypeStruct((4, bsum_up.shape[1]), F32)],
        scratch_shapes=scratch,
        compiler_params=pltpu.CompilerParams(collective_id=1, has_side_effects=True, vmem_limit_bytes=62 * 2**20),
        name="backward_reduce",
    )(tokens, dhid, qkv, prob, n1, w_one, vec, *grads, sums_two, bsum_up)


def per_device(
    patch_counts, tokens, cotangent, attn_gain, attn_shift, w_qkv, b_qv, w_proj, b_proj,
    ffn_gain, ffn_shift, w_up, b_up, w_down, b_down,
):
    pairs_all, rows, width = tokens.shape
    n_mp = lax.axis_size("mp")
    n_dp = lax.axis_size("dp")
    direct = n_dp == Z * Y * C and n_mp == 2
    pairs = pairs_all // n_mp
    part = w_qkv.shape[0]
    lw = w_qkv.shape[2]
    fw = w_up.shape[1]
    mine = lax.axis_index("mp")
    off = jnp.reshape(mine * pairs, (1,)).astype(jnp.int32)
    lens = TEXT + lax.dynamic_slice_in_dim(patch_counts, mine * pairs, pairs, 0)

    vectors = jnp.stack([attn_gain, attn_shift, b_proj, ffn_gain, ffn_shift, b_down], axis=1)
    first = jnp.concatenate(
        [w_qkv.reshape(part, 3 * lw), w_proj.T, vectors, jnp.zeros((part, EXTRA - 6), F32)], axis=1
    ).astype(LOW)
    second_a = w_up.astype(LOW)
    second_b = w_down.T.astype(LOW)
    bias = jnp.concatenate([b_qv.reshape(-1), b_up]).astype(LOW).astype(F32)
    bias = jnp.broadcast_to(bias, (8,) + bias.shape)
    if direct:
        w_one, w_two, bias = gather_weights(first, second_a, second_b, bias)
    else:
        both_axes = ("mp", "dp")
        w_one = lax.all_gather(first, both_axes, axis=0, tiled=True).reshape(n_mp, width, -1)
        second = jnp.concatenate([second_a, second_b], axis=1)
        w_two = lax.all_gather(second, both_axes, axis=0, tiled=True).reshape(n_mp, width, -1)
        bias = lax.all_gather(bias, "mp", axis=0)

    qkv, att, prob, hid, n1, n2, vec = attention_forward(lens, off, tokens, w_one, bias)
    out_here, act, dpre, dhid, dlow, upl, sums_two, bsum_up = ffn(lens, off, n2, hid, cotangent, w_two, bias, vec)

    def grad(left, right):
        return jnp.einsum(
            "rd,rf->df", left.reshape(pairs * rows, width), right.reshape(pairs * rows, -1),
            preferred_element_type=F32,
        )

    def reduce(grads, small):
        axes = ("mp", "dp")
        done = [
            lax.psum_scatter(
                g.reshape(width, n_mp, -1).swapaxes(0, 1).reshape(n_mp * width, -1), axes,
                scatter_dimension=0, tiled=True,
            )
            for g in grads
        ]
        if small is not None:
            done.append(lax.psum(small, axes))
        return done

    def both(array, other=None):
        if other is None:
            other = lax.ppermute(array, "mp", [(0, 1), (1, 0)])
        return jnp.where(mine == 0, jnp.concatenate([array, other]), jnp.concatenate([other, array]))

    block_out = both(out_here)
    grads = [grad(n2, dpre), grad(upl, act), grad(dlow, att)]
    if direct:
        tok_here, tok_other, r_up, r_down, r_proj, r_qkv, small = backward_reduce(
            tokens, dhid, qkv, prob, n1, w_one, vec, [g.astype(LOW) for g in grads], sums_two, bsum_up)
        tokens_grad = both(tok_here, tok_other)
        flat = small[1, : 3 * width].reshape(n_mp, 3, lw)
        small = jnp.concatenate([
            small[2], small[3, : 2 * width], flat[:, 0].reshape(-1), flat[:, 2].reshape(-1), small[0]])
    else:
        tok_here, dqkv, sums_one, bsum_qkv = attention_backward(lens, off, tokens, dhid, qkv, prob, w_one, vec)
        tokens_grad = both(tok_here)
        flat = bsum_qkv[0].reshape(n_mp, 3, lw)
        small = jnp.concatenate([
            sums_one[0], sums_one[1], sums_two[2], sums_two[0], sums_two[1], sums_two[3],
            flat[:, 0].reshape(-1), flat[:, 2].reshape(-1), bsum_up[0]])
        r_up, r_down, r_proj, r_qkv, small = reduce(grads + [grad(n1, dqkv)], small)
    place_dp = lax.axis_index("dp") * part

    def piece(i):
        return lax.dynamic_slice_in_dim(small, i * width + place_dp, part, 0)

    rest = small[6 * width :]
    o_b_q = lax.dynamic_slice_in_dim(rest, mine * lw, lw, 0)
    o_b_v = lax.dynamic_slice_in_dim(rest, (n_mp + mine) * lw, lw, 0)
    o_b_up = lax.dynamic_slice_in_dim(rest, 2 * n_mp * lw + mine * fw, fw, 0)
    return (
        block_out, tokens_grad, piece(0), piece(1),
        r_qkv.reshape(part, 3, lw), jnp.stack([o_b_q, o_b_v]),
        r_proj.T, piece(2), piece(3), piece(4), r_up, o_b_up, r_down.T, piece(5),
    )


def solution(mesh):
    vec, mat = P("dp"), P("dp", "mp")
    tok = P("dp", None, None)
    in_specs = (
        vec, tok, tok, vec, vec, P("dp", None, "mp"), P(None, "mp"), P("mp", "dp"), vec, vec, vec,
        mat, P("mp"), P("mp", "dp"), vec,
    )
    out_specs = (
        tok, tok, vec, vec, P("dp", None, "mp"), P(None, "mp"), P("mp", "dp"), vec, vec, vec,
        mat, P("mp"), P("mp", "dp"), vec,
    )
    return jax.shard_map(per_device, mesh=mesh, in_specs=in_specs, out_specs=out_specs, check_vma=False)
```

```python
import functools

import jax
import jax.numpy as jnp
from jax import lax
from jax.experimental import pallas as pl
from jax.experimental.pallas import tpu as pltpu
from jax.sharding import PartitionSpec as P

HEADS = 12
HEAD_DIM = 64
TEXT = 40
LOW = jnp.bfloat16
F32 = jnp.float32
EXTRA = 128
NT = (((1,), (1,)), ((), ()))
NN = (((1,), (0,)), ((), ()))


def dot(a, b, dims=NN):
    return lax.dot_general(a, b, dims, preferred_element_type=F32)


def moments(v):
    center = v - jnp.mean(v, axis=-1, keepdims=True)
    spread = jnp.mean(center * center, axis=-1, keepdims=True)
    r = lax.rsqrt(spread + 1e-06)
    return center * r, r


def row_ids(rows):
    return lax.broadcasted_iota(jnp.int32, (rows, 1), 0)


def attn_body(p, count, x, w_ref, bias_ref, vec_ref, qkv_ref, att_ref, prob_ref, hid_ref, n1_ref, n2_ref, hook):
    rows, width = x.shape
    groups = w_ref.shape[0]
    lw = width // groups
    tiles = lw // 128
    x = x.astype(F32)
    xhat, _ = moments(x)
    n1 = (xhat * vec_ref[0:1] + vec_ref[1:2]).astype(LOW)
    n1_ref[0] = n1
    for m in range(groups):
        y = dot(n1, w_ref[m, :, : 3 * lw])
        base = m * 3 * lw
        qkv_ref[0, :, base : base + lw] = (y[:, :lw] + bias_ref[m, 0:1, :lw]).astype(LOW)
        qkv_ref[0, :, base + lw : base + 2 * lw] = y[:, lw : 2 * lw].astype(LOW)
        qkv_ref[0, :, base + 2 * lw : base + 3 * lw] = (
            y[:, 2 * lw :] + bias_ref[m, 0:1, lw : 2 * lw]
        ).astype(LOW)
    keep = row_ids(rows) < count
    first = lax.broadcasted_iota(jnp.int32, (1, 128), 1) < HEAD_DIM

    def pair(hp, carry):
        base = (hp // tiles) * 3 * lw + lax.rem(hp, tiles) * 128

        def cols(t):
            return pl.ds(pl.multiple_of(base + t * lw, 128), 128)

        q2 = qkv_ref[0, :, cols(0)] * 0.125
        k2 = qkv_ref[0, :, cols(1)]
        v2t = qkv_ref[0, :, cols(2)].T
        outs = []
        for h in range(2):
            qh = jnp.where(first if h == 0 else ~first, q2, 0)
            st = dot(k2, qh, NT)
            st = jnp.where(keep, st, -1e30)
            e = jnp.exp(st - jnp.max(st, axis=0, keepdims=True))
            pt = (e * (1.0 / jnp.sum(e, axis=0, keepdims=True))).astype(LOW)
            prob_ref[0, hp * 2 + h] = pt
            outs.append(dot(v2t[h * HEAD_DIM : (h + 1) * HEAD_DIM], pt))
        att_ref[0, :, pl.ds(pl.multiple_of(hp * 128, 128), 128)] = jnp.concatenate(outs, axis=0).T.astype(LOW)
        hook(hp)
        return carry

    lax.fori_loop(0, groups * tiles, pair, 0)
    proj = sum(dot(att_ref[0, :, m * lw : (m + 1) * lw], w_ref[m, :, 3 * lw : 4 * lw], NT) for m in range(groups))
    hid = x + proj + vec_ref[2:3]
    hid_ref[0] = hid
    xhat2, _ = moments(hid)
    n2_ref[0] = (xhat2 * vec_ref[3:4] + vec_ref[4:5]).astype(LOW)


def attn_kernel(lens, off, x_ref, w_ref, bias_ref, qkv_ref, att_ref, prob_ref, hid_ref, n1_ref, n2_ref, vec_ref):
    p = pl.program_id(0)
    lw = x_ref.shape[2] // w_ref.shape[0]

    @pl.when(p == 0)
    def _():
        vec_ref[...] = w_ref[0, :, 4 * lw :].astype(F32).T[:8]

    attn_body(p, lens[p], x_ref[0], w_ref, bias_ref, vec_ref, qkv_ref, att_ref, prob_ref, hid_ref, n1_ref, n2_ref,
              lambda hp: None)


def const_spec(shape):
    return pl.BlockSpec(shape, lambda *_: (0,) * len(shape), pipeline_mode=pl.Buffered(1))


def pair_spec(*shape):
    return pl.BlockSpec((1,) + shape, lambda p, *_: (p,) + (0,) * len(shape))


def attention_forward(lens, off, tokens, w_one, bias):
    pairs = lens.shape[0]
    _, rows, width = tokens.shape
    out = lambda dt, *s: jax.ShapeDtypeStruct((pairs,) + s, dt)
    return pl.pallas_call(
        attn_kernel,
        grid_spec=pltpu.PrefetchScalarGridSpec(
            num_scalar_prefetch=2,
            grid=(pairs,),
            in_specs=[
                pl.BlockSpec((1, rows, width), lambda p, lens, off: (off[0] + p, 0, 0)),
                const_spec(w_one.shape),
                const_spec(bias.shape),
            ],
            out_specs=[
                pair_spec(rows, 3 * width), pair_spec(rows, width), pair_spec(HEADS, rows, rows),
                pair_spec(rows, width), pair_spec(rows, width), pair_spec(rows, width),
                pl.BlockSpec((8, width), lambda *_: (0, 0)),
            ],
        ),
        out_shape=[
            out(LOW, rows, 3 * width), out(LOW, rows, width), out(LOW, HEADS, rows, rows),
            out(F32, rows, width), out(LOW, rows, width), out(LOW, rows, width),
            jax.ShapeDtypeStruct((8, width), F32),
        ],
        compiler_params=pltpu.CompilerParams(vmem_limit_bytes=60 * 2**20),
        name="attention_forward",
    )(lens, off, tokens, w_one, bias)


def ffn_kernel(lens, off, n2_ref, hid_ref, cot_ref, w_ref, bias_ref, vec_ref,
               out_ref, act_ref, dpre_ref, dhid_ref, dlow_ref, upl_ref, sums_ref, bsum_ref):
    p = pl.program_id(0)
    rows, width = n2_ref.shape[1], n2_ref.shape[2]
    groups = w_ref.shape[0]
    fw = w_ref.shape[2] // 2
    lw = width // groups
    step = 512
    keep = row_ids(rows) < lens[p]
    n2 = n2_ref[0]
    upl = jnp.where(keep, cot_ref[0], 0)
    upl_ref[0] = upl

    @pl.when(p == 0)
    def _():
        sums_ref[...] = jnp.zeros_like(sums_ref)
        bsum_ref[...] = jnp.zeros_like(bsum_ref)

    for m in range(groups):
        for c in range(0, fw, step):
            pre = dot(n2, w_ref[m, :, c : c + step]) + bias_ref[m, 0:1, 2 * lw + c : 2 * lw + c + step]
            cdf = 0.5 * (1.0 + lax.erf(pre * (2.0 ** -0.5)))
            at = m * fw + c
            act_ref[0, :, at : at + step] = (pre * cdf).astype(LOW)
            slope = cdf + pre * (0.3989422804014327 * jnp.exp(-0.5 * pre * pre))
            dpre = slope * dot(upl, w_ref[m, :, fw + c : fw + c + step])
            dpre_ref[0, :, at : at + step] = dpre.astype(LOW)
            bsum_ref[0:1, at : at + step] += jnp.sum(dpre, axis=0, keepdims=True)
    hid = hid_ref[0]
    down = sum(dot(act_ref[0, :, m * fw : (m + 1) * fw], w_ref[m, :, fw:], NT) for m in range(groups))
    out_ref[0] = jnp.where(keep, hid + down + vec_ref[5:6], 0.0).astype(LOW)
    dtwo = sum(dot(dpre_ref[0, :, m * fw : (m + 1) * fw], w_ref[m, :, :fw], NT) for m in range(groups))
    xhat, r = moments(hid)
    dg = dtwo * vec_ref[3:4]
    dn = r * (dg - jnp.mean(dg, axis=-1, keepdims=True) - xhat * jnp.mean(dg * xhat, axis=-1, keepdims=True))
    upf = upl.astype(F32)
    dhid = upf + dn
    dhid_ref[0] = dhid
    dlow_ref[0] = dhid.astype(LOW)
    sums_ref[0:1] += jnp.sum(dtwo * xhat, axis=0, keepdims=True)
    sums_ref[1:2] += jnp.sum(dtwo, axis=0, keepdims=True)
    sums_ref[2:3] += jnp.sum(dhid, axis=0, keepdims=True)
    sums_ref[3:4] += jnp.sum(upf, axis=0, keepdims=True)


def ffn(lens, off, n2, hid, cotangent, w_two, bias, vec):
    pairs, rows, width = n2.shape
    ff = w_two.shape[0] * w_two.shape[2] // 2
    out = lambda dt, *s: jax.ShapeDtypeStruct((pairs,) + s, dt)
    return pl.pallas_call(
        ffn_kernel,
        grid_spec=pltpu.PrefetchScalarGridSpec(
            num_scalar_prefetch=2,
            grid=(pairs,),
            in_specs=[
                pair_spec(rows, width), pair_spec(rows, width),
                pl.BlockSpec((1, rows, width), lambda p, lens, off: (off[0] + p, 0, 0)),
                const_spec(w_two.shape), const_spec(bias.shape), const_spec(vec.shape),
            ],
            out_specs=[
                pair_spec(rows, width), pair_spec(rows, ff), pair_spec(rows, ff), pair_spec(rows, width),
                pair_spec(rows, width), pair_spec(rows, width),
                pl.BlockSpec((8, width), lambda *_: (0, 0)), pl.BlockSpec((8, ff), lambda *_: (0, 0)),
            ],
        ),
        out_shape=[
            out(LOW, rows, width), out(LOW, rows, ff), out(LOW, rows, ff), out(F32, rows, width),
            out(LOW, rows, width), out(LOW, rows, width),
            jax.ShapeDtypeStruct((8, width), F32), jax.ShapeDtypeStruct((8, ff), F32),
        ],
        compiler_params=pltpu.CompilerParams(vmem_limit_bytes=60 * 2**20),
        name="feed_forward",
    )(lens, off, n2, hid, cotangent, w_two, bias, vec)


def plain_back_kernel(lens, off, x_ref, dhid_ref, qkv_ref, prob_ref, w_ref, vec_ref,
                tok_ref, dqkv_ref, sums_ref, bsum_ref, do_ref):
    p = pl.program_id(0)
    rows, width = x_ref.shape[1], x_ref.shape[2]
    groups = w_ref.shape[0]
    lw = width // groups
    tiles = lw // 128

    @pl.when(p == 0)
    def _():
        sums_ref[...] = jnp.zeros_like(sums_ref)
        bsum_ref[...] = jnp.zeros_like(bsum_ref)

    dhid = dhid_ref[0]
    dlow = dhid.astype(LOW)
    for m in range(groups):
        do_ref[:, m * lw : (m + 1) * lw] = dot(dlow, w_ref[m, :, 3 * lw : 4 * lw]).astype(LOW)
    first = lax.broadcasted_iota(jnp.int32, (1, 128), 1) < HEAD_DIM

    def pair(hp, carry):
        base = (hp // tiles) * 3 * lw + (hp % tiles) * 128

        def cols(t):
            return pl.ds(pl.multiple_of(base + t * lw, 128), 128)

        q2 = qkv_ref[0, :, cols(0)] * 0.125
        k2t = qkv_ref[0, :, cols(1)].T
        v2 = qkv_ref[0, :, cols(2)]
        do2 = do_ref[:, pl.ds(pl.multiple_of(hp * 128, 128), 128)]
        dq_t = []
        dk = dv = 0.0
        for h in range(2):
            mine = first if h == 0 else ~first
            doh = jnp.where(mine, do2, 0)
            qh = jnp.where(mine, q2, 0)
            dpt = dot(v2, doh, NT)
            plow = prob_ref[0, hp * 2 + h]
            pt = plow.astype(F32)
            inner = jnp.sum(pt * dpt, axis=0, keepdims=True)
            dst = (pt * (dpt - inner)).astype(LOW)
            dv = dv + dot(plow, doh)
            dk = dk + dot(dst, qh)
            dq_t.append(dot(k2t[h * HEAD_DIM : (h + 1) * HEAD_DIM], dst))
        dq = (jnp.concatenate(dq_t, axis=0) * 0.125).T
        dqkv_ref[0, :, cols(0)] = dq.astype(LOW)
        dqkv_ref[0, :, cols(1)] = dk.astype(LOW)
        dqkv_ref[0, :, cols(2)] = dv.astype(LOW)
        bsum_ref[0:1, cols(0)] += jnp.sum(dq, axis=0, keepdims=True)
        bsum_ref[0:1, cols(2)] += jnp.sum(dv, axis=0, keepdims=True)
        return carry

    lax.fori_loop(0, groups * tiles, pair, 0)
    done = sum(dot(dqkv_ref[0, :, m * 3 * lw : (m + 1) * 3 * lw], w_ref[m, :, : 3 * lw], NT) for m in range(groups))
    xhat, r = moments(x_ref[0].astype(F32))
    dg = done * vec_ref[0:1]
    dn = r * (dg - jnp.mean(dg, axis=-1, keepdims=True) - xhat * jnp.mean(dg * xhat, axis=-1, keepdims=True))
    tok_ref[0] = (dhid + dn).astype(LOW)
    sums_ref[0:1] += jnp.sum(done * xhat, axis=0, keepdims=True)
    sums_ref[1:2] += jnp.sum(done, axis=0, keepdims=True)


def attention_backward(lens, off, tokens, dhid, qkv, prob, w_one, vec):
    pairs, rows, width = dhid.shape
    out = lambda dt, *s: jax.ShapeDtypeStruct((pairs,) + s, dt)
    return pl.pallas_call(
        plain_back_kernel,
        grid_spec=pltpu.PrefetchScalarGridSpec(
            num_scalar_prefetch=2,
            grid=(pairs,),
            in_specs=[
                pl.BlockSpec((1, rows, width), lambda p, lens, off: (off[0] + p, 0, 0)),
                pair_spec(rows, width), pair_spec(rows, 3 * width), pair_spec(HEADS, rows, rows),
                const_spec(w_one.shape), const_spec(vec.shape),
            ],
            out_specs=[
                pair_spec(rows, width), pair_spec(rows, 3 * width),
                pl.BlockSpec((8, width), lambda *_: (0, 0)), pl.BlockSpec((8, 3 * width), lambda *_: (0, 0)),
            ],
            scratch_shapes=[pltpu.VMEM((rows, width), LOW)],
        ),
        out_shape=[
            out(LOW, rows, width), out(LOW, rows, 3 * width),
            jax.ShapeDtypeStruct((8, width), F32), jax.ShapeDtypeStruct((8, 3 * width), F32),
        ],
        compiler_params=pltpu.CompilerParams(vmem_limit_bytes=60 * 2**20),
        name="attention_backward",
    )(lens, off, tokens, dhid, qkv, prob, w_one, vec)
MESH_ID = pl.DeviceIdType.MESH
Z, Y, C = 4, 2, 2


def place():
    dp = lax.axis_index("dp")
    m = lax.axis_index("mp")
    c = lax.rem(dp, 2)
    y = lax.rem(dp // 2, 2)
    z = dp // 4
    return z, y, c, m


def index(z, y, c):
    return (z * Y + y) * C + c


def flips(y, c, m):
    one = (y + c * (1 - 2 * y), m + (1 - c) * (1 - 2 * m))
    two = (y + (1 - c) * (1 - 2 * y), m + c * (1 - 2 * m))
    return one, two


def greet(z, y, c, m):
    barrier = pltpu.get_barrier_semaphore()
    (y1, m1), (y2, m2) = flips(y, c, m)
    peers = [(index(lax.rem(z + k, Z), y, c), m) for k in (1, 2, 3)]
    peers += [(index(z, y1, c), m1), (index(z, y2, c), m2), (index(z, y, 1 - c), m)]
    for dp, mp in peers:
        pl.semaphore_signal(barrier, inc=1, device_id={"dp": dp, "mp": mp}, device_id_type=MESH_ID)
    pl.semaphore_wait(barrier, len(peers))
    return peers


def gather_attn_kernel(lens, tok_all, first_ref, second_ref, b_in,
                       w_one_out, w_two, b_out, qkv_ref, att_ref, prob_ref, hid_ref, n1_ref, n2_ref, vec_ref,
                       w_one, bias, xbuf, send, recv, bsem, local):
    p = pl.program_id(0)
    z, y, c, m = place()
    (y1, m1), (y2, m2) = flips(y, c, m)
    pairs, rows, width = xbuf.shape
    part = first_ref.shape[0]
    cols = second_ref.shape[1] // 2
    lw = width // 2
    per_pair = width // 128
    me = index(z, y, c)
    one, two, sib = (index(z, y1, c), m1), (index(z, y2, c), m2), (index(z, y, 1 - c), m)

    def spot(g, dp, mp):
        at = pl.ds(pl.multiple_of(dp * part, part), part)
        if g is None:
            return w_one.at[mp, at]
        return w_two.at[mp, at, pl.ds(pl.multiple_of(g * cols, 128), cols)]

    def shard(g):
        return first_ref if g is None else second_ref.at[:, pl.ds(pl.multiple_of(g * cols, 128), cols)]

    def row(g):
        return 0 if g is None else g + 1

    def copy_of(g, src, dst, out_sem, in_sem, to):
        return pltpu.make_async_remote_copy(
            src_ref=src, dst_ref=dst, send_sem=send.at[row(g), out_sem], recv_sem=recv.at[row(g), in_sem],
            device_id={"dp": to[0], "mp": to[1]}, device_id_type=MESH_ID,
        )

    def push(g, src, dp, mp, to, sem):
        copy_of(g, src, spot(g, dp, mp), sem, mp * (Z * Y * C) + dp, to).start()

    def arrived(g, dp, mp):
        at = spot(g, dp, mp)
        copy_of(g, at, at, 0, mp * (Z * Y * C) + dp, sib).wait_recv()
        return at

    def own_z(g):
        for k in (1, 3, 2):
            push(g, shard(g), me, m, (index(lax.rem(z + k, Z), y, c), m), k - 1)

    def own_near(g):
        for n, to in enumerate((one, two, sib)):
            push(g, shard(g), me, m, to, 3 + n)

    def event_z(g, i):
        dp = index(lax.rem(z + 1 + lax.rem(2 * i, 3), Z), y, c)
        at = arrived(g, dp, m)
        for n, to in enumerate((one, two, sib)):
            push(g, at, dp, m, to, 6 + 3 * i + n)

    def event_one(g, i):
        dp = index(lax.rem(z + i, Z), y1, c)
        at = arrived(g, dp, m1)
        for n, to in enumerate((two, sib)):
            push(g, at, dp, m1, to, 15 + 2 * i + n)

    def event_two(g, i):
        far = lax.rem(i, 2)
        yy = y2 + far * (1 - y - y2)
        mm = m2 + far * (1 - m - m2)
        dp = index(lax.rem(z + i // 2, Z), yy, c)
        push(g, arrived(g, dp, mm), dp, mm, sib, 23 + i)

    def event_core(g, i):
        arrived(g, index(i // 4, lax.rem(i // 2, 2), 1 - c), lax.rem(i, 2))

    def loop(n, event, g):
        def run(i, carry):
            event(g, i)
            return carry

        lax.fori_loop(0, n, run, 0)

    bias_copy = pltpu.make_async_remote_copy(
        src_ref=b_in, dst_ref=bias.at[m], send_sem=bsem.at[0], recv_sem=bsem.at[1],
        device_id={"dp": me, "mp": 1 - m}, device_id_type=MESH_ID,
    )
    x_copy = pltpu.make_async_copy(tok_all.at[pl.ds(m * pairs, pairs)], xbuf, local.at[0])
    mine = [
        pltpu.make_async_copy(b_in, bias.at[m], local.at[1]),
        pltpu.make_async_copy(first_ref, spot(None, me, m), local.at[2]),
    ]
    mine_two = [pltpu.make_async_copy(shard(g), spot(g, me, m), local.at[3 + g]) for g in range(2)]
    keep_one = pltpu.make_async_copy(w_one, w_one_out, local.at[5])
    keep_bias = pltpu.make_async_copy(bias, b_out, local.at[6])

    @pl.when(p == 0)
    def _():
        for copy in mine + mine_two:
            copy.start()
        x_copy.start()
        greet(z, y, c, m)
        own_z(None)
        own_near(None)
        bias_copy.start()
        own_z(0)
        own_z(1)
        loop(3, event_z, None)
        loop(4, event_one, None)
        loop(8, event_two, None)
        for copy in mine + [x_copy, bias_copy]:
            copy.wait()
        loop(16, event_core, None)
        keep_one.start()
        keep_bias.start()
        vec_ref[...] = w_one[0, :, 4 * lw :].astype(F32).T[:8]

    def hook(hp):
        step = p * per_pair + hp

        def event(e, carry):
            g = e // 16
            i = lax.rem(e, 16)

            @pl.when(i == 0)
            def _():
                own_near(g)

            @pl.when((i >= 1) & (i < 4))
            def _():
                event_z(g, i - 1)

            @pl.when((i >= 4) & (i < 8))
            def _():
                event_one(g, i - 4)

            @pl.when(i >= 8)
            def _():
                event_two(g, i - 8)

            return carry

        total = pairs * per_pair
        lax.fori_loop(step * 32 // total, (step + 1) * 32 // total, event, 0)

    attn_body(p, lens[p], xbuf[p], w_one, bias, vec_ref, qkv_ref, att_ref, prob_ref, hid_ref, n1_ref, n2_ref, hook)

    @pl.when(p == pairs - 1)
    def _():
        for g in range(2):
            loop(16, event_core, g)
        for copy in mine_two + [keep_one, keep_bias]:
            copy.wait()
        for g in (None, 0, 1):
            def sent(i, carry):
                copy_of(g, shard(g), shard(g), i, 0, sib).wait_send()
                return carry

            lax.fori_loop(0, 31, sent, 0)


def gather_attention(lens, tokens, first, second, bias):
    pairs = lens.shape[0]
    _, rows, width = tokens.shape
    part = first.shape[0]
    total = Z * Y * C
    hbm = pl.BlockSpec(memory_space=pl.ANY)
    out = lambda dt, *s: jax.ShapeDtypeStruct((pairs,) + s, dt)
    return pl.pallas_call(
        gather_attn_kernel,
        grid_spec=pltpu.PrefetchScalarGridSpec(
            num_scalar_prefetch=1,
            grid=(pairs,),
            in_specs=[hbm, const_spec(first.shape), const_spec(second.shape), const_spec(bias.shape)],
            out_specs=[
                hbm, hbm, hbm,
                pair_spec(rows, 3 * width), pair_spec(rows, width), pair_spec(HEADS, rows, rows),
                pair_spec(rows, width), pair_spec(rows, width), pair_spec(rows, width),
                pl.BlockSpec((8, width), lambda *_: (0, 0)),
            ],
            scratch_shapes=[
                pltpu.VMEM((2, total * part, first.shape[1]), LOW), pltpu.VMEM((2,) + bias.shape, F32),
                pltpu.VMEM((pairs, rows, width), LOW),
                pltpu.SemaphoreType.DMA((3, 31)), pltpu.SemaphoreType.DMA((3, 32)),
                pltpu.SemaphoreType.DMA((2,)), pltpu.SemaphoreType.DMA((7,)),
            ],
        ),
        out_shape=[
            jax.ShapeDtypeStruct((2, total * part, first.shape[1]), LOW),
            jax.ShapeDtypeStruct((2, total * part, second.shape[1]), LOW),
            jax.ShapeDtypeStruct((2,) + bias.shape, F32),
            out(LOW, rows, 3 * width), out(LOW, rows, width), out(LOW, HEADS, rows, rows),
            out(F32, rows, width), out(LOW, rows, width), out(LOW, rows, width),
            jax.ShapeDtypeStruct((8, width), F32),
        ],
        compiler_params=pltpu.CompilerParams(collective_id=0, has_side_effects=True, vmem_limit_bytes=60 * 2**20),
        name="gather_attention",
    )(lens, tokens, first, second, bias)


BLOCKS = 31


def back_kernel(tok_all, dhid_ref, qkv_ref, prob_ref, n1_ref, w_ref, vec_ref, g_up, g_down, g_proj, sums_two, bsum_up,
                tok_ref, tok_other, r_up, r_down, r_proj, r_qkv, small_out,
                do_ref, xbuf, tokbuf, n1t, dq_all, gq, sums, bsum,
                own_up, own_down, own_proj, rc0, rs0, rz0, rx0, rc1, rs1, rz1, rx1, rc2, rs2, rz2, rx2,
                rc3, rs3, rz3, rx3, sbuf, send, recv, local, tsem, ssem):
    p = pl.program_id(0)
    pairs, rows, width = xbuf.shape
    groups = w_ref.shape[0]
    lw = width // groups
    tiles = lw // 128
    z, y, c, m = place()
    outs = (r_up, r_down, r_proj, r_qkv)
    grads = (g_up, g_down, g_proj, gq)
    owns = (own_up, own_down, own_proj)
    rcs, rss, rzs, rxs = (rc0, rc1, rc2, rc3), (rs0, rs1, rs2, rs3), (rz0, rz1, rz2, rz3), (rx0, rx1, rx2, rx3)
    part = r_up.shape[0]
    me = index(z, y, c)
    sib = (index(z, y, 1 - c), m)

    def beside(k):
        return (index(lax.rem(z + k, Z), y, c), m)

    def x_first(g, cc):
        return cc if g == 0 else 0

    def target(g, cc, ra, rb):
        fx = x_first(g, cc)
        dy = fx * rb + (1 - fx) * ra
        dm = fx * ra + (1 - fx) * rb
        return y + dy * (1 - 2 * y), m + dm * (1 - 2 * m)

    def chip(g, ra, rb):
        yy, mm = target(g, c, ra, rb)
        return (index(z, yy, c), mm)

    def column(g, mm):
        cols = outs[g].shape[1]
        return pl.ds(pl.multiple_of(mm * cols, 128), cols)

    def copy_of(g, src, dst, out_sem, in_sem, to):
        return pltpu.make_async_remote_copy(
            src_ref=src, dst_ref=dst, send_sem=send.at[g, out_sem], recv_sem=recv.at[g, in_sem],
            device_id={"dp": to[0], "mp": to[1]}, device_id_type=MESH_ID,
        )

    def to_sibling(g):
        def one(i, carry):
            slot = 15 - i
            ra, rb, k = slot // 8, lax.rem(slot // 4, 2), lax.rem(slot, 4)
            yy, mm = target(g, 1 - c, ra, rb)
            src = grads[g].at[lax.rem(z + k, Z) * Y + yy, 1 - c, :, column(g, mm)]
            copy_of(g, src, rcs[g].at[slot], slot, slot, sib).start()
            return carry

        lax.fori_loop(0, 16, one, 0)

    def arrived(g, ref, sem):
        copy_of(g, ref, ref, 0, sem, sib).wait_recv()

    def base(g, ra, rb, k):
        slot = (ra * 2 + rb) * 4 + k
        arrived(g, rcs[g].at[slot], slot)
        yy, mm = target(g, c, ra, rb)
        row = lax.rem(z + k, Z) * Y + yy
        mine = owns[g][row, :, column(g, mm)] if g < 3 else gq[row, c, :, column(g, mm)]
        return mine.astype(F32) + rcs[g][slot].astype(F32)

    def level(g, rb, k):
        value = base(g, 0, rb, k)
        at = rb * 4 + k
        arrived(g, rss[g].at[at], 16 + at)
        return value + rss[g][at].astype(F32)

    def lined(g, rb):
        value = level(g, rb, 0)
        for k in (1, 2, 3):
            at = (k - 1) * 2 + rb
            arrived(g, rzs[g].at[at], 24 + at)
            value = value + rzs[g][at].astype(F32)
        return value

    def event_s(g, r):
        rb, k = 1 - r // 4, lax.rem(r + 1, 4)
        slot = (2 + rb) * 4 + k
        at = rb * 4 + k
        rcs[g][slot] = base(g, 1, rb, k).astype(LOW)
        copy_of(g, rcs[g].at[slot], rss[g].at[at], 16 + at, 16 + at, chip(g, 1, 0)).start()

    def event_z(g, r):
        rb, k = 1 - lax.rem(r, 2), 1 + r // 2
        slot = rb * 4 + k
        at = (k - 1) * 2 + rb
        rcs[g][slot] = level(g, rb, k).astype(LOW)
        copy_of(g, rcs[g].at[slot], rzs[g].at[at], 24 + at, 24 + at, beside(k)).start()

    def event_x(g):
        rcs[g][4] = lined(g, 1).astype(LOW)
        copy_of(g, rcs[g].at[4], rxs[g].at[0], 30, 30, chip(g, 0, 1)).start()

    def final(g):
        value = lined(g, 0)
        arrived(g, rxs[g].at[0], 30)
        outs[g][...] = value + rxs[g][0].astype(F32)

        def one(i, carry):
            copy_of(g, rcs[g].at[0], rcs[g].at[0], i, 0, sib).wait_send()
            return carry

        lax.fori_loop(0, BLOCKS, one, 0)

    def tok_copy(i):
        return pltpu.make_async_remote_copy(
            src_ref=tokbuf.at[i], dst_ref=tok_other.at[i], send_sem=tsem.at[0, i], recv_sem=tsem.at[1, i],
            device_id={"dp": me, "mp": 1 - m}, device_id_type=MESH_ID,
        )

    def own_copy(g):
        return pltpu.make_async_copy(grads[g].at[:, c], owns[g], local.at[g])

    x_copy = pltpu.make_async_copy(tok_all.at[pl.ds(m * pairs, pairs)], xbuf, local.at[3])

    @pl.when(p == 0)
    def _():
        for g in range(3):
            own_copy(g).start()
        x_copy.start()
        greet(z, y, c, m)
        for g in range(3):
            to_sibling(g)
        sums[...] = jnp.zeros_like(sums)
        bsum[...] = jnp.zeros_like(bsum)
        for g in range(3):
            own_copy(g).wait()
        x_copy.wait()

    dhid = dhid_ref[0]
    dlow = dhid.astype(LOW)
    for mm in range(groups):
        do_ref[:, mm * lw : (mm + 1) * lw] = dot(dlow, w_ref[mm, :, 3 * lw : 4 * lw]).astype(LOW)
    n1t[p] = n1_ref[0].T
    first = lax.broadcasted_iota(jnp.int32, (1, 128), 1) < HEAD_DIM

    def pair(hp, carry):
        lane = (hp // tiles) * 3 * lw + lax.rem(hp, tiles) * 128

        def cols(t):
            return pl.ds(pl.multiple_of(lane + t * lw, 128), 128)

        q2 = qkv_ref[0, :, cols(0)] * 0.125
        k2t = qkv_ref[0, :, cols(1)].T
        v2 = qkv_ref[0, :, cols(2)]
        do2 = do_ref[:, pl.ds(pl.multiple_of(hp * 128, 128), 128)]
        dq_t = []
        dk = dv = 0.0
        for h in range(2):
            mine = first if h == 0 else ~first
            doh = jnp.where(mine, do2, 0)
            qh = jnp.where(mine, q2, 0)
            dpt = dot(v2, doh, NT)
            plow = prob_ref[0, hp * 2 + h]
            pt = plow.astype(F32)
            inner = jnp.sum(pt * dpt, axis=0, keepdims=True)
            dst = (pt * (dpt - inner)).astype(LOW)
            dv = dv + dot(plow, doh)
            dk = dk + dot(dst, qh)
            dq_t.append(dot(k2t[h * HEAD_DIM : (h + 1) * HEAD_DIM], dst))
        dq = (jnp.concatenate(dq_t, axis=0) * 0.125).T
        dq_all[p, :, cols(0)] = dq.astype(LOW)
        dq_all[p, :, cols(1)] = dk.astype(LOW)
        dq_all[p, :, cols(2)] = dv.astype(LOW)
        bsum[0:1, cols(0)] += jnp.sum(dq, axis=0, keepdims=True)
        bsum[0:1, cols(2)] += jnp.sum(dv, axis=0, keepdims=True)

        step = p * (groups * tiles) + hp
        for g in range(3):

            @pl.when((step >= 4 * g) & (step < 4 * g + 4))
            def _():
                event_s(g, 2 * step - 8 * g)
                event_s(g, 2 * step - 8 * g + 1)

        @pl.when((step >= 17) & (step < 23))
        def _():
            event_z(0, step - 17)

        return carry

    lax.fori_loop(0, groups * tiles, pair, 0)
    done = sum(dot(dq_all[p, :, mm * 3 * lw : (mm + 1) * 3 * lw], w_ref[mm, :, : 3 * lw], NT) for mm in range(groups))
    xhat, r = moments(xbuf[p].astype(F32))
    dg = done * vec_ref[0:1]
    dn = r * (dg - jnp.mean(dg, axis=-1, keepdims=True) - xhat * jnp.mean(dg * xhat, axis=-1, keepdims=True))
    tok = (dhid + dn).astype(LOW)
    tok_ref[0] = tok
    tokbuf[p] = tok
    tok_copy(p).start()
    sums[0:1] += jnp.sum(done * xhat, axis=0, keepdims=True)
    sums[1:2] += jnp.sum(done, axis=0, keepdims=True)

    def small_copy(slot, src, to, sem):
        return pltpu.make_async_remote_copy(
            src_ref=sbuf.at[src], dst_ref=sbuf.at[slot], send_sem=ssem.at[0, sem], recv_sem=ssem.at[1, sem],
            device_id={"dp": to[0], "mp": to[1]}, device_id_type=MESH_ID,
        )

    @pl.when(p == pairs - 1)
    def _():
        sbuf[6] = jnp.zeros_like(sbuf[6])
        sbuf[6, 0:1] = bsum_up[0:1]
        sbuf[6, 1:2, : 3 * width] = bsum[0:1]
        sbuf[6, 2:3, :width] = sums[0:1]
        sbuf[6, 2:3, width : 2 * width] = sums[1:2]
        sbuf[6, 2:3, 2 * width : 3 * width] = sums_two[2:3]
        sbuf[6, 2:3, 3 * width :] = sums_two[0:1]
        sbuf[6, 3:4, :width] = sums_two[1:2]
        sbuf[6, 3:4, width : 2 * width] = sums_two[3:4]
        s0 = small_copy(0, 6, sib, 0)
        s0.start()

        def chunk(i, carry):
            at = pl.ds(pl.multiple_of(i * lw, 128), lw)
            acc = dot(n1t[0], dq_all[0, :, at])
            for q in range(1, pairs):
                acc = acc + dot(n1t[q], dq_all[q, :, at])
            gq[:, :, :, at] = acc.astype(LOW).reshape(Z * Y, C, part, lw)
            event_z(1, i)
            return carry

        lax.fori_loop(0, 3 * groups, chunk, 0)
        to_sibling(3)
        s0.wait()
        sbuf[7] = sbuf[6] + sbuf[0]
        s1 = small_copy(1, 7, chip(1, 1, 0), 1)
        s1.start()

        def loop(n, event, g):
            def one(i, carry):
                event(g, i)
                return carry

            lax.fori_loop(0, n, one, 0)

        loop(8, event_s, 3)
        s1.wait()
        sbuf[8] = sbuf[7] + sbuf[1]
        s2 = small_copy(2, 8, chip(1, 0, 1), 2)
        s2.start()
        event_x(0)
        loop(6, event_z, 2)
        s2.wait()
        sbuf[9] = sbuf[8] + sbuf[2]
        zs = [small_copy(2 + k, 9, beside(k), 2 + k) for k in (1, 2, 3)]
        for copy in zs:
            copy.start()
        event_x(1)
        loop(6, event_z, 3)
        final(0)
        event_x(2)
        for copy in zs:
            copy.wait()
        small_out[...] = (sbuf[9] + sbuf[3] + sbuf[4] + sbuf[5])[:4]
        final(1)
        event_x(3)
        final(2)
        final(3)

        def finish(i, carry):
            tok_copy(i).wait()
            return carry

        lax.fori_loop(0, pairs, finish, 0)


def backward_reduce(tokens, dhid, qkv, prob, n1, w_one, vec, grads, sums_two, bsum_up):
    pairs, rows, width = dhid.shape
    total = Z * Y * C
    part = grads[0].shape[0] // total
    grads = [g.reshape(Z * Y, C, part, g.shape[1]) for g in grads]
    widths = [g.shape[3] // 2 for g in grads] + [3 * width // 2]
    hbm = pl.BlockSpec(memory_space=pl.ANY)
    scratch = [
        pltpu.VMEM((rows, width), LOW), pltpu.VMEM((pairs, rows, width), LOW), pltpu.VMEM((pairs, rows, width), LOW),
        pltpu.VMEM((pairs, width, rows), LOW), pltpu.VMEM((pairs, rows, 3 * width), LOW),
        pltpu.VMEM((Z * Y, C, part, 3 * width), LOW), pltpu.VMEM((8, width), F32), pltpu.VMEM((8, 3 * width), F32),
    ]
    scratch += [pltpu.VMEM((Z * Y, part, 2 * w), LOW) for w in widths[:3]]
    for w in widths:
        scratch += [pltpu.VMEM((n, part, w), LOW) for n in (16, 8, 6, 1)]
    scratch += [
        pltpu.VMEM((10, 8, bsum_up.shape[1]), F32),
        pltpu.SemaphoreType.DMA((4, BLOCKS)), pltpu.SemaphoreType.DMA((4, BLOCKS)), pltpu.SemaphoreType.DMA((4,)),
        pltpu.SemaphoreType.DMA((2, pairs)), pltpu.SemaphoreType.DMA((2, 6)),
    ]
    whole = lambda *s: pl.BlockSpec(s, lambda p: (0,) * len(s))
    return pl.pallas_call(
        back_kernel,
        grid=(pairs,),
        in_specs=[
            hbm, pair_spec(rows, width), pair_spec(rows, 3 * width), pair_spec(HEADS, rows, rows),
            pair_spec(rows, width), const_spec(w_one.shape), const_spec(vec.shape), hbm, hbm, hbm,
            const_spec(sums_two.shape), const_spec(bsum_up.shape),
        ],
        out_specs=[pair_spec(rows, width), hbm] + [whole(part, w) for w in widths] + [whole(4, bsum_up.shape[1])],
        out_shape=[
            jax.ShapeDtypeStruct((pairs, rows, width), LOW), jax.ShapeDtypeStruct((pairs, rows, width), LOW),
        ]
        + [jax.ShapeDtypeStruct((part, w), F32) for w in widths]
        + [jax.ShapeDtypeStruct((4, bsum_up.shape[1]), F32)],
        scratch_shapes=scratch,
        compiler_params=pltpu.CompilerParams(collective_id=1, has_side_effects=True, vmem_limit_bytes=62 * 2**20),
        name="backward_reduce",
    )(tokens, dhid, qkv, prob, n1, w_one, vec, *grads, sums_two, bsum_up)


def per_device(
    patch_counts, tokens, cotangent, attn_gain, attn_shift, w_qkv, b_qv, w_proj, b_proj,
    ffn_gain, ffn_shift, w_up, b_up, w_down, b_down,
):
    pairs_all, rows, width = tokens.shape
    n_mp = lax.axis_size("mp")
    n_dp = lax.axis_size("dp")
    direct = n_dp == Z * Y * C and n_mp == 2
    pairs = pairs_all // n_mp
    part = w_qkv.shape[0]
    lw = w_qkv.shape[2]
    fw = w_up.shape[1]
    mine = lax.axis_index("mp")
    off = jnp.reshape(mine * pairs, (1,)).astype(jnp.int32)
    lens = TEXT + lax.dynamic_slice_in_dim(patch_counts, mine * pairs, pairs, 0)

    vectors = jnp.stack([attn_gain, attn_shift, b_proj, ffn_gain, ffn_shift, b_down], axis=1)
    first = jnp.concatenate(
        [w_qkv.reshape(part, 3 * lw), w_proj.T, vectors, jnp.zeros((part, EXTRA - 6), F32)], axis=1
    ).astype(LOW)
    second = jnp.concatenate([w_up, w_down.T], axis=1).astype(LOW)
    bias = jnp.concatenate([b_qv.reshape(-1), b_up]).astype(LOW).astype(F32)
    bias = jnp.broadcast_to(bias, (8,) + bias.shape)
    if direct:
        w_one, w_two, bias, qkv, att, prob, hid, n1, n2, vec = gather_attention(lens, tokens, first, second, bias)
    else:
        both_axes = ("mp", "dp")
        w_one = lax.all_gather(first, both_axes, axis=0, tiled=True).reshape(n_mp, width, -1)
        w_two = lax.all_gather(second, both_axes, axis=0, tiled=True).reshape(n_mp, width, -1)
        bias = lax.all_gather(bias, "mp", axis=0)
        qkv, att, prob, hid, n1, n2, vec = attention_forward(lens, off, tokens, w_one, bias)
    out_here, act, dpre, dhid, dlow, upl, sums_two, bsum_up = ffn(lens, off, n2, hid, cotangent, w_two, bias, vec)

    def grad(left, right):
        return jnp.einsum(
            "rd,rf->df", left.reshape(pairs * rows, width), right.reshape(pairs * rows, -1),
            preferred_element_type=F32,
        )

    def reduce(grads, small):
        axes = ("mp", "dp")
        done = [
            lax.psum_scatter(
                g.reshape(width, n_mp, -1).swapaxes(0, 1).reshape(n_mp * width, -1), axes,
                scatter_dimension=0, tiled=True,
            )
            for g in grads
        ]
        if small is not None:
            done.append(lax.psum(small, axes))
        return done

    def both(array, other=None):
        if other is None:
            other = lax.ppermute(array, "mp", [(0, 1), (1, 0)])
        return jnp.where(mine == 0, jnp.concatenate([array, other]), jnp.concatenate([other, array]))

    block_out = both(out_here)
    grads = [grad(n2, dpre), grad(upl, act), grad(dlow, att)]
    if direct:
        tok_here, tok_other, r_up, r_down, r_proj, r_qkv, small = backward_reduce(
            tokens, dhid, qkv, prob, n1, w_one, vec, [g.astype(LOW) for g in grads], sums_two, bsum_up)
        tokens_grad = both(tok_here, tok_other)
        flat = small[1, : 3 * width].reshape(n_mp, 3, lw)
        small = jnp.concatenate([
            small[2], small[3, : 2 * width], flat[:, 0].reshape(-1), flat[:, 2].reshape(-1), small[0]])
    else:
        tok_here, dqkv, sums_one, bsum_qkv = attention_backward(lens, off, tokens, dhid, qkv, prob, w_one, vec)
        tokens_grad = both(tok_here)
        flat = bsum_qkv[0].reshape(n_mp, 3, lw)
        small = jnp.concatenate([
            sums_one[0], sums_one[1], sums_two[2], sums_two[0], sums_two[1], sums_two[3],
            flat[:, 0].reshape(-1), flat[:, 2].reshape(-1), bsum_up[0]])
        r_up, r_down, r_proj, r_qkv, small = reduce(grads + [grad(n1, dqkv)], small)
    place_dp = lax.axis_index("dp") * part

    def piece(i):
        return lax.dynamic_slice_in_dim(small, i * width + place_dp, part, 0)

    rest = small[6 * width :]
    o_b_q = lax.dynamic_slice_in_dim(rest, mine * lw, lw, 0)
    o_b_v = lax.dynamic_slice_in_dim(rest, (n_mp + mine) * lw, lw, 0)
    o_b_up = lax.dynamic_slice_in_dim(rest, 2 * n_mp * lw + mine * fw, fw, 0)
    return (
        block_out, tokens_grad, piece(0), piece(1),
        r_qkv.reshape(part, 3, lw), jnp.stack([o_b_q, o_b_v]),
        r_proj.T, piece(2), piece(3), piece(4), r_up, o_b_up, r_down.T, piece(5),
    )


def solution(mesh):
    vec, mat = P("dp"), P("dp", "mp")
    tok = P("dp", None, None)
    in_specs = (
        vec, tok, tok, vec, vec, P("dp", None, "mp"), P(None, "mp"), P("mp", "dp"), vec, vec, vec,
        mat, P("mp"), P("mp", "dp"), vec,
    )
    out_specs = (
        tok, tok, vec, vec, P("dp", None, "mp"), P(None, "mp"), P("mp", "dp"), vec, vec, vec,
        mat, P("mp"), P("mp", "dp"), vec,
    )
    return jax.shard_map(per_device, mesh=mesh, in_specs=in_specs, out_specs=out_specs, check_vma=False)
```

```python
import functools

import jax
import jax.numpy as jnp
from jax import lax
from jax.experimental import pallas as pl
from jax.experimental.pallas import tpu as pltpu
from jax.sharding import PartitionSpec as P

HEADS = 12
HEAD_DIM = 64
TEXT = 40
LOW = jnp.bfloat16
F32 = jnp.float32
EXTRA = 128
NT = (((1,), (1,)), ((), ()))
NN = (((1,), (0,)), ((), ()))


def dot(a, b, dims=NN):
    return lax.dot_general(a, b, dims, preferred_element_type=F32)


def moments(v):
    center = v - jnp.mean(v, axis=-1, keepdims=True)
    spread = jnp.mean(center * center, axis=-1, keepdims=True)
    r = lax.rsqrt(spread + 1e-06)
    return center * r, r


def row_ids(rows):
    return lax.broadcasted_iota(jnp.int32, (rows, 1), 0)


def attn_body(p, count, x, w_ref, bias_ref, vec_ref, qkv_ref, att_ref, prob_ref, hid_ref, n1_ref, n2_ref, hook):
    rows, width = x.shape
    groups = w_ref.shape[0]
    lw = width // groups
    tiles = lw // 128
    x = x.astype(F32)
    xhat, _ = moments(x)
    n1 = (xhat * vec_ref[0:1] + vec_ref[1:2]).astype(LOW)
    n1_ref[0] = n1
    for m in range(groups):
        y = dot(n1, w_ref[m, :, : 3 * lw])
        base = m * 3 * lw
        qkv_ref[0, :, base : base + lw] = (y[:, :lw] + bias_ref[m, 0:1, :lw]).astype(LOW)
        qkv_ref[0, :, base + lw : base + 2 * lw] = y[:, lw : 2 * lw].astype(LOW)
        qkv_ref[0, :, base + 2 * lw : base + 3 * lw] = (
            y[:, 2 * lw :] + bias_ref[m, 0:1, lw : 2 * lw]
        ).astype(LOW)
    keep = row_ids(rows) < count
    first = lax.broadcasted_iota(jnp.int32, (1, 128), 1) < HEAD_DIM

    def pair(hp, carry):
        base = (hp // tiles) * 3 * lw + lax.rem(hp, tiles) * 128

        def cols(t):
            return pl.ds(pl.multiple_of(base + t * lw, 128), 128)

        q2 = qkv_ref[0, :, cols(0)] * 0.125
        k2 = qkv_ref[0, :, cols(1)]
        v2t = qkv_ref[0, :, cols(2)].T
        outs = []
        for h in range(2):
            qh = jnp.where(first if h == 0 else ~first, q2, 0)
            st = dot(k2, qh, NT)
            st = jnp.where(keep, st, -1e30)
            e = jnp.exp(st - jnp.max(st, axis=0, keepdims=True))
            pt = (e * (1.0 / jnp.sum(e, axis=0, keepdims=True))).astype(LOW)
            prob_ref[0, hp * 2 + h] = pt
            outs.append(dot(v2t[h * HEAD_DIM : (h + 1) * HEAD_DIM], pt))
        att_ref[0, :, pl.ds(pl.multiple_of(hp * 128, 128), 128)] = jnp.concatenate(outs, axis=0).T.astype(LOW)
        hook(hp)
        return carry

    lax.fori_loop(0, groups * tiles, pair, 0)
    proj = sum(dot(att_ref[0, :, m * lw : (m + 1) * lw], w_ref[m, :, 3 * lw : 4 * lw], NT) for m in range(groups))
    hid = x + proj + vec_ref[2:3]
    hid_ref[0] = hid
    xhat2, _ = moments(hid)
    n2_ref[0] = (xhat2 * vec_ref[3:4] + vec_ref[4:5]).astype(LOW)


def attn_kernel(lens, off, x_ref, w_ref, bias_ref, qkv_ref, att_ref, prob_ref, hid_ref, n1_ref, n2_ref, vec_ref):
    p = pl.program_id(0)
    lw = x_ref.shape[2] // w_ref.shape[0]

    @pl.when(p == 0)
    def _():
        vec_ref[...] = w_ref[0, :, 4 * lw :].astype(F32).T[:8]

    attn_body(p, lens[p], x_ref[0], w_ref, bias_ref, vec_ref, qkv_ref, att_ref, prob_ref, hid_ref, n1_ref, n2_ref,
              lambda hp: None)


def const_spec(shape):
    return pl.BlockSpec(shape, lambda *_: (0,) * len(shape), pipeline_mode=pl.Buffered(1))


def pair_spec(*shape):
    return pl.BlockSpec((1,) + shape, lambda p, *_: (p,) + (0,) * len(shape))


def attention_forward(lens, off, tokens, w_one, bias):
    pairs = lens.shape[0]
    _, rows, width = tokens.shape
    out = lambda dt, *s: jax.ShapeDtypeStruct((pairs,) + s, dt)
    return pl.pallas_call(
        attn_kernel,
        grid_spec=pltpu.PrefetchScalarGridSpec(
            num_scalar_prefetch=2,
            grid=(pairs,),
            in_specs=[
                pl.BlockSpec((1, rows, width), lambda p, lens, off: (off[0] + p, 0, 0)),
                const_spec(w_one.shape),
                const_spec(bias.shape),
            ],
            out_specs=[
                pair_spec(rows, 3 * width), pair_spec(rows, width), pair_spec(HEADS, rows, rows),
                pair_spec(rows, width), pair_spec(rows, width), pair_spec(rows, width),
                pl.BlockSpec((8, width), lambda *_: (0, 0)),
            ],
        ),
        out_shape=[
            out(LOW, rows, 3 * width), out(LOW, rows, width), out(LOW, HEADS, rows, rows),
            out(F32, rows, width), out(LOW, rows, width), out(LOW, rows, width),
            jax.ShapeDtypeStruct((8, width), F32),
        ],
        compiler_params=pltpu.CompilerParams(vmem_limit_bytes=60 * 2**20),
        name="attention_forward",
    )(lens, off, tokens, w_one, bias)


def ffn_kernel(lens, off, n2_ref, hid_ref, cot_ref, w_ref, bias_ref, vec_ref,
               out_ref, act_ref, dpre_ref, dhid_ref, dlow_ref, upl_ref, sums_ref, bsum_ref):
    p = pl.program_id(0)
    rows, width = n2_ref.shape[1], n2_ref.shape[2]
    groups = w_ref.shape[0]
    fw = w_ref.shape[2] // 2
    lw = width // groups
    step = 512
    keep = row_ids(rows) < lens[p]
    n2 = n2_ref[0]
    upl = jnp.where(keep, cot_ref[0], 0)
    upl_ref[0] = upl

    @pl.when(p == 0)
    def _():
        sums_ref[...] = jnp.zeros_like(sums_ref)
        bsum_ref[...] = jnp.zeros_like(bsum_ref)

    for m in range(groups):
        for c in range(0, fw, step):
            pre = dot(n2, w_ref[m, :, c : c + step]) + bias_ref[m, 0:1, 2 * lw + c : 2 * lw + c + step]
            cdf = 0.5 * (1.0 + lax.erf(pre * (2.0 ** -0.5)))
            at = m * fw + c
            act_ref[0, :, at : at + step] = (pre * cdf).astype(LOW)
            slope = cdf + pre * (0.3989422804014327 * jnp.exp(-0.5 * pre * pre))
            dpre = slope * dot(upl, w_ref[m, :, fw + c : fw + c + step])
            dpre_ref[0, :, at : at + step] = dpre.astype(LOW)
            bsum_ref[0:1, at : at + step] += jnp.sum(dpre, axis=0, keepdims=True)
    hid = hid_ref[0]
    down = sum(dot(act_ref[0, :, m * fw : (m + 1) * fw], w_ref[m, :, fw:], NT) for m in range(groups))
    out_ref[0] = jnp.where(keep, hid + down + vec_ref[5:6], 0.0).astype(LOW)
    dtwo = sum(dot(dpre_ref[0, :, m * fw : (m + 1) * fw], w_ref[m, :, :fw], NT) for m in range(groups))
    xhat, r = moments(hid)
    dg = dtwo * vec_ref[3:4]
    dn = r * (dg - jnp.mean(dg, axis=-1, keepdims=True) - xhat * jnp.mean(dg * xhat, axis=-1, keepdims=True))
    upf = upl.astype(F32)
    dhid = upf + dn
    dhid_ref[0] = dhid
    dlow_ref[0] = dhid.astype(LOW)
    sums_ref[0:1] += jnp.sum(dtwo * xhat, axis=0, keepdims=True)
    sums_ref[1:2] += jnp.sum(dtwo, axis=0, keepdims=True)
    sums_ref[2:3] += jnp.sum(dhid, axis=0, keepdims=True)
    sums_ref[3:4] += jnp.sum(upf, axis=0, keepdims=True)


def ffn(lens, off, n2, hid, cotangent, w_two, bias, vec):
    pairs, rows, width = n2.shape
    ff = w_two.shape[0] * w_two.shape[2] // 2
    out = lambda dt, *s: jax.ShapeDtypeStruct((pairs,) + s, dt)
    return pl.pallas_call(
        ffn_kernel,
        grid_spec=pltpu.PrefetchScalarGridSpec(
            num_scalar_prefetch=2,
            grid=(pairs,),
            in_specs=[
                pair_spec(rows, width), pair_spec(rows, width),
                pl.BlockSpec((1, rows, width), lambda p, lens, off: (off[0] + p, 0, 0)),
                const_spec(w_two.shape), const_spec(bias.shape), const_spec(vec.shape),
            ],
            out_specs=[
                pair_spec(rows, width), pair_spec(rows, ff), pair_spec(rows, ff), pair_spec(rows, width),
                pair_spec(rows, width), pair_spec(rows, width),
                pl.BlockSpec((8, width), lambda *_: (0, 0)), pl.BlockSpec((8, ff), lambda *_: (0, 0)),
            ],
        ),
        out_shape=[
            out(LOW, rows, width), out(LOW, rows, ff), out(LOW, rows, ff), out(F32, rows, width),
            out(LOW, rows, width), out(LOW, rows, width),
            jax.ShapeDtypeStruct((8, width), F32), jax.ShapeDtypeStruct((8, ff), F32),
        ],
        compiler_params=pltpu.CompilerParams(vmem_limit_bytes=60 * 2**20),
        name="feed_forward",
    )(lens, off, n2, hid, cotangent, w_two, bias, vec)


def plain_back_kernel(lens, off, x_ref, dhid_ref, qkv_ref, prob_ref, w_ref, vec_ref,
                tok_ref, dqkv_ref, sums_ref, bsum_ref, do_ref):
    p = pl.program_id(0)
    rows, width = x_ref.shape[1], x_ref.shape[2]
    groups = w_ref.shape[0]
    lw = width // groups
    tiles = lw // 128

    @pl.when(p == 0)
    def _():
        sums_ref[...] = jnp.zeros_like(sums_ref)
        bsum_ref[...] = jnp.zeros_like(bsum_ref)

    dhid = dhid_ref[0]
    dlow = dhid.astype(LOW)
    for m in range(groups):
        do_ref[:, m * lw : (m + 1) * lw] = dot(dlow, w_ref[m, :, 3 * lw : 4 * lw]).astype(LOW)
    first = lax.broadcasted_iota(jnp.int32, (1, 128), 1) < HEAD_DIM

    def pair(hp, carry):
        base = (hp // tiles) * 3 * lw + (hp % tiles) * 128

        def cols(t):
            return pl.ds(pl.multiple_of(base + t * lw, 128), 128)

        q2 = qkv_ref[0, :, cols(0)] * 0.125
        k2t = qkv_ref[0, :, cols(1)].T
        v2 = qkv_ref[0, :, cols(2)]
        do2 = do_ref[:, pl.ds(pl.multiple_of(hp * 128, 128), 128)]
        dq_t = []
        dk = dv = 0.0
        for h in range(2):
            mine = first if h == 0 else ~first
            doh = jnp.where(mine, do2, 0)
            qh = jnp.where(mine, q2, 0)
            dpt = dot(v2, doh, NT)
            plow = prob_ref[0, hp * 2 + h]
            pt = plow.astype(F32)
            inner = jnp.sum(pt * dpt, axis=0, keepdims=True)
            dst = (pt * (dpt - inner)).astype(LOW)
            dv = dv + dot(plow, doh)
            dk = dk + dot(dst, qh)
            dq_t.append(dot(k2t[h * HEAD_DIM : (h + 1) * HEAD_DIM], dst))
        dq = (jnp.concatenate(dq_t, axis=0) * 0.125).T
        dqkv_ref[0, :, cols(0)] = dq.astype(LOW)
        dqkv_ref[0, :, cols(1)] = dk.astype(LOW)
        dqkv_ref[0, :, cols(2)] = dv.astype(LOW)
        bsum_ref[0:1, cols(0)] += jnp.sum(dq, axis=0, keepdims=True)
        bsum_ref[0:1, cols(2)] += jnp.sum(dv, axis=0, keepdims=True)
        return carry

    lax.fori_loop(0, groups * tiles, pair, 0)
    done = sum(dot(dqkv_ref[0, :, m * 3 * lw : (m + 1) * 3 * lw], w_ref[m, :, : 3 * lw], NT) for m in range(groups))
    xhat, r = moments(x_ref[0].astype(F32))
    dg = done * vec_ref[0:1]
    dn = r * (dg - jnp.mean(dg, axis=-1, keepdims=True) - xhat * jnp.mean(dg * xhat, axis=-1, keepdims=True))
    tok_ref[0] = (dhid + dn).astype(LOW)
    sums_ref[0:1] += jnp.sum(done * xhat, axis=0, keepdims=True)
    sums_ref[1:2] += jnp.sum(done, axis=0, keepdims=True)


def attention_backward(lens, off, tokens, dhid, qkv, prob, w_one, vec):
    pairs, rows, width = dhid.shape
    out = lambda dt, *s: jax.ShapeDtypeStruct((pairs,) + s, dt)
    return pl.pallas_call(
        plain_back_kernel,
        grid_spec=pltpu.PrefetchScalarGridSpec(
            num_scalar_prefetch=2,
            grid=(pairs,),
            in_specs=[
                pl.BlockSpec((1, rows, width), lambda p, lens, off: (off[0] + p, 0, 0)),
                pair_spec(rows, width), pair_spec(rows, 3 * width), pair_spec(HEADS, rows, rows),
                const_spec(w_one.shape), const_spec(vec.shape),
            ],
            out_specs=[
                pair_spec(rows, width), pair_spec(rows, 3 * width),
                pl.BlockSpec((8, width), lambda *_: (0, 0)), pl.BlockSpec((8, 3 * width), lambda *_: (0, 0)),
            ],
            scratch_shapes=[pltpu.VMEM((rows, width), LOW)],
        ),
        out_shape=[
            out(LOW, rows, width), out(LOW, rows, 3 * width),
            jax.ShapeDtypeStruct((8, width), F32), jax.ShapeDtypeStruct((8, 3 * width), F32),
        ],
        compiler_params=pltpu.CompilerParams(vmem_limit_bytes=60 * 2**20),
        name="attention_backward",
    )(lens, off, tokens, dhid, qkv, prob, w_one, vec)
MESH_ID = pl.DeviceIdType.MESH
Z, Y, C = 4, 2, 2


def place():
    dp = lax.axis_index("dp")
    m = lax.axis_index("mp")
    c = lax.rem(dp, 2)
    y = lax.rem(dp // 2, 2)
    z = dp // 4
    return z, y, c, m


def index(z, y, c):
    return (z * Y + y) * C + c


def flips(y, c, m):
    one = (y + c * (1 - 2 * y), m + (1 - c) * (1 - 2 * m))
    two = (y + (1 - c) * (1 - 2 * y), m + c * (1 - 2 * m))
    return one, two


def greet(z, y, c, m):
    barrier = pltpu.get_barrier_semaphore()
    (y1, m1), (y2, m2) = flips(y, c, m)
    peers = [(index(lax.rem(z + k, Z), y, c), m) for k in (1, 2, 3)]
    peers += [(index(z, y1, c), m1), (index(z, y2, c), m2), (index(z, y, 1 - c), m)]
    for dp, mp in peers:
        pl.semaphore_signal(barrier, inc=1, device_id={"dp": dp, "mp": mp}, device_id_type=MESH_ID)
    pl.semaphore_wait(barrier, len(peers))
    return peers


def gather_attn_kernel(lens, tok_all, first_ref, second_ref, b_in,
                       w_one_out, w_two, b_out, qkv_ref, att_ref, prob_ref, hid_ref, n1_ref, n2_ref, vec_ref,
                       w_one, bias, xbuf, send, recv, bsem, local):
    p = pl.program_id(0)
    z, y, c, m = place()
    (y1, m1), (y2, m2) = flips(y, c, m)
    pairs, rows, width = xbuf.shape
    part = first_ref.shape[0]
    cols = second_ref.shape[1] // 2
    lw = width // 2
    per_pair = width // 128
    me = index(z, y, c)
    one, two, sib = (index(z, y1, c), m1), (index(z, y2, c), m2), (index(z, y, 1 - c), m)

    def spot(g, dp, mp):
        at = pl.ds(pl.multiple_of(dp * part, part), part)
        if g is None:
            return w_one.at[mp, at]
        return w_two.at[mp, at, pl.ds(pl.multiple_of(g * cols, 128), cols)]

    def shard(g):
        return first_ref if g is None else second_ref.at[:, pl.ds(pl.multiple_of(g * cols, 128), cols)]

    def row(g):
        return 0 if g is None else g + 1

    def copy_of(g, src, dst, out_sem, in_sem, to):
        return pltpu.make_async_remote_copy(
            src_ref=src, dst_ref=dst, send_sem=send.at[row(g), out_sem], recv_sem=recv.at[row(g), in_sem],
            device_id={"dp": to[0], "mp": to[1]}, device_id_type=MESH_ID,
        )

    def push(g, src, dp, mp, to, sem):
        copy_of(g, src, spot(g, dp, mp), sem, mp * (Z * Y * C) + dp, to).start()

    def arrived(g, dp, mp):
        at = spot(g, dp, mp)
        copy_of(g, at, at, 0, mp * (Z * Y * C) + dp, sib).wait_recv()
        return at

    def own_z(g):
        for k in (1, 3, 2):
            push(g, shard(g), me, m, (index(lax.rem(z + k, Z), y, c), m), k - 1)

    def own_near(g):
        for n, to in enumerate((one, two, sib)):
            push(g, shard(g), me, m, to, 3 + n)

    def event_z(g, i):
        dp = index(lax.rem(z + 1 + lax.rem(2 * i, 3), Z), y, c)
        at = arrived(g, dp, m)
        for n, to in enumerate((one, two, sib)):
            push(g, at, dp, m, to, 6 + 3 * i + n)

    def event_one(g, i):
        dp = index(lax.rem(z + i, Z), y1, c)
        at = arrived(g, dp, m1)
        for n, to in enumerate((two, sib)):
            push(g, at, dp, m1, to, 15 + 2 * i + n)

    def event_two(g, i):
        far = lax.rem(i, 2)
        yy = y2 + far * (1 - y - y2)
        mm = m2 + far * (1 - m - m2)
        dp = index(lax.rem(z + i // 2, Z), yy, c)
        push(g, arrived(g, dp, mm), dp, mm, sib, 23 + i)

    def event_core(g, i):
        arrived(g, index(i // 4, lax.rem(i // 2, 2), 1 - c), lax.rem(i, 2))

    def loop(n, event, g):
        def run(i, carry):
            event(g, i)
            return carry

        lax.fori_loop(0, n, run, 0)

    bias_copy = pltpu.make_async_remote_copy(
        src_ref=b_in, dst_ref=bias.at[m], send_sem=bsem.at[0], recv_sem=bsem.at[1],
        device_id={"dp": me, "mp": 1 - m}, device_id_type=MESH_ID,
    )
    x_copy = pltpu.make_async_copy(tok_all.at[pl.ds(m * pairs, pairs)], xbuf, local.at[0])
    mine = [
        pltpu.make_async_copy(b_in, bias.at[m], local.at[1]),
        pltpu.make_async_copy(first_ref, spot(None, me, m), local.at[2]),
    ]
    mine_two = [pltpu.make_async_copy(shard(g), spot(g, me, m), local.at[3 + g]) for g in range(2)]
    keep_one = pltpu.make_async_copy(w_one, w_one_out, local.at[5])
    keep_bias = pltpu.make_async_copy(bias, b_out, local.at[6])

    @pl.when(p == 0)
    def _():
        for copy in mine + mine_two:
            copy.start()
        x_copy.start()
        greet(z, y, c, m)
        own_z(None)
        own_near(None)
        bias_copy.start()
        own_z(0)
        own_z(1)
        loop(3, event_z, None)
        loop(4, event_one, None)
        own_near(0)
        loop(3, event_z, 0)
        loop(8, event_two, None)
        for copy in mine + [x_copy, bias_copy]:
            copy.wait()
        loop(16, event_core, None)
        keep_one.start()
        keep_bias.start()
        vec_ref[...] = w_one[0, :, 4 * lw :].astype(F32).T[:8]

    def hook(hp):
        step = p * per_pair + hp

        def event(e, carry):
            @pl.when(e == 0)
            def _():
                own_near(1)

            @pl.when(((e >= 1) & (e < 5)) | ((e >= 16) & (e < 20)))
            def _():
                g = e // 16
                event_one(g, e - 1 - 15 * g)

            @pl.when((e >= 5) & (e < 8))
            def _():
                event_z(1, e - 5)

            @pl.when(((e >= 8) & (e < 16)) | (e >= 20))
            def _():
                g = e // 20
                event_two(g, e - 8 - 12 * g)

            return carry

        total = pairs * per_pair
        lax.fori_loop(step * 28 // total, (step + 1) * 28 // total, event, 0)

    attn_body(p, lens[p], xbuf[p], w_one, bias, vec_ref, qkv_ref, att_ref, prob_ref, hid_ref, n1_ref, n2_ref, hook)

    @pl.when(p == pairs - 1)
    def _():
        for g in range(2):
            loop(16, event_core, g)
        for copy in mine_two + [keep_one, keep_bias]:
            copy.wait()
        for g in (None, 0, 1):
            def sent(i, carry):
                copy_of(g, shard(g), shard(g), i, 0, sib).wait_send()
                return carry

            lax.fori_loop(0, 31, sent, 0)


def gather_attention(lens, tokens, first, second, bias):
    pairs = lens.shape[0]
    _, rows, width = tokens.shape
    part = first.shape[0]
    total = Z * Y * C
    hbm = pl.BlockSpec(memory_space=pl.ANY)
    out = lambda dt, *s: jax.ShapeDtypeStruct((pairs,) + s, dt)
    return pl.pallas_call(
        gather_attn_kernel,
        grid_spec=pltpu.PrefetchScalarGridSpec(
            num_scalar_prefetch=1,
            grid=(pairs,),
            in_specs=[hbm, const_spec(first.shape), const_spec(second.shape), const_spec(bias.shape)],
            out_specs=[
                hbm, hbm, hbm,
                pair_spec(rows, 3 * width), pair_spec(rows, width), pair_spec(HEADS, rows, rows),
                pair_spec(rows, width), pair_spec(rows, width), pair_spec(rows, width),
                pl.BlockSpec((8, width), lambda *_: (0, 0)),
            ],
            scratch_shapes=[
                pltpu.VMEM((2, total * part, first.shape[1]), LOW), pltpu.VMEM((2,) + bias.shape, F32),
                pltpu.VMEM((pairs, rows, width), LOW),
                pltpu.SemaphoreType.DMA((3, 31)), pltpu.SemaphoreType.DMA((3, 32)),
                pltpu.SemaphoreType.DMA((2,)), pltpu.SemaphoreType.DMA((7,)),
            ],
        ),
        out_shape=[
            jax.ShapeDtypeStruct((2, total * part, first.shape[1]), LOW),
            jax.ShapeDtypeStruct((2, total * part, second.shape[1]), LOW),
            jax.ShapeDtypeStruct((2,) + bias.shape, F32),
            out(LOW, rows, 3 * width), out(LOW, rows, width), out(LOW, HEADS, rows, rows),
            out(F32, rows, width), out(LOW, rows, width), out(LOW, rows, width),
            jax.ShapeDtypeStruct((8, width), F32),
        ],
        compiler_params=pltpu.CompilerParams(collective_id=0, has_side_effects=True, vmem_limit_bytes=60 * 2**20),
        name="gather_attention",
    )(lens, tokens, first, second, bias)


BLOCKS = 31


def back_kernel(lens, cot, hid_in, n2_in, att_in, n1_all, qkv_all, prob_all, tok_all, w_one_in, w_two, bias_ref, vec_ref,
                block_out, tok_out, r_ff, r_proj, r_qkv, small_out,
                g_ff, g_proj, g_qkv, rc_ff, rs_ff, rz_ff, rx_ff, rc_p, rs_p, rz_p, rx_p, rc_q, rs_q, rz_q, rx_q,
                dhid_ref, outbuf, sums, bsum, bsum_up, sbuf, send, recv, local, osem, tsem, ssem):
    flat, width = outbuf.shape
    pairs, rows = qkv_all.shape[0], qkv_all.shape[1]
    groups = w_two.shape[0]
    fw = w_two.shape[2] // 2
    fc = fw // 3
    lw = width // groups
    tiles = lw // 128
    half = flat // 2
    part = r_proj.shape[1]
    z, y, c, m = place()
    me = index(z, y, c)
    sib = (index(z, y, 1 - c), m)

    def beside(k):
        return (index(lax.rem(z + k, Z), y, c), m)

    def loop(n, event):
        def one(i, carry):
            event(i)
            return carry

        lax.fori_loop(0, n, one, 0)

    def family(grad, rc, rs, rz, rx, out, row0):
        cols = rc.shape[2]

        def copy_of(u, src, dst, out_sem, in_sem, to):
            return pltpu.make_async_remote_copy(
                src_ref=src, dst_ref=dst, send_sem=send.at[row0 + u, out_sem], recv_sem=recv.at[row0 + u, in_sem],
                device_id={"dp": to[0], "mp": to[1]}, device_id_type=MESH_ID,
            )

        def block(u, ra, rb, k, cc):
            yy = y + ra * (1 - 2 * y)
            mm = m + rb * (1 - 2 * m)
            return u, lax.rem(z + k, Z) * Y + yy, cc, slice(None), pl.ds(pl.multiple_of(mm * cols, 128), cols)

        def to_sibling(u, rb):
            def one(i):
                ra, k = 1 - i // 4, lax.rem(i + 1, 4)
                slot = (ra * 2 + rb) * 4 + k
                copy_of(u, grad.at[block(u, ra, rb, k, 1 - c)], rc.at[u * 16 + slot], slot, slot, sib).start()

            loop(8, one)

        def arrived(u, ref, sem):
            copy_of(u, ref, ref, 0, sem, sib).wait_recv()

        def base(u, ra, rb, k):
            slot = (ra * 2 + rb) * 4 + k
            arrived(u, rc.at[u * 16 + slot], slot)
            return grad[block(u, ra, rb, k, c)].astype(F32) + rc[u * 16 + slot].astype(F32)

        def level(u, rb, k):
            at = rb * 4 + k
            value = base(u, 0, rb, k)
            arrived(u, rs.at[u * 8 + at], 16 + at)
            return value + rs[u * 8 + at].astype(F32)

        def lined(u, rb):
            value = level(u, rb, 0)
            for k in (1, 2, 3):
                at = (k - 1) * 2 + rb
                arrived(u, rz.at[u * 6 + at], 24 + at)
                value = value + rz[u * 6 + at].astype(F32)
            return value

        def event_y(u, rb, i):
            k = lax.rem(i + 1, 4)
            slot = u * 16 + (2 + rb) * 4 + k
            at = rb * 4 + k
            rc[slot] = base(u, 1, rb, k).astype(LOW)
            copy_of(u, rc.at[slot], rs.at[u * 8 + at], 16 + at, 16 + at, (index(z, 1 - y, c), m)).start()

        def event_z(u, rb, i):
            k = 1 + i
            slot = u * 16 + rb * 4 + k
            at = (k - 1) * 2 + rb
            rc[slot] = level(u, rb, k).astype(LOW)
            copy_of(u, rc.at[slot], rz.at[u * 6 + at], 24 + at, 24 + at, beside(k)).start()

        def event_x(u):
            rc[u * 16 + 4] = lined(u, 1).astype(LOW)
            copy_of(u, rc.at[u * 16 + 4], rx.at[u], 30, 30, (me, 1 - m)).start()

        def final(u):
            value = lined(u, 0)
            arrived(u, rx.at[u], 30)
            out[u] = value + rx[u].astype(F32)

            def one(i):
                copy_of(u, rc.at[0], rc.at[0], i, 0, sib).wait_send()

            loop(BLOCKS, one)

        return to_sibling, event_y, event_z, event_x, final

    ff_sib, ff_y, ff_z, ff_x, ff_final = family(g_ff, rc_ff, rs_ff, rz_ff, rx_ff, r_ff, 0)
    p_sib, p_y, p_z, p_x, p_final = family(g_proj, rc_p, rs_p, rz_p, rx_p, r_proj, 2)
    q_sib, q_y, q_z, q_x, q_final = family(g_qkv, rc_q, rs_q, rz_q, rx_q, r_qkv, 3)

    def out_copies(r):
        src = outbuf.at[pl.ds(pl.multiple_of(r * half, 16), half)]
        dst = block_out.at[pl.ds(pl.multiple_of(m * flat + r * half, 16), half)]
        return pltpu.make_async_copy(src, dst, osem.at[0, r]), pltpu.make_async_remote_copy(
            src_ref=src, dst_ref=dst, send_sem=osem.at[1, r], recv_sem=osem.at[2, r],
            device_id={"dp": me, "mp": 1 - m}, device_id_type=MESH_ID,
        )

    def keep_of(r):
        ids = row_ids(half)
        return ids < jnp.where(ids < rows, lens[2 * r], lens[2 * r + 1] + rows)

    def span(r):
        return pl.ds(pl.multiple_of(r * half, 16), half)

    sums[...] = jnp.zeros_like(sums)
    bsum[...] = jnp.zeros_like(bsum)
    bsum_up[...] = jnp.zeros_like(bsum_up)

    def feed_forward(n2, n2t, upl, uplt, hid, acc, slope, chunk, wbuf):
        def place_of(f):
            i = lax.rem(f, 6)
            return lax.rem(m + 1 + i // 3, 2), lax.rem(i, 3) * fc

        def weights(f):
            mm, at = place_of(f)
            slot = lax.rem(f, 2)
            return [
                pltpu.make_async_copy(
                    w_two.at[mm, :, pl.ds(pl.multiple_of(t * fw + at, 128), fc)], wbuf.at[slot, t], local.at[slot * 2 + t])
                for t in range(2)
            ]

        n2_copy = pltpu.make_async_copy(n2_in, n2, local.at[4])
        up_copy = pltpu.make_async_copy(cot.at[pl.ds(pl.multiple_of(m * flat, 16), flat)], upl, local.at[5])
        hid_copy = pltpu.make_async_copy(hid_in, hid, local.at[6])
        att_copy = pltpu.make_async_copy(att_in, slope.at[:, pl.ds(0, width)], local.at[7])
        n2_copy.start()
        up_copy.start()
        for copy in weights(0):
            copy.start()
        hid_copy.start()
        greet(z, y, c, m)
        up_copy.wait()

        def prepare(r):
            value = jnp.where(keep_of(r), upl[span(r)], 0)
            upl[span(r)] = value
            sums[3:4] += jnp.sum(value.astype(F32), axis=0, keepdims=True)
            acc[span(r)] = jnp.zeros((half, width), F32)

        loop(2, prepare)
        uplt[...] = upl[...].T
        n2_copy.wait()
        n2t[...] = n2[...].T

        def traffic(f):
            @pl.when(lax.rem(f, 3) == 2)
            def _():
                n = f // 3
                ff_sib(n // 2, 1 - lax.rem(n, 2))

            @pl.when((lax.rem(f, 3) == 0) & (f > 0))
            def _():
                n = f // 3 - 1
                loop(4, lambda i: ff_y(n // 2, 1 - lax.rem(n, 2), i))

            @pl.when((lax.rem(f, 3) == 1) & (f > 4))
            def _():
                n = (f - 7) // 3
                loop(3, lambda i: ff_z(n // 2, 1 - lax.rem(n, 2), i))

        def store(u, at, value):
            g_ff[u, :, :, :, at] = value.astype(LOW).reshape(Z * Y, C, part, fc)

        def forward(f):
            slot = lax.rem(f, 2)
            for copy in weights(f + 1):
                copy.start()
            for copy in weights(f):
                copy.wait()
            mm, off = place_of(f)
            at = pl.ds(pl.multiple_of(mm * fw + off, 128), fc)
            shift = bias_ref[mm, 0:1, pl.ds(pl.multiple_of(2 * lw + off, 128), fc)]

            def block(r):
                pre = dot(n2[span(r)], wbuf[slot, 0]) + shift
                cdf = 0.5 * (1.0 + lax.erf(pre * (2.0 ** -0.5)))
                chunk[span(r)] = (pre * cdf).astype(LOW)
                slope[span(r), at] = (cdf + pre * (0.3989422804014327 * jnp.exp(-0.5 * pre * pre))).astype(LOW)
                acc[span(r)] += dot(chunk[span(r)], wbuf[slot, 1], NT)

            loop(2, block)
            store(0, at, dot(uplt[...], chunk[...]))
            traffic(f)

        loop(6, forward)
        hid_copy.wait()

        def leave(r):
            outbuf[span(r)] = jnp.where(keep_of(r), hid[span(r)] + acc[span(r)] + vec_ref[5:6], 0.0).astype(LOW)
            acc[span(r)] = jnp.zeros((half, width), F32)
            for copy in out_copies(r):
                copy.start()

        loop(2, leave)

        def backward(i):
            f = 6 + i
            slot = lax.rem(f, 2)

            @pl.when(f < 11)
            def _():
                for copy in weights(f + 1):
                    copy.start()

            for copy in weights(f):
                copy.wait()
            mm, off = place_of(f)
            at = pl.ds(pl.multiple_of(mm * fw + off, 128), fc)

            def block(r):
                dpre = slope[span(r), at].astype(F32) * dot(upl[span(r)], wbuf[slot, 1])
                chunk[span(r)] = dpre.astype(LOW)
                bsum_up[0:1, at] += jnp.sum(dpre, axis=0, keepdims=True)
                acc[span(r)] += dot(chunk[span(r)], wbuf[slot, 0], NT)

            loop(2, block)
            store(1, at, dot(n2t[...], chunk[...]))
            traffic(f)

        loop(6, backward)
        att_copy.start()

        def norm_back(r):
            dtwo = acc[span(r)]
            xhat, rr = moments(hid[span(r)])
            dg = dtwo * vec_ref[3:4]
            dn = rr * (dg - jnp.mean(dg, axis=-1, keepdims=True) - xhat * jnp.mean(dg * xhat, axis=-1, keepdims=True))
            dhid = upl[span(r)].astype(F32) + dn
            dhid_ref[span(r)] = dhid
            n2[span(r)] = dhid.astype(LOW)
            sums[4:5] += jnp.sum(dtwo * xhat, axis=0, keepdims=True)
            sums[5:6] += jnp.sum(dtwo, axis=0, keepdims=True)
            sums[2:3] += jnp.sum(dhid, axis=0, keepdims=True)

        loop(2, norm_back)
        att_copy.wait()
        n2t[...] = n2[...].T
        for mm in range(groups):
            at = slice(mm * lw, (mm + 1) * lw)
            g_proj[0, :, :, :, at] = dot(n2t[...], slope[:, at]).astype(LOW).reshape(Z * Y, C, part, lw)
        p_sib(0, 1)
        p_sib(0, 0)

    pl.run_scoped(
        feed_forward,
        pltpu.VMEM((flat, width), LOW), pltpu.VMEM((width, flat), LOW),
        pltpu.VMEM((flat, width), LOW), pltpu.VMEM((width, flat), LOW),
        pltpu.VMEM((flat, width), F32), pltpu.VMEM((flat, width), F32),
        pltpu.VMEM((flat, groups * fw), LOW), pltpu.VMEM((flat, fc), LOW), pltpu.VMEM((2, 2, width, fc), LOW),
    )

    def attention(w_ref, qkv_buf, prob_buf, n1_buf, x_buf, do_ref, n1t, dq_all, tokbuf):
        w_copy = pltpu.make_async_copy(w_one_in, w_ref, local.at[8])

        def loads(p):
            slot = lax.rem(p, 2)
            pieces = [
                (qkv_all.at[p], qkv_buf), (prob_all.at[p], prob_buf), (n1_all.at[p], n1_buf),
                (tok_all.at[m * pairs + p], x_buf),
            ]
            return [
                pltpu.make_async_copy(src, dst.at[slot], local.at[slot * 4 + t])
                for t, (src, dst) in enumerate(pieces)
            ]

        def tok_copies(p):
            src, dst = tokbuf.at[p], tok_out.at[m * pairs + p]
            return pltpu.make_async_copy(src, dst, tsem.at[0, p]), pltpu.make_async_remote_copy(
                src_ref=src, dst_ref=dst, send_sem=tsem.at[1, p], recv_sem=tsem.at[2, p],
                device_id={"dp": me, "mp": 1 - m}, device_id_type=MESH_ID,
            )

        w_copy.start()
        for copy in loads(0):
            copy.start()
        w_copy.wait()
        first = lax.broadcasted_iota(jnp.int32, (1, 128), 1) < HEAD_DIM

        def one_pair(p):
            slot = lax.rem(p, 2)

            @pl.when(p < pairs - 1)
            def _():
                for copy in loads(p + 1):
                    copy.start()

            dhid = dhid_ref[pl.ds(pl.multiple_of(p * rows, 8), rows)]
            dlow = dhid.astype(LOW)
            for mm in range(groups):
                do_ref[:, mm * lw : (mm + 1) * lw] = dot(dlow, w_ref[mm, :, 3 * lw : 4 * lw]).astype(LOW)
            for copy in loads(p):
                copy.wait()
            n1t[p] = n1_buf[slot].T

            def heads(hp):
                lane = (hp // tiles) * 3 * lw + lax.rem(hp, tiles) * 128

                def cols(t):
                    return pl.ds(pl.multiple_of(lane + t * lw, 128), 128)

                q2 = qkv_buf[slot, :, cols(0)] * 0.125
                k2t = qkv_buf[slot, :, cols(1)].T
                v2 = qkv_buf[slot, :, cols(2)]
                do2 = do_ref[:, pl.ds(pl.multiple_of(hp * 128, 128), 128)]
                dq_t = []
                dk = dv = 0.0
                for h in range(2):
                    mine = first if h == 0 else ~first
                    doh = jnp.where(mine, do2, 0)
                    qh = jnp.where(mine, q2, 0)
                    dpt = dot(v2, doh, NT)
                    plow = prob_buf[slot, hp * 2 + h]
                    pt = plow.astype(F32)
                    inner = jnp.sum(pt * dpt, axis=0, keepdims=True)
                    dst = (pt * (dpt - inner)).astype(LOW)
                    dv = dv + dot(plow, doh)
                    dk = dk + dot(dst, qh)
                    dq_t.append(dot(k2t[h * HEAD_DIM : (h + 1) * HEAD_DIM], dst))
                dq = (jnp.concatenate(dq_t, axis=0) * 0.125).T
                dq_all[p, :, cols(0)] = dq.astype(LOW)
                dq_all[p, :, cols(1)] = dk.astype(LOW)
                dq_all[p, :, cols(2)] = dv.astype(LOW)
                bsum[0:1, cols(0)] += jnp.sum(dq, axis=0, keepdims=True)
                bsum[0:1, cols(2)] += jnp.sum(dv, axis=0, keepdims=True)
                step = p * (groups * tiles) + hp

                @pl.when(step == 0)
                def _():
                    loop(4, lambda i: ff_y(1, 0, i))

                @pl.when((step == 2) | (step == 11))
                def _():
                    loop(3, lambda i: ff_z(1, 1 - step // 11, i))

                @pl.when((step >= 3) & (step < 7))
                def _():
                    loop(2, lambda i: p_y(0, 1 - (step - 3) // 2, 2 * lax.rem(step - 3, 2) + i))

                @pl.when((step == 13) | (step == 14))
                def _():
                    loop(3, lambda i: p_z(0, 14 - step, i))

                @pl.when((step == 16) | (step == 18))
                def _():
                    ff_x((step - 16) // 2)

                @pl.when(step == 20)
                def _():
                    p_x(0)

            loop(groups * tiles, heads)
            done = sum(
                dot(dq_all[p, :, mm * 3 * lw : (mm + 1) * 3 * lw], w_ref[mm, :, : 3 * lw], NT) for mm in range(groups))
            xhat, r = moments(x_buf[slot].astype(F32))
            dg = done * vec_ref[0:1]
            dn = r * (dg - jnp.mean(dg, axis=-1, keepdims=True) - xhat * jnp.mean(dg * xhat, axis=-1, keepdims=True))
            tokbuf[p] = (dhid + dn).astype(LOW)
            for copy in tok_copies(p):
                copy.start()
            sums[0:1] += jnp.sum(done * xhat, axis=0, keepdims=True)
            sums[1:2] += jnp.sum(done, axis=0, keepdims=True)

        loop(pairs, one_pair)

        def small_copy(slot, src, to, sem):
            return pltpu.make_async_remote_copy(
                src_ref=sbuf.at[src], dst_ref=sbuf.at[slot], send_sem=ssem.at[0, sem], recv_sem=ssem.at[1, sem],
                device_id={"dp": to[0], "mp": to[1]}, device_id_type=MESH_ID,
            )

        sbuf[6] = jnp.zeros_like(sbuf[6])
        sbuf[6, 0:1] = bsum_up[0:1]
        sbuf[6, 1:2, : 3 * width] = bsum[0:1]
        for n, (line, at) in enumerate(((2, 0), (2, 1), (2, 2), (3, 1), (2, 3), (3, 0))):
            sbuf[6, line : line + 1, at * width : (at + 1) * width] = sums[n : n + 1]
        s0 = small_copy(0, 6, sib, 0)
        s0.start()

        def chunk(i):
            mm = lax.rem(m + 1 + i // 3, 2)
            at = pl.ds(pl.multiple_of(mm * 3 * lw + lax.rem(i, 3) * lw, 128), lw)
            acc = dot(n1t[0], dq_all[0, :, at])
            for q in range(1, pairs):
                acc = acc + dot(n1t[q], dq_all[q, :, at])
            g_qkv[0, :, :, :, at] = acc.astype(LOW).reshape(Z * Y, C, part, lw)

            @pl.when(lax.rem(i, 3) == 2)
            def _():
                q_sib(0, 1 - i // 3)

            @pl.when(i == 4)
            def _():
                loop(4, lambda k: q_y(0, 1, k))

        loop(6, chunk)
        s0.wait()
        sbuf[7] = sbuf[6] + sbuf[0]
        s1 = small_copy(1, 7, (index(z, 1 - y, c), m), 1)
        s1.start()
        loop(4, lambda i: q_y(0, 0, i))
        s1.wait()
        sbuf[8] = sbuf[7] + sbuf[1]
        s2 = small_copy(2, 8, (me, 1 - m), 2)
        s2.start()
        ff_final(0)
        loop(3, lambda i: q_z(0, 1, i))
        s2.wait()
        sbuf[9] = sbuf[8] + sbuf[2]
        zs = [small_copy(2 + k, 9, beside(k), 2 + k) for k in (1, 2, 3)]
        for copy in zs:
            copy.start()
        ff_final(1)
        loop(3, lambda i: q_z(0, 0, i))
        p_final(0)
        for copy in zs:
            copy.wait()
        small_out[...] = (sbuf[9] + sbuf[3] + sbuf[4] + sbuf[5])[:4]
        q_x(0)
        q_final(0)

        def finish(p):
            for copy in tok_copies(p):
                copy.wait()

        loop(pairs, finish)

        def finish_out(r):
            for copy in out_copies(r):
                copy.wait()

        loop(2, finish_out)

    pl.run_scoped(
        attention,
        pltpu.VMEM(w_one_in.shape, LOW), pltpu.VMEM((2, rows, 3 * width), LOW), pltpu.VMEM((2, HEADS, rows, rows), LOW),
        pltpu.VMEM((2, rows, width), LOW), pltpu.VMEM((2, rows, width), LOW), pltpu.VMEM((rows, width), LOW),
        pltpu.VMEM((pairs, width, rows), LOW), pltpu.VMEM((pairs, rows, 3 * width), LOW),
        pltpu.VMEM((pairs, rows, width), LOW),
    )


def backward_reduce(lens, tokens, cotangent, hid, n2, att, n1, qkv, prob, w_one, w_two, bias, vec):
    pairs, rows, width = n1.shape
    flat = pairs * rows
    part = width // (Z * Y * C)
    fw = w_two.shape[2] // 2
    hbm = pl.BlockSpec(memory_space=pl.ANY)
    vm = pl.BlockSpec(memory_space=pltpu.VMEM)
    kinds = ((2, fw), (1, width // 2), (1, 3 * width // 2))
    scratch = [pltpu.VMEM((n, Z * Y, C, part, 2 * w), LOW) for n, w in kinds]
    for n, w in kinds:
        scratch += [pltpu.VMEM((n * k, part, w), LOW) for k in (16, 8, 6, 1)]
    scratch += [
        pltpu.VMEM((flat, width), F32), pltpu.VMEM((flat, width), LOW), pltpu.VMEM((8, width), F32),
        pltpu.VMEM((8, 3 * width), F32), pltpu.VMEM((8, 2 * fw), F32), pltpu.VMEM((10, 8, 2 * fw), F32),
        pltpu.SemaphoreType.DMA((4, BLOCKS)), pltpu.SemaphoreType.DMA((4, BLOCKS)), pltpu.SemaphoreType.DMA((9,)),
        pltpu.SemaphoreType.DMA((3, 2)), pltpu.SemaphoreType.DMA((3, pairs)), pltpu.SemaphoreType.DMA((2, 6)),
    ]
    plane = lambda a: a.reshape(-1, width)
    return pl.pallas_call(
        back_kernel,
        in_specs=[pl.BlockSpec(memory_space=pltpu.SMEM)] + [hbm] * 10 + [vm] * 2,
        out_specs=[hbm] * 2 + [vm] * 4,
        out_shape=[
            jax.ShapeDtypeStruct((2 * flat, width), LOW), jax.ShapeDtypeStruct((2 * pairs, rows, width), LOW),
        ]
        + [jax.ShapeDtypeStruct((n, part, w), F32) for n, w in kinds]
        + [jax.ShapeDtypeStruct((4, 2 * fw), F32)],
        scratch_shapes=scratch,
        compiler_params=pltpu.CompilerParams(collective_id=1, has_side_effects=True, vmem_limit_bytes=63 * 2**20),
        name="backward_reduce",
    )(lens, plane(cotangent), plane(hid), plane(n2), plane(att), n1, qkv, prob, tokens, w_one, w_two, bias, vec)


def per_device(
    patch_counts, tokens, cotangent, attn_gain, attn_shift, w_qkv, b_qv, w_proj, b_proj,
    ffn_gain, ffn_shift, w_up, b_up, w_down, b_down,
):
    pairs_all, rows, width = tokens.shape
    n_mp = lax.axis_size("mp")
    n_dp = lax.axis_size("dp")
    pairs = pairs_all // n_mp
    direct = n_dp == Z * Y * C and n_mp == 2 and pairs == 4
    part = w_qkv.shape[0]
    lw = w_qkv.shape[2]
    fw = w_up.shape[1]
    mine = lax.axis_index("mp")
    off = jnp.reshape(mine * pairs, (1,)).astype(jnp.int32)
    lens = TEXT + lax.dynamic_slice_in_dim(patch_counts, mine * pairs, pairs, 0)

    vectors = jnp.stack([attn_gain, attn_shift, b_proj, ffn_gain, ffn_shift, b_down], axis=1)
    first = jnp.concatenate(
        [w_qkv.reshape(part, 3 * lw), w_proj.T, vectors, jnp.zeros((part, EXTRA - 6), F32)], axis=1
    ).astype(LOW)
    second = jnp.concatenate([w_up, w_down.T], axis=1).astype(LOW)
    bias = jnp.concatenate([b_qv.reshape(-1), b_up]).astype(LOW).astype(F32)
    bias = jnp.broadcast_to(bias, (8,) + bias.shape)
    if direct:
        w_one, w_two, bias, qkv, att, prob, hid, n1, n2, vec = gather_attention(lens, tokens, first, second, bias)
    else:
        both_axes = ("mp", "dp")
        w_one = lax.all_gather(first, both_axes, axis=0, tiled=True).reshape(n_mp, width, -1)
        w_two = lax.all_gather(second, both_axes, axis=0, tiled=True).reshape(n_mp, width, -1)
        bias = lax.all_gather(bias, "mp", axis=0)
        qkv, att, prob, hid, n1, n2, vec = attention_forward(lens, off, tokens, w_one, bias)

    def grad(left, right):
        return jnp.einsum(
            "rd,rf->df", left.reshape(pairs * rows, width), right.reshape(pairs * rows, -1),
            preferred_element_type=F32,
        )

    def reduce(grads, small):
        axes = ("mp", "dp")
        done = [
            lax.psum_scatter(
                g.reshape(width, n_mp, -1).swapaxes(0, 1).reshape(n_mp * width, -1), axes,
                scatter_dimension=0, tiled=True,
            )
            for g in grads
        ]
        return done + [lax.psum(small, axes)]

    def both(array):
        other = lax.ppermute(array, "mp", [(0, 1), (1, 0)])
        return jnp.where(mine == 0, jnp.concatenate([array, other]), jnp.concatenate([other, array]))

    if direct:
        block_out, tokens_grad, r_ff, r_proj, r_qkv, small = backward_reduce(
            lens, tokens, cotangent, hid, n2, att, n1, qkv, prob, w_one, w_two, bias, vec)
        block_out = block_out.reshape(tokens.shape)
        r_down, r_up, r_proj, r_qkv = r_ff[0], r_ff[1], r_proj[0], r_qkv[0]
        flat = small[1, : 3 * width].reshape(n_mp, 3, lw)
        small = jnp.concatenate([
            small[2], small[3, : 2 * width], flat[:, 0].reshape(-1), flat[:, 2].reshape(-1), small[0]])
    else:
        out_here, act, dpre, dhid, dlow, upl, sums_two, bsum_up = ffn(lens, off, n2, hid, cotangent, w_two, bias, vec)
        block_out = both(out_here)
        tok_here, dqkv, sums_one, bsum_qkv = attention_backward(lens, off, tokens, dhid, qkv, prob, w_one, vec)
        tokens_grad = both(tok_here)
        flat = bsum_qkv[0].reshape(n_mp, 3, lw)
        small = jnp.concatenate([
            sums_one[0], sums_one[1], sums_two[2], sums_two[0], sums_two[1], sums_two[3],
            flat[:, 0].reshape(-1), flat[:, 2].reshape(-1), bsum_up[0]])
        r_up, r_down, r_proj, r_qkv, small = reduce(
            [grad(n2, dpre), grad(upl, act), grad(dlow, att), grad(n1, dqkv)], small)
    place_dp = lax.axis_index("dp") * part

    def piece(i):
        return lax.dynamic_slice_in_dim(small, i * width + place_dp, part, 0)

    rest = small[6 * width :]
    o_b_q = lax.dynamic_slice_in_dim(rest, mine * lw, lw, 0)
    o_b_v = lax.dynamic_slice_in_dim(rest, (n_mp + mine) * lw, lw, 0)
    o_b_up = lax.dynamic_slice_in_dim(rest, 2 * n_mp * lw + mine * fw, fw, 0)
    return (
        block_out, tokens_grad, piece(0), piece(1),
        r_qkv.reshape(part, 3, lw), jnp.stack([o_b_q, o_b_v]),
        r_proj.T, piece(2), piece(3), piece(4), r_up, o_b_up, r_down.T, piece(5),
    )


def solution(mesh):
    vec, mat = P("dp"), P("dp", "mp")
    tok = P("dp", None, None)
    in_specs = (
        vec, tok, tok, vec, vec, P("dp", None, "mp"), P(None, "mp"), P("mp", "dp"), vec, vec, vec,
        mat, P("mp"), P("mp", "dp"), vec,
    )
    out_specs = (
        tok, tok, vec, vec, P("dp", None, "mp"), P(None, "mp"), P("mp", "dp"), vec, vec, vec,
        mat, P("mp"), P("mp", "dp"), vec,
    )
    return jax.shard_map(per_device, mesh=mesh, in_specs=in_specs, out_specs=out_specs, check_vma=False)
```

```python
import functools

import jax
import jax.numpy as jnp
from jax import lax
from jax.experimental import pallas as pl
from jax.experimental.pallas import tpu as pltpu
from jax.sharding import PartitionSpec as P

HEADS = 12
HEAD_DIM = 64
TEXT = 40
LOW = jnp.bfloat16
F32 = jnp.float32
EXTRA = 128
NT = (((1,), (1,)), ((), ()))
NN = (((1,), (0,)), ((), ()))


def dot(a, b, dims=NN):
    return lax.dot_general(a, b, dims, preferred_element_type=F32)


def moments(v):
    center = v - jnp.mean(v, axis=-1, keepdims=True)
    spread = jnp.mean(center * center, axis=-1, keepdims=True)
    r = lax.rsqrt(spread + 1e-06)
    return center * r, r


def row_ids(rows):
    return lax.broadcasted_iota(jnp.int32, (rows, 1), 0)


def attn_body(p, count, x, w_ref, bias_ref, vec_ref, qkv_ref, att_ref, prob_ref, hid_ref, n1_ref, n2_ref, hook):
    rows, width = x.shape
    groups = w_ref.shape[0]
    lw = width // groups
    tiles = lw // 128
    x = x.astype(F32)
    xhat, _ = moments(x)
    n1 = (xhat * vec_ref[0:1] + vec_ref[1:2]).astype(LOW)
    n1_ref[0] = n1
    for m in range(groups):
        y = dot(n1, w_ref[m, :, : 3 * lw])
        base = m * 3 * lw
        qkv_ref[0, :, base : base + lw] = (y[:, :lw] + bias_ref[m, 0:1, :lw]).astype(LOW)
        qkv_ref[0, :, base + lw : base + 2 * lw] = y[:, lw : 2 * lw].astype(LOW)
        qkv_ref[0, :, base + 2 * lw : base + 3 * lw] = (
            y[:, 2 * lw :] + bias_ref[m, 0:1, lw : 2 * lw]
        ).astype(LOW)
    keep = row_ids(rows) < count
    first = lax.broadcasted_iota(jnp.int32, (1, 128), 1) < HEAD_DIM

    def pair(hp, carry):
        base = (hp // tiles) * 3 * lw + lax.rem(hp, tiles) * 128

        def cols(t):
            return pl.ds(pl.multiple_of(base + t * lw, 128), 128)

        q2 = qkv_ref[0, :, cols(0)] * 0.125
        k2 = qkv_ref[0, :, cols(1)]
        v2t = qkv_ref[0, :, cols(2)].T
        outs = []
        for h in range(2):
            qh = jnp.where(first if h == 0 else ~first, q2, 0)
            st = dot(k2, qh, NT)
            st = jnp.where(keep, st, -1e30)
            e = jnp.exp(st - jnp.max(st, axis=0, keepdims=True))
            pt = (e * (1.0 / jnp.sum(e, axis=0, keepdims=True))).astype(LOW)
            prob_ref[0, hp * 2 + h] = pt
            outs.append(dot(v2t[h * HEAD_DIM : (h + 1) * HEAD_DIM], pt))
        att_ref[0, :, pl.ds(pl.multiple_of(hp * 128, 128), 128)] = jnp.concatenate(outs, axis=0).T.astype(LOW)
        hook(hp)
        return carry

    lax.fori_loop(0, groups * tiles, pair, 0)
    proj = sum(dot(att_ref[0, :, m * lw : (m + 1) * lw], w_ref[m, :, 3 * lw : 4 * lw], NT) for m in range(groups))
    hid = x + proj + vec_ref[2:3]
    hid_ref[0] = hid
    xhat2, _ = moments(hid)
    n2_ref[0] = (xhat2 * vec_ref[3:4] + vec_ref[4:5]).astype(LOW)


def attn_kernel(lens, off, x_ref, w_ref, bias_ref, qkv_ref, att_ref, prob_ref, hid_ref, n1_ref, n2_ref, vec_ref):
    p = pl.program_id(0)
    lw = x_ref.shape[2] // w_ref.shape[0]

    @pl.when(p == 0)
    def _():
        vec_ref[...] = w_ref[0, :, 4 * lw :].astype(F32).T[:8]

    attn_body(p, lens[p], x_ref[0], w_ref, bias_ref, vec_ref, qkv_ref, att_ref, prob_ref, hid_ref, n1_ref, n2_ref,
              lambda hp: None)


def const_spec(shape):
    return pl.BlockSpec(shape, lambda *_: (0,) * len(shape), pipeline_mode=pl.Buffered(1))


def pair_spec(*shape):
    return pl.BlockSpec((1,) + shape, lambda p, *_: (p,) + (0,) * len(shape))


def attention_forward(lens, off, tokens, w_one, bias):
    pairs = lens.shape[0]
    _, rows, width = tokens.shape
    out = lambda dt, *s: jax.ShapeDtypeStruct((pairs,) + s, dt)
    return pl.pallas_call(
        attn_kernel,
        grid_spec=pltpu.PrefetchScalarGridSpec(
            num_scalar_prefetch=2,
            grid=(pairs,),
            in_specs=[
                pl.BlockSpec((1, rows, width), lambda p, lens, off: (off[0] + p, 0, 0)),
                const_spec(w_one.shape),
                const_spec(bias.shape),
            ],
            out_specs=[
                pair_spec(rows, 3 * width), pair_spec(rows, width), pair_spec(HEADS, rows, rows),
                pair_spec(rows, width), pair_spec(rows, width), pair_spec(rows, width),
                pl.BlockSpec((8, width), lambda *_: (0, 0)),
            ],
        ),
        out_shape=[
            out(LOW, rows, 3 * width), out(LOW, rows, width), out(LOW, HEADS, rows, rows),
            out(F32, rows, width), out(LOW, rows, width), out(LOW, rows, width),
            jax.ShapeDtypeStruct((8, width), F32),
        ],
        compiler_params=pltpu.CompilerParams(vmem_limit_bytes=60 * 2**20),
        name="attention_forward",
    )(lens, off, tokens, w_one, bias)


def ffn_kernel(lens, off, n2_ref, hid_ref, cot_ref, w_ref, bias_ref, vec_ref,
               out_ref, act_ref, dpre_ref, dhid_ref, dlow_ref, upl_ref, sums_ref, bsum_ref):
    p = pl.program_id(0)
    rows, width = n2_ref.shape[1], n2_ref.shape[2]
    groups = w_ref.shape[0]
    fw = w_ref.shape[2] // 2
    lw = width // groups
    step = 512
    keep = row_ids(rows) < lens[p]
    n2 = n2_ref[0]
    upl = jnp.where(keep, cot_ref[0], 0)
    upl_ref[0] = upl

    @pl.when(p == 0)
    def _():
        sums_ref[...] = jnp.zeros_like(sums_ref)
        bsum_ref[...] = jnp.zeros_like(bsum_ref)

    for m in range(groups):
        for c in range(0, fw, step):
            pre = dot(n2, w_ref[m, :, c : c + step]) + bias_ref[m, 0:1, 2 * lw + c : 2 * lw + c + step]
            cdf = 0.5 * (1.0 + lax.erf(pre * (2.0 ** -0.5)))
            at = m * fw + c
            act_ref[0, :, at : at + step] = (pre * cdf).astype(LOW)
            slope = cdf + pre * (0.3989422804014327 * jnp.exp(-0.5 * pre * pre))
            dpre = slope * dot(upl, w_ref[m, :, fw + c : fw + c + step])
            dpre_ref[0, :, at : at + step] = dpre.astype(LOW)
            bsum_ref[0:1, at : at + step] += jnp.sum(dpre, axis=0, keepdims=True)
    hid = hid_ref[0]
    down = sum(dot(act_ref[0, :, m * fw : (m + 1) * fw], w_ref[m, :, fw:], NT) for m in range(groups))
    out_ref[0] = jnp.where(keep, hid + down + vec_ref[5:6], 0.0).astype(LOW)
    dtwo = sum(dot(dpre_ref[0, :, m * fw : (m + 1) * fw], w_ref[m, :, :fw], NT) for m in range(groups))
    xhat, r = moments(hid)
    dg = dtwo * vec_ref[3:4]
    dn = r * (dg - jnp.mean(dg, axis=-1, keepdims=True) - xhat * jnp.mean(dg * xhat, axis=-1, keepdims=True))
    upf = upl.astype(F32)
    dhid = upf + dn
    dhid_ref[0] = dhid
    dlow_ref[0] = dhid.astype(LOW)
    sums_ref[0:1] += jnp.sum(dtwo * xhat, axis=0, keepdims=True)
    sums_ref[1:2] += jnp.sum(dtwo, axis=0, keepdims=True)
    sums_ref[2:3] += jnp.sum(dhid, axis=0, keepdims=True)
    sums_ref[3:4] += jnp.sum(upf, axis=0, keepdims=True)


def ffn(lens, off, n2, hid, cotangent, w_two, bias, vec):
    pairs, rows, width = n2.shape
    ff = w_two.shape[0] * w_two.shape[2] // 2
    out = lambda dt, *s: jax.ShapeDtypeStruct((pairs,) + s, dt)
    return pl.pallas_call(
        ffn_kernel,
        grid_spec=pltpu.PrefetchScalarGridSpec(
            num_scalar_prefetch=2,
            grid=(pairs,),
            in_specs=[
                pair_spec(rows, width), pair_spec(rows, width),
                pl.BlockSpec((1, rows, width), lambda p, lens, off: (off[0] + p, 0, 0)),
                const_spec(w_two.shape), const_spec(bias.shape), const_spec(vec.shape),
            ],
            out_specs=[
                pair_spec(rows, width), pair_spec(rows, ff), pair_spec(rows, ff), pair_spec(rows, width),
                pair_spec(rows, width), pair_spec(rows, width),
                pl.BlockSpec((8, width), lambda *_: (0, 0)), pl.BlockSpec((8, ff), lambda *_: (0, 0)),
            ],
        ),
        out_shape=[
            out(LOW, rows, width), out(LOW, rows, ff), out(LOW, rows, ff), out(F32, rows, width),
            out(LOW, rows, width), out(LOW, rows, width),
            jax.ShapeDtypeStruct((8, width), F32), jax.ShapeDtypeStruct((8, ff), F32),
        ],
        compiler_params=pltpu.CompilerParams(vmem_limit_bytes=60 * 2**20),
        name="feed_forward",
    )(lens, off, n2, hid, cotangent, w_two, bias, vec)


def plain_back_kernel(lens, off, x_ref, dhid_ref, qkv_ref, prob_ref, w_ref, vec_ref,
                tok_ref, dqkv_ref, sums_ref, bsum_ref, do_ref):
    p = pl.program_id(0)
    rows, width = x_ref.shape[1], x_ref.shape[2]
    groups = w_ref.shape[0]
    lw = width // groups
    tiles = lw // 128

    @pl.when(p == 0)
    def _():
        sums_ref[...] = jnp.zeros_like(sums_ref)
        bsum_ref[...] = jnp.zeros_like(bsum_ref)

    dhid = dhid_ref[0]
    dlow = dhid.astype(LOW)
    for m in range(groups):
        do_ref[:, m * lw : (m + 1) * lw] = dot(dlow, w_ref[m, :, 3 * lw : 4 * lw]).astype(LOW)
    first = lax.broadcasted_iota(jnp.int32, (1, 128), 1) < HEAD_DIM

    def pair(hp, carry):
        base = (hp // tiles) * 3 * lw + (hp % tiles) * 128

        def cols(t):
            return pl.ds(pl.multiple_of(base + t * lw, 128), 128)

        q2 = qkv_ref[0, :, cols(0)] * 0.125
        k2t = qkv_ref[0, :, cols(1)].T
        v2 = qkv_ref[0, :, cols(2)]
        do2 = do_ref[:, pl.ds(pl.multiple_of(hp * 128, 128), 128)]
        dq_t = []
        dk = dv = 0.0
        for h in range(2):
            mine = first if h == 0 else ~first
            doh = jnp.where(mine, do2, 0)
            qh = jnp.where(mine, q2, 0)
            dpt = dot(v2, doh, NT)
            plow = prob_ref[0, hp * 2 + h]
            pt = plow.astype(F32)
            inner = jnp.sum(pt * dpt, axis=0, keepdims=True)
            dst = (pt * (dpt - inner)).astype(LOW)
            dv = dv + dot(plow, doh)
            dk = dk + dot(dst, qh)
            dq_t.append(dot(k2t[h * HEAD_DIM : (h + 1) * HEAD_DIM], dst))
        dq = (jnp.concatenate(dq_t, axis=0) * 0.125).T
        dqkv_ref[0, :, cols(0)] = dq.astype(LOW)
        dqkv_ref[0, :, cols(1)] = dk.astype(LOW)
        dqkv_ref[0, :, cols(2)] = dv.astype(LOW)
        bsum_ref[0:1, cols(0)] += jnp.sum(dq, axis=0, keepdims=True)
        bsum_ref[0:1, cols(2)] += jnp.sum(dv, axis=0, keepdims=True)
        return carry

    lax.fori_loop(0, groups * tiles, pair, 0)
    done = sum(dot(dqkv_ref[0, :, m * 3 * lw : (m + 1) * 3 * lw], w_ref[m, :, : 3 * lw], NT) for m in range(groups))
    xhat, r = moments(x_ref[0].astype(F32))
    dg = done * vec_ref[0:1]
    dn = r * (dg - jnp.mean(dg, axis=-1, keepdims=True) - xhat * jnp.mean(dg * xhat, axis=-1, keepdims=True))
    tok_ref[0] = (dhid + dn).astype(LOW)
    sums_ref[0:1] += jnp.sum(done * xhat, axis=0, keepdims=True)
    sums_ref[1:2] += jnp.sum(done, axis=0, keepdims=True)


def attention_backward(lens, off, tokens, dhid, qkv, prob, w_one, vec):
    pairs, rows, width = dhid.shape
    out = lambda dt, *s: jax.ShapeDtypeStruct((pairs,) + s, dt)
    return pl.pallas_call(
        plain_back_kernel,
        grid_spec=pltpu.PrefetchScalarGridSpec(
            num_scalar_prefetch=2,
            grid=(pairs,),
            in_specs=[
                pl.BlockSpec((1, rows, width), lambda p, lens, off: (off[0] + p, 0, 0)),
                pair_spec(rows, width), pair_spec(rows, 3 * width), pair_spec(HEADS, rows, rows),
                const_spec(w_one.shape), const_spec(vec.shape),
            ],
            out_specs=[
                pair_spec(rows, width), pair_spec(rows, 3 * width),
                pl.BlockSpec((8, width), lambda *_: (0, 0)), pl.BlockSpec((8, 3 * width), lambda *_: (0, 0)),
            ],
            scratch_shapes=[pltpu.VMEM((rows, width), LOW)],
        ),
        out_shape=[
            out(LOW, rows, width), out(LOW, rows, 3 * width),
            jax.ShapeDtypeStruct((8, width), F32), jax.ShapeDtypeStruct((8, 3 * width), F32),
        ],
        compiler_params=pltpu.CompilerParams(vmem_limit_bytes=60 * 2**20),
        name="attention_backward",
    )(lens, off, tokens, dhid, qkv, prob, w_one, vec)
MESH_ID = pl.DeviceIdType.MESH
Z, Y, C = 4, 2, 2


def place():
    dp = lax.axis_index("dp")
    m = lax.axis_index("mp")
    c = lax.rem(dp, 2)
    y = lax.rem(dp // 2, 2)
    z = dp // 4
    return z, y, c, m


def index(z, y, c):
    return (z * Y + y) * C + c


def flips(y, c, m):
    one = (y + c * (1 - 2 * y), m + (1 - c) * (1 - 2 * m))
    two = (y + (1 - c) * (1 - 2 * y), m + c * (1 - 2 * m))
    return one, two


def greet(z, y, c, m):
    barrier = pltpu.get_barrier_semaphore()
    (y1, m1), (y2, m2) = flips(y, c, m)
    peers = [(index(lax.rem(z + k, Z), y, c), m) for k in (1, 2, 3)]
    peers += [(index(z, y1, c), m1), (index(z, y2, c), m2), (index(z, y, 1 - c), m)]
    for dp, mp in peers:
        pl.semaphore_signal(barrier, inc=1, device_id={"dp": dp, "mp": mp}, device_id_type=MESH_ID)
    pl.semaphore_wait(barrier, len(peers))
    return peers


def gather_attn_kernel(counts, tok_all, wq_in, wp_in, wu_in, wd_in, bq_in, bu_in, v0, v1, v2, v3, v4, v5,
                       w_one_out, w_two, b_out, qkv_ref, att_ref, prob_ref, hid_ref, n1_ref, n2_ref, vec_ref,
                       w_one, bias, xbuf, first_ref, second_ref, b_in, vbuf, send, recv, bsem, local):
    p = pl.program_id(0)
    z, y, c, m = place()
    (y1, m1), (y2, m2) = flips(y, c, m)
    pairs, rows, width = xbuf.shape
    part = first_ref.shape[0]
    cols = second_ref.shape[1] // 2
    lw = width // 2
    per_pair = width // 128
    me = index(z, y, c)
    one, two, sib = (index(z, y1, c), m1), (index(z, y2, c), m2), (index(z, y, 1 - c), m)

    def spot(g, dp, mp):
        at = pl.ds(pl.multiple_of(dp * part, part), part)
        if g is None:
            return w_one.at[mp, at]
        return w_two.at[mp, at, pl.ds(pl.multiple_of(g * cols, 128), cols)]

    def shard(g):
        return first_ref if g is None else second_ref.at[:, pl.ds(pl.multiple_of(g * cols, 128), cols)]

    def row(g):
        return 0 if g is None else g + 1

    def copy_of(g, src, dst, out_sem, in_sem, to):
        return pltpu.make_async_remote_copy(
            src_ref=src, dst_ref=dst, send_sem=send.at[row(g), out_sem], recv_sem=recv.at[row(g), in_sem],
            device_id={"dp": to[0], "mp": to[1]}, device_id_type=MESH_ID,
        )

    def push(g, src, dp, mp, to, sem):
        copy_of(g, src, spot(g, dp, mp), sem, mp * (Z * Y * C) + dp, to).start()

    def arrived(g, dp, mp):
        at = spot(g, dp, mp)
        copy_of(g, at, at, 0, mp * (Z * Y * C) + dp, sib).wait_recv()
        return at

    def own_z(g):
        for k in (1, 3, 2):
            push(g, shard(g), me, m, (index(lax.rem(z + k, Z), y, c), m), k - 1)

    def own_near(g):
        for n, to in enumerate((one, two, sib)):
            push(g, shard(g), me, m, to, 3 + n)

    def event_z(g, i):
        dp = index(lax.rem(z + 1 + lax.rem(2 * i, 3), Z), y, c)
        at = arrived(g, dp, m)
        for n, to in enumerate((one, two, sib)):
            push(g, at, dp, m, to, 6 + 3 * i + n)

    def event_one(g, i):
        dp = index(lax.rem(z + i, Z), y1, c)
        at = arrived(g, dp, m1)
        for n, to in enumerate((two, sib)):
            push(g, at, dp, m1, to, 15 + 2 * i + n)

    def event_two(g, i):
        far = lax.rem(i, 2)
        yy = y2 + far * (1 - y - y2)
        mm = m2 + far * (1 - m - m2)
        dp = index(lax.rem(z + i // 2, Z), yy, c)
        push(g, arrived(g, dp, mm), dp, mm, sib, 23 + i)

    def event_core(g, i):
        arrived(g, index(i // 4, lax.rem(i // 2, 2), 1 - c), lax.rem(i, 2))

    def loop(n, event, g):
        def run(i, carry):
            event(g, i)
            return carry

        lax.fori_loop(0, n, run, 0)

    bias_copy = pltpu.make_async_remote_copy(
        src_ref=b_in, dst_ref=bias.at[m], send_sem=bsem.at[0], recv_sem=bsem.at[1],
        device_id={"dp": me, "mp": 1 - m}, device_id_type=MESH_ID,
    )
    x_copy = pltpu.make_async_copy(tok_all.at[pl.ds(m * pairs, pairs)], xbuf, local.at[0])
    mine = [
        pltpu.make_async_copy(b_in, bias.at[m], local.at[1]),
        pltpu.make_async_copy(first_ref, spot(None, me, m), local.at[2]),
    ]
    mine_two = [pltpu.make_async_copy(shard(g), spot(g, me, m), local.at[3 + g]) for g in range(2)]
    keep_one = pltpu.make_async_copy(w_one, w_one_out, local.at[5])
    keep_bias = pltpu.make_async_copy(bias, b_out, local.at[6])

    @pl.when(p == 0)
    def _():
        x_copy.start()
        for t in range(3):
            first_ref[:, t * lw : (t + 1) * lw] = wq_in[t].astype(LOW)
        first_ref[:, 3 * lw : 4 * lw] = wp_in[...].astype(LOW)
        vbuf[...] = jnp.zeros_like(vbuf)
        for n, v in enumerate((v0, v1, v2, v3, v4, v5)):
            vbuf[n : n + 1, :part] = v[...]
        first_ref[:, 4 * lw :] = vbuf[...].T[:part].astype(LOW)
        second_ref[:, :cols] = wu_in[...].astype(LOW)
        second_ref[:, cols:] = wd_in[...].astype(LOW)
        b_in[...] = jnp.zeros_like(b_in)
        b_in[0:1, :lw] = bq_in[0:1].astype(LOW).astype(F32)
        b_in[0:1, lw : 2 * lw] = bq_in[1:2].astype(LOW).astype(F32)
        b_in[0:1, 2 * lw :] = bu_in[...].astype(LOW).astype(F32)
        greet(z, y, c, m)
        own_z(None)
        own_near(None)
        bias_copy.start()
        for copy in mine + mine_two:
            copy.start()
        own_z(0)
        own_z(1)
        loop(3, event_z, None)
        loop(4, event_one, None)
        own_near(0)
        loop(3, event_z, 0)
        loop(8, event_two, None)
        for copy in mine + [x_copy, bias_copy]:
            copy.wait()
        loop(16, event_core, None)
        keep_one.start()
        keep_bias.start()
        vec_ref[...] = w_one[0, :, 4 * lw :].astype(F32).T[:8]

    def hook(hp):
        step = p * per_pair + hp

        def event(e, carry):
            @pl.when(e == 0)
            def _():
                own_near(1)

            @pl.when(((e >= 1) & (e < 5)) | ((e >= 16) & (e < 20)))
            def _():
                g = e // 16
                event_one(g, e - 1 - 15 * g)

            @pl.when((e >= 5) & (e < 8))
            def _():
                event_z(1, e - 5)

            @pl.when(((e >= 8) & (e < 16)) | (e >= 20))
            def _():
                g = e // 20
                event_two(g, e - 8 - 12 * g)

            return carry

        total = pairs * per_pair
        lax.fori_loop(step * 28 // total, (step + 1) * 28 // total, event, 0)

    attn_body(p, TEXT + counts[m * pairs + p], xbuf[p], w_one, bias, vec_ref, qkv_ref, att_ref, prob_ref, hid_ref, n1_ref, n2_ref, hook)

    @pl.when(p == pairs - 1)
    def _():
        for g in range(2):
            loop(16, event_core, g)
        for copy in mine_two + [keep_one, keep_bias]:
            copy.wait()
        for g in (None, 0, 1):
            def sent(i, carry):
                copy_of(g, shard(g), shard(g), i, 0, sib).wait_send()
                return carry

            lax.fori_loop(0, 31, sent, 0)


def gather_attention(counts, tokens, w_qkv, w_proj, w_up, w_down, b_qv, b_up, vectors):
    pairs = counts.shape[0] // 2
    _, rows, width = tokens.shape
    part, fw = w_up.shape
    lw = width // 2
    total = Z * Y * C
    hbm = pl.BlockSpec(memory_space=pl.ANY)
    out = lambda dt, *s: jax.ShapeDtypeStruct((pairs,) + s, dt)
    small = [w_qkv.transpose(1, 0, 2), w_proj.T, w_up, w_down.T, b_qv, b_up.reshape(1, fw)]
    small += [v.reshape(1, part) for v in vectors]
    one, two, bias = 4 * lw + EXTRA, 2 * fw, (8, 2 * lw + fw)
    return pl.pallas_call(
        gather_attn_kernel,
        grid_spec=pltpu.PrefetchScalarGridSpec(
            num_scalar_prefetch=1,
            grid=(pairs,),
            in_specs=[hbm] + [const_spec(a.shape) for a in small],
            out_specs=[
                hbm, hbm, hbm,
                pair_spec(rows, 3 * width), pair_spec(rows, width), pair_spec(HEADS, rows, rows),
                pair_spec(rows, width), pair_spec(rows, width), pair_spec(rows, width),
                pl.BlockSpec((8, width), lambda *_: (0, 0)),
            ],
            scratch_shapes=[
                pltpu.VMEM((2, width, one), LOW), pltpu.VMEM((2,) + bias, F32), pltpu.VMEM((pairs, rows, width), LOW),
                pltpu.VMEM((part, one), LOW), pltpu.VMEM((part, two), LOW), pltpu.VMEM(bias, F32),
                pltpu.VMEM((EXTRA, EXTRA), F32),
                pltpu.SemaphoreType.DMA((3, 31)), pltpu.SemaphoreType.DMA((3, 32)),
                pltpu.SemaphoreType.DMA((2,)), pltpu.SemaphoreType.DMA((7,)),
            ],
        ),
        out_shape=[
            jax.ShapeDtypeStruct((2, width, one), LOW),
            jax.ShapeDtypeStruct((2, width, two), LOW),
            jax.ShapeDtypeStruct((2,) + bias, F32),
            out(LOW, rows, 3 * width), out(LOW, rows, width), out(LOW, HEADS, rows, rows),
            out(F32, rows, width), out(LOW, rows, width), out(LOW, rows, width),
            jax.ShapeDtypeStruct((8, width), F32),
        ],
        compiler_params=pltpu.CompilerParams(collective_id=0, has_side_effects=True, vmem_limit_bytes=60 * 2**20),
        name="gather_attention",
    )(counts, tokens, *small)


BLOCKS = 31


def back_kernel(counts, cot, hid_in, n2_in, att_in, n1_all, qkv_all, prob_all, tok_all, w_one_in, w_two, bias_ref, vec_ref,
                block_out, tok_out, r_ff, r_proj, r_qkv, o_up, o_qv, o_vec,
                g_ff, g_proj, g_qkv, rc_ff, rs_ff, rz_ff, rx_ff, rc_p, rs_p, rz_p, rx_p, rc_q, rs_q, rz_q, rx_q,
                dhid_ref, outbuf, sums, bsum, bsum_up, sbuf, send, recv, local, osem, tsem, ssem):
    flat, width = dhid_ref.shape
    pairs, rows = qkv_all.shape[0], qkv_all.shape[1]
    groups = w_two.shape[0]
    fw = w_two.shape[2] // 2
    fc = fw // 3
    lw = width // groups
    tiles = lw // 128
    half = flat // 2
    part = r_proj.shape[1]
    z, y, c, m = place()
    me = index(z, y, c)
    sib = (index(z, y, 1 - c), m)

    def beside(k):
        return (index(lax.rem(z + k, Z), y, c), m)

    def loop(n, event):
        def one(i, carry):
            event(i)
            return carry

        lax.fori_loop(0, n, one, 0)

    def family(grad, rc, rs, rz, rx, out, row0):
        cols = rc.shape[2]

        def copy_of(u, src, dst, out_sem, in_sem, to):
            return pltpu.make_async_remote_copy(
                src_ref=src, dst_ref=dst, send_sem=send.at[row0 + u, out_sem], recv_sem=recv.at[row0 + u, in_sem],
                device_id={"dp": to[0], "mp": to[1]}, device_id_type=MESH_ID,
            )

        def block(u, ra, rb, k, cc):
            yy = y + ra * (1 - 2 * y)
            mm = m + rb * (1 - 2 * m)
            return u, lax.rem(z + k, Z) * Y + yy, cc, slice(None), pl.ds(pl.multiple_of(mm * cols, 128), cols)

        def to_sibling(u, rb):
            def one(i):
                ra, k = 1 - i // 4, lax.rem(i + 1, 4)
                slot = (ra * 2 + rb) * 4 + k
                copy_of(u, grad.at[block(u, ra, rb, k, 1 - c)], rc.at[u * 16 + slot], slot, slot, sib).start()

            loop(8, one)

        def arrived(u, ref, sem):
            copy_of(u, ref, ref, 0, sem, sib).wait_recv()

        def base(u, ra, rb, k):
            slot = (ra * 2 + rb) * 4 + k
            arrived(u, rc.at[u * 16 + slot], slot)
            return grad[block(u, ra, rb, k, c)].astype(F32) + rc[u * 16 + slot].astype(F32)

        def level(u, rb, k):
            at = rb * 4 + k
            value = base(u, 0, rb, k)
            arrived(u, rs.at[u * 8 + at], 16 + at)
            return value + rs[u * 8 + at].astype(F32)

        def lined(u, rb):
            value = level(u, rb, 0)
            for k in (1, 2, 3):
                at = (k - 1) * 2 + rb
                arrived(u, rz.at[u * 6 + at], 24 + at)
                value = value + rz[u * 6 + at].astype(F32)
            return value

        def event_y(u, rb, i):
            k = lax.rem(i + 1, 4)
            slot = u * 16 + (2 + rb) * 4 + k
            at = rb * 4 + k
            rc[slot] = base(u, 1, rb, k).astype(LOW)
            copy_of(u, rc.at[slot], rs.at[u * 8 + at], 16 + at, 16 + at, (index(z, 1 - y, c), m)).start()

        def event_z(u, rb, i):
            k = 1 + i
            slot = u * 16 + rb * 4 + k
            at = (k - 1) * 2 + rb
            rc[slot] = level(u, rb, k).astype(LOW)
            copy_of(u, rc.at[slot], rz.at[u * 6 + at], 24 + at, 24 + at, beside(k)).start()

        def event_x(u):
            rc[u * 16 + 4] = lined(u, 1).astype(LOW)
            copy_of(u, rc.at[u * 16 + 4], rx.at[u], 30, 30, (me, 1 - m)).start()

        def final(u):
            value = lined(u, 0)
            arrived(u, rx.at[u], 30)
            out(u, value + rx[u].astype(F32))

            def one(i):
                copy_of(u, rc.at[0], rc.at[0], i, 0, sib).wait_send()

            loop(BLOCKS, one)

        return to_sibling, event_y, event_z, event_x, final

    def put(ref):
        def store(u, value):
            ref[u] = value

        return store

    def put_qkv(u, value):
        for t in range(3):
            r_qkv[t] = value[:, t * lw : (t + 1) * lw]

    ff_sib, ff_y, ff_z, ff_x, ff_final = family(g_ff, rc_ff, rs_ff, rz_ff, rx_ff, put(r_ff), 0)
    p_sib, p_y, p_z, p_x, p_final = family(g_proj, rc_p, rs_p, rz_p, rx_p, put(r_proj), 2)
    q_sib, q_y, q_z, q_x, q_final = family(g_qkv, rc_q, rs_q, rz_q, rx_q, put_qkv, 3)

    def out_copies(q):
        src = outbuf.at[q]
        dst = block_out.at[m * pairs + q]
        return pltpu.make_async_copy(src, dst, osem.at[0, q]), pltpu.make_async_remote_copy(
            src_ref=src, dst_ref=dst, send_sem=osem.at[1, q], recv_sem=osem.at[2, q],
            device_id={"dp": me, "mp": 1 - m}, device_id_type=MESH_ID,
        )

    def keep_of(r):
        ids = row_ids(half)
        here = m * pairs + 2 * r
        return ids < TEXT + jnp.where(ids < rows, counts[here], counts[here + 1] + rows)

    def span(r):
        return pl.ds(pl.multiple_of(r * half, 16), half)

    sums[...] = jnp.zeros_like(sums)
    bsum[...] = jnp.zeros_like(bsum)
    bsum_up[...] = jnp.zeros_like(bsum_up)

    def feed_forward(n2, n2t, upl, uplt, hid, acc, slope, chunk, wbuf):
        def place_of(f):
            i = lax.rem(f, 6)
            return lax.rem(m + 1 + i // 3, 2), lax.rem(i, 3) * fc

        def weights(f):
            mm, at = place_of(f)
            slot = lax.rem(f, 2)
            return [
                pltpu.make_async_copy(
                    w_two.at[mm, :, pl.ds(pl.multiple_of(t * fw + at, 128), fc)], wbuf.at[slot, t], local.at[slot * 2 + t])
                for t in range(2)
            ]

        n2_copy = pltpu.make_async_copy(n2_in, n2, local.at[4])
        up_copy = pltpu.make_async_copy(cot.at[pl.ds(pl.multiple_of(m * flat, 16), flat)], upl, local.at[5])
        hid_copy = pltpu.make_async_copy(hid_in, hid, local.at[6])
        att_copy = pltpu.make_async_copy(att_in, slope.at[:, pl.ds(0, width)], local.at[7])
        n2_copy.start()
        up_copy.start()
        for copy in weights(0):
            copy.start()
        hid_copy.start()
        greet(z, y, c, m)
        up_copy.wait()

        def prepare(r):
            value = jnp.where(keep_of(r), upl[span(r)], 0)
            upl[span(r)] = value
            sums[3:4] += jnp.sum(value.astype(F32), axis=0, keepdims=True)
            acc[span(r)] = jnp.zeros((half, width), F32)

        loop(2, prepare)
        uplt[...] = upl[...].T
        n2_copy.wait()
        n2t[...] = n2[...].T

        def traffic(f):
            @pl.when(lax.rem(f, 3) == 2)
            def _():
                n = f // 3
                ff_sib(n // 2, 1 - lax.rem(n, 2))

            @pl.when((lax.rem(f, 3) == 0) & (f > 0))
            def _():
                n = f // 3 - 1
                loop(4, lambda i: ff_y(n // 2, 1 - lax.rem(n, 2), i))

            @pl.when((lax.rem(f, 3) == 1) & (f > 4))
            def _():
                n = (f - 7) // 3
                loop(3, lambda i: ff_z(n // 2, 1 - lax.rem(n, 2), i))

        def store(u, at, value):
            g_ff[u, :, :, :, at] = value.astype(LOW).reshape(Z * Y, C, part, fc)

        def forward(f):
            slot = lax.rem(f, 2)
            for copy in weights(f + 1):
                copy.start()
            for copy in weights(f):
                copy.wait()
            mm, off = place_of(f)
            at = pl.ds(pl.multiple_of(mm * fw + off, 128), fc)
            shift = bias_ref[mm, 0:1, pl.ds(pl.multiple_of(2 * lw + off, 128), fc)]

            def block(r):
                pre = dot(n2[span(r)], wbuf[slot, 0]) + shift
                cdf = 0.5 * (1.0 + lax.erf(pre * (2.0 ** -0.5)))
                chunk[span(r)] = (pre * cdf).astype(LOW)
                slope[span(r), at] = (cdf + pre * (0.3989422804014327 * jnp.exp(-0.5 * pre * pre))).astype(LOW)
                acc[span(r)] += dot(chunk[span(r)], wbuf[slot, 1], NT)

            loop(2, block)
            store(0, at, dot(uplt[...], chunk[...]))
            traffic(f)

        loop(6, forward)
        hid_copy.wait()

        def leave(r):
            value = jnp.where(keep_of(r), hid[span(r)] + acc[span(r)] + vec_ref[5:6], 0.0)
            acc[span(r)] = jnp.zeros((half, width), F32)
            for n in range(2):
                outbuf[2 * r + n] = value[n * rows : (n + 1) * rows].astype(LOW)
                for copy in out_copies(2 * r + n):
                    copy.start()

        loop(2, leave)

        def backward(i):
            f = 6 + i
            slot = lax.rem(f, 2)

            @pl.when(f < 11)
            def _():
                for copy in weights(f + 1):
                    copy.start()

            for copy in weights(f):
                copy.wait()
            mm, off = place_of(f)
            at = pl.ds(pl.multiple_of(mm * fw + off, 128), fc)

            def block(r):
                dpre = slope[span(r), at].astype(F32) * dot(upl[span(r)], wbuf[slot, 1])
                chunk[span(r)] = dpre.astype(LOW)
                bsum_up[0:1, at] += jnp.sum(dpre, axis=0, keepdims=True)
                acc[span(r)] += dot(chunk[span(r)], wbuf[slot, 0], NT)

            loop(2, block)
            store(1, at, dot(n2t[...], chunk[...]))
            traffic(f)

        loop(6, backward)
        att_copy.start()

        def norm_back(r):
            dtwo = acc[span(r)]
            xhat, rr = moments(hid[span(r)])
            dg = dtwo * vec_ref[3:4]
            dn = rr * (dg - jnp.mean(dg, axis=-1, keepdims=True) - xhat * jnp.mean(dg * xhat, axis=-1, keepdims=True))
            dhid = upl[span(r)].astype(F32) + dn
            dhid_ref[span(r)] = dhid
            n2[span(r)] = dhid.astype(LOW)
            sums[4:5] += jnp.sum(dtwo * xhat, axis=0, keepdims=True)
            sums[5:6] += jnp.sum(dtwo, axis=0, keepdims=True)
            sums[2:3] += jnp.sum(dhid, axis=0, keepdims=True)

        loop(2, norm_back)
        att_copy.wait()
        n2t[...] = n2[...].T
        for mm in range(groups):
            at = slice(mm * lw, (mm + 1) * lw)
            g_proj[0, :, :, :, at] = dot(n2t[...], slope[:, at]).astype(LOW).reshape(Z * Y, C, part, lw)
        p_sib(0, 1)
        p_sib(0, 0)

    pl.run_scoped(
        feed_forward,
        pltpu.VMEM((flat, width), LOW), pltpu.VMEM((width, flat), LOW),
        pltpu.VMEM((flat, width), LOW), pltpu.VMEM((width, flat), LOW),
        pltpu.VMEM((flat, width), F32), pltpu.VMEM((flat, width), F32),
        pltpu.VMEM((flat, groups * fw), LOW), pltpu.VMEM((flat, fc), LOW), pltpu.VMEM((2, 2, width, fc), LOW),
    )

    def attention(w_ref, qkv_buf, prob_buf, n1_buf, x_buf, do_ref, n1t, dq_all, tokbuf):
        w_copy = pltpu.make_async_copy(w_one_in, w_ref, local.at[8])

        def loads(p):
            slot = lax.rem(p, 2)
            pieces = [
                (qkv_all.at[p], qkv_buf), (prob_all.at[p], prob_buf), (n1_all.at[p], n1_buf),
                (tok_all.at[m * pairs + p], x_buf),
            ]
            return [
                pltpu.make_async_copy(src, dst.at[slot], local.at[slot * 4 + t])
                for t, (src, dst) in enumerate(pieces)
            ]

        def tok_copies(p):
            src, dst = tokbuf.at[p], tok_out.at[m * pairs + p]
            return pltpu.make_async_copy(src, dst, tsem.at[0, p]), pltpu.make_async_remote_copy(
                src_ref=src, dst_ref=dst, send_sem=tsem.at[1, p], recv_sem=tsem.at[2, p],
                device_id={"dp": me, "mp": 1 - m}, device_id_type=MESH_ID,
            )

        w_copy.start()
        for copy in loads(0):
            copy.start()
        w_copy.wait()
        first = lax.broadcasted_iota(jnp.int32, (1, 128), 1) < HEAD_DIM

        def one_pair(p):
            slot = lax.rem(p, 2)

            @pl.when(p < pairs - 1)
            def _():
                for copy in loads(p + 1):
                    copy.start()

            dhid = dhid_ref[pl.ds(pl.multiple_of(p * rows, 8), rows)]
            dlow = dhid.astype(LOW)
            for mm in range(groups):
                do_ref[:, mm * lw : (mm + 1) * lw] = dot(dlow, w_ref[mm, :, 3 * lw : 4 * lw]).astype(LOW)
            for copy in loads(p):
                copy.wait()
            n1t[p] = n1_buf[slot].T

            def heads(hp):
                lane = (hp // tiles) * 3 * lw + lax.rem(hp, tiles) * 128

                def cols(t):
                    return pl.ds(pl.multiple_of(lane + t * lw, 128), 128)

                q2 = qkv_buf[slot, :, cols(0)] * 0.125
                k2t = qkv_buf[slot, :, cols(1)].T
                v2 = qkv_buf[slot, :, cols(2)]
                do2 = do_ref[:, pl.ds(pl.multiple_of(hp * 128, 128), 128)]
                dq_t = []
                dk = dv = 0.0
                for h in range(2):
                    mine = first if h == 0 else ~first
                    doh = jnp.where(mine, do2, 0)
                    qh = jnp.where(mine, q2, 0)
                    dpt = dot(v2, doh, NT)
                    plow = prob_buf[slot, hp * 2 + h]
                    pt = plow.astype(F32)
                    inner = jnp.sum(pt * dpt, axis=0, keepdims=True)
                    dst = (pt * (dpt - inner)).astype(LOW)
                    dv = dv + dot(plow, doh)
                    dk = dk + dot(dst, qh)
                    dq_t.append(dot(k2t[h * HEAD_DIM : (h + 1) * HEAD_DIM], dst))
                dq = (jnp.concatenate(dq_t, axis=0) * 0.125).T
                dq_all[p, :, cols(0)] = dq.astype(LOW)
                dq_all[p, :, cols(1)] = dk.astype(LOW)
                dq_all[p, :, cols(2)] = dv.astype(LOW)
                bsum[0:1, cols(0)] += jnp.sum(dq, axis=0, keepdims=True)
                bsum[0:1, cols(2)] += jnp.sum(dv, axis=0, keepdims=True)
                step = p * (groups * tiles) + hp

                @pl.when(step == 0)
                def _():
                    loop(4, lambda i: ff_y(1, 0, i))

                @pl.when((step == 2) | (step == 13))
                def _():
                    loop(3, lambda i: ff_z(1, 1 - step // 13, i))

                @pl.when((step >= 3) & (step < 7))
                def _():
                    loop(2, lambda i: p_y(0, 1 - (step - 3) // 2, 2 * lax.rem(step - 3, 2) + i))

                @pl.when((step == 18) | (step == 19))
                def _():
                    loop(3, lambda i: p_z(0, 19 - step, i))

                @pl.when((step == 16) | (step == 21))
                def _():
                    ff_x((step - 16) // 5)

            loop(groups * tiles, heads)
            done = sum(
                dot(dq_all[p, :, mm * 3 * lw : (mm + 1) * 3 * lw], w_ref[mm, :, : 3 * lw], NT) for mm in range(groups))
            xhat, r = moments(x_buf[slot].astype(F32))
            dg = done * vec_ref[0:1]
            dn = r * (dg - jnp.mean(dg, axis=-1, keepdims=True) - xhat * jnp.mean(dg * xhat, axis=-1, keepdims=True))
            tokbuf[p] = (dhid + dn).astype(LOW)
            for copy in tok_copies(p):
                copy.start()
            sums[0:1] += jnp.sum(done * xhat, axis=0, keepdims=True)
            sums[1:2] += jnp.sum(done, axis=0, keepdims=True)

        loop(pairs, one_pair)

        def small_copy(slot, src, to, sem):
            return pltpu.make_async_remote_copy(
                src_ref=sbuf.at[src], dst_ref=sbuf.at[slot], send_sem=ssem.at[0, sem], recv_sem=ssem.at[1, sem],
                device_id={"dp": to[0], "mp": to[1]}, device_id_type=MESH_ID,
            )

        sbuf[6] = jnp.zeros_like(sbuf[6])
        sbuf[6, 0:1] = bsum_up[0:1]
        sbuf[6, 1:2, : 3 * width] = bsum[0:1]
        for n, (line, at) in enumerate(((2, 0), (2, 1), (2, 2), (3, 1), (2, 3), (3, 0))):
            sbuf[6, line : line + 1, at * width : (at + 1) * width] = sums[n : n + 1]
        s0 = small_copy(0, 6, sib, 0)
        s1 = small_copy(1, 7, (index(z, 1 - y, c), m), 1)
        zs = [small_copy(1 + k, 8, beside(k), 1 + k) for k in (1, 2, 3)]
        s2 = small_copy(5, 9, (me, 1 - m), 5)
        s0.start()

        def chunk(i):
            mm = lax.rem(m + 1 + i // 3, 2)
            at = pl.ds(pl.multiple_of(mm * 3 * lw + lax.rem(i, 3) * lw, 128), lw)
            acc = dot(n1t[0], dq_all[0, :, at])
            for q in range(1, pairs):
                acc = acc + dot(n1t[q], dq_all[q, :, at])
            g_qkv[0, :, :, :, at] = acc.astype(LOW).reshape(Z * Y, C, part, lw)

            @pl.when(i == 0)
            def _():
                s0.wait()
                sbuf[7] = sbuf[6] + sbuf[0]
                s1.start()

            @pl.when(i == 1)
            def _():
                p_x(0)

            @pl.when(lax.rem(i, 3) == 2)
            def _():
                q_sib(0, 1 - i // 3)

            @pl.when(i == 2)
            def _():
                s1.wait()
                sbuf[8] = sbuf[7] + sbuf[1]
                for copy in zs:
                    copy.start()

            @pl.when(i == 3)
            def _():
                loop(4, lambda k: q_y(0, 1, k))

            @pl.when(i == 4)
            def _():
                for copy in zs:
                    copy.wait()
                sbuf[9] = sbuf[8] + sbuf[2] + sbuf[3] + sbuf[4]
                s2.start()

        loop(6, chunk)
        ff_final(0)
        loop(4, lambda i: q_y(0, 0, i))
        loop(3, lambda i: q_z(0, 1, i))
        ff_final(1)
        s2.wait()
        sbuf[6] = sbuf[9] + sbuf[5]
        o_up[...] = sbuf[6, 0:1, pl.ds(pl.multiple_of(m * fw, 128), fw)]
        for n in range(2):
            o_qv[n : n + 1] = sbuf[6, 1:2, pl.ds(pl.multiple_of((3 * m + 2 * n) * lw, 128), lw)]
        dp = lax.axis_index("dp")
        for n, (line, at) in enumerate(((2, 0), (2, 1), (2, 2), (3, 1), (2, 3), (3, 0))):
            row = sbuf[6, line : line + 1, at * width : (at + 1) * width]
            pick = row[:, :part]
            for d in range(1, Z * Y * C):
                pick = jnp.where(dp == d, row[:, d * part : (d + 1) * part], pick)
            o_vec[n : n + 1] = pick
        loop(3, lambda i: q_z(0, 0, i))
        p_final(0)
        q_x(0)
        q_final(0)

        def finish(p):
            for copy in tok_copies(p):
                copy.wait()

        loop(pairs, finish)

        def finish_out(q):
            for copy in out_copies(q):
                copy.wait()

        loop(pairs, finish_out)

    pl.run_scoped(
        attention,
        pltpu.VMEM(w_one_in.shape, LOW), pltpu.VMEM((2, rows, 3 * width), LOW), pltpu.VMEM((2, HEADS, rows, rows), LOW),
        pltpu.VMEM((2, rows, width), LOW), pltpu.VMEM((2, rows, width), LOW), pltpu.VMEM((rows, width), LOW),
        pltpu.VMEM((pairs, width, rows), LOW), pltpu.VMEM((pairs, rows, 3 * width), LOW),
        pltpu.VMEM((pairs, rows, width), LOW),
    )


def backward_reduce(counts, tokens, cotangent, hid, n2, att, n1, qkv, prob, w_one, w_two, bias, vec):
    pairs, rows, width = n1.shape
    flat = pairs * rows
    part = width // (Z * Y * C)
    fw = w_two.shape[2] // 2
    hbm = pl.BlockSpec(memory_space=pl.ANY)
    vm = pl.BlockSpec(memory_space=pltpu.VMEM)
    kinds = ((2, fw), (1, width // 2), (1, 3 * width // 2))
    scratch = [pltpu.VMEM((n, Z * Y, C, part, 2 * w), LOW) for n, w in kinds]
    for n, w in kinds:
        scratch += [pltpu.VMEM((n * k, part, w), LOW) for k in (16, 8, 6, 1)]
    scratch += [
        pltpu.VMEM((flat, width), F32), pltpu.VMEM((pairs, rows, width), LOW), pltpu.VMEM((8, width), F32),
        pltpu.VMEM((8, 3 * width), F32), pltpu.VMEM((8, 2 * fw), F32), pltpu.VMEM((10, 8, 2 * fw), F32),
        pltpu.SemaphoreType.DMA((4, BLOCKS)), pltpu.SemaphoreType.DMA((4, BLOCKS)), pltpu.SemaphoreType.DMA((9,)),
        pltpu.SemaphoreType.DMA((3, pairs)), pltpu.SemaphoreType.DMA((3, pairs)), pltpu.SemaphoreType.DMA((2, 6)),
    ]
    plane = lambda a: a.reshape(-1, width)
    return pl.pallas_call(
        back_kernel,
        in_specs=[pl.BlockSpec(memory_space=pltpu.SMEM)] + [hbm] * 10 + [vm] * 2,
        out_specs=[hbm] * 2 + [vm] * 6,
        out_shape=[
            jax.ShapeDtypeStruct((2 * pairs, rows, width), LOW), jax.ShapeDtypeStruct((2 * pairs, rows, width), LOW),
            jax.ShapeDtypeStruct((2, part, fw), F32), jax.ShapeDtypeStruct((1, part, width // 2), F32),
            jax.ShapeDtypeStruct((3, part, width // 2), F32), jax.ShapeDtypeStruct((1, fw), F32),
            jax.ShapeDtypeStruct((2, width // 2), F32), jax.ShapeDtypeStruct((6, part), F32),
        ],
        scratch_shapes=scratch,
        compiler_params=pltpu.CompilerParams(collective_id=1, has_side_effects=True, vmem_limit_bytes=63 * 2**20),
        name="backward_reduce",
    )(counts, plane(cotangent), plane(hid), plane(n2), plane(att), n1, qkv, prob, tokens, w_one, w_two, bias, vec)


def per_device(
    patch_counts, tokens, cotangent, attn_gain, attn_shift, w_qkv, b_qv, w_proj, b_proj,
    ffn_gain, ffn_shift, w_up, b_up, w_down, b_down,
):
    pairs_all, rows, width = tokens.shape
    n_mp = lax.axis_size("mp")
    n_dp = lax.axis_size("dp")
    pairs = pairs_all // n_mp
    direct = n_dp == Z * Y * C and n_mp == 2 and pairs == 4
    part = w_qkv.shape[0]
    lw = w_qkv.shape[2]
    fw = w_up.shape[1]
    mine = lax.axis_index("mp")
    vectors = [attn_gain, attn_shift, b_proj, ffn_gain, ffn_shift, b_down]
    if direct:
        w_one, w_two, bias, qkv, att, prob, hid, n1, n2, vec = gather_attention(
            patch_counts, tokens, w_qkv, w_proj, w_up, w_down, b_qv, b_up, vectors)
        block_out, tokens_grad, r_ff, r_proj, r_qkv, o_b_up, o_b_qv, o_vec = backward_reduce(
            patch_counts, tokens, cotangent, hid, n2, att, n1, qkv, prob, w_one, w_two, bias, vec)
        o_gain, o_shift, o_b_proj, o_b_down, o_ffn_gain, o_ffn_shift = [o_vec[i] for i in range(6)]
        return (
            block_out, tokens_grad, o_gain, o_shift, r_qkv.transpose(1, 0, 2), o_b_qv,
            r_proj[0].T, o_b_proj, o_ffn_gain, o_ffn_shift, r_ff[1], o_b_up[0], r_ff[0].T, o_b_down,
        )

    off = jnp.reshape(mine * pairs, (1,)).astype(jnp.int32)
    lens = TEXT + lax.dynamic_slice_in_dim(patch_counts, mine * pairs, pairs, 0)
    first = jnp.concatenate(
        [w_qkv.reshape(part, 3 * lw), w_proj.T, jnp.stack(vectors, axis=1), jnp.zeros((part, EXTRA - 6), F32)], axis=1
    ).astype(LOW)
    second = jnp.concatenate([w_up, w_down.T], axis=1).astype(LOW)
    bias = jnp.concatenate([b_qv.reshape(-1), b_up]).astype(LOW).astype(F32)
    bias = jnp.broadcast_to(bias, (8,) + bias.shape)
    both_axes = ("mp", "dp")
    w_one = lax.all_gather(first, both_axes, axis=0, tiled=True).reshape(n_mp, width, -1)
    w_two = lax.all_gather(second, both_axes, axis=0, tiled=True).reshape(n_mp, width, -1)
    bias = lax.all_gather(bias, "mp", axis=0)
    qkv, att, prob, hid, n1, n2, vec = attention_forward(lens, off, tokens, w_one, bias)

    def grad(left, right):
        return jnp.einsum(
            "rd,rf->df", left.reshape(pairs * rows, width), right.reshape(pairs * rows, -1),
            preferred_element_type=F32,
        )

    def reduce(grads, small):
        axes = ("mp", "dp")
        done = [
            lax.psum_scatter(
                g.reshape(width, n_mp, -1).swapaxes(0, 1).reshape(n_mp * width, -1), axes,
                scatter_dimension=0, tiled=True,
            )
            for g in grads
        ]
        return done + [lax.psum(small, axes)]

    def both(array):
        other = lax.ppermute(array, "mp", [(0, 1), (1, 0)])
        return jnp.where(mine == 0, jnp.concatenate([array, other]), jnp.concatenate([other, array]))

    out_here, act, dpre, dhid, dlow, upl, sums_two, bsum_up = ffn(lens, off, n2, hid, cotangent, w_two, bias, vec)
    block_out = both(out_here)
    tok_here, dqkv, sums_one, bsum_qkv = attention_backward(lens, off, tokens, dhid, qkv, prob, w_one, vec)
    tokens_grad = both(tok_here)
    flat = bsum_qkv[0].reshape(n_mp, 3, lw)
    small = jnp.concatenate([
        sums_one[0], sums_one[1], sums_two[2], sums_two[0], sums_two[1], sums_two[3],
        flat[:, 0].reshape(-1), flat[:, 2].reshape(-1), bsum_up[0]])
    r_up, r_down, r_proj, r_qkv, small = reduce(
        [grad(n2, dpre), grad(upl, act), grad(dlow, att), grad(n1, dqkv)], small)
    place_dp = lax.axis_index("dp") * part

    def piece(i):
        return lax.dynamic_slice_in_dim(small, i * width + place_dp, part, 0)

    rest = small[6 * width :]
    o_b_q = lax.dynamic_slice_in_dim(rest, mine * lw, lw, 0)
    o_b_v = lax.dynamic_slice_in_dim(rest, (n_mp + mine) * lw, lw, 0)
    o_b_up = lax.dynamic_slice_in_dim(rest, 2 * n_mp * lw + mine * fw, fw, 0)
    return (
        block_out, tokens_grad, piece(0), piece(1),
        r_qkv.reshape(part, 3, lw), jnp.stack([o_b_q, o_b_v]),
        r_proj.T, piece(2), piece(3), piece(4), r_up, o_b_up, r_down.T, piece(5),
    )


def solution(mesh):
    vec, mat = P("dp"), P("dp", "mp")
    tok = P("dp", None, None)
    in_specs = (
        vec, tok, tok, vec, vec, P("dp", None, "mp"), P(None, "mp"), P("mp", "dp"), vec, vec, vec,
        mat, P("mp"), P("mp", "dp"), vec,
    )
    out_specs = (
        tok, tok, vec, vec, P("dp", None, "mp"), P(None, "mp"), P("mp", "dp"), vec, vec, vec,
        mat, P("mp"), P("mp", "dp"), vec,
    )
    return jax.shard_map(per_device, mesh=mesh, in_specs=in_specs, out_specs=out_specs, check_vma=False)
```

```python
import functools

import jax
import jax.numpy as jnp
from jax import lax
from jax.experimental import pallas as pl
from jax.experimental.pallas import tpu as pltpu
from jax.sharding import PartitionSpec as P

HEADS = 12
HEAD_DIM = 64
TEXT = 40
LOW = jnp.bfloat16
F32 = jnp.float32
EXTRA = 128
NT = (((1,), (1,)), ((), ()))
NN = (((1,), (0,)), ((), ()))


def dot(a, b, dims=NN):
    return lax.dot_general(a, b, dims, preferred_element_type=F32)


def moments(v):
    center = v - jnp.mean(v, axis=-1, keepdims=True)
    spread = jnp.mean(center * center, axis=-1, keepdims=True)
    r = lax.rsqrt(spread + 1e-06)
    return center * r, r


def row_ids(rows):
    return lax.broadcasted_iota(jnp.int32, (rows, 1), 0)


def attn_body(p, count, x, w_ref, bias_ref, vec_ref, qkv_ref, att_ref, prob_ref, hid_ref, n1_ref, n2_ref, hook):
    rows, width = x.shape
    groups = w_ref.shape[0]
    lw = width // groups
    tiles = lw // 128
    x = x.astype(F32)
    xhat, _ = moments(x)
    n1 = (xhat * vec_ref[0:1] + vec_ref[1:2]).astype(LOW)
    n1_ref[0] = n1
    for m in range(groups):
        y = dot(n1, w_ref[m, :, : 3 * lw])
        base = m * 3 * lw
        qkv_ref[0, :, base : base + lw] = (y[:, :lw] + bias_ref[m, 0:1, :lw]).astype(LOW)
        qkv_ref[0, :, base + lw : base + 2 * lw] = y[:, lw : 2 * lw].astype(LOW)
        qkv_ref[0, :, base + 2 * lw : base + 3 * lw] = (
            y[:, 2 * lw :] + bias_ref[m, 0:1, lw : 2 * lw]
        ).astype(LOW)
    keep = row_ids(rows) < count
    first = lax.broadcasted_iota(jnp.int32, (1, 128), 1) < HEAD_DIM

    def pair(hp, carry):
        base = (hp // tiles) * 3 * lw + lax.rem(hp, tiles) * 128

        def cols(t):
            return pl.ds(pl.multiple_of(base + t * lw, 128), 128)

        q2 = qkv_ref[0, :, cols(0)] * 0.125
        k2 = qkv_ref[0, :, cols(1)]
        v2t = qkv_ref[0, :, cols(2)].T
        outs = []
        for h in range(2):
            qh = jnp.where(first if h == 0 else ~first, q2, 0)
            st = dot(k2, qh, NT)
            st = jnp.where(keep, st, -1e30)
            e = jnp.exp(st - jnp.max(st, axis=0, keepdims=True))
            pt = (e * (1.0 / jnp.sum(e, axis=0, keepdims=True))).astype(LOW)
            prob_ref[0, hp * 2 + h] = pt
            outs.append(dot(v2t[h * HEAD_DIM : (h + 1) * HEAD_DIM], pt))
        att_ref[0, :, pl.ds(pl.multiple_of(hp * 128, 128), 128)] = jnp.concatenate(outs, axis=0).T.astype(LOW)
        hook(hp)
        return carry

    lax.fori_loop(0, groups * tiles, pair, 0)
    proj = sum(dot(att_ref[0, :, m * lw : (m + 1) * lw], w_ref[m, :, 3 * lw : 4 * lw], NT) for m in range(groups))
    hid = x + proj + vec_ref[2:3]
    hid_ref[0] = hid
    xhat2, _ = moments(hid)
    n2_ref[0] = (xhat2 * vec_ref[3:4] + vec_ref[4:5]).astype(LOW)


def attn_kernel(lens, off, x_ref, w_ref, bias_ref, qkv_ref, att_ref, prob_ref, hid_ref, n1_ref, n2_ref, vec_ref):
    p = pl.program_id(0)
    lw = x_ref.shape[2] // w_ref.shape[0]

    @pl.when(p == 0)
    def _():
        vec_ref[...] = w_ref[0, :, 4 * lw :].astype(F32).T[:8]

    attn_body(p, lens[p], x_ref[0], w_ref, bias_ref, vec_ref, qkv_ref, att_ref, prob_ref, hid_ref, n1_ref, n2_ref,
              lambda hp: None)


def const_spec(shape):
    return pl.BlockSpec(shape, lambda *_: (0,) * len(shape), pipeline_mode=pl.Buffered(1))


def pair_spec(*shape):
    return pl.BlockSpec((1,) + shape, lambda p, *_: (p,) + (0,) * len(shape))


def attention_forward(lens, off, tokens, w_one, bias):
    pairs = lens.shape[0]
    _, rows, width = tokens.shape
    out = lambda dt, *s: jax.ShapeDtypeStruct((pairs,) + s, dt)
    return pl.pallas_call(
        attn_kernel,
        grid_spec=pltpu.PrefetchScalarGridSpec(
            num_scalar_prefetch=2,
            grid=(pairs,),
            in_specs=[
                pl.BlockSpec((1, rows, width), lambda p, lens, off: (off[0] + p, 0, 0)),
                const_spec(w_one.shape),
                const_spec(bias.shape),
            ],
            out_specs=[
                pair_spec(rows, 3 * width), pair_spec(rows, width), pair_spec(HEADS, rows, rows),
                pair_spec(rows, width), pair_spec(rows, width), pair_spec(rows, width),
                pl.BlockSpec((8, width), lambda *_: (0, 0)),
            ],
        ),
        out_shape=[
            out(LOW, rows, 3 * width), out(LOW, rows, width), out(LOW, HEADS, rows, rows),
            out(F32, rows, width), out(LOW, rows, width), out(LOW, rows, width),
            jax.ShapeDtypeStruct((8, width), F32),
        ],
        compiler_params=pltpu.CompilerParams(vmem_limit_bytes=60 * 2**20),
        name="attention_forward",
    )(lens, off, tokens, w_one, bias)


def ffn_kernel(lens, off, n2_ref, hid_ref, cot_ref, w_ref, bias_ref, vec_ref,
               out_ref, act_ref, dpre_ref, dhid_ref, dlow_ref, upl_ref, sums_ref, bsum_ref):
    p = pl.program_id(0)
    rows, width = n2_ref.shape[1], n2_ref.shape[2]
    groups = w_ref.shape[0]
    fw = w_ref.shape[2] // 2
    lw = width // groups
    step = 512
    keep = row_ids(rows) < lens[p]
    n2 = n2_ref[0]
    upl = jnp.where(keep, cot_ref[0], 0)
    upl_ref[0] = upl

    @pl.when(p == 0)
    def _():
        sums_ref[...] = jnp.zeros_like(sums_ref)
        bsum_ref[...] = jnp.zeros_like(bsum_ref)

    for m in range(groups):
        for c in range(0, fw, step):
            pre = dot(n2, w_ref[m, :, c : c + step]) + bias_ref[m, 0:1, 2 * lw + c : 2 * lw + c + step]
            cdf = 0.5 * (1.0 + lax.erf(pre * (2.0 ** -0.5)))
            at = m * fw + c
            act_ref[0, :, at : at + step] = (pre * cdf).astype(LOW)
            slope = cdf + pre * (0.3989422804014327 * jnp.exp(-0.5 * pre * pre))
            dpre = slope * dot(upl, w_ref[m, :, fw + c : fw + c + step])
            dpre_ref[0, :, at : at + step] = dpre.astype(LOW)
            bsum_ref[0:1, at : at + step] += jnp.sum(dpre, axis=0, keepdims=True)
    hid = hid_ref[0]
    down = sum(dot(act_ref[0, :, m * fw : (m + 1) * fw], w_ref[m, :, fw:], NT) for m in range(groups))
    out_ref[0] = jnp.where(keep, hid + down + vec_ref[5:6], 0.0).astype(LOW)
    dtwo = sum(dot(dpre_ref[0, :, m * fw : (m + 1) * fw], w_ref[m, :, :fw], NT) for m in range(groups))
    xhat, r = moments(hid)
    dg = dtwo * vec_ref[3:4]
    dn = r * (dg - jnp.mean(dg, axis=-1, keepdims=True) - xhat * jnp.mean(dg * xhat, axis=-1, keepdims=True))
    upf = upl.astype(F32)
    dhid = upf + dn
    dhid_ref[0] = dhid
    dlow_ref[0] = dhid.astype(LOW)
    sums_ref[0:1] += jnp.sum(dtwo * xhat, axis=0, keepdims=True)
    sums_ref[1:2] += jnp.sum(dtwo, axis=0, keepdims=True)
    sums_ref[2:3] += jnp.sum(dhid, axis=0, keepdims=True)
    sums_ref[3:4] += jnp.sum(upf, axis=0, keepdims=True)


def ffn(lens, off, n2, hid, cotangent, w_two, bias, vec):
    pairs, rows, width = n2.shape
    ff = w_two.shape[0] * w_two.shape[2] // 2
    out = lambda dt, *s: jax.ShapeDtypeStruct((pairs,) + s, dt)
    return pl.pallas_call(
        ffn_kernel,
        grid_spec=pltpu.PrefetchScalarGridSpec(
            num_scalar_prefetch=2,
            grid=(pairs,),
            in_specs=[
                pair_spec(rows, width), pair_spec(rows, width),
                pl.BlockSpec((1, rows, width), lambda p, lens, off: (off[0] + p, 0, 0)),
                const_spec(w_two.shape), const_spec(bias.shape), const_spec(vec.shape),
            ],
            out_specs=[
                pair_spec(rows, width), pair_spec(rows, ff), pair_spec(rows, ff), pair_spec(rows, width),
                pair_spec(rows, width), pair_spec(rows, width),
                pl.BlockSpec((8, width), lambda *_: (0, 0)), pl.BlockSpec((8, ff), lambda *_: (0, 0)),
            ],
        ),
        out_shape=[
            out(LOW, rows, width), out(LOW, rows, ff), out(LOW, rows, ff), out(F32, rows, width),
            out(LOW, rows, width), out(LOW, rows, width),
            jax.ShapeDtypeStruct((8, width), F32), jax.ShapeDtypeStruct((8, ff), F32),
        ],
        compiler_params=pltpu.CompilerParams(vmem_limit_bytes=60 * 2**20),
        name="feed_forward",
    )(lens, off, n2, hid, cotangent, w_two, bias, vec)


def plain_back_kernel(lens, off, x_ref, dhid_ref, qkv_ref, prob_ref, w_ref, vec_ref,
                tok_ref, dqkv_ref, sums_ref, bsum_ref, do_ref):
    p = pl.program_id(0)
    rows, width = x_ref.shape[1], x_ref.shape[2]
    groups = w_ref.shape[0]
    lw = width // groups
    tiles = lw // 128

    @pl.when(p == 0)
    def _():
        sums_ref[...] = jnp.zeros_like(sums_ref)
        bsum_ref[...] = jnp.zeros_like(bsum_ref)

    dhid = dhid_ref[0]
    dlow = dhid.astype(LOW)
    for m in range(groups):
        do_ref[:, m * lw : (m + 1) * lw] = dot(dlow, w_ref[m, :, 3 * lw : 4 * lw]).astype(LOW)
    first = lax.broadcasted_iota(jnp.int32, (1, 128), 1) < HEAD_DIM

    def pair(hp, carry):
        base = (hp // tiles) * 3 * lw + (hp % tiles) * 128

        def cols(t):
            return pl.ds(pl.multiple_of(base + t * lw, 128), 128)

        q2 = qkv_ref[0, :, cols(0)] * 0.125
        k2t = qkv_ref[0, :, cols(1)].T
        v2 = qkv_ref[0, :, cols(2)]
        do2 = do_ref[:, pl.ds(pl.multiple_of(hp * 128, 128), 128)]
        dq_t = []
        dk = dv = 0.0
        for h in range(2):
            mine = first if h == 0 else ~first
            doh = jnp.where(mine, do2, 0)
            qh = jnp.where(mine, q2, 0)
            dpt = dot(v2, doh, NT)
            plow = prob_ref[0, hp * 2 + h]
            pt = plow.astype(F32)
            inner = jnp.sum(pt * dpt, axis=0, keepdims=True)
            dst = (pt * (dpt - inner)).astype(LOW)
            dv = dv + dot(plow, doh)
            dk = dk + dot(dst, qh)
            dq_t.append(dot(k2t[h * HEAD_DIM : (h + 1) * HEAD_DIM], dst))
        dq = (jnp.concatenate(dq_t, axis=0) * 0.125).T
        dqkv_ref[0, :, cols(0)] = dq.astype(LOW)
        dqkv_ref[0, :, cols(1)] = dk.astype(LOW)
        dqkv_ref[0, :, cols(2)] = dv.astype(LOW)
        bsum_ref[0:1, cols(0)] += jnp.sum(dq, axis=0, keepdims=True)
        bsum_ref[0:1, cols(2)] += jnp.sum(dv, axis=0, keepdims=True)
        return carry

    lax.fori_loop(0, groups * tiles, pair, 0)
    done = sum(dot(dqkv_ref[0, :, m * 3 * lw : (m + 1) * 3 * lw], w_ref[m, :, : 3 * lw], NT) for m in range(groups))
    xhat, r = moments(x_ref[0].astype(F32))
    dg = done * vec_ref[0:1]
    dn = r * (dg - jnp.mean(dg, axis=-1, keepdims=True) - xhat * jnp.mean(dg * xhat, axis=-1, keepdims=True))
    tok_ref[0] = (dhid + dn).astype(LOW)
    sums_ref[0:1] += jnp.sum(done * xhat, axis=0, keepdims=True)
    sums_ref[1:2] += jnp.sum(done, axis=0, keepdims=True)


def attention_backward(lens, off, tokens, dhid, qkv, prob, w_one, vec):
    pairs, rows, width = dhid.shape
    out = lambda dt, *s: jax.ShapeDtypeStruct((pairs,) + s, dt)
    return pl.pallas_call(
        plain_back_kernel,
        grid_spec=pltpu.PrefetchScalarGridSpec(
            num_scalar_prefetch=2,
            grid=(pairs,),
            in_specs=[
                pl.BlockSpec((1, rows, width), lambda p, lens, off: (off[0] + p, 0, 0)),
                pair_spec(rows, width), pair_spec(rows, 3 * width), pair_spec(HEADS, rows, rows),
                const_spec(w_one.shape), const_spec(vec.shape),
            ],
            out_specs=[
                pair_spec(rows, width), pair_spec(rows, 3 * width),
                pl.BlockSpec((8, width), lambda *_: (0, 0)), pl.BlockSpec((8, 3 * width), lambda *_: (0, 0)),
            ],
            scratch_shapes=[pltpu.VMEM((rows, width), LOW)],
        ),
        out_shape=[
            out(LOW, rows, width), out(LOW, rows, 3 * width),
            jax.ShapeDtypeStruct((8, width), F32), jax.ShapeDtypeStruct((8, 3 * width), F32),
        ],
        compiler_params=pltpu.CompilerParams(vmem_limit_bytes=60 * 2**20),
        name="attention_backward",
    )(lens, off, tokens, dhid, qkv, prob, w_one, vec)
MESH_ID = pl.DeviceIdType.MESH
Z, Y, C = 4, 2, 2


def place():
    dp = lax.axis_index("dp")
    m = lax.axis_index("mp")
    c = lax.rem(dp, 2)
    y = lax.rem(dp // 2, 2)
    z = dp // 4
    return z, y, c, m


def index(z, y, c):
    return (z * Y + y) * C + c


def flips(y, c, m):
    one = (y + c * (1 - 2 * y), m + (1 - c) * (1 - 2 * m))
    two = (y + (1 - c) * (1 - 2 * y), m + c * (1 - 2 * m))
    return one, two


def greet(z, y, c, m):
    barrier = pltpu.get_barrier_semaphore()
    (y1, m1), (y2, m2) = flips(y, c, m)
    peers = [(index(lax.rem(z + k, Z), y, c), m) for k in (1, 2, 3)]
    peers += [(index(z, y1, c), m1), (index(z, y2, c), m2), (index(z, y, 1 - c), m)]
    for dp, mp in peers:
        pl.semaphore_signal(barrier, inc=1, device_id={"dp": dp, "mp": mp}, device_id_type=MESH_ID)
    pl.semaphore_wait(barrier, len(peers))
    return peers


def gather_attn_kernel(counts, tok_all, wq_in, wp_in, wu_in, wd_in, bq_in, bu_in, v0, v1, v2, v3, v4, v5,
                       w_one_out, w_two, b_out, qkv_ref, att_ref, prob_ref, hid_ref, n1_ref, n2_ref, vec_ref,
                       w_one, bias, xbuf, first_ref, second_ref, b_in, vbuf, send, recv, bsem, local):
    p = pl.program_id(0)
    z, y, c, m = place()
    (y1, m1), (y2, m2) = flips(y, c, m)
    pairs, rows, width = xbuf.shape
    part = first_ref.shape[0]
    cols = second_ref.shape[1] // 2
    lw = width // 2
    per_pair = width // 128
    me = index(z, y, c)
    one, two, sib = (index(z, y1, c), m1), (index(z, y2, c), m2), (index(z, y, 1 - c), m)

    def spot(g, dp, mp):
        at = pl.ds(pl.multiple_of(dp * part, part), part)
        if g is None:
            return w_one.at[mp, at]
        return w_two.at[mp, at, pl.ds(pl.multiple_of(g * cols, 128), cols)]

    def shard(g):
        return first_ref if g is None else second_ref.at[:, pl.ds(pl.multiple_of(g * cols, 128), cols)]

    def row(g):
        return 0 if g is None else g + 1

    def copy_of(g, src, dst, out_sem, in_sem, to):
        return pltpu.make_async_remote_copy(
            src_ref=src, dst_ref=dst, send_sem=send.at[row(g), out_sem], recv_sem=recv.at[row(g), in_sem],
            device_id={"dp": to[0], "mp": to[1]}, device_id_type=MESH_ID,
        )

    def push(g, src, dp, mp, to, sem):
        copy_of(g, src, spot(g, dp, mp), sem, mp * (Z * Y * C) + dp, to).start()

    def arrived(g, dp, mp):
        at = spot(g, dp, mp)
        copy_of(g, at, at, 0, mp * (Z * Y * C) + dp, sib).wait_recv()
        return at

    def own_z(g):
        for k in (1, 3, 2):
            push(g, shard(g), me, m, (index(lax.rem(z + k, Z), y, c), m), k - 1)

    def own_near(g):
        for n, to in enumerate((one, two, sib)):
            push(g, shard(g), me, m, to, 3 + n)

    def event_z(g, i):
        dp = index(lax.rem(z + 1 + lax.rem(2 * i, 3), Z), y, c)
        at = arrived(g, dp, m)
        for n, to in enumerate((one, two, sib)):
            push(g, at, dp, m, to, 6 + 3 * i + n)

    def event_one(g, i):
        dp = index(lax.rem(z + i, Z), y1, c)
        at = arrived(g, dp, m1)
        for n, to in enumerate((two, sib)):
            push(g, at, dp, m1, to, 15 + 2 * i + n)

    def event_two(g, i):
        far = lax.rem(i, 2)
        yy = y2 + far * (1 - y - y2)
        mm = m2 + far * (1 - m - m2)
        dp = index(lax.rem(z + i // 2, Z), yy, c)
        push(g, arrived(g, dp, mm), dp, mm, sib, 23 + i)

    def event_core(g, i):
        arrived(g, index(i // 4, lax.rem(i // 2, 2), 1 - c), lax.rem(i, 2))

    def loop(n, event, g):
        def run(i, carry):
            event(g, i)
            return carry

        lax.fori_loop(0, n, run, 0)

    bias_copy = pltpu.make_async_remote_copy(
        src_ref=b_in, dst_ref=bias.at[m], send_sem=bsem.at[0], recv_sem=bsem.at[1],
        device_id={"dp": me, "mp": 1 - m}, device_id_type=MESH_ID,
    )
    x_copy = pltpu.make_async_copy(tok_all.at[pl.ds(m * pairs, pairs)], xbuf, local.at[0])
    mine = [
        pltpu.make_async_copy(b_in, bias.at[m], local.at[1]),
        pltpu.make_async_copy(first_ref, spot(None, me, m), local.at[2]),
    ]
    mine_two = [pltpu.make_async_copy(shard(g), spot(g, me, m), local.at[3 + g]) for g in range(2)]
    keep_one = pltpu.make_async_copy(w_one, w_one_out, local.at[5])
    keep_bias = pltpu.make_async_copy(bias, b_out, local.at[6])

    @pl.when(p == 0)
    def _():
        x_copy.start()
        for t in range(3):
            first_ref[:, t * lw : (t + 1) * lw] = wq_in[t].astype(LOW)
        first_ref[:, 3 * lw : 4 * lw] = wp_in[...].astype(LOW)
        vbuf[...] = jnp.zeros_like(vbuf)
        for n, v in enumerate((v0, v1, v2, v3, v4, v5)):
            vbuf[n : n + 1, :part] = v[...]
        first_ref[:, 4 * lw :] = vbuf[...].T[:part].astype(LOW)
        second_ref[:, :cols] = wu_in[...].astype(LOW)
        second_ref[:, cols:] = wd_in[...].astype(LOW)
        b_in[...] = jnp.zeros_like(b_in)
        b_in[0:1, :lw] = bq_in[0:1].astype(LOW).astype(F32)
        b_in[0:1, lw : 2 * lw] = bq_in[1:2].astype(LOW).astype(F32)
        b_in[0:1, 2 * lw :] = bu_in[...].astype(LOW).astype(F32)
        greet(z, y, c, m)
        own_z(None)
        own_near(None)
        bias_copy.start()
        for copy in mine + mine_two:
            copy.start()
        loop(3, event_z, None)
        own_z(0)
        own_z(1)
        loop(4, event_one, None)
        own_near(0)
        loop(3, event_z, 0)
        loop(8, event_two, None)
        for copy in mine + [x_copy, bias_copy]:
            copy.wait()
        loop(16, event_core, None)
        keep_one.start()
        keep_bias.start()
        vec_ref[...] = w_one[0, :, 4 * lw :].astype(F32).T[:8]

    def hook(hp):
        step = p * per_pair + hp

        def event(e, carry):
            @pl.when(e == 0)
            def _():
                own_near(1)

            @pl.when(((e >= 1) & (e < 5)) | ((e >= 16) & (e < 20)))
            def _():
                g = e // 16
                event_one(g, e - 1 - 15 * g)

            @pl.when((e >= 5) & (e < 8))
            def _():
                event_z(1, e - 5)

            @pl.when(((e >= 8) & (e < 16)) | (e >= 20))
            def _():
                g = e // 20
                event_two(g, e - 8 - 12 * g)

            return carry

        total = pairs * per_pair
        lax.fori_loop(step * 28 // total, (step + 1) * 28 // total, event, 0)

    attn_body(p, TEXT + counts[m * pairs + p], xbuf[p], w_one, bias, vec_ref, qkv_ref, att_ref, prob_ref, hid_ref, n1_ref, n2_ref, hook)

    @pl.when(p == pairs - 1)
    def _():
        for g in range(2):
            loop(16, event_core, g)
        for copy in mine_two + [keep_one, keep_bias]:
            copy.wait()
        for g in (None, 0, 1):
            def sent(i, carry):
                copy_of(g, shard(g), shard(g), i, 0, sib).wait_send()
                return carry

            lax.fori_loop(0, 31, sent, 0)


def gather_attention(counts, tokens, w_qkv, w_proj, w_up, w_down, b_qv, b_up, vectors):
    pairs = counts.shape[0] // 2
    _, rows, width = tokens.shape
    part, fw = w_up.shape
    lw = width // 2
    total = Z * Y * C
    hbm = pl.BlockSpec(memory_space=pl.ANY)
    out = lambda dt, *s: jax.ShapeDtypeStruct((pairs,) + s, dt)
    small = [w_qkv.transpose(1, 0, 2), w_proj.T, w_up, w_down.T, b_qv, b_up.reshape(1, fw)]
    small += [v.reshape(1, part) for v in vectors]
    one, two, bias = 4 * lw + EXTRA, 2 * fw, (8, 2 * lw + fw)
    return pl.pallas_call(
        gather_attn_kernel,
        grid_spec=pltpu.PrefetchScalarGridSpec(
            num_scalar_prefetch=1,
            grid=(pairs,),
            in_specs=[hbm] + [const_spec(a.shape) for a in small],
            out_specs=[
                hbm, hbm, hbm,
                pair_spec(rows, 3 * width), pair_spec(rows, width), pair_spec(HEADS, rows, rows),
                pair_spec(rows, width), pair_spec(rows, width), pair_spec(rows, width),
                pl.BlockSpec((8, width), lambda *_: (0, 0)),
            ],
            scratch_shapes=[
                pltpu.VMEM((2, width, one), LOW), pltpu.VMEM((2,) + bias, F32), pltpu.VMEM((pairs, rows, width), LOW),
                pltpu.VMEM((part, one), LOW), pltpu.VMEM((part, two), LOW), pltpu.VMEM(bias, F32),
                pltpu.VMEM((EXTRA, EXTRA), F32),
                pltpu.SemaphoreType.DMA((3, 31)), pltpu.SemaphoreType.DMA((3, 32)),
                pltpu.SemaphoreType.DMA((2,)), pltpu.SemaphoreType.DMA((7,)),
            ],
        ),
        out_shape=[
            jax.ShapeDtypeStruct((2, width, one), LOW),
            jax.ShapeDtypeStruct((2, width, two), LOW),
            jax.ShapeDtypeStruct((2,) + bias, F32),
            out(LOW, rows, 3 * width), out(LOW, rows, width), out(LOW, HEADS, rows, rows),
            out(F32, rows, width), out(LOW, rows, width), out(LOW, rows, width),
            jax.ShapeDtypeStruct((8, width), F32),
        ],
        compiler_params=pltpu.CompilerParams(collective_id=0, has_side_effects=True, vmem_limit_bytes=60 * 2**20),
        name="gather_attention",
    )(counts, tokens, *small)


BLOCKS = 31


def back_kernel(counts, cot, hid_in, n2_in, att_in, n1_all, qkv_all, prob_all, tok_all, w_one_in, w_two, bias_ref, vec_ref,
                block_out, tok_out, r_down, r_up, r_proj, r_qkv, o_up, o_qv, o_vec,
                g_ff, g_proj, g_qkv, rc_ff, rs_ff, rz_ff, rx_ff, rc_p, rs_p, rz_p, rx_p, rc_q, rs_q, rz_q, rx_q,
                dhid_ref, outbuf, sums, bsum, bsum_up, sbuf, send, recv, local, osem, tsem, ssem, n1_sem):
    flat, width = dhid_ref.shape
    pairs, rows = qkv_all.shape[0], qkv_all.shape[1]
    groups = w_two.shape[0]
    fw = w_two.shape[2] // 2
    fc = fw // 3
    lw = width // groups
    tiles = lw // 128
    half = flat // 2
    part = r_proj.shape[1]
    high = pairs * (rows + (-rows) % 16)
    z, y, c, m = place()
    me = index(z, y, c)
    sib = (index(z, y, 1 - c), m)

    def beside(k):
        return (index(lax.rem(z + k, Z), y, c), m)

    def loop(n, event):
        def one(i, carry):
            event(i)
            return carry

        lax.fori_loop(0, n, one, 0)

    def family(grad, rc, rs, rz, rx, out, row0):
        cols = rc.shape[2]

        def copy_of(u, src, dst, out_sem, in_sem, to):
            return pltpu.make_async_remote_copy(
                src_ref=src, dst_ref=dst, send_sem=send.at[row0 + u, out_sem], recv_sem=recv.at[row0 + u, in_sem],
                device_id={"dp": to[0], "mp": to[1]}, device_id_type=MESH_ID,
            )

        def block(u, ra, rb, k, cc):
            yy = y + ra * (1 - 2 * y)
            mm = m + rb * (1 - 2 * m)
            return u, lax.rem(z + k, Z) * Y + yy, cc, slice(None), pl.ds(pl.multiple_of(mm * cols, 128), cols)

        def to_sibling(u, rb):
            def one(i):
                ra, k = 1 - i // 4, lax.rem(i + 1, 4)
                slot = (ra * 2 + rb) * 4 + k
                copy_of(u, grad.at[block(u, ra, rb, k, 1 - c)], rc.at[u * 16 + slot], slot, slot, sib).start()

            loop(8, one)

        def arrived(u, ref, sem):
            copy_of(u, ref, ref, 0, sem, sib).wait_recv()

        def base(u, ra, rb, k):
            slot = (ra * 2 + rb) * 4 + k
            arrived(u, rc.at[u * 16 + slot], slot)
            return grad[block(u, ra, rb, k, c)].astype(F32) + rc[u * 16 + slot].astype(F32)

        def level(u, rb, k):
            at = rb * 4 + k
            value = base(u, 0, rb, k)
            arrived(u, rs.at[u * 8 + at], 16 + at)
            return value + rs[u * 8 + at].astype(F32)

        def lined(u, rb):
            value = level(u, rb, 0)
            for k in (1, 2, 3):
                at = (k - 1) * 2 + rb
                arrived(u, rz.at[u * 6 + at], 24 + at)
                value = value + rz[u * 6 + at].astype(F32)
            return value

        def event_y(u, rb, i):
            k = lax.rem(i + 1, 4)
            slot = u * 16 + (2 + rb) * 4 + k
            at = rb * 4 + k
            rc[slot] = base(u, 1, rb, k).astype(LOW)
            copy_of(u, rc.at[slot], rs.at[u * 8 + at], 16 + at, 16 + at, (index(z, 1 - y, c), m)).start()

        def event_z(u, rb, i):
            k = 1 + i
            slot = u * 16 + rb * 4 + k
            at = (k - 1) * 2 + rb
            rc[slot] = level(u, rb, k).astype(LOW)
            copy_of(u, rc.at[slot], rz.at[u * 6 + at], 24 + at, 24 + at, beside(k)).start()

        def event_x(u):
            rc[u * 16 + 4] = lined(u, 1).astype(LOW)
            copy_of(u, rc.at[u * 16 + 4], rx.at[u], 30, 30, (me, 1 - m)).start()

        def final(u):
            value = lined(u, 0)
            arrived(u, rx.at[u], 30)
            out(u, value + rx[u].astype(F32))

            def one(i):
                copy_of(u, rc.at[0], rc.at[0], i, 0, sib).wait_send()

            loop(BLOCKS, one)

        return to_sibling, event_y, event_z, event_x, final

    def put(ref):
        def store(u, value):
            ref[u] = value

        return store

    def put_ff(u, value):
        (r_down, r_up)[u][...] = value

    def put_qkv(u, value):
        for t in range(3):
            r_qkv[t] = value[:, t * lw : (t + 1) * lw]

    ff_sib, ff_y, ff_z, ff_x, ff_final = family(g_ff, rc_ff, rs_ff, rz_ff, rx_ff, put_ff, 0)
    p_sib, p_y, p_z, p_x, p_final = family(g_proj, rc_p, rs_p, rz_p, rx_p, put(r_proj), 2)
    q_sib, q_y, q_z, q_x, q_final = family(g_qkv, rc_q, rs_q, rz_q, rx_q, put_qkv, 3)

    def out_copies(q):
        src = outbuf.at[q]
        dst = block_out.at[m * pairs + q]
        return pltpu.make_async_copy(src, dst, osem.at[0, q]), pltpu.make_async_remote_copy(
            src_ref=src, dst_ref=dst, send_sem=osem.at[1, q], recv_sem=osem.at[2, q],
            device_id={"dp": me, "mp": 1 - m}, device_id_type=MESH_ID,
        )

    def keep_of(r):
        ids = row_ids(half)
        here = m * pairs + 2 * r
        return ids < TEXT + jnp.where(ids < rows, counts[here], counts[here + 1] + rows)

    def span(r):
        return pl.ds(pl.multiple_of(r * half, 16), half)

    sums[...] = jnp.zeros_like(sums)
    bsum[...] = jnp.zeros_like(bsum)
    bsum_up[...] = jnp.zeros_like(bsum_up)

    def feed_forward(n2, n2t, upl, uplt, hid, acc, slope, chunk, wbuf):
        def place_of(f):
            i = lax.rem(f, 6)
            return lax.rem(m + 1 + i // 3, 2), lax.rem(i, 3) * fc

        def weights(f):
            mm, at = place_of(f)
            slot = lax.rem(f, 2)
            return [
                pltpu.make_async_copy(
                    w_two.at[mm, :, pl.ds(pl.multiple_of(t * fw + at, 128), fc)], wbuf.at[slot, t], local.at[slot * 2 + t])
                for t in range(2)
            ]

        n2_copy = pltpu.make_async_copy(n2_in, n2, local.at[4])
        up_copy = pltpu.make_async_copy(cot.at[pl.ds(pl.multiple_of(m * flat, 16), flat)], upl, local.at[5])
        hid_copy = pltpu.make_async_copy(hid_in, hid, local.at[6])
        att_copy = pltpu.make_async_copy(att_in, slope.at[:, pl.ds(0, width)], local.at[7])
        n2_copy.start()
        up_copy.start()
        for copy in weights(0):
            copy.start()
        hid_copy.start()
        greet(z, y, c, m)
        up_copy.wait()

        def prepare(r):
            value = jnp.where(keep_of(r), upl[span(r)], 0)
            upl[span(r)] = value
            sums[3:4] += jnp.sum(value.astype(F32), axis=0, keepdims=True)
            acc[span(r)] = jnp.zeros((half, width), F32)

        loop(2, prepare)
        uplt[...] = upl[...].T
        n2_copy.wait()
        n2t[...] = n2[...].T

        def traffic(f):
            @pl.when(lax.rem(f, 3) == 2)
            def _():
                n = f // 3
                ff_sib(n // 2, 1 - lax.rem(n, 2))

            @pl.when((lax.rem(f, 3) == 0) & (f > 0))
            def _():
                n = f // 3 - 1
                loop(4, lambda i: ff_y(n // 2, 1 - lax.rem(n, 2), i))

            @pl.when((lax.rem(f, 3) == 1) & (f > 4))
            def _():
                n = (f - 7) // 3
                loop(3, lambda i: ff_z(n // 2, 1 - lax.rem(n, 2), i))

        def store(u, at, value):
            g_ff[u, :, :, :, at] = value.astype(LOW).reshape(Z * Y, C, part, fc)

        def forward(f):
            slot = lax.rem(f, 2)
            for copy in weights(f + 1):
                copy.start()
            for copy in weights(f):
                copy.wait()
            mm, off = place_of(f)
            at = pl.ds(pl.multiple_of(mm * fw + off, 128), fc)
            shift = bias_ref[mm, 0:1, pl.ds(pl.multiple_of(2 * lw + off, 128), fc)]

            def block(r):
                pre = dot(n2[span(r)], wbuf[slot, 0]) + shift
                cdf = 0.5 * (1.0 + lax.erf(pre * (2.0 ** -0.5)))
                chunk[span(r)] = (pre * cdf).astype(LOW)
                slope[span(r), at] = (cdf + pre * (0.3989422804014327 * jnp.exp(-0.5 * pre * pre))).astype(LOW)
                acc[span(r)] += dot(chunk[span(r)], wbuf[slot, 1], NT)

            loop(2, block)
            store(0, at, dot(uplt[...], chunk[...]))
            traffic(f)

        loop(6, forward)
        hid_copy.wait()

        def leave(r):
            value = jnp.where(keep_of(r), hid[span(r)] + acc[span(r)] + vec_ref[5:6], 0.0)
            acc[span(r)] = jnp.zeros((half, width), F32)
            for n in range(2):
                outbuf[2 * r + n] = value[n * rows : (n + 1) * rows].astype(LOW)
                for copy in out_copies(2 * r + n):
                    copy.start()

        loop(2, leave)

        def backward(i):
            f = 6 + i
            slot = lax.rem(f, 2)

            @pl.when(f < 11)
            def _():
                for copy in weights(f + 1):
                    copy.start()

            for copy in weights(f):
                copy.wait()
            mm, off = place_of(f)
            at = pl.ds(pl.multiple_of(mm * fw + off, 128), fc)

            def block(r):
                dpre = slope[span(r), at].astype(F32) * dot(upl[span(r)], wbuf[slot, 1])
                chunk[span(r)] = dpre.astype(LOW)
                bsum_up[0:1, at] += jnp.sum(dpre, axis=0, keepdims=True)
                acc[span(r)] += dot(chunk[span(r)], wbuf[slot, 0], NT)

            loop(2, block)
            store(1, at, dot(n2t[...], chunk[...]))
            traffic(f)

        loop(6, backward)
        att_copy.start()

        def norm_back(r):
            dtwo = acc[span(r)]
            xhat, rr = moments(hid[span(r)])
            dg = dtwo * vec_ref[3:4]
            dn = rr * (dg - jnp.mean(dg, axis=-1, keepdims=True) - xhat * jnp.mean(dg * xhat, axis=-1, keepdims=True))
            dhid = upl[span(r)].astype(F32) + dn
            dhid_ref[span(r)] = dhid
            n2[span(r)] = dhid.astype(LOW)
            sums[4:5] += jnp.sum(dtwo * xhat, axis=0, keepdims=True)
            sums[5:6] += jnp.sum(dtwo, axis=0, keepdims=True)
            sums[2:3] += jnp.sum(dhid, axis=0, keepdims=True)

        loop(2, norm_back)
        att_copy.wait()
        n2t[...] = n2[...].T
        for mm in range(groups):
            at = slice(mm * lw, (mm + 1) * lw)
            g_proj[0, :, :, :, at] = dot(n2t[...], slope[:, at]).astype(LOW).reshape(Z * Y, C, part, lw)
        p_sib(0, 1)
        p_sib(0, 0)

    pl.run_scoped(
        feed_forward,
        pltpu.VMEM((flat, width), LOW), pltpu.VMEM((width, flat), LOW),
        pltpu.VMEM((flat, width), LOW), pltpu.VMEM((width, flat), LOW),
        pltpu.VMEM((flat, width), F32), pltpu.VMEM((flat, width), F32),
        pltpu.VMEM((flat, groups * fw), LOW), pltpu.VMEM((flat, fc), LOW), pltpu.VMEM((2, 2, width, fc), LOW),
    )

    def attention(w_ref, qkv_buf, prob_buf, x_buf, do_ref, n1, n1t, dq_all):
        high = n1.shape[0] // pairs
        w_copy = pltpu.make_async_copy(w_one_in, w_ref, local.at[8])

        def loads(p):
            slot = lax.rem(p, 2)
            pieces = [
                (qkv_all.at[p], qkv_buf), (prob_all.at[p], prob_buf), (tok_all.at[m * pairs + p], x_buf),
            ]
            return [
                pltpu.make_async_copy(src, dst.at[slot], local.at[slot * 3 + t])
                for t, (src, dst) in enumerate(pieces)
            ]

        def tok_copies(p):
            src, dst = n1.at[pl.ds(pl.multiple_of(p * high, 16), rows)], tok_out.at[m * pairs + p]
            return pltpu.make_async_copy(src, dst, tsem.at[0, p]), pltpu.make_async_remote_copy(
                src_ref=src, dst_ref=dst, send_sem=tsem.at[1, p], recv_sem=tsem.at[2, p],
                device_id={"dp": me, "mp": 1 - m}, device_id_type=MESH_ID,
            )

        w_copy.start()
        for copy in loads(0):
            copy.start()
        n1_copies = [
            pltpu.make_async_copy(n1_all.at[p], n1.at[pl.ds(p * high, rows)], n1_sem.at[p]) for p in range(pairs)
        ]
        for copy in n1_copies:
            copy.start()
        w_copy.wait()

        def attended_back(r):
            dlow = dhid_ref[span(r)].astype(LOW)
            for mm in range(groups):
                value = dot(dlow, w_ref[mm, :, 3 * lw : 4 * lw])
                for n in range(2):
                    do_ref[2 * r + n, :, mm * lw : (mm + 1) * lw] = value[n * rows : (n + 1) * rows].astype(LOW)

        loop(2, attended_back)
        for p, copy in enumerate(n1_copies):
            copy.wait()
            n1[p * high + rows : (p + 1) * high] = jnp.zeros((high - rows, width), LOW)
            dq_all[p * high + rows : (p + 1) * high] = jnp.zeros((high - rows, 3 * width), LOW)
        n1t[...] = n1[...].T
        first = lax.broadcasted_iota(jnp.int32, (1, 128), 1) < HEAD_DIM

        def one_pair(p):
            slot = lax.rem(p, 2)

            @pl.when(p < pairs - 1)
            def _():
                for copy in loads(p + 1):
                    copy.start()

            dhid = dhid_ref[pl.ds(pl.multiple_of(p * rows, 8), rows)]
            here = pl.ds(pl.multiple_of(p * high, 16), rows)
            for copy in loads(p):
                copy.wait()

            def heads(hp):
                lane = (hp // tiles) * 3 * lw + lax.rem(hp, tiles) * 128

                def cols(t):
                    return pl.ds(pl.multiple_of(lane + t * lw, 128), 128)

                q2 = qkv_buf[slot, :, cols(0)] * 0.125
                k2t = qkv_buf[slot, :, cols(1)].T
                v2 = qkv_buf[slot, :, cols(2)]
                do2 = do_ref[p, :, pl.ds(pl.multiple_of(hp * 128, 128), 128)]
                dq_t = []
                dk = dv = 0.0
                for h in range(2):
                    mine = first if h == 0 else ~first
                    doh = jnp.where(mine, do2, 0)
                    qh = jnp.where(mine, q2, 0)
                    dpt = dot(v2, doh, NT)
                    plow = prob_buf[slot, hp * 2 + h]
                    pt = plow.astype(F32)
                    inner = jnp.sum(pt * dpt, axis=0, keepdims=True)
                    dst = (pt * (dpt - inner)).astype(LOW)
                    dv = dv + dot(plow, doh)
                    dk = dk + dot(dst, qh)
                    dq_t.append(dot(k2t[h * HEAD_DIM : (h + 1) * HEAD_DIM], dst))
                dq = (jnp.concatenate(dq_t, axis=0) * 0.125).T
                dq_all[here, cols(0)] = dq.astype(LOW)
                dq_all[here, cols(1)] = dk.astype(LOW)
                dq_all[here, cols(2)] = dv.astype(LOW)
                bsum[0:1, cols(0)] += jnp.sum(dq, axis=0, keepdims=True)
                bsum[0:1, cols(2)] += jnp.sum(dv, axis=0, keepdims=True)
                step = p * (groups * tiles) + hp

                @pl.when(step == 0)
                def _():
                    loop(4, lambda i: ff_y(1, 0, i))

                @pl.when((step == 2) | (step == 13))
                def _():
                    loop(3, lambda i: ff_z(1, 1 - step // 13, i))

                @pl.when((step >= 3) & (step < 7))
                def _():
                    loop(2, lambda i: p_y(0, 1 - (step - 3) // 2, 2 * lax.rem(step - 3, 2) + i))

                @pl.when((step == 18) | (step == 19))
                def _():
                    loop(3, lambda i: p_z(0, 19 - step, i))

                @pl.when((step == 16) | (step == 21))
                def _():
                    ff_x((step - 16) // 5)

            loop(groups * tiles, heads)
            done = sum(
                dot(dq_all[here, mm * 3 * lw : (mm + 1) * 3 * lw], w_ref[mm, :, : 3 * lw], NT) for mm in range(groups))
            xhat, r = moments(x_buf[slot].astype(F32))
            dg = done * vec_ref[0:1]
            dn = r * (dg - jnp.mean(dg, axis=-1, keepdims=True) - xhat * jnp.mean(dg * xhat, axis=-1, keepdims=True))
            n1[here] = (dhid + dn).astype(LOW)
            for copy in tok_copies(p):
                copy.start()
            sums[0:1] += jnp.sum(done * xhat, axis=0, keepdims=True)
            sums[1:2] += jnp.sum(done, axis=0, keepdims=True)

        loop(pairs, one_pair)

        def small_copy(slot, src, to, sem):
            return pltpu.make_async_remote_copy(
                src_ref=sbuf.at[src], dst_ref=sbuf.at[slot], send_sem=ssem.at[0, sem], recv_sem=ssem.at[1, sem],
                device_id={"dp": to[0], "mp": to[1]}, device_id_type=MESH_ID,
            )

        sbuf[6] = jnp.zeros_like(sbuf[6])
        sbuf[6, 0:1] = bsum_up[0:1]
        sbuf[6, 1:2, : 3 * width] = bsum[0:1]
        for n, (line, at) in enumerate(((2, 0), (2, 1), (2, 2), (3, 1), (2, 3), (3, 0))):
            sbuf[6, line : line + 1, at * width : (at + 1) * width] = sums[n : n + 1]
        s0 = small_copy(0, 6, sib, 0)
        s1 = small_copy(1, 7, (index(z, 1 - y, c), m), 1)
        zs = [small_copy(1 + k, 8, beside(k), 1 + k) for k in (1, 2, 3)]
        s2 = small_copy(5, 9, (me, 1 - m), 5)
        s0.start()

        def chunk(i):
            mm = lax.rem(m + 1 + i // 3, 2)
            at = pl.ds(pl.multiple_of(mm * 3 * lw + lax.rem(i, 3) * lw, 128), lw)
            g_qkv[0, :, :, :, at] = dot(n1t[...], dq_all[:, at]).astype(LOW).reshape(Z * Y, C, part, lw)

            @pl.when(i == 0)
            def _():
                s0.wait()
                sbuf[7] = sbuf[6] + sbuf[0]
                s1.start()

            @pl.when(i == 1)
            def _():
                p_x(0)

            @pl.when(lax.rem(i, 3) == 2)
            def _():
                q_sib(0, 1 - i // 3)

            @pl.when(i == 2)
            def _():
                s1.wait()
                sbuf[8] = sbuf[7] + sbuf[1]
                for copy in zs:
                    copy.start()

            @pl.when(i == 3)
            def _():
                loop(4, lambda k: q_y(0, 1, k))

            @pl.when(i == 4)
            def _():
                for copy in zs:
                    copy.wait()
                sbuf[9] = sbuf[8] + sbuf[2] + sbuf[3] + sbuf[4]
                s2.start()

        loop(6, chunk)
        ff_final(0)
        loop(4, lambda i: q_y(0, 0, i))
        loop(3, lambda i: q_z(0, 1, i))
        ff_final(1)
        s2.wait()
        sbuf[6] = sbuf[9] + sbuf[5]
        o_up[...] = sbuf[6, 0:1, pl.ds(pl.multiple_of(m * fw, 128), fw)]
        for n in range(2):
            o_qv[n : n + 1] = sbuf[6, 1:2, pl.ds(pl.multiple_of((3 * m + 2 * n) * lw, 128), lw)]
        dp = lax.axis_index("dp")
        for n, (line, at) in enumerate(((2, 0), (2, 1), (2, 2), (3, 1), (2, 3), (3, 0))):
            row = sbuf[6, line : line + 1, at * width : (at + 1) * width]
            pick = row[:, :part]
            for d in range(1, Z * Y * C):
                pick = jnp.where(dp == d, row[:, d * part : (d + 1) * part], pick)
            o_vec[n : n + 1] = pick
        loop(3, lambda i: q_z(0, 0, i))
        p_final(0)
        q_x(0)
        q_final(0)

        def finish(p):
            for copy in tok_copies(p):
                copy.wait()

        loop(pairs, finish)

        def finish_out(q):
            for copy in out_copies(q):
                copy.wait()

        loop(pairs, finish_out)

    pl.run_scoped(
        attention,
        pltpu.VMEM(w_one_in.shape, LOW), pltpu.VMEM((2, rows, 3 * width), LOW), pltpu.VMEM((2, HEADS, rows, rows), LOW),
        pltpu.VMEM((2, rows, width), LOW), pltpu.VMEM((pairs, rows, width), LOW),
        pltpu.VMEM((high, width), LOW), pltpu.VMEM((width, high), LOW), pltpu.VMEM((high, 3 * width), LOW),
    )


def backward_reduce(counts, tokens, cotangent, hid, n2, att, n1, qkv, prob, w_one, w_two, bias, vec):
    pairs, rows, width = n1.shape
    flat = pairs * rows
    part = width // (Z * Y * C)
    fw = w_two.shape[2] // 2
    hbm = pl.BlockSpec(memory_space=pl.ANY)
    vm = pl.BlockSpec(memory_space=pltpu.VMEM)
    kinds = ((2, fw), (1, width // 2), (1, 3 * width // 2))
    scratch = [pltpu.VMEM((n, Z * Y, C, part, 2 * w), LOW) for n, w in kinds]
    for n, w in kinds:
        scratch += [pltpu.VMEM((n * k, part, w), LOW) for k in (16, 8, 6, 1)]
    scratch += [
        pltpu.VMEM((flat, width), F32), pltpu.VMEM((pairs, rows, width), LOW), pltpu.VMEM((8, width), F32),
        pltpu.VMEM((8, 3 * width), F32), pltpu.VMEM((8, 2 * fw), F32), pltpu.VMEM((10, 8, 2 * fw), F32),
        pltpu.SemaphoreType.DMA((4, BLOCKS)), pltpu.SemaphoreType.DMA((4, BLOCKS)), pltpu.SemaphoreType.DMA((9,)),
        pltpu.SemaphoreType.DMA((3, pairs)), pltpu.SemaphoreType.DMA((3, pairs)), pltpu.SemaphoreType.DMA((2, 6)),
        pltpu.SemaphoreType.DMA((pairs,)),
    ]
    plane = lambda a: a.reshape(-1, width)
    return pl.pallas_call(
        back_kernel,
        in_specs=[pl.BlockSpec(memory_space=pltpu.SMEM)] + [hbm] * 10 + [vm] * 2,
        out_specs=[hbm] * 2 + [vm] * 7,
        out_shape=[
            jax.ShapeDtypeStruct((2 * pairs, rows, width), LOW), jax.ShapeDtypeStruct((2 * pairs, rows, width), LOW),
            jax.ShapeDtypeStruct((part, fw), F32), jax.ShapeDtypeStruct((part, fw), F32),
            jax.ShapeDtypeStruct((1, part, width // 2), F32),
            jax.ShapeDtypeStruct((3, part, width // 2), F32), jax.ShapeDtypeStruct((1, fw), F32),
            jax.ShapeDtypeStruct((2, width // 2), F32), jax.ShapeDtypeStruct((6, part), F32),
        ],
        scratch_shapes=scratch,
        compiler_params=pltpu.CompilerParams(collective_id=1, has_side_effects=True, vmem_limit_bytes=63 * 2**20),
        name="backward_reduce",
    )(counts, plane(cotangent), plane(hid), plane(n2), plane(att), n1, qkv, prob, tokens, w_one, w_two, bias, vec)


def per_device(
    patch_counts, tokens, cotangent, attn_gain, attn_shift, w_qkv, b_qv, w_proj, b_proj,
    ffn_gain, ffn_shift, w_up, b_up, w_down, b_down,
):
    pairs_all, rows, width = tokens.shape
    n_mp = lax.axis_size("mp")
    n_dp = lax.axis_size("dp")
    pairs = pairs_all // n_mp
    direct = n_dp == Z * Y * C and n_mp == 2 and pairs == 4
    part = w_qkv.shape[0]
    lw = w_qkv.shape[2]
    fw = w_up.shape[1]
    mine = lax.axis_index("mp")
    vectors = [attn_gain, attn_shift, b_proj, ffn_gain, ffn_shift, b_down]
    if direct:
        w_one, w_two, bias, qkv, att, prob, hid, n1, n2, vec = gather_attention(
            patch_counts, tokens, w_qkv, w_proj, w_up, w_down, b_qv, b_up, vectors)
        block_out, tokens_grad, r_down, r_up, r_proj, r_qkv, o_b_up, o_b_qv, o_vec = backward_reduce(
            patch_counts, tokens, cotangent, hid, n2, att, n1, qkv, prob, w_one, w_two, bias, vec)
        o_gain, o_shift, o_b_proj, o_b_down, o_ffn_gain, o_ffn_shift = [o_vec[i] for i in range(6)]
        return (
            block_out, tokens_grad, o_gain, o_shift, r_qkv.transpose(1, 0, 2), o_b_qv,
            r_proj[0].T, o_b_proj, o_ffn_gain, o_ffn_shift, r_up, o_b_up[0], r_down.T, o_b_down,
        )

    off = jnp.reshape(mine * pairs, (1,)).astype(jnp.int32)
    lens = TEXT + lax.dynamic_slice_in_dim(patch_counts, mine * pairs, pairs, 0)
    first = jnp.concatenate(
        [w_qkv.reshape(part, 3 * lw), w_proj.T, jnp.stack(vectors, axis=1), jnp.zeros((part, EXTRA - 6), F32)], axis=1
    ).astype(LOW)
    second = jnp.concatenate([w_up, w_down.T], axis=1).astype(LOW)
    bias = jnp.concatenate([b_qv.reshape(-1), b_up]).astype(LOW).astype(F32)
    bias = jnp.broadcast_to(bias, (8,) + bias.shape)
    both_axes = ("mp", "dp")
    w_one = lax.all_gather(first, both_axes, axis=0, tiled=True).reshape(n_mp, width, -1)
    w_two = lax.all_gather(second, both_axes, axis=0, tiled=True).reshape(n_mp, width, -1)
    bias = lax.all_gather(bias, "mp", axis=0)
    qkv, att, prob, hid, n1, n2, vec = attention_forward(lens, off, tokens, w_one, bias)

    def grad(left, right):
        return jnp.einsum(
            "rd,rf->df", left.reshape(pairs * rows, width), right.reshape(pairs * rows, -1),
            preferred_element_type=F32,
        )

    def reduce(grads, small):
        axes = ("mp", "dp")
        done = [
            lax.psum_scatter(
                g.reshape(width, n_mp, -1).swapaxes(0, 1).reshape(n_mp * width, -1), axes,
                scatter_dimension=0, tiled=True,
            )
            for g in grads
        ]
        return done + [lax.psum(small, axes)]

    def both(array):
        other = lax.ppermute(array, "mp", [(0, 1), (1, 0)])
        return jnp.where(mine == 0, jnp.concatenate([array, other]), jnp.concatenate([other, array]))

    out_here, act, dpre, dhid, dlow, upl, sums_two, bsum_up = ffn(lens, off, n2, hid, cotangent, w_two, bias, vec)
    block_out = both(out_here)
    tok_here, dqkv, sums_one, bsum_qkv = attention_backward(lens, off, tokens, dhid, qkv, prob, w_one, vec)
    tokens_grad = both(tok_here)
    flat = bsum_qkv[0].reshape(n_mp, 3, lw)
    small = jnp.concatenate([
        sums_one[0], sums_one[1], sums_two[2], sums_two[0], sums_two[1], sums_two[3],
        flat[:, 0].reshape(-1), flat[:, 2].reshape(-1), bsum_up[0]])
    r_up, r_down, r_proj, r_qkv, small = reduce(
        [grad(n2, dpre), grad(upl, act), grad(dlow, att), grad(n1, dqkv)], small)
    place_dp = lax.axis_index("dp") * part

    def piece(i):
        return lax.dynamic_slice_in_dim(small, i * width + place_dp, part, 0)

    rest = small[6 * width :]
    o_b_q = lax.dynamic_slice_in_dim(rest, mine * lw, lw, 0)
    o_b_v = lax.dynamic_slice_in_dim(rest, (n_mp + mine) * lw, lw, 0)
    o_b_up = lax.dynamic_slice_in_dim(rest, 2 * n_mp * lw + mine * fw, fw, 0)
    return (
        block_out, tokens_grad, piece(0), piece(1),
        r_qkv.reshape(part, 3, lw), jnp.stack([o_b_q, o_b_v]),
        r_proj.T, piece(2), piece(3), piece(4), r_up, o_b_up, r_down.T, piece(5),
    )


def solution(mesh):
    vec, mat = P("dp"), P("dp", "mp")
    tok = P("dp", None, None)
    in_specs = (
        vec, tok, tok, vec, vec, P("dp", None, "mp"), P(None, "mp"), P("mp", "dp"), vec, vec, vec,
        mat, P("mp"), P("mp", "dp"), vec,
    )
    out_specs = (
        tok, tok, vec, vec, P("dp", None, "mp"), P(None, "mp"), P("mp", "dp"), vec, vec, vec,
        mat, P("mp"), P("mp", "dp"), vec,
    )
    return jax.shard_map(per_device, mesh=mesh, in_specs=in_specs, out_specs=out_specs, check_vma=False)
```

```python
import functools

import jax
import jax.numpy as jnp
from jax import lax
from jax.experimental import pallas as pl
from jax.experimental.pallas import tpu as pltpu
from jax.sharding import PartitionSpec as P

HEADS = 12
HEAD_DIM = 64
TEXT = 40
LOW = jnp.bfloat16
F32 = jnp.float32
EXTRA = 128
NT = (((1,), (1,)), ((), ()))
NN = (((1,), (0,)), ((), ()))


def dot(a, b, dims=NN):
    return lax.dot_general(a, b, dims, preferred_element_type=F32)


def moments(v):
    center = v - jnp.mean(v, axis=-1, keepdims=True)
    spread = jnp.mean(center * center, axis=-1, keepdims=True)
    r = lax.rsqrt(spread + 1e-06)
    return center * r, r


def row_ids(rows):
    return lax.broadcasted_iota(jnp.int32, (rows, 1), 0)


def attn_body(p, count, x, w_ref, bias_ref, vec_ref, qkv_ref, att_ref, prob_ref, hid_ref, n1_ref, n2_ref, hook):
    rows, width = x.shape
    groups = w_ref.shape[0]
    lw = width // groups
    tiles = lw // 128
    x = x.astype(F32)
    xhat, _ = moments(x)
    n1 = (xhat * vec_ref[0:1] + vec_ref[1:2]).astype(LOW)
    n1_ref[0] = n1
    for m in range(groups):
        y = dot(n1, w_ref[m, :, : 3 * lw])
        base = m * 3 * lw
        qkv_ref[0, :, base : base + lw] = (y[:, :lw] + bias_ref[m, 0:1, :lw]).astype(LOW)
        qkv_ref[0, :, base + lw : base + 2 * lw] = y[:, lw : 2 * lw].astype(LOW)
        qkv_ref[0, :, base + 2 * lw : base + 3 * lw] = (
            y[:, 2 * lw :] + bias_ref[m, 0:1, lw : 2 * lw]
        ).astype(LOW)
    keep = row_ids(rows) < count
    first = lax.broadcasted_iota(jnp.int32, (1, 128), 1) < HEAD_DIM

    def pair(hp, carry):
        base = (hp // tiles) * 3 * lw + lax.rem(hp, tiles) * 128

        def cols(t):
            return pl.ds(pl.multiple_of(base + t * lw, 128), 128)

        q2 = qkv_ref[0, :, cols(0)] * 0.125
        k2 = qkv_ref[0, :, cols(1)]
        v2t = qkv_ref[0, :, cols(2)].T
        outs = []
        for h in range(2):
            qh = jnp.where(first if h == 0 else ~first, q2, 0)
            st = dot(k2, qh, NT)
            st = jnp.where(keep, st, -1e30)
            e = jnp.exp(st - jnp.max(st, axis=0, keepdims=True))
            pt = (e * (1.0 / jnp.sum(e, axis=0, keepdims=True))).astype(LOW)
            prob_ref[0, hp * 2 + h] = pt
            outs.append(dot(v2t[h * HEAD_DIM : (h + 1) * HEAD_DIM], pt))
        att_ref[0, :, pl.ds(pl.multiple_of(hp * 128, 128), 128)] = jnp.concatenate(outs, axis=0).T.astype(LOW)
        hook(hp)
        return carry

    lax.fori_loop(0, groups * tiles, pair, 0)
    proj = sum(dot(att_ref[0, :, m * lw : (m + 1) * lw], w_ref[m, :, 3 * lw : 4 * lw], NT) for m in range(groups))
    hid = x + proj + vec_ref[2:3]
    hid_ref[0] = hid
    xhat2, _ = moments(hid)
    n2_ref[0] = (xhat2 * vec_ref[3:4] + vec_ref[4:5]).astype(LOW)


def attn_kernel(lens, off, x_ref, w_ref, bias_ref, qkv_ref, att_ref, prob_ref, hid_ref, n1_ref, n2_ref, vec_ref):
    p = pl.program_id(0)
    lw = x_ref.shape[2] // w_ref.shape[0]

    @pl.when(p == 0)
    def _():
        vec_ref[...] = w_ref[0, :, 4 * lw :].astype(F32).T[:8]

    attn_body(p, lens[p], x_ref[0], w_ref, bias_ref, vec_ref, qkv_ref, att_ref, prob_ref, hid_ref, n1_ref, n2_ref,
              lambda hp: None)


def const_spec(shape):
    return pl.BlockSpec(shape, lambda *_: (0,) * len(shape), pipeline_mode=pl.Buffered(1))


def pair_spec(*shape):
    return pl.BlockSpec((1,) + shape, lambda p, *_: (p,) + (0,) * len(shape))


def attention_forward(lens, off, tokens, w_one, bias):
    pairs = lens.shape[0]
    _, rows, width = tokens.shape
    out = lambda dt, *s: jax.ShapeDtypeStruct((pairs,) + s, dt)
    return pl.pallas_call(
        attn_kernel,
        grid_spec=pltpu.PrefetchScalarGridSpec(
            num_scalar_prefetch=2,
            grid=(pairs,),
            in_specs=[
                pl.BlockSpec((1, rows, width), lambda p, lens, off: (off[0] + p, 0, 0)),
                const_spec(w_one.shape),
                const_spec(bias.shape),
            ],
            out_specs=[
                pair_spec(rows, 3 * width), pair_spec(rows, width), pair_spec(HEADS, rows, rows),
                pair_spec(rows, width), pair_spec(rows, width), pair_spec(rows, width),
                pl.BlockSpec((8, width), lambda *_: (0, 0)),
            ],
        ),
        out_shape=[
            out(LOW, rows, 3 * width), out(LOW, rows, width), out(LOW, HEADS, rows, rows),
            out(F32, rows, width), out(LOW, rows, width), out(LOW, rows, width),
            jax.ShapeDtypeStruct((8, width), F32),
        ],
        compiler_params=pltpu.CompilerParams(vmem_limit_bytes=60 * 2**20),
        name="attention_forward",
    )(lens, off, tokens, w_one, bias)


def ffn_kernel(lens, off, n2_ref, hid_ref, cot_ref, w_ref, bias_ref, vec_ref,
               out_ref, act_ref, dpre_ref, dhid_ref, dlow_ref, upl_ref, sums_ref, bsum_ref):
    p = pl.program_id(0)
    rows, width = n2_ref.shape[1], n2_ref.shape[2]
    groups = w_ref.shape[0]
    fw = w_ref.shape[2] // 2
    lw = width // groups
    step = 512
    keep = row_ids(rows) < lens[p]
    n2 = n2_ref[0]
    upl = jnp.where(keep, cot_ref[0], 0)
    upl_ref[0] = upl

    @pl.when(p == 0)
    def _():
        sums_ref[...] = jnp.zeros_like(sums_ref)
        bsum_ref[...] = jnp.zeros_like(bsum_ref)

    for m in range(groups):
        for c in range(0, fw, step):
            pre = dot(n2, w_ref[m, :, c : c + step]) + bias_ref[m, 0:1, 2 * lw + c : 2 * lw + c + step]
            cdf = 0.5 * (1.0 + lax.erf(pre * (2.0 ** -0.5)))
            at = m * fw + c
            act_ref[0, :, at : at + step] = (pre * cdf).astype(LOW)
            slope = cdf + pre * (0.3989422804014327 * jnp.exp(-0.5 * pre * pre))
            dpre = slope * dot(upl, w_ref[m, :, fw + c : fw + c + step])
            dpre_ref[0, :, at : at + step] = dpre.astype(LOW)
            bsum_ref[0:1, at : at + step] += jnp.sum(dpre, axis=0, keepdims=True)
    hid = hid_ref[0]
    down = sum(dot(act_ref[0, :, m * fw : (m + 1) * fw], w_ref[m, :, fw:], NT) for m in range(groups))
    out_ref[0] = jnp.where(keep, hid + down + vec_ref[5:6], 0.0).astype(LOW)
    dtwo = sum(dot(dpre_ref[0, :, m * fw : (m + 1) * fw], w_ref[m, :, :fw], NT) for m in range(groups))
    xhat, r = moments(hid)
    dg = dtwo * vec_ref[3:4]
    dn = r * (dg - jnp.mean(dg, axis=-1, keepdims=True) - xhat * jnp.mean(dg * xhat, axis=-1, keepdims=True))
    upf = upl.astype(F32)
    dhid = upf + dn
    dhid_ref[0] = dhid
    dlow_ref[0] = dhid.astype(LOW)
    sums_ref[0:1] += jnp.sum(dtwo * xhat, axis=0, keepdims=True)
    sums_ref[1:2] += jnp.sum(dtwo, axis=0, keepdims=True)
    sums_ref[2:3] += jnp.sum(dhid, axis=0, keepdims=True)
    sums_ref[3:4] += jnp.sum(upf, axis=0, keepdims=True)


def ffn(lens, off, n2, hid, cotangent, w_two, bias, vec):
    pairs, rows, width = n2.shape
    ff = w_two.shape[0] * w_two.shape[2] // 2
    out = lambda dt, *s: jax.ShapeDtypeStruct((pairs,) + s, dt)
    return pl.pallas_call(
        ffn_kernel,
        grid_spec=pltpu.PrefetchScalarGridSpec(
            num_scalar_prefetch=2,
            grid=(pairs,),
            in_specs=[
                pair_spec(rows, width), pair_spec(rows, width),
                pl.BlockSpec((1, rows, width), lambda p, lens, off: (off[0] + p, 0, 0)),
                const_spec(w_two.shape), const_spec(bias.shape), const_spec(vec.shape),
            ],
            out_specs=[
                pair_spec(rows, width), pair_spec(rows, ff), pair_spec(rows, ff), pair_spec(rows, width),
                pair_spec(rows, width), pair_spec(rows, width),
                pl.BlockSpec((8, width), lambda *_: (0, 0)), pl.BlockSpec((8, ff), lambda *_: (0, 0)),
            ],
        ),
        out_shape=[
            out(LOW, rows, width), out(LOW, rows, ff), out(LOW, rows, ff), out(F32, rows, width),
            out(LOW, rows, width), out(LOW, rows, width),
            jax.ShapeDtypeStruct((8, width), F32), jax.ShapeDtypeStruct((8, ff), F32),
        ],
        compiler_params=pltpu.CompilerParams(vmem_limit_bytes=60 * 2**20),
        name="feed_forward",
    )(lens, off, n2, hid, cotangent, w_two, bias, vec)


def plain_back_kernel(lens, off, x_ref, dhid_ref, qkv_ref, prob_ref, w_ref, vec_ref,
                tok_ref, dqkv_ref, sums_ref, bsum_ref, do_ref):
    p = pl.program_id(0)
    rows, width = x_ref.shape[1], x_ref.shape[2]
    groups = w_ref.shape[0]
    lw = width // groups
    tiles = lw // 128

    @pl.when(p == 0)
    def _():
        sums_ref[...] = jnp.zeros_like(sums_ref)
        bsum_ref[...] = jnp.zeros_like(bsum_ref)

    dhid = dhid_ref[0]
    dlow = dhid.astype(LOW)
    for m in range(groups):
        do_ref[:, m * lw : (m + 1) * lw] = dot(dlow, w_ref[m, :, 3 * lw : 4 * lw]).astype(LOW)
    first = lax.broadcasted_iota(jnp.int32, (1, 128), 1) < HEAD_DIM

    def pair(hp, carry):
        base = (hp // tiles) * 3 * lw + (hp % tiles) * 128

        def cols(t):
            return pl.ds(pl.multiple_of(base + t * lw, 128), 128)

        q2 = qkv_ref[0, :, cols(0)] * 0.125
        k2t = qkv_ref[0, :, cols(1)].T
        v2 = qkv_ref[0, :, cols(2)]
        do2 = do_ref[:, pl.ds(pl.multiple_of(hp * 128, 128), 128)]
        dq_t = []
        dk = dv = 0.0
        for h in range(2):
            mine = first if h == 0 else ~first
            doh = jnp.where(mine, do2, 0)
            qh = jnp.where(mine, q2, 0)
            dpt = dot(v2, doh, NT)
            plow = prob_ref[0, hp * 2 + h]
            pt = plow.astype(F32)
            inner = jnp.sum(pt * dpt, axis=0, keepdims=True)
            dst = (pt * (dpt - inner)).astype(LOW)
            dv = dv + dot(plow, doh)
            dk = dk + dot(dst, qh)
            dq_t.append(dot(k2t[h * HEAD_DIM : (h + 1) * HEAD_DIM], dst))
        dq = (jnp.concatenate(dq_t, axis=0) * 0.125).T
        dqkv_ref[0, :, cols(0)] = dq.astype(LOW)
        dqkv_ref[0, :, cols(1)] = dk.astype(LOW)
        dqkv_ref[0, :, cols(2)] = dv.astype(LOW)
        bsum_ref[0:1, cols(0)] += jnp.sum(dq, axis=0, keepdims=True)
        bsum_ref[0:1, cols(2)] += jnp.sum(dv, axis=0, keepdims=True)
        return carry

    lax.fori_loop(0, groups * tiles, pair, 0)
    done = sum(dot(dqkv_ref[0, :, m * 3 * lw : (m + 1) * 3 * lw], w_ref[m, :, : 3 * lw], NT) for m in range(groups))
    xhat, r = moments(x_ref[0].astype(F32))
    dg = done * vec_ref[0:1]
    dn = r * (dg - jnp.mean(dg, axis=-1, keepdims=True) - xhat * jnp.mean(dg * xhat, axis=-1, keepdims=True))
    tok_ref[0] = (dhid + dn).astype(LOW)
    sums_ref[0:1] += jnp.sum(done * xhat, axis=0, keepdims=True)
    sums_ref[1:2] += jnp.sum(done, axis=0, keepdims=True)


def attention_backward(lens, off, tokens, dhid, qkv, prob, w_one, vec):
    pairs, rows, width = dhid.shape
    out = lambda dt, *s: jax.ShapeDtypeStruct((pairs,) + s, dt)
    return pl.pallas_call(
        plain_back_kernel,
        grid_spec=pltpu.PrefetchScalarGridSpec(
            num_scalar_prefetch=2,
            grid=(pairs,),
            in_specs=[
                pl.BlockSpec((1, rows, width), lambda p, lens, off: (off[0] + p, 0, 0)),
                pair_spec(rows, width), pair_spec(rows, 3 * width), pair_spec(HEADS, rows, rows),
                const_spec(w_one.shape), const_spec(vec.shape),
            ],
            out_specs=[
                pair_spec(rows, width), pair_spec(rows, 3 * width),
                pl.BlockSpec((8, width), lambda *_: (0, 0)), pl.BlockSpec((8, 3 * width), lambda *_: (0, 0)),
            ],
            scratch_shapes=[pltpu.VMEM((rows, width), LOW)],
        ),
        out_shape=[
            out(LOW, rows, width), out(LOW, rows, 3 * width),
            jax.ShapeDtypeStruct((8, width), F32), jax.ShapeDtypeStruct((8, 3 * width), F32),
        ],
        compiler_params=pltpu.CompilerParams(vmem_limit_bytes=60 * 2**20),
        name="attention_backward",
    )(lens, off, tokens, dhid, qkv, prob, w_one, vec)
MESH_ID = pl.DeviceIdType.MESH
Z, Y, C = 4, 2, 2


def place():
    dp = lax.axis_index("dp")
    m = lax.axis_index("mp")
    c = lax.rem(dp, 2)
    y = lax.rem(dp // 2, 2)
    z = dp // 4
    return z, y, c, m


def index(z, y, c):
    return (z * Y + y) * C + c


def flips(y, c, m):
    one = (y + c * (1 - 2 * y), m + (1 - c) * (1 - 2 * m))
    two = (y + (1 - c) * (1 - 2 * y), m + c * (1 - 2 * m))
    return one, two


def greet(z, y, c, m):
    barrier = pltpu.get_barrier_semaphore()
    (y1, m1), (y2, m2) = flips(y, c, m)
    peers = [(index(lax.rem(z + k, Z), y, c), m) for k in (1, 2, 3)]
    peers += [(index(z, y1, c), m1), (index(z, y2, c), m2), (index(z, y, 1 - c), m)]
    for dp, mp in peers:
        pl.semaphore_signal(barrier, inc=1, device_id={"dp": dp, "mp": mp}, device_id_type=MESH_ID)
    pl.semaphore_wait(barrier, len(peers))
    return peers


def gather_attn_kernel(counts, tok_all, wq_in, wp_in, wu_in, wd_in, bq_in, bu_in, v0, v1, v2, v3, v4, v5,
                       w_one_out, w_two, b_out, qkv_ref, att_ref, prob_ref, hid_ref, n1_ref, n2_ref, vec_ref,
                       w_one, bias, xbuf, first_ref, second_ref, b_in, vbuf, send, recv, bsem, local):
    p = pl.program_id(0)
    z, y, c, m = place()
    (y1, m1), (y2, m2) = flips(y, c, m)
    pairs, rows, width = xbuf.shape
    part = first_ref.shape[0]
    cols = second_ref.shape[1] // 2
    lw = width // 2
    per_pair = width // 128
    me = index(z, y, c)
    one, two, sib = (index(z, y1, c), m1), (index(z, y2, c), m2), (index(z, y, 1 - c), m)

    def spot(g, dp, mp):
        at = pl.ds(pl.multiple_of(dp * part, part), part)
        if g is None:
            return w_one.at[mp, at]
        return w_two.at[mp, at, pl.ds(pl.multiple_of(g * cols, 128), cols)]

    def shard(g):
        return first_ref if g is None else second_ref.at[:, pl.ds(pl.multiple_of(g * cols, 128), cols)]

    def row(g):
        return 0 if g is None else g + 1

    def copy_of(g, src, dst, out_sem, in_sem, to):
        return pltpu.make_async_remote_copy(
            src_ref=src, dst_ref=dst, send_sem=send.at[row(g), out_sem], recv_sem=recv.at[row(g), in_sem],
            device_id={"dp": to[0], "mp": to[1]}, device_id_type=MESH_ID,
        )

    def push(g, src, dp, mp, to, sem):
        copy_of(g, src, spot(g, dp, mp), sem, mp * (Z * Y * C) + dp, to).start()

    def arrived(g, dp, mp):
        at = spot(g, dp, mp)
        copy_of(g, at, at, 0, mp * (Z * Y * C) + dp, sib).wait_recv()
        return at

    def own_z(g):
        for k in (1, 3, 2):
            push(g, shard(g), me, m, (index(lax.rem(z + k, Z), y, c), m), k - 1)

    def own_near(g):
        for n, to in enumerate((one, two, sib)):
            push(g, shard(g), me, m, to, 3 + n)

    def event_z(g, i):
        dp = index(lax.rem(z + 1 + lax.rem(2 * i, 3), Z), y, c)
        at = arrived(g, dp, m)
        for n, to in enumerate((one, two, sib)):
            push(g, at, dp, m, to, 6 + 3 * i + n)

    def event_one(g, i):
        dp = index(lax.rem(z + i, Z), y1, c)
        at = arrived(g, dp, m1)
        for n, to in enumerate((two, sib)):
            push(g, at, dp, m1, to, 15 + 2 * i + n)

    def event_two(g, i):
        far = lax.rem(i, 2)
        yy = y2 + far * (1 - y - y2)
        mm = m2 + far * (1 - m - m2)
        dp = index(lax.rem(z + i // 2, Z), yy, c)
        push(g, arrived(g, dp, mm), dp, mm, sib, 23 + i)

    def event_core(g, i):
        arrived(g, index(i // 4, lax.rem(i // 2, 2), 1 - c), lax.rem(i, 2))

    def loop(n, event, g):
        def run(i, carry):
            event(g, i)
            return carry

        lax.fori_loop(0, n, run, 0)

    bias_copy = pltpu.make_async_remote_copy(
        src_ref=b_in, dst_ref=bias.at[m], send_sem=bsem.at[0], recv_sem=bsem.at[1],
        device_id={"dp": me, "mp": 1 - m}, device_id_type=MESH_ID,
    )
    x_copy = pltpu.make_async_copy(tok_all.at[pl.ds(m * pairs, pairs)], xbuf, local.at[0])
    mine = [
        pltpu.make_async_copy(b_in, bias.at[m], local.at[1]),
        pltpu.make_async_copy(first_ref, spot(None, me, m), local.at[2]),
    ]
    mine_two = [pltpu.make_async_copy(shard(g), spot(g, me, m), local.at[3 + g]) for g in range(2)]
    keep_one = pltpu.make_async_copy(w_one, w_one_out, local.at[5])
    keep_bias = pltpu.make_async_copy(bias, b_out, local.at[6])

    @pl.when(p == 0)
    def _():
        x_copy.start()
        for t in range(3):
            first_ref[:, t * lw : (t + 1) * lw] = wq_in[t].astype(LOW)
        first_ref[:, 3 * lw : 4 * lw] = wp_in[...].astype(LOW)
        vbuf[...] = jnp.zeros_like(vbuf)
        for n, v in enumerate((v0, v1, v2, v3, v4, v5)):
            vbuf[n : n + 1, :part] = v[...]
        first_ref[:, 4 * lw :] = vbuf[...].T[:part].astype(LOW)
        second_ref[:, :cols] = wu_in[...].astype(LOW)
        second_ref[:, cols:] = wd_in[...].astype(LOW)
        b_in[...] = jnp.zeros_like(b_in)
        b_in[0:1, :lw] = bq_in[0:1].astype(LOW).astype(F32)
        b_in[0:1, lw : 2 * lw] = bq_in[1:2].astype(LOW).astype(F32)
        b_in[0:1, 2 * lw :] = bu_in[...].reshape(1, cols).astype(LOW).astype(F32)
        greet(z, y, c, m)
        own_z(None)
        own_near(None)
        bias_copy.start()
        for copy in mine + mine_two:
            copy.start()
        loop(3, event_z, None)
        own_z(0)
        own_z(1)
        loop(4, event_one, None)
        own_near(0)
        loop(3, event_z, 0)
        loop(8, event_two, None)
        for copy in mine + [x_copy, bias_copy]:
            copy.wait()
        loop(16, event_core, None)
        keep_one.start()
        keep_bias.start()
        vec_ref[...] = w_one[0, :, 4 * lw :].astype(F32).T[:8]

    def hook(hp):
        step = p * per_pair + hp

        def event(e, carry):
            @pl.when(e == 0)
            def _():
                own_near(1)

            @pl.when(((e >= 1) & (e < 5)) | ((e >= 16) & (e < 20)))
            def _():
                g = e // 16
                event_one(g, e - 1 - 15 * g)

            @pl.when((e >= 5) & (e < 8))
            def _():
                event_z(1, e - 5)

            @pl.when(((e >= 8) & (e < 16)) | (e >= 20))
            def _():
                g = e // 20
                event_two(g, e - 8 - 12 * g)

            return carry

        total = pairs * per_pair
        lax.fori_loop(step * 28 // total, (step + 1) * 28 // total, event, 0)

    attn_body(p, TEXT + counts[m * pairs + p], xbuf[p], w_one, bias, vec_ref, qkv_ref, att_ref, prob_ref, hid_ref, n1_ref, n2_ref, hook)

    @pl.when(p == pairs - 1)
    def _():
        for g in range(2):
            loop(16, event_core, g)
        for copy in mine_two + [keep_one, keep_bias]:
            copy.wait()
        for g in (None, 0, 1):
            def sent(i, carry):
                copy_of(g, shard(g), shard(g), i, 0, sib).wait_send()
                return carry

            lax.fori_loop(0, 31, sent, 0)


def gather_attention(counts, tokens, w_qkv, w_proj, w_up, w_down, b_qv, b_up, vectors):
    pairs = counts.shape[0] // 2
    _, rows, width = tokens.shape
    part, fw = w_up.shape
    lw = width // 2
    total = Z * Y * C
    hbm = pl.BlockSpec(memory_space=pl.ANY)
    out = lambda dt, *s: jax.ShapeDtypeStruct((pairs,) + s, dt)
    small = [w_qkv.transpose(1, 0, 2), w_proj.T, w_up, w_down.T, b_qv, b_up]
    small += [v.reshape(1, part) for v in vectors]
    one, two, bias = 4 * lw + EXTRA, 2 * fw, (8, 2 * lw + fw)
    return pl.pallas_call(
        gather_attn_kernel,
        grid_spec=pltpu.PrefetchScalarGridSpec(
            num_scalar_prefetch=1,
            grid=(pairs,),
            in_specs=[hbm] + [const_spec(a.shape) for a in small],
            out_specs=[
                hbm, hbm, hbm,
                pair_spec(rows, 3 * width), pair_spec(rows, width), pair_spec(HEADS, rows, rows),
                pair_spec(rows, width), pair_spec(rows, width), pair_spec(rows, width),
                pl.BlockSpec((8, width), lambda *_: (0, 0)),
            ],
            scratch_shapes=[
                pltpu.VMEM((2, width, one), LOW), pltpu.VMEM((2,) + bias, F32), pltpu.VMEM((pairs, rows, width), LOW),
                pltpu.VMEM((part, one), LOW), pltpu.VMEM((part, two), LOW), pltpu.VMEM(bias, F32),
                pltpu.VMEM((EXTRA, EXTRA), F32),
                pltpu.SemaphoreType.DMA((3, 31)), pltpu.SemaphoreType.DMA((3, 32)),
                pltpu.SemaphoreType.DMA((2,)), pltpu.SemaphoreType.DMA((7,)),
            ],
        ),
        out_shape=[
            jax.ShapeDtypeStruct((2, width, one), LOW),
            jax.ShapeDtypeStruct((2, width, two), LOW),
            jax.ShapeDtypeStruct((2,) + bias, F32),
            out(LOW, rows, 3 * width), out(LOW, rows, width), out(LOW, HEADS, rows, rows),
            out(F32, rows, width), out(LOW, rows, width), out(LOW, rows, width),
            jax.ShapeDtypeStruct((8, width), F32),
        ],
        compiler_params=pltpu.CompilerParams(collective_id=0, has_side_effects=True, vmem_limit_bytes=60 * 2**20),
        name="gather_attention",
    )(counts, tokens, *small)


BLOCKS = 31


def back_kernel(counts, cot, hid_in, n2_in, att_in, n1_all, qkv_all, prob_all, tok_all, w_one_in, w_two, bias_ref, vec_ref,
                block_out, tok_out, r_down, r_up, r_proj, r_qkv, o_up, o_qv, o_vec,
                g_ff, g_proj, g_qkv, rc_ff, rs_ff, rz_ff, rx_ff, rc_p, rs_p, rz_p, rx_p, rc_q, rs_q, rz_q, rx_q,
                dhid_ref, outbuf, sums, bsum, bsum_up, sbuf, send, recv, local, osem, tsem, ssem, n1_sem):
    flat, width = dhid_ref.shape
    pairs, rows = qkv_all.shape[0], qkv_all.shape[1]
    groups = w_two.shape[0]
    fw = w_two.shape[2] // 2
    fc = fw // 3
    lw = width // groups
    tiles = lw // 128
    half = flat // 2
    part = r_proj.shape[1]
    high = pairs * (rows + (-rows) % 16)
    z, y, c, m = place()
    me = index(z, y, c)
    sib = (index(z, y, 1 - c), m)

    def beside(k):
        return (index(lax.rem(z + k, Z), y, c), m)

    def loop(n, event):
        def one(i, carry):
            event(i)
            return carry

        lax.fori_loop(0, n, one, 0)

    def family(grad, rc, rs, rz, rx, out, row0, split):
        cols = rc.shape[2]
        fx = c * split
        near = (index(z, y + (1 - fx) * (1 - 2 * y), c), m + fx * (1 - 2 * m))
        far = (index(z, y + fx * (1 - 2 * y), c), m + (1 - fx) * (1 - 2 * m))

        def copy_of(u, src, dst, out_sem, in_sem, to):
            return pltpu.make_async_remote_copy(
                src_ref=src, dst_ref=dst, send_sem=send.at[row0 + u, out_sem], recv_sem=recv.at[row0 + u, in_sem],
                device_id={"dp": to[0], "mp": to[1]}, device_id_type=MESH_ID,
            )

        def swap(ra, rb, cc):
            f = cc * split
            return f * rb + (1 - f) * ra, f * ra + (1 - f) * rb

        def block(u, ra, rb, k, cc):
            dy, dm = swap(ra, rb, cc)
            yy = y + dy * (1 - 2 * y)
            mm = m + dm * (1 - 2 * m)
            return u, lax.rem(z + k, Z) * Y + yy, cc, slice(None), pl.ds(pl.multiple_of(mm * cols, 128), cols)

        def to_sibling(u, dm):
            def one(i):
                ra, rb = swap(1 - i // 4, dm, 1 - c)
                k = lax.rem(i + 1, 4)
                slot = (ra * 2 + rb) * 4 + k
                copy_of(u, grad.at[block(u, ra, rb, k, 1 - c)], rc.at[u * 16 + slot], slot, slot, sib).start()

            loop(8, one)

        def arrived(u, ref, sem):
            copy_of(u, ref, ref, 0, sem, sib).wait_recv()

        def base(u, ra, rb, k):
            slot = (ra * 2 + rb) * 4 + k
            arrived(u, rc.at[u * 16 + slot], slot)
            return grad[block(u, ra, rb, k, c)].astype(F32) + rc[u * 16 + slot].astype(F32)

        def level(u, rb, k):
            at = rb * 4 + k
            value = base(u, 0, rb, k)
            arrived(u, rs.at[u * 8 + at], 16 + at)
            return value + rs[u * 8 + at].astype(F32)

        def lined(u, rb):
            value = level(u, rb, 0)
            for k in (1, 2, 3):
                at = (k - 1) * 2 + rb
                arrived(u, rz.at[u * 6 + at], 24 + at)
                value = value + rz[u * 6 + at].astype(F32)
            return value

        def event_y(u, rb, i):
            k = lax.rem(i + 1, 4)
            slot = u * 16 + (2 + rb) * 4 + k
            at = rb * 4 + k
            rc[slot] = base(u, 1, rb, k).astype(LOW)
            copy_of(u, rc.at[slot], rs.at[u * 8 + at], 16 + at, 16 + at, near).start()

        def event_z(u, rb, i):
            k = 1 + i
            slot = u * 16 + rb * 4 + k
            at = (k - 1) * 2 + rb
            rc[slot] = level(u, rb, k).astype(LOW)
            copy_of(u, rc.at[slot], rz.at[u * 6 + at], 24 + at, 24 + at, beside(k)).start()

        def event_x(u):
            rc[u * 16 + 4] = lined(u, 1).astype(LOW)
            copy_of(u, rc.at[u * 16 + 4], rx.at[u], 30, 30, far).start()

        def final(u):
            value = lined(u, 0)
            arrived(u, rx.at[u], 30)
            out(u, value + rx[u].astype(F32))

            def one(i):
                copy_of(u, rc.at[0], rc.at[0], i, 0, sib).wait_send()

            loop(BLOCKS, one)

        return to_sibling, event_y, event_z, event_x, final

    def put(ref):
        def store(u, value):
            ref[u] = value

        return store

    def put_ff(u, value):
        (r_down, r_up)[u][...] = value

    def put_qkv(u, value):
        for t in range(3):
            r_qkv[t] = value[:, t * lw : (t + 1) * lw]

    ff_sib, ff_y, ff_z, ff_x, ff_final = family(g_ff, rc_ff, rs_ff, rz_ff, rx_ff, put_ff, 0, 0)
    p_sib, p_y, p_z, p_x, p_final = family(g_proj, rc_p, rs_p, rz_p, rx_p, put(r_proj), 2, 0)
    q_sib, q_y, q_z, q_x, q_final = family(g_qkv, rc_q, rs_q, rz_q, rx_q, put_qkv, 3, 1)

    def out_copies(q):
        src = outbuf.at[q]
        dst = block_out.at[m * pairs + q]
        return pltpu.make_async_copy(src, dst, osem.at[0, q]), pltpu.make_async_remote_copy(
            src_ref=src, dst_ref=dst, send_sem=osem.at[1, q], recv_sem=osem.at[2, q],
            device_id={"dp": me, "mp": 1 - m}, device_id_type=MESH_ID,
        )

    def keep_of(r):
        ids = row_ids(half)
        here = m * pairs + 2 * r
        return ids < TEXT + jnp.where(ids < rows, counts[here], counts[here + 1] + rows)

    def span(r):
        return pl.ds(pl.multiple_of(r * half, 16), half)

    sums[...] = jnp.zeros_like(sums)
    bsum[...] = jnp.zeros_like(bsum)
    bsum_up[...] = jnp.zeros_like(bsum_up)

    def feed_forward(n2, n2t, upl, uplt, hid, acc, slope, chunk, wbuf):
        def place_of(f):
            i = lax.rem(f, 6)
            return lax.rem(m + 1 + i // 3, 2), lax.rem(i, 3) * fc

        def weights(f):
            mm, at = place_of(f)
            slot = lax.rem(f, 2)
            return [
                pltpu.make_async_copy(
                    w_two.at[mm, :, pl.ds(pl.multiple_of(t * fw + at, 128), fc)], wbuf.at[slot, t], local.at[slot * 2 + t])
                for t in range(2)
            ]

        n2_copy = pltpu.make_async_copy(n2_in, n2, local.at[4])
        up_copy = pltpu.make_async_copy(cot.at[pl.ds(pl.multiple_of(m * flat, 16), flat)], upl, local.at[5])
        hid_copy = pltpu.make_async_copy(hid_in, hid, local.at[6])
        att_copy = pltpu.make_async_copy(att_in, slope.at[:, pl.ds(0, width)], local.at[7])
        n2_copy.start()
        up_copy.start()
        for copy in weights(0):
            copy.start()
        hid_copy.start()
        greet(z, y, c, m)
        up_copy.wait()

        def prepare(r):
            value = jnp.where(keep_of(r), upl[span(r)], 0)
            upl[span(r)] = value
            sums[3:4] += jnp.sum(value.astype(F32), axis=0, keepdims=True)
            acc[span(r)] = jnp.zeros((half, width), F32)

        loop(2, prepare)
        uplt[...] = upl[...].T
        n2_copy.wait()
        n2t[...] = n2[...].T

        def traffic(f):
            @pl.when(lax.rem(f, 3) == 2)
            def _():
                n = f // 3
                ff_sib(n // 2, 1 - lax.rem(n, 2))

            @pl.when((lax.rem(f, 3) == 0) & (f > 0))
            def _():
                n = f // 3 - 1
                loop(4, lambda i: ff_y(n // 2, 1 - lax.rem(n, 2), i))

            @pl.when((lax.rem(f, 3) == 1) & (f > 4))
            def _():
                n = (f - 7) // 3
                loop(3, lambda i: ff_z(n // 2, 1 - lax.rem(n, 2), i))

        def store(u, at, value):
            g_ff[u, :, :, :, at] = value.astype(LOW).reshape(Z * Y, C, part, fc)

        def forward(f):
            slot = lax.rem(f, 2)
            for copy in weights(f + 1):
                copy.start()
            for copy in weights(f):
                copy.wait()
            mm, off = place_of(f)
            at = pl.ds(pl.multiple_of(mm * fw + off, 128), fc)
            shift = bias_ref[mm, 0:1, pl.ds(pl.multiple_of(2 * lw + off, 128), fc)]

            def block(r):
                pre = dot(n2[span(r)], wbuf[slot, 0]) + shift
                cdf = 0.5 * (1.0 + lax.erf(pre * (2.0 ** -0.5)))
                chunk[span(r)] = (pre * cdf).astype(LOW)
                slope[span(r), at] = (cdf + pre * (0.3989422804014327 * jnp.exp(-0.5 * pre * pre))).astype(LOW)
                acc[span(r)] += dot(chunk[span(r)], wbuf[slot, 1], NT)

            loop(2, block)
            store(0, at, dot(uplt[...], chunk[...]))
            traffic(f)

        loop(6, forward)
        hid_copy.wait()

        def leave(r):
            value = jnp.where(keep_of(r), hid[span(r)] + acc[span(r)] + vec_ref[5:6], 0.0)
            acc[span(r)] = jnp.zeros((half, width), F32)
            for n in range(2):
                outbuf[2 * r + n] = value[n * rows : (n + 1) * rows].astype(LOW)
                for copy in out_copies(2 * r + n):
                    copy.start()

        loop(2, leave)

        def backward(i):
            f = 6 + i
            slot = lax.rem(f, 2)

            @pl.when(f < 11)
            def _():
                for copy in weights(f + 1):
                    copy.start()

            for copy in weights(f):
                copy.wait()
            mm, off = place_of(f)
            at = pl.ds(pl.multiple_of(mm * fw + off, 128), fc)

            def block(r):
                dpre = slope[span(r), at].astype(F32) * dot(upl[span(r)], wbuf[slot, 1])
                chunk[span(r)] = dpre.astype(LOW)
                bsum_up[0:1, at] += jnp.sum(dpre, axis=0, keepdims=True)
                acc[span(r)] += dot(chunk[span(r)], wbuf[slot, 0], NT)

            loop(2, block)
            store(1, at, dot(n2t[...], chunk[...]))
            traffic(f)

        loop(6, backward)
        att_copy.start()

        def norm_back(r):
            dtwo = acc[span(r)]
            xhat, rr = moments(hid[span(r)])
            dg = dtwo * vec_ref[3:4]
            dn = rr * (dg - jnp.mean(dg, axis=-1, keepdims=True) - xhat * jnp.mean(dg * xhat, axis=-1, keepdims=True))
            dhid = upl[span(r)].astype(F32) + dn
            dhid_ref[span(r)] = dhid
            n2[span(r)] = dhid.astype(LOW)
            sums[4:5] += jnp.sum(dtwo * xhat, axis=0, keepdims=True)
            sums[5:6] += jnp.sum(dtwo, axis=0, keepdims=True)
            sums[2:3] += jnp.sum(dhid, axis=0, keepdims=True)

        loop(2, norm_back)
        att_copy.wait()
        n2t[...] = n2[...].T
        for mm in range(groups):
            at = slice(mm * lw, (mm + 1) * lw)
            g_proj[0, :, :, :, at] = dot(n2t[...], slope[:, at]).astype(LOW).reshape(Z * Y, C, part, lw)
        p_sib(0, 1)
        p_sib(0, 0)

    pl.run_scoped(
        feed_forward,
        pltpu.VMEM((flat, width), LOW), pltpu.VMEM((width, flat), LOW),
        pltpu.VMEM((flat, width), LOW), pltpu.VMEM((width, flat), LOW),
        pltpu.VMEM((flat, width), F32), pltpu.VMEM((flat, width), F32),
        pltpu.VMEM((flat, groups * fw), LOW), pltpu.VMEM((flat, fc), LOW), pltpu.VMEM((2, 2, width, fc), LOW),
    )

    def attention(w_ref, qkv_buf, prob_buf, x_buf, do_ref, n1, n1t, dq_all):
        high = n1.shape[0] // pairs
        w_copy = pltpu.make_async_copy(w_one_in, w_ref, local.at[8])

        def loads(p):
            slot = lax.rem(p, 2)
            pieces = [
                (qkv_all.at[p], qkv_buf), (prob_all.at[p], prob_buf), (tok_all.at[m * pairs + p], x_buf),
            ]
            return [
                pltpu.make_async_copy(src, dst.at[slot], local.at[slot * 3 + t])
                for t, (src, dst) in enumerate(pieces)
            ]

        def tok_copies(p):
            src, dst = n1.at[pl.ds(pl.multiple_of(p * high, 16), rows)], tok_out.at[m * pairs + p]
            return pltpu.make_async_copy(src, dst, tsem.at[0, p]), pltpu.make_async_remote_copy(
                src_ref=src, dst_ref=dst, send_sem=tsem.at[1, p], recv_sem=tsem.at[2, p],
                device_id={"dp": me, "mp": 1 - m}, device_id_type=MESH_ID,
            )

        w_copy.start()
        for copy in loads(0):
            copy.start()
        n1_copies = [
            pltpu.make_async_copy(n1_all.at[p], n1.at[pl.ds(p * high, rows)], n1_sem.at[p]) for p in range(pairs)
        ]
        for copy in n1_copies:
            copy.start()
        w_copy.wait()

        def attended_back(r):
            dlow = dhid_ref[span(r)].astype(LOW)
            for mm in range(groups):
                value = dot(dlow, w_ref[mm, :, 3 * lw : 4 * lw])
                for n in range(2):
                    do_ref[2 * r + n, :, mm * lw : (mm + 1) * lw] = value[n * rows : (n + 1) * rows].astype(LOW)

        loop(2, attended_back)
        for p, copy in enumerate(n1_copies):
            copy.wait()
            n1[p * high + rows : (p + 1) * high] = jnp.zeros((high - rows, width), LOW)
            dq_all[p * high + rows : (p + 1) * high] = jnp.zeros((high - rows, 3 * width), LOW)
        n1t[...] = n1[...].T
        first = lax.broadcasted_iota(jnp.int32, (1, 128), 1) < HEAD_DIM

        def one_pair(p):
            slot = lax.rem(p, 2)

            @pl.when(p < pairs - 1)
            def _():
                for copy in loads(p + 1):
                    copy.start()

            dhid = dhid_ref[pl.ds(pl.multiple_of(p * rows, 8), rows)]
            here = pl.ds(pl.multiple_of(p * high, 16), rows)
            for copy in loads(p):
                copy.wait()

            def heads(hp):
                lane = (hp // tiles) * 3 * lw + lax.rem(hp, tiles) * 128

                def cols(t):
                    return pl.ds(pl.multiple_of(lane + t * lw, 128), 128)

                q2 = qkv_buf[slot, :, cols(0)] * 0.125
                k2t = qkv_buf[slot, :, cols(1)].T
                v2 = qkv_buf[slot, :, cols(2)]
                do2 = do_ref[p, :, pl.ds(pl.multiple_of(hp * 128, 128), 128)]
                dq_t = []
                dk = dv = 0.0
                for h in range(2):
                    mine = first if h == 0 else ~first
                    doh = jnp.where(mine, do2, 0)
                    qh = jnp.where(mine, q2, 0)
                    dpt = dot(v2, doh, NT)
                    plow = prob_buf[slot, hp * 2 + h]
                    pt = plow.astype(F32)
                    inner = jnp.sum(pt * dpt, axis=0, keepdims=True)
                    dst = (pt * (dpt - inner)).astype(LOW)
                    dv = dv + dot(plow, doh)
                    dk = dk + dot(dst, qh)
                    dq_t.append(dot(k2t[h * HEAD_DIM : (h + 1) * HEAD_DIM], dst))
                dq = (jnp.concatenate(dq_t, axis=0) * 0.125).T
                dq_all[here, cols(0)] = dq.astype(LOW)
                dq_all[here, cols(1)] = dk.astype(LOW)
                dq_all[here, cols(2)] = dv.astype(LOW)
                bsum[0:1, cols(0)] += jnp.sum(dq, axis=0, keepdims=True)
                bsum[0:1, cols(2)] += jnp.sum(dv, axis=0, keepdims=True)
                step = p * (groups * tiles) + hp

                @pl.when(step == 0)
                def _():
                    loop(4, lambda i: ff_y(1, 0, i))

                @pl.when((step == 2) | (step == 13))
                def _():
                    loop(3, lambda i: ff_z(1, 1 - step // 13, i))

                @pl.when((step >= 3) & (step < 7))
                def _():
                    loop(2, lambda i: p_y(0, 1 - (step - 3) // 2, 2 * lax.rem(step - 3, 2) + i))

                @pl.when((step == 18) | (step == 19))
                def _():
                    loop(3, lambda i: p_z(0, 19 - step, i))

                @pl.when((step == 16) | (step == 21))
                def _():
                    ff_x((step - 16) // 5)

            loop(groups * tiles, heads)
            done = sum(
                dot(dq_all[here, mm * 3 * lw : (mm + 1) * 3 * lw], w_ref[mm, :, : 3 * lw], NT) for mm in range(groups))
            xhat, r = moments(x_buf[slot].astype(F32))
            dg = done * vec_ref[0:1]
            dn = r * (dg - jnp.mean(dg, axis=-1, keepdims=True) - xhat * jnp.mean(dg * xhat, axis=-1, keepdims=True))
            n1[here] = (dhid + dn).astype(LOW)
            for copy in tok_copies(p):
                copy.start()
            sums[0:1] += jnp.sum(done * xhat, axis=0, keepdims=True)
            sums[1:2] += jnp.sum(done, axis=0, keepdims=True)

        loop(pairs, one_pair)

        def small_copy(slot, src, to, sem):
            return pltpu.make_async_remote_copy(
                src_ref=sbuf.at[src], dst_ref=sbuf.at[slot], send_sem=ssem.at[0, sem], recv_sem=ssem.at[1, sem],
                device_id={"dp": to[0], "mp": to[1]}, device_id_type=MESH_ID,
            )

        sbuf[6] = jnp.zeros_like(sbuf[6])
        sbuf[6, 0:1] = bsum_up[0:1]
        sbuf[6, 1:2, : 3 * width] = bsum[0:1]
        for n, (line, at) in enumerate(((2, 0), (2, 1), (2, 2), (3, 1), (2, 3), (3, 0))):
            sbuf[6, line : line + 1, at * width : (at + 1) * width] = sums[n : n + 1]
        s0 = small_copy(0, 6, sib, 0)
        s1 = small_copy(1, 7, (index(z, 1 - y, c), m), 1)
        zs = [small_copy(1 + k, 8, beside(k), 1 + k) for k in (1, 2, 3)]
        s2 = small_copy(5, 9, (me, 1 - m), 5)
        s0.start()

        def chunk(i):
            mm = lax.rem(m + 1 + i // 3, 2)
            at = pl.ds(pl.multiple_of(mm * 3 * lw + lax.rem(i, 3) * lw, 128), lw)
            g_qkv[0, :, :, :, at] = dot(n1t[...], dq_all[:, at]).astype(LOW).reshape(Z * Y, C, part, lw)

            @pl.when(i == 0)
            def _():
                s0.wait()
                sbuf[7] = sbuf[6] + sbuf[0]
                s1.start()

            @pl.when(i == 1)
            def _():
                p_x(0)

            @pl.when(lax.rem(i, 3) == 2)
            def _():
                q_sib(0, 1 - i // 3)

            @pl.when(i == 2)
            def _():
                s1.wait()
                sbuf[8] = sbuf[7] + sbuf[1]
                for copy in zs:
                    copy.start()

            @pl.when(i == 3)
            def _():
                loop(4, lambda k: q_y(0, 1, k))

            @pl.when(i == 4)
            def _():
                for copy in zs:
                    copy.wait()
                sbuf[9] = sbuf[8] + sbuf[2] + sbuf[3] + sbuf[4]
                s2.start()

        loop(6, chunk)
        ff_final(0)
        loop(4, lambda i: q_y(0, 0, i))
        loop(3, lambda i: q_z(0, 1, i))
        ff_final(1)
        s2.wait()
        sbuf[6] = sbuf[9] + sbuf[5]
        o_up[...] = sbuf[6, 0:1, pl.ds(pl.multiple_of(m * fw, 128), fw)].reshape(fw)
        for n in range(2):
            o_qv[n : n + 1] = sbuf[6, 1:2, pl.ds(pl.multiple_of((3 * m + 2 * n) * lw, 128), lw)]
        dp = lax.axis_index("dp")
        for n, (line, at) in enumerate(((2, 0), (2, 1), (2, 2), (3, 1), (2, 3), (3, 0))):
            row = sbuf[6, line : line + 1, at * width : (at + 1) * width]
            pick = row[:, :part]
            for d in range(1, Z * Y * C):
                pick = jnp.where(dp == d, row[:, d * part : (d + 1) * part], pick)
            o_vec[n : n + 1] = pick
        loop(3, lambda i: q_z(0, 0, i))
        p_final(0)
        q_x(0)
        q_final(0)

        def finish(p):
            for copy in tok_copies(p):
                copy.wait()

        loop(pairs, finish)

        def finish_out(q):
            for copy in out_copies(q):
                copy.wait()

        loop(pairs, finish_out)

    pl.run_scoped(
        attention,
        pltpu.VMEM(w_one_in.shape, LOW), pltpu.VMEM((2, rows, 3 * width), LOW), pltpu.VMEM((2, HEADS, rows, rows), LOW),
        pltpu.VMEM((2, rows, width), LOW), pltpu.VMEM((pairs, rows, width), LOW),
        pltpu.VMEM((high, width), LOW), pltpu.VMEM((width, high), LOW), pltpu.VMEM((high, 3 * width), LOW),
    )


def backward_reduce(counts, tokens, cotangent, hid, n2, att, n1, qkv, prob, w_one, w_two, bias, vec):
    pairs, rows, width = n1.shape
    flat = pairs * rows
    part = width // (Z * Y * C)
    fw = w_two.shape[2] // 2
    hbm = pl.BlockSpec(memory_space=pl.ANY)
    vm = pl.BlockSpec(memory_space=pltpu.VMEM)
    kinds = ((2, fw), (1, width // 2), (1, 3 * width // 2))
    scratch = [pltpu.VMEM((n, Z * Y, C, part, 2 * w), LOW) for n, w in kinds]
    for n, w in kinds:
        scratch += [pltpu.VMEM((n * k, part, w), LOW) for k in (16, 8, 6, 1)]
    scratch += [
        pltpu.VMEM((flat, width), F32), pltpu.VMEM((pairs, rows, width), LOW), pltpu.VMEM((8, width), F32),
        pltpu.VMEM((8, 3 * width), F32), pltpu.VMEM((8, 2 * fw), F32), pltpu.VMEM((10, 8, 2 * fw), F32),
        pltpu.SemaphoreType.DMA((4, BLOCKS)), pltpu.SemaphoreType.DMA((4, BLOCKS)), pltpu.SemaphoreType.DMA((9,)),
        pltpu.SemaphoreType.DMA((3, pairs)), pltpu.SemaphoreType.DMA((3, pairs)), pltpu.SemaphoreType.DMA((2, 6)),
        pltpu.SemaphoreType.DMA((pairs,)),
    ]
    plane = lambda a: a.reshape(-1, width)
    return pl.pallas_call(
        back_kernel,
        in_specs=[pl.BlockSpec(memory_space=pltpu.SMEM)] + [hbm] * 10 + [vm] * 2,
        out_specs=[hbm] * 2 + [vm] * 7,
        out_shape=[
            jax.ShapeDtypeStruct((2 * pairs, rows, width), LOW), jax.ShapeDtypeStruct((2 * pairs, rows, width), LOW),
            jax.ShapeDtypeStruct((part, fw), F32), jax.ShapeDtypeStruct((part, fw), F32),
            jax.ShapeDtypeStruct((1, part, width // 2), F32),
            jax.ShapeDtypeStruct((3, part, width // 2), F32), jax.ShapeDtypeStruct((fw,), F32),
            jax.ShapeDtypeStruct((2, width // 2), F32), jax.ShapeDtypeStruct((6, part), F32),
        ],
        scratch_shapes=scratch,
        compiler_params=pltpu.CompilerParams(collective_id=1, has_side_effects=True, vmem_limit_bytes=63 * 2**20),
        name="backward_reduce",
    )(counts, plane(cotangent), plane(hid), plane(n2), plane(att), n1, qkv, prob, tokens, w_one, w_two, bias, vec)


def per_device(
    patch_counts, tokens, cotangent, attn_gain, attn_shift, w_qkv, b_qv, w_proj, b_proj,
    ffn_gain, ffn_shift, w_up, b_up, w_down, b_down,
):
    pairs_all, rows, width = tokens.shape
    n_mp = lax.axis_size("mp")
    n_dp = lax.axis_size("dp")
    pairs = pairs_all // n_mp
    direct = n_dp == Z * Y * C and n_mp == 2 and pairs == 4
    part = w_qkv.shape[0]
    lw = w_qkv.shape[2]
    fw = w_up.shape[1]
    mine = lax.axis_index("mp")
    vectors = [attn_gain, attn_shift, b_proj, ffn_gain, ffn_shift, b_down]
    if direct:
        w_one, w_two, bias, qkv, att, prob, hid, n1, n2, vec = gather_attention(
            patch_counts, tokens, w_qkv, w_proj, w_up, w_down, b_qv, b_up, vectors)
        block_out, tokens_grad, r_down, r_up, r_proj, r_qkv, o_b_up, o_b_qv, o_vec = backward_reduce(
            patch_counts, tokens, cotangent, hid, n2, att, n1, qkv, prob, w_one, w_two, bias, vec)
        o_gain, o_shift, o_b_proj, o_b_down, o_ffn_gain, o_ffn_shift = [o_vec[i] for i in range(6)]
        return (
            block_out, tokens_grad, o_gain, o_shift, r_qkv.transpose(1, 0, 2), o_b_qv,
            r_proj[0].T, o_b_proj, o_ffn_gain, o_ffn_shift, r_up, o_b_up, r_down.T, o_b_down,
        )

    off = jnp.reshape(mine * pairs, (1,)).astype(jnp.int32)
    lens = TEXT + lax.dynamic_slice_in_dim(patch_counts, mine * pairs, pairs, 0)
    first = jnp.concatenate(
        [w_qkv.reshape(part, 3 * lw), w_proj.T, jnp.stack(vectors, axis=1), jnp.zeros((part, EXTRA - 6), F32)], axis=1
    ).astype(LOW)
    second = jnp.concatenate([w_up, w_down.T], axis=1).astype(LOW)
    bias = jnp.concatenate([b_qv.reshape(-1), b_up]).astype(LOW).astype(F32)
    bias = jnp.broadcast_to(bias, (8,) + bias.shape)
    both_axes = ("mp", "dp")
    w_one = lax.all_gather(first, both_axes, axis=0, tiled=True).reshape(n_mp, width, -1)
    w_two = lax.all_gather(second, both_axes, axis=0, tiled=True).reshape(n_mp, width, -1)
    bias = lax.all_gather(bias, "mp", axis=0)
    qkv, att, prob, hid, n1, n2, vec = attention_forward(lens, off, tokens, w_one, bias)

    def grad(left, right):
        return jnp.einsum(
            "rd,rf->df", left.reshape(pairs * rows, width), right.reshape(pairs * rows, -1),
            preferred_element_type=F32,
        )

    def reduce(grads, small):
        axes = ("mp", "dp")
        done = [
            lax.psum_scatter(
                g.reshape(width, n_mp, -1).swapaxes(0, 1).reshape(n_mp * width, -1), axes,
                scatter_dimension=0, tiled=True,
            )
            for g in grads
        ]
        return done + [lax.psum(small, axes)]

    def both(array):
        other = lax.ppermute(array, "mp", [(0, 1), (1, 0)])
        return jnp.where(mine == 0, jnp.concatenate([array, other]), jnp.concatenate([other, array]))

    out_here, act, dpre, dhid, dlow, upl, sums_two, bsum_up = ffn(lens, off, n2, hid, cotangent, w_two, bias, vec)
    block_out = both(out_here)
    tok_here, dqkv, sums_one, bsum_qkv = attention_backward(lens, off, tokens, dhid, qkv, prob, w_one, vec)
    tokens_grad = both(tok_here)
    flat = bsum_qkv[0].reshape(n_mp, 3, lw)
    small = jnp.concatenate([
        sums_one[0], sums_one[1], sums_two[2], sums_two[0], sums_two[1], sums_two[3],
        flat[:, 0].reshape(-1), flat[:, 2].reshape(-1), bsum_up[0]])
    r_up, r_down, r_proj, r_qkv, small = reduce(
        [grad(n2, dpre), grad(upl, act), grad(dlow, att), grad(n1, dqkv)], small)
    place_dp = lax.axis_index("dp") * part

    def piece(i):
        return lax.dynamic_slice_in_dim(small, i * width + place_dp, part, 0)

    rest = small[6 * width :]
    o_b_q = lax.dynamic_slice_in_dim(rest, mine * lw, lw, 0)
    o_b_v = lax.dynamic_slice_in_dim(rest, (n_mp + mine) * lw, lw, 0)
    o_b_up = lax.dynamic_slice_in_dim(rest, 2 * n_mp * lw + mine * fw, fw, 0)
    return (
        block_out, tokens_grad, piece(0), piece(1),
        r_qkv.reshape(part, 3, lw), jnp.stack([o_b_q, o_b_v]),
        r_proj.T, piece(2), piece(3), piece(4), r_up, o_b_up, r_down.T, piece(5),
    )


def solution(mesh):
    vec, mat = P("dp"), P("dp", "mp")
    tok = P("dp", None, None)
    in_specs = (
        vec, tok, tok, vec, vec, P("dp", None, "mp"), P(None, "mp"), P("mp", "dp"), vec, vec, vec,
        mat, P("mp"), P("mp", "dp"), vec,
    )
    out_specs = (
        tok, tok, vec, vec, P("dp", None, "mp"), P(None, "mp"), P("mp", "dp"), vec, vec, vec,
        mat, P("mp"), P("mp", "dp"), vec,
    )
    return jax.shard_map(per_device, mesh=mesh, in_specs=in_specs, out_specs=out_specs, check_vma=False)
```

```python
import functools

import jax
import jax.numpy as jnp
from jax import lax
from jax.experimental import pallas as pl
from jax.experimental.pallas import tpu as pltpu
from jax.sharding import PartitionSpec as P

HEADS = 12
HEAD_DIM = 64
TEXT = 40
LOW = jnp.bfloat16
F32 = jnp.float32
EXTRA = 128
NT = (((1,), (1,)), ((), ()))
NN = (((1,), (0,)), ((), ()))


def dot(a, b, dims=NN):
    return lax.dot_general(a, b, dims, preferred_element_type=F32)


def moments(v):
    center = v - jnp.mean(v, axis=-1, keepdims=True)
    spread = jnp.mean(center * center, axis=-1, keepdims=True)
    r = lax.rsqrt(spread + 1e-06)
    return center * r, r


def row_ids(rows):
    return lax.broadcasted_iota(jnp.int32, (rows, 1), 0)


def attn_body(p, count, x, w_ref, bias_ref, vec_ref, qkv_ref, att_ref, prob_ref, hid_ref, n1_ref, n2_ref, hook):
    rows, width = x.shape
    groups = w_ref.shape[0]
    lw = width // groups
    tiles = lw // 128
    x = x.astype(F32)
    xhat, _ = moments(x)
    n1 = (xhat * vec_ref[0:1] + vec_ref[1:2]).astype(LOW)
    n1_ref[0] = n1
    for m in range(groups):
        y = dot(n1, w_ref[m, :, : 3 * lw])
        base = m * 3 * lw
        qkv_ref[0, :, base : base + lw] = (y[:, :lw] + bias_ref[m, 0:1, :lw]).astype(LOW)
        qkv_ref[0, :, base + lw : base + 2 * lw] = y[:, lw : 2 * lw].astype(LOW)
        qkv_ref[0, :, base + 2 * lw : base + 3 * lw] = (
            y[:, 2 * lw :] + bias_ref[m, 0:1, lw : 2 * lw]
        ).astype(LOW)
    keep = row_ids(rows) < count
    first = lax.broadcasted_iota(jnp.int32, (1, 128), 1) < HEAD_DIM

    def pair(hp, carry):
        base = (hp // tiles) * 3 * lw + lax.rem(hp, tiles) * 128

        def cols(t):
            return pl.ds(pl.multiple_of(base + t * lw, 128), 128)

        q2 = qkv_ref[0, :, cols(0)] * 0.125
        k2 = qkv_ref[0, :, cols(1)]
        v2t = qkv_ref[0, :, cols(2)].T
        outs = []
        for h in range(2):
            qh = jnp.where(first if h == 0 else ~first, q2, 0)
            st = dot(k2, qh, NT)
            st = jnp.where(keep, st, -1e30)
            e = jnp.exp(st - jnp.max(st, axis=0, keepdims=True))
            pt = (e * (1.0 / jnp.sum(e, axis=0, keepdims=True))).astype(LOW)
            prob_ref[0, hp * 2 + h] = pt
            outs.append(dot(v2t[h * HEAD_DIM : (h + 1) * HEAD_DIM], pt))
        att_ref[0, :, pl.ds(pl.multiple_of(hp * 128, 128), 128)] = jnp.concatenate(outs, axis=0).T.astype(LOW)
        hook(hp)
        return carry

    lax.fori_loop(0, groups * tiles, pair, 0)
    proj = sum(dot(att_ref[0, :, m * lw : (m + 1) * lw], w_ref[m, :, 3 * lw : 4 * lw], NT) for m in range(groups))
    hid = x + proj + vec_ref[2:3]
    hid_ref[0] = hid
    xhat2, _ = moments(hid)
    n2_ref[0] = (xhat2 * vec_ref[3:4] + vec_ref[4:5]).astype(LOW)


def attn_kernel(lens, off, x_ref, w_ref, bias_ref, qkv_ref, att_ref, prob_ref, hid_ref, n1_ref, n2_ref, vec_ref):
    p = pl.program_id(0)
    lw = x_ref.shape[2] // w_ref.shape[0]

    @pl.when(p == 0)
    def _():
        vec_ref[...] = w_ref[0, :, 4 * lw :].astype(F32).T[:8]

    attn_body(p, lens[p], x_ref[0], w_ref, bias_ref, vec_ref, qkv_ref, att_ref, prob_ref, hid_ref, n1_ref, n2_ref,
              lambda hp: None)


def const_spec(shape):
    return pl.BlockSpec(shape, lambda *_: (0,) * len(shape), pipeline_mode=pl.Buffered(1))


def pair_spec(*shape):
    return pl.BlockSpec((1,) + shape, lambda p, *_: (p,) + (0,) * len(shape))


def attention_forward(lens, off, tokens, w_one, bias):
    pairs = lens.shape[0]
    _, rows, width = tokens.shape
    out = lambda dt, *s: jax.ShapeDtypeStruct((pairs,) + s, dt)
    return pl.pallas_call(
        attn_kernel,
        grid_spec=pltpu.PrefetchScalarGridSpec(
            num_scalar_prefetch=2,
            grid=(pairs,),
            in_specs=[
                pl.BlockSpec((1, rows, width), lambda p, lens, off: (off[0] + p, 0, 0)),
                const_spec(w_one.shape),
                const_spec(bias.shape),
            ],
            out_specs=[
                pair_spec(rows, 3 * width), pair_spec(rows, width), pair_spec(HEADS, rows, rows),
                pair_spec(rows, width), pair_spec(rows, width), pair_spec(rows, width),
                pl.BlockSpec((8, width), lambda *_: (0, 0)),
            ],
        ),
        out_shape=[
            out(LOW, rows, 3 * width), out(LOW, rows, width), out(LOW, HEADS, rows, rows),
            out(F32, rows, width), out(LOW, rows, width), out(LOW, rows, width),
            jax.ShapeDtypeStruct((8, width), F32),
        ],
        compiler_params=pltpu.CompilerParams(vmem_limit_bytes=60 * 2**20),
        name="attention_forward",
    )(lens, off, tokens, w_one, bias)


def ffn_kernel(lens, off, n2_ref, hid_ref, cot_ref, w_ref, bias_ref, vec_ref,
               out_ref, act_ref, dpre_ref, dhid_ref, dlow_ref, upl_ref, sums_ref, bsum_ref):
    p = pl.program_id(0)
    rows, width = n2_ref.shape[1], n2_ref.shape[2]
    groups = w_ref.shape[0]
    fw = w_ref.shape[2] // 2
    lw = width // groups
    step = 512
    keep = row_ids(rows) < lens[p]
    n2 = n2_ref[0]
    upl = jnp.where(keep, cot_ref[0], 0)
    upl_ref[0] = upl

    @pl.when(p == 0)
    def _():
        sums_ref[...] = jnp.zeros_like(sums_ref)
        bsum_ref[...] = jnp.zeros_like(bsum_ref)

    for m in range(groups):
        for c in range(0, fw, step):
            pre = dot(n2, w_ref[m, :, c : c + step]) + bias_ref[m, 0:1, 2 * lw + c : 2 * lw + c + step]
            cdf = 0.5 * (1.0 + lax.erf(pre * (2.0 ** -0.5)))
            at = m * fw + c
            act_ref[0, :, at : at + step] = (pre * cdf).astype(LOW)
            slope = cdf + pre * (0.3989422804014327 * jnp.exp(-0.5 * pre * pre))
            dpre = slope * dot(upl, w_ref[m, :, fw + c : fw + c + step])
            dpre_ref[0, :, at : at + step] = dpre.astype(LOW)
            bsum_ref[0:1, at : at + step] += jnp.sum(dpre, axis=0, keepdims=True)
    hid = hid_ref[0]
    down = sum(dot(act_ref[0, :, m * fw : (m + 1) * fw], w_ref[m, :, fw:], NT) for m in range(groups))
    out_ref[0] = jnp.where(keep, hid + down + vec_ref[5:6], 0.0).astype(LOW)
    dtwo = sum(dot(dpre_ref[0, :, m * fw : (m + 1) * fw], w_ref[m, :, :fw], NT) for m in range(groups))
    xhat, r = moments(hid)
    dg = dtwo * vec_ref[3:4]
    dn = r * (dg - jnp.mean(dg, axis=-1, keepdims=True) - xhat * jnp.mean(dg * xhat, axis=-1, keepdims=True))
    upf = upl.astype(F32)
    dhid = upf + dn
    dhid_ref[0] = dhid
    dlow_ref[0] = dhid.astype(LOW)
    sums_ref[0:1] += jnp.sum(dtwo * xhat, axis=0, keepdims=True)
    sums_ref[1:2] += jnp.sum(dtwo, axis=0, keepdims=True)
    sums_ref[2:3] += jnp.sum(dhid, axis=0, keepdims=True)
    sums_ref[3:4] += jnp.sum(upf, axis=0, keepdims=True)


def ffn(lens, off, n2, hid, cotangent, w_two, bias, vec):
    pairs, rows, width = n2.shape
    ff = w_two.shape[0] * w_two.shape[2] // 2
    out = lambda dt, *s: jax.ShapeDtypeStruct((pairs,) + s, dt)
    return pl.pallas_call(
        ffn_kernel,
        grid_spec=pltpu.PrefetchScalarGridSpec(
            num_scalar_prefetch=2,
            grid=(pairs,),
            in_specs=[
                pair_spec(rows, width), pair_spec(rows, width),
                pl.BlockSpec((1, rows, width), lambda p, lens, off: (off[0] + p, 0, 0)),
                const_spec(w_two.shape), const_spec(bias.shape), const_spec(vec.shape),
            ],
            out_specs=[
                pair_spec(rows, width), pair_spec(rows, ff), pair_spec(rows, ff), pair_spec(rows, width),
                pair_spec(rows, width), pair_spec(rows, width),
                pl.BlockSpec((8, width), lambda *_: (0, 0)), pl.BlockSpec((8, ff), lambda *_: (0, 0)),
            ],
        ),
        out_shape=[
            out(LOW, rows, width), out(LOW, rows, ff), out(LOW, rows, ff), out(F32, rows, width),
            out(LOW, rows, width), out(LOW, rows, width),
            jax.ShapeDtypeStruct((8, width), F32), jax.ShapeDtypeStruct((8, ff), F32),
        ],
        compiler_params=pltpu.CompilerParams(vmem_limit_bytes=60 * 2**20),
        name="feed_forward",
    )(lens, off, n2, hid, cotangent, w_two, bias, vec)


def plain_back_kernel(lens, off, x_ref, dhid_ref, qkv_ref, prob_ref, w_ref, vec_ref,
                tok_ref, dqkv_ref, sums_ref, bsum_ref, do_ref):
    p = pl.program_id(0)
    rows, width = x_ref.shape[1], x_ref.shape[2]
    groups = w_ref.shape[0]
    lw = width // groups
    tiles = lw // 128

    @pl.when(p == 0)
    def _():
        sums_ref[...] = jnp.zeros_like(sums_ref)
        bsum_ref[...] = jnp.zeros_like(bsum_ref)

    dhid = dhid_ref[0]
    dlow = dhid.astype(LOW)
    for m in range(groups):
        do_ref[:, m * lw : (m + 1) * lw] = dot(dlow, w_ref[m, :, 3 * lw : 4 * lw]).astype(LOW)
    first = lax.broadcasted_iota(jnp.int32, (1, 128), 1) < HEAD_DIM

    def pair(hp, carry):
        base = (hp // tiles) * 3 * lw + (hp % tiles) * 128

        def cols(t):
            return pl.ds(pl.multiple_of(base + t * lw, 128), 128)

        q2 = qkv_ref[0, :, cols(0)] * 0.125
        k2t = qkv_ref[0, :, cols(1)].T
        v2 = qkv_ref[0, :, cols(2)]
        do2 = do_ref[:, pl.ds(pl.multiple_of(hp * 128, 128), 128)]
        dq_t = []
        dk = dv = 0.0
        for h in range(2):
            mine = first if h == 0 else ~first
            doh = jnp.where(mine, do2, 0)
            qh = jnp.where(mine, q2, 0)
            dpt = dot(v2, doh, NT)
            plow = prob_ref[0, hp * 2 + h]
            pt = plow.astype(F32)
            inner = jnp.sum(pt * dpt, axis=0, keepdims=True)
            dst = (pt * (dpt - inner)).astype(LOW)
            dv = dv + dot(plow, doh)
            dk = dk + dot(dst, qh)
            dq_t.append(dot(k2t[h * HEAD_DIM : (h + 1) * HEAD_DIM], dst))
        dq = (jnp.concatenate(dq_t, axis=0) * 0.125).T
        dqkv_ref[0, :, cols(0)] = dq.astype(LOW)
        dqkv_ref[0, :, cols(1)] = dk.astype(LOW)
        dqkv_ref[0, :, cols(2)] = dv.astype(LOW)
        bsum_ref[0:1, cols(0)] += jnp.sum(dq, axis=0, keepdims=True)
        bsum_ref[0:1, cols(2)] += jnp.sum(dv, axis=0, keepdims=True)
        return carry

    lax.fori_loop(0, groups * tiles, pair, 0)
    done = sum(dot(dqkv_ref[0, :, m * 3 * lw : (m + 1) * 3 * lw], w_ref[m, :, : 3 * lw], NT) for m in range(groups))
    xhat, r = moments(x_ref[0].astype(F32))
    dg = done * vec_ref[0:1]
    dn = r * (dg - jnp.mean(dg, axis=-1, keepdims=True) - xhat * jnp.mean(dg * xhat, axis=-1, keepdims=True))
    tok_ref[0] = (dhid + dn).astype(LOW)
    sums_ref[0:1] += jnp.sum(done * xhat, axis=0, keepdims=True)
    sums_ref[1:2] += jnp.sum(done, axis=0, keepdims=True)


def attention_backward(lens, off, tokens, dhid, qkv, prob, w_one, vec):
    pairs, rows, width = dhid.shape
    out = lambda dt, *s: jax.ShapeDtypeStruct((pairs,) + s, dt)
    return pl.pallas_call(
        plain_back_kernel,
        grid_spec=pltpu.PrefetchScalarGridSpec(
            num_scalar_prefetch=2,
            grid=(pairs,),
            in_specs=[
                pl.BlockSpec((1, rows, width), lambda p, lens, off: (off[0] + p, 0, 0)),
                pair_spec(rows, width), pair_spec(rows, 3 * width), pair_spec(HEADS, rows, rows),
                const_spec(w_one.shape), const_spec(vec.shape),
            ],
            out_specs=[
                pair_spec(rows, width), pair_spec(rows, 3 * width),
                pl.BlockSpec((8, width), lambda *_: (0, 0)), pl.BlockSpec((8, 3 * width), lambda *_: (0, 0)),
            ],
            scratch_shapes=[pltpu.VMEM((rows, width), LOW)],
        ),
        out_shape=[
            out(LOW, rows, width), out(LOW, rows, 3 * width),
            jax.ShapeDtypeStruct((8, width), F32), jax.ShapeDtypeStruct((8, 3 * width), F32),
        ],
        compiler_params=pltpu.CompilerParams(vmem_limit_bytes=60 * 2**20),
        name="attention_backward",
    )(lens, off, tokens, dhid, qkv, prob, w_one, vec)
MESH_ID = pl.DeviceIdType.MESH
Z, Y, C = 4, 2, 2


def place():
    dp = lax.axis_index("dp")
    m = lax.axis_index("mp")
    c = lax.rem(dp, 2)
    y = lax.rem(dp // 2, 2)
    z = dp // 4
    return z, y, c, m


def index(z, y, c):
    return (z * Y + y) * C + c


def flips(y, c, m):
    one = (y + c * (1 - 2 * y), m + (1 - c) * (1 - 2 * m))
    two = (y + (1 - c) * (1 - 2 * y), m + c * (1 - 2 * m))
    return one, two


def greet(z, y, c, m):
    barrier = pltpu.get_barrier_semaphore()
    (y1, m1), (y2, m2) = flips(y, c, m)
    peers = [(index(lax.rem(z + k, Z), y, c), m) for k in (1, 2, 3)]
    peers += [(index(z, y1, c), m1), (index(z, y2, c), m2), (index(z, y, 1 - c), m)]
    for dp, mp in peers:
        pl.semaphore_signal(barrier, inc=1, device_id={"dp": dp, "mp": mp}, device_id_type=MESH_ID)
    pl.semaphore_wait(barrier, len(peers))
    return peers


def gather_attn_kernel(counts, tok_all, wq_in, wp_in, wu_in, wd_in, bq_in, bu_in, v0, v1, v2, v3, v4, v5,
                       w_one_out, w_two, b_out, qkv_ref, att_ref, prob_ref, hid_ref, n1_ref, n2_ref, vec_ref,
                       w_one, bias, xbuf, first_ref, second_ref, b_in, vbuf, send, recv, bsem, local):
    p = pl.program_id(0)
    z, y, c, m = place()
    (y1, m1), (y2, m2) = flips(y, c, m)
    pairs, rows, width = xbuf.shape
    part = first_ref.shape[0]
    cols = second_ref.shape[1] // 2
    lw = width // 2
    per_pair = width // 128
    me = index(z, y, c)
    one, two, sib = (index(z, y1, c), m1), (index(z, y2, c), m2), (index(z, y, 1 - c), m)

    def spot(g, dp, mp):
        at = pl.ds(pl.multiple_of(dp * part, part), part)
        if g is None:
            return w_one.at[mp, at]
        return w_two.at[mp, at, pl.ds(pl.multiple_of(g * cols, 128), cols)]

    def shard(g):
        return first_ref if g is None else second_ref.at[:, pl.ds(pl.multiple_of(g * cols, 128), cols)]

    def row(g):
        return 0 if g is None else g + 1

    def copy_of(g, src, dst, out_sem, in_sem, to):
        return pltpu.make_async_remote_copy(
            src_ref=src, dst_ref=dst, send_sem=send.at[row(g), out_sem], recv_sem=recv.at[row(g), in_sem],
            device_id={"dp": to[0], "mp": to[1]}, device_id_type=MESH_ID,
        )

    def push(g, src, dp, mp, to, sem):
        copy_of(g, src, spot(g, dp, mp), sem, mp * (Z * Y * C) + dp, to).start()

    def arrived(g, dp, mp):
        at = spot(g, dp, mp)
        copy_of(g, at, at, 0, mp * (Z * Y * C) + dp, sib).wait_recv()
        return at

    def own_z(g):
        for k in (1, 3, 2):
            push(g, shard(g), me, m, (index(lax.rem(z + k, Z), y, c), m), k - 1)

    def own_near(g):
        for n, to in enumerate((one, two, sib)):
            push(g, shard(g), me, m, to, 3 + n)

    def event_z(g, i):
        dp = index(lax.rem(z + 1 + lax.rem(2 * i, 3), Z), y, c)
        at = arrived(g, dp, m)
        for n, to in enumerate((one, two, sib)):
            push(g, at, dp, m, to, 6 + 3 * i + n)

    def event_one(g, i):
        dp = index(lax.rem(z + i, Z), y1, c)
        at = arrived(g, dp, m1)
        for n, to in enumerate((two, sib)):
            push(g, at, dp, m1, to, 15 + 2 * i + n)

    def event_two(g, i):
        far = lax.rem(i, 2)
        yy = y2 + far * (1 - y - y2)
        mm = m2 + far * (1 - m - m2)
        dp = index(lax.rem(z + i // 2, Z), yy, c)
        push(g, arrived(g, dp, mm), dp, mm, sib, 23 + i)

    def event_core(g, i):
        arrived(g, index(i // 4, lax.rem(i // 2, 2), 1 - c), lax.rem(i, 2))

    def loop(n, event, g):
        def run(i, carry):
            event(g, i)
            return carry

        lax.fori_loop(0, n, run, 0)

    bias_copy = pltpu.make_async_remote_copy(
        src_ref=b_in, dst_ref=bias.at[m], send_sem=bsem.at[0], recv_sem=bsem.at[1],
        device_id={"dp": me, "mp": 1 - m}, device_id_type=MESH_ID,
    )
    x_copy = pltpu.make_async_copy(tok_all.at[pl.ds(m * pairs, pairs)], xbuf, local.at[0])
    mine = [
        pltpu.make_async_copy(b_in, bias.at[m], local.at[1]),
        pltpu.make_async_copy(first_ref, spot(None, me, m), local.at[2]),
    ]
    mine_two = [pltpu.make_async_copy(shard(g), spot(g, me, m), local.at[3 + g]) for g in range(2)]
    keep_one = pltpu.make_async_copy(w_one, w_one_out, local.at[5])
    keep_bias = pltpu.make_async_copy(bias, b_out, local.at[6])

    @pl.when(p == 0)
    def _():
        x_copy.start()
        for t in range(3):
            first_ref[:, t * lw : (t + 1) * lw] = wq_in[t].astype(LOW)
        first_ref[:, 3 * lw : 4 * lw] = wp_in[...].astype(LOW)
        vbuf[...] = jnp.zeros_like(vbuf)
        for n, v in enumerate((v0, v1, v2, v3, v4, v5)):
            vbuf[n : n + 1, :part] = v[...]
        first_ref[:, 4 * lw :] = vbuf[...].T[:part].astype(LOW)
        second_ref[:, :cols] = wu_in[...].astype(LOW)
        second_ref[:, cols:] = wd_in[...].astype(LOW)
        b_in[...] = jnp.zeros_like(b_in)
        b_in[0:1, :lw] = bq_in[0:1].astype(LOW).astype(F32)
        b_in[0:1, lw : 2 * lw] = bq_in[1:2].astype(LOW).astype(F32)
        b_in[0:1, 2 * lw :] = bu_in[...].reshape(1, cols).astype(LOW).astype(F32)
        greet(z, y, c, m)
        own_z(None)
        own_near(None)
        bias_copy.start()
        for copy in mine + mine_two:
            copy.start()
        loop(3, event_z, None)
        own_z(0)
        own_z(1)
        loop(4, event_one, None)
        own_near(0)
        loop(3, event_z, 0)
        loop(8, event_two, None)
        for copy in mine + [x_copy, bias_copy]:
            copy.wait()
        loop(16, event_core, None)
        keep_one.start()
        keep_bias.start()
        vec_ref[...] = w_one[0, :, 4 * lw :].astype(F32).T[:8]

    def hook(hp):
        step = p * per_pair + hp

        def event(e, carry):
            @pl.when(e == 0)
            def _():
                own_near(1)

            @pl.when(((e >= 1) & (e < 5)) | ((e >= 16) & (e < 20)))
            def _():
                g = e // 16
                event_one(g, e - 1 - 15 * g)

            @pl.when((e >= 5) & (e < 8))
            def _():
                event_z(1, e - 5)

            @pl.when(((e >= 8) & (e < 16)) | (e >= 20))
            def _():
                g = e // 20
                event_two(g, e - 8 - 12 * g)

            return carry

        total = pairs * per_pair
        lax.fori_loop(step * 28 // total, (step + 1) * 28 // total, event, 0)

    attn_body(p, TEXT + counts[m * pairs + p], xbuf[p], w_one, bias, vec_ref, qkv_ref, att_ref, prob_ref, hid_ref, n1_ref, n2_ref, hook)

    @pl.when(p == pairs - 1)
    def _():
        for g in range(2):
            loop(16, event_core, g)
        for copy in mine_two + [keep_one, keep_bias]:
            copy.wait()
        for g in (None, 0, 1):
            def sent(i, carry):
                copy_of(g, shard(g), shard(g), i, 0, sib).wait_send()
                return carry

            lax.fori_loop(0, 31, sent, 0)


def gather_attention(counts, tokens, w_qkv, w_proj, w_up, w_down, b_qv, b_up, vectors):
    pairs = counts.shape[0] // 2
    _, rows, width = tokens.shape
    part, fw = w_up.shape
    lw = width // 2
    total = Z * Y * C
    hbm = pl.BlockSpec(memory_space=pl.ANY)
    out = lambda dt, *s: jax.ShapeDtypeStruct((pairs,) + s, dt)
    small = [w_qkv.transpose(1, 0, 2), w_proj.T, w_up, w_down.T, b_qv, b_up]
    small += [v.reshape(1, part) for v in vectors]
    one, two, bias = 4 * lw + EXTRA, 2 * fw, (8, 2 * lw + fw)
    return pl.pallas_call(
        gather_attn_kernel,
        grid_spec=pltpu.PrefetchScalarGridSpec(
            num_scalar_prefetch=1,
            grid=(pairs,),
            in_specs=[hbm] + [const_spec(a.shape) for a in small],
            out_specs=[
                hbm, hbm, hbm,
                pair_spec(rows, 3 * width), pair_spec(rows, width), pair_spec(HEADS, rows, rows),
                pair_spec(rows, width), pair_spec(rows, width), pair_spec(rows, width),
                pl.BlockSpec((8, width), lambda *_: (0, 0)),
            ],
            scratch_shapes=[
                pltpu.VMEM((2, width, one), LOW), pltpu.VMEM((2,) + bias, F32), pltpu.VMEM((pairs, rows, width), LOW),
                pltpu.VMEM((part, one), LOW), pltpu.VMEM((part, two), LOW), pltpu.VMEM(bias, F32),
                pltpu.VMEM((EXTRA, EXTRA), F32),
                pltpu.SemaphoreType.DMA((3, 31)), pltpu.SemaphoreType.DMA((3, 32)),
                pltpu.SemaphoreType.DMA((2,)), pltpu.SemaphoreType.DMA((7,)),
            ],
        ),
        out_shape=[
            jax.ShapeDtypeStruct((2, width, one), LOW),
            jax.ShapeDtypeStruct((2, width, two), LOW),
            jax.ShapeDtypeStruct((2,) + bias, F32),
            out(LOW, rows, 3 * width), out(LOW, rows, width), out(LOW, HEADS, rows, rows),
            out(F32, rows, width), out(LOW, rows, width), out(LOW, rows, width),
            jax.ShapeDtypeStruct((8, width), F32),
        ],
        compiler_params=pltpu.CompilerParams(collective_id=0, has_side_effects=True, vmem_limit_bytes=60 * 2**20),
        name="gather_attention",
    )(counts, tokens, *small)


BLOCKS = 31


def back_kernel(counts, cot, hid_in, n2_in, att_in, n1_all, qkv_all, prob_all, tok_all, w_one_in, w_two, bias_ref, vec_ref,
                block_out, tok_out, r_down, r_up, r_proj, r_qkv, o_up, o_qv, o_vec,
                g_ff, g_proj, g_qkv, rc_ff, rs_ff, rz_ff, rx_ff, rc_p, rs_p, rz_p, rx_p, rc_q, rs_q, rz_q, rx_q,
                dhid_ref, outbuf, sums, bsum, bsum_up, sbuf, send, recv, local, osem, tsem, ssem, n1_sem):
    flat, width = dhid_ref.shape
    pairs, rows = qkv_all.shape[0], qkv_all.shape[1]
    groups = w_two.shape[0]
    fw = w_two.shape[2] // 2
    fc = fw // 3
    lw = width // groups
    tiles = lw // 128
    half = flat // 2
    part = r_proj.shape[1]
    high = pairs * (rows + (-rows) % 16)
    z, y, c, m = place()
    me = index(z, y, c)
    sib = (index(z, y, 1 - c), m)

    def beside(k):
        return (index(lax.rem(z + k, Z), y, c), m)

    def loop(n, event):
        def one(i, carry):
            event(i)
            return carry

        lax.fori_loop(0, n, one, 0)

    def family(grad, rc, rs, rz, rx, out, row0, split):
        cols = rc.shape[2]
        fx = c * split
        near = (index(z, y + (1 - fx) * (1 - 2 * y), c), m + fx * (1 - 2 * m))
        far = (index(z, y + fx * (1 - 2 * y), c), m + (1 - fx) * (1 - 2 * m))

        def copy_of(u, src, dst, out_sem, in_sem, to):
            return pltpu.make_async_remote_copy(
                src_ref=src, dst_ref=dst, send_sem=send.at[row0 + u, out_sem], recv_sem=recv.at[row0 + u, in_sem],
                device_id={"dp": to[0], "mp": to[1]}, device_id_type=MESH_ID,
            )

        def swap(ra, rb, cc):
            f = cc * split
            return f * rb + (1 - f) * ra, f * ra + (1 - f) * rb

        def block(u, ra, rb, k, cc):
            dy, dm = swap(ra, rb, cc)
            yy = y + dy * (1 - 2 * y)
            mm = m + dm * (1 - 2 * m)
            return u, lax.rem(z + k, Z) * Y + yy, cc, slice(None), pl.ds(pl.multiple_of(mm * cols, 128), cols)

        def to_sibling(u, dm):
            def one(i):
                ra, rb = swap(1 - i // 4, dm, 1 - c)
                k = lax.rem(i + 1, 4)
                slot = (ra * 2 + rb) * 4 + k
                copy_of(u, grad.at[block(u, ra, rb, k, 1 - c)], rc.at[u * 16 + slot], slot, slot, sib).start()

            loop(8, one)

        def arrived(u, ref, sem):
            copy_of(u, ref, ref, 0, sem, sib).wait_recv()

        def base(u, ra, rb, k):
            slot = (ra * 2 + rb) * 4 + k
            arrived(u, rc.at[u * 16 + slot], slot)
            return grad[block(u, ra, rb, k, c)].astype(F32) + rc[u * 16 + slot].astype(F32)

        def level(u, rb, k):
            at = rb * 4 + k
            value = base(u, 0, rb, k)
            arrived(u, rs.at[u * 8 + at], 16 + at)
            return value + rs[u * 8 + at].astype(F32)

        def lined(u, rb):
            value = level(u, rb, 0)
            for k in (1, 2, 3):
                at = (k - 1) * 2 + rb
                arrived(u, rz.at[u * 6 + at], 24 + at)
                value = value + rz[u * 6 + at].astype(F32)
            return value

        def event_y(u, rb, i):
            k = lax.rem(i + 1, 4)
            slot = u * 16 + (2 + rb) * 4 + k
            at = rb * 4 + k
            rc[slot] = base(u, 1, rb, k).astype(LOW)
            copy_of(u, rc.at[slot], rs.at[u * 8 + at], 16 + at, 16 + at, near).start()

        def event_z(u, rb, i):
            k = 1 + i
            slot = u * 16 + rb * 4 + k
            at = (k - 1) * 2 + rb
            rc[slot] = level(u, rb, k).astype(LOW)
            copy_of(u, rc.at[slot], rz.at[u * 6 + at], 24 + at, 24 + at, beside(k)).start()

        def event_x(u):
            rc[u * 16 + 4] = lined(u, 1).astype(LOW)
            copy_of(u, rc.at[u * 16 + 4], rx.at[u], 30, 30, far).start()

        def final(u):
            value = lined(u, 0)
            arrived(u, rx.at[u], 30)
            out(u, value + rx[u].astype(F32))

            def one(i):
                copy_of(u, rc.at[0], rc.at[0], i, 0, sib).wait_send()

            loop(BLOCKS, one)

        return to_sibling, event_y, event_z, event_x, final

    def put(ref):
        def store(u, value):
            ref[u] = value

        return store

    def put_ff(u, value):
        (r_down, r_up)[u][...] = value

    def put_qkv(u, value):
        for t in range(3):
            r_qkv[t] = value[:, t * lw : (t + 1) * lw]

    ff_sib, ff_y, ff_z, ff_x, ff_final = family(g_ff, rc_ff, rs_ff, rz_ff, rx_ff, put_ff, 0, 0)
    p_sib, p_y, p_z, p_x, p_final = family(g_proj, rc_p, rs_p, rz_p, rx_p, put(r_proj), 2, 0)
    q_sib, q_y, q_z, q_x, q_final = family(g_qkv, rc_q, rs_q, rz_q, rx_q, put_qkv, 3, 0)

    def out_copies(q):
        src = outbuf.at[q]
        dst = block_out.at[m * pairs + q]
        return pltpu.make_async_copy(src, dst, osem.at[0, q]), pltpu.make_async_remote_copy(
            src_ref=src, dst_ref=dst, send_sem=osem.at[1, q], recv_sem=osem.at[2, q],
            device_id={"dp": me, "mp": 1 - m}, device_id_type=MESH_ID,
        )

    def keep_of(r):
        ids = row_ids(half)
        here = m * pairs + 2 * r
        return ids < TEXT + jnp.where(ids < rows, counts[here], counts[here + 1] + rows)

    def span(r):
        return pl.ds(pl.multiple_of(r * half, 16), half)

    sums[...] = jnp.zeros_like(sums)
    bsum[...] = jnp.zeros_like(bsum)
    bsum_up[...] = jnp.zeros_like(bsum_up)

    def feed_forward(n2, n2t, upl, uplt, hid, acc, slope, chunk, wbuf):
        def place_of(f):
            i = lax.rem(f, 6)
            return lax.rem(m + 1 + i // 3, 2), lax.rem(i, 3) * fc

        def weights(f):
            mm, at = place_of(f)
            slot = lax.rem(f, 2)
            return [
                pltpu.make_async_copy(
                    w_two.at[mm, :, pl.ds(pl.multiple_of(t * fw + at, 128), fc)], wbuf.at[slot, t], local.at[slot * 2 + t])
                for t in range(2)
            ]

        n2_copy = pltpu.make_async_copy(n2_in, n2, local.at[4])
        up_copy = pltpu.make_async_copy(cot.at[pl.ds(pl.multiple_of(m * flat, 16), flat)], upl, local.at[5])
        hid_copy = pltpu.make_async_copy(hid_in, hid, local.at[6])
        att_copy = pltpu.make_async_copy(att_in, slope.at[:, pl.ds(0, width)], local.at[7])
        n2_copy.start()
        up_copy.start()
        for copy in weights(0):
            copy.start()
        hid_copy.start()
        greet(z, y, c, m)
        up_copy.wait()

        def prepare(r):
            value = jnp.where(keep_of(r), upl[span(r)], 0)
            upl[span(r)] = value
            sums[3:4] += jnp.sum(value.astype(F32), axis=0, keepdims=True)
            acc[span(r)] = jnp.zeros((half, width), F32)

        loop(2, prepare)
        uplt[...] = upl[...].T
        n2_copy.wait()
        n2t[...] = n2[...].T

        def traffic(f):
            @pl.when(lax.rem(f, 3) == 2)
            def _():
                n = f // 3
                ff_sib(n // 2, 1 - lax.rem(n, 2))

            @pl.when((lax.rem(f, 3) == 0) & (f > 0))
            def _():
                n = f // 3 - 1
                loop(4, lambda i: ff_y(n // 2, 1 - lax.rem(n, 2), i))

            @pl.when((lax.rem(f, 3) == 1) & (f > 4))
            def _():
                n = (f - 7) // 3
                loop(3, lambda i: ff_z(n // 2, 1 - lax.rem(n, 2), i))

        def store(u, at, value):
            g_ff[u, :, :, :, at] = value.astype(LOW).reshape(Z * Y, C, part, fc)

        def forward(f):
            slot = lax.rem(f, 2)
            for copy in weights(f + 1):
                copy.start()
            for copy in weights(f):
                copy.wait()
            mm, off = place_of(f)
            at = pl.ds(pl.multiple_of(mm * fw + off, 128), fc)
            shift = bias_ref[mm, 0:1, pl.ds(pl.multiple_of(2 * lw + off, 128), fc)]

            def block(r):
                pre = dot(n2[span(r)], wbuf[slot, 0]) + shift
                cdf = 0.5 * (1.0 + lax.erf(pre * (2.0 ** -0.5)))
                chunk[span(r)] = (pre * cdf).astype(LOW)
                slope[span(r), at] = (cdf + pre * (0.3989422804014327 * jnp.exp(-0.5 * pre * pre))).astype(LOW)
                acc[span(r)] += dot(chunk[span(r)], wbuf[slot, 1], NT)

            loop(2, block)
            store(0, at, dot(uplt[...], chunk[...]))
            traffic(f)

        loop(6, forward)
        hid_copy.wait()

        def leave(r):
            value = jnp.where(keep_of(r), hid[span(r)] + acc[span(r)] + vec_ref[5:6], 0.0)
            acc[span(r)] = jnp.zeros((half, width), F32)
            for n in range(2):
                outbuf[2 * r + n] = value[n * rows : (n + 1) * rows].astype(LOW)
                for copy in out_copies(2 * r + n):
                    copy.start()

        loop(2, leave)

        def backward(i):
            f = 6 + i
            slot = lax.rem(f, 2)

            @pl.when(f < 11)
            def _():
                for copy in weights(f + 1):
                    copy.start()

            for copy in weights(f):
                copy.wait()
            mm, off = place_of(f)
            at = pl.ds(pl.multiple_of(mm * fw + off, 128), fc)

            def block(r):
                dpre = slope[span(r), at].astype(F32) * dot(upl[span(r)], wbuf[slot, 1])
                chunk[span(r)] = dpre.astype(LOW)
                bsum_up[0:1, at] += jnp.sum(dpre, axis=0, keepdims=True)
                acc[span(r)] += dot(chunk[span(r)], wbuf[slot, 0], NT)

            loop(2, block)
            store(1, at, dot(n2t[...], chunk[...]))
            traffic(f)

        loop(6, backward)
        att_copy.start()

        def norm_back(r):
            dtwo = acc[span(r)]
            xhat, rr = moments(hid[span(r)])
            dg = dtwo * vec_ref[3:4]
            dn = rr * (dg - jnp.mean(dg, axis=-1, keepdims=True) - xhat * jnp.mean(dg * xhat, axis=-1, keepdims=True))
            dhid = upl[span(r)].astype(F32) + dn
            dhid_ref[span(r)] = dhid
            n2[span(r)] = dhid.astype(LOW)
            sums[4:5] += jnp.sum(dtwo * xhat, axis=0, keepdims=True)
            sums[5:6] += jnp.sum(dtwo, axis=0, keepdims=True)
            sums[2:3] += jnp.sum(dhid, axis=0, keepdims=True)

        loop(2, norm_back)
        att_copy.wait()
        n2t[...] = n2[...].T
        for mm in range(groups):
            at = slice(mm * lw, (mm + 1) * lw)
            g_proj[0, :, :, :, at] = dot(n2t[...], slope[:, at]).astype(LOW).reshape(Z * Y, C, part, lw)
        p_sib(0, 1)
        p_sib(0, 0)

    pl.run_scoped(
        feed_forward,
        pltpu.VMEM((flat, width), LOW), pltpu.VMEM((width, flat), LOW),
        pltpu.VMEM((flat, width), LOW), pltpu.VMEM((width, flat), LOW),
        pltpu.VMEM((flat, width), F32), pltpu.VMEM((flat, width), F32),
        pltpu.VMEM((flat, groups * fw), LOW), pltpu.VMEM((flat, fc), LOW), pltpu.VMEM((2, 2, width, fc), LOW),
    )

    def attention(w_ref, qkv_buf, prob_buf, x_buf, do_ref, n1, n1t, dq_all):
        high = n1.shape[0] // pairs
        proj_cols = pl.ds(3 * lw, lw)
        qkv_cols = pl.ds(0, 3 * lw)
        w_copy = pltpu.make_async_copy(w_one_in.at[:, :, proj_cols], w_ref.at[:, :, proj_cols], local.at[8])
        w_qkv_copy = pltpu.make_async_copy(w_one_in.at[:, :, qkv_cols], w_ref.at[:, :, qkv_cols], local.at[6])

        def loads(p):
            slot = lax.rem(p, 2)
            pieces = [
                (qkv_all.at[p], qkv_buf), (prob_all.at[p], prob_buf), (tok_all.at[m * pairs + p], x_buf),
            ]
            return [
                pltpu.make_async_copy(src, dst.at[slot], local.at[slot * 3 + t])
                for t, (src, dst) in enumerate(pieces)
            ]

        def tok_copies(p):
            src, dst = n1.at[pl.ds(pl.multiple_of(p * high, 16), rows)], tok_out.at[m * pairs + p]
            return pltpu.make_async_copy(src, dst, tsem.at[0, p]), pltpu.make_async_remote_copy(
                src_ref=src, dst_ref=dst, send_sem=tsem.at[1, p], recv_sem=tsem.at[2, p],
                device_id={"dp": me, "mp": 1 - m}, device_id_type=MESH_ID,
            )

        w_copy.start()
        for copy in loads(0):
            copy.start()
        n1_copies = [
            pltpu.make_async_copy(n1_all.at[p], n1.at[pl.ds(p * high, rows)], n1_sem.at[p]) for p in range(pairs)
        ]
        for copy in n1_copies:
            copy.start()
        w_qkv_copy.start()
        w_copy.wait()

        def attended_back(r):
            dlow = dhid_ref[span(r)].astype(LOW)
            for mm in range(groups):
                value = dot(dlow, w_ref[mm, :, 3 * lw : 4 * lw])
                for n in range(2):
                    do_ref[2 * r + n, :, mm * lw : (mm + 1) * lw] = value[n * rows : (n + 1) * rows].astype(LOW)

        loop(2, attended_back)
        for p, copy in enumerate(n1_copies):
            copy.wait()
            n1[p * high + rows : (p + 1) * high] = jnp.zeros((high - rows, width), LOW)
            dq_all[p * high + rows : (p + 1) * high] = jnp.zeros((high - rows, 3 * width), LOW)
        n1t[...] = n1[...].T
        first = lax.broadcasted_iota(jnp.int32, (1, 128), 1) < HEAD_DIM

        def one_pair(p):
            slot = lax.rem(p, 2)

            @pl.when(p < pairs - 1)
            def _():
                for copy in loads(p + 1):
                    copy.start()

            dhid = dhid_ref[pl.ds(pl.multiple_of(p * rows, 8), rows)]
            here = pl.ds(pl.multiple_of(p * high, 16), rows)
            for copy in loads(p):
                copy.wait()

            def heads(hp):
                lane = (hp // tiles) * 3 * lw + lax.rem(hp, tiles) * 128

                def cols(t):
                    return pl.ds(pl.multiple_of(lane + t * lw, 128), 128)

                q2 = qkv_buf[slot, :, cols(0)] * 0.125
                k2t = qkv_buf[slot, :, cols(1)].T
                v2 = qkv_buf[slot, :, cols(2)]
                do2 = do_ref[p, :, pl.ds(pl.multiple_of(hp * 128, 128), 128)]
                dq_t = []
                dk = dv = 0.0
                for h in range(2):
                    mine = first if h == 0 else ~first
                    doh = jnp.where(mine, do2, 0)
                    qh = jnp.where(mine, q2, 0)
                    dpt = dot(v2, doh, NT)
                    plow = prob_buf[slot, hp * 2 + h]
                    pt = plow.astype(F32)
                    inner = jnp.sum(pt * dpt, axis=0, keepdims=True)
                    dst = (pt * (dpt - inner)).astype(LOW)
                    dv = dv + dot(plow, doh)
                    dk = dk + dot(dst, qh)
                    dq_t.append(dot(k2t[h * HEAD_DIM : (h + 1) * HEAD_DIM], dst))
                dq = (jnp.concatenate(dq_t, axis=0) * 0.125).T
                dq_all[here, cols(0)] = dq.astype(LOW)
                dq_all[here, cols(1)] = dk.astype(LOW)
                dq_all[here, cols(2)] = dv.astype(LOW)
                bsum[0:1, cols(0)] += jnp.sum(dq, axis=0, keepdims=True)
                bsum[0:1, cols(2)] += jnp.sum(dv, axis=0, keepdims=True)
                step = p * (groups * tiles) + hp

                @pl.when(step == 0)
                def _():
                    loop(4, lambda i: ff_y(1, 0, i))

                @pl.when((step == 2) | (step == 13))
                def _():
                    loop(3, lambda i: ff_z(1, 1 - step // 13, i))

                @pl.when((step >= 3) & (step < 7))
                def _():
                    loop(2, lambda i: p_y(0, 1 - (step - 3) // 2, 2 * lax.rem(step - 3, 2) + i))

                @pl.when((step == 18) | (step == 19))
                def _():
                    loop(3, lambda i: p_z(0, 19 - step, i))

                @pl.when((step == 16) | (step == 21))
                def _():
                    ff_x((step - 16) // 5)

            loop(groups * tiles, heads)

            @pl.when(p == 0)
            def _():
                w_qkv_copy.wait()

            done = sum(
                dot(dq_all[here, mm * 3 * lw : (mm + 1) * 3 * lw], w_ref[mm, :, : 3 * lw], NT) for mm in range(groups))
            xhat, r = moments(x_buf[slot].astype(F32))
            dg = done * vec_ref[0:1]
            dn = r * (dg - jnp.mean(dg, axis=-1, keepdims=True) - xhat * jnp.mean(dg * xhat, axis=-1, keepdims=True))
            n1[here] = (dhid + dn).astype(LOW)
            for copy in tok_copies(p):
                copy.start()
            sums[0:1] += jnp.sum(done * xhat, axis=0, keepdims=True)
            sums[1:2] += jnp.sum(done, axis=0, keepdims=True)

        loop(pairs, one_pair)

        def small_copy(slot, src, to, sem):
            return pltpu.make_async_remote_copy(
                src_ref=sbuf.at[src], dst_ref=sbuf.at[slot], send_sem=ssem.at[0, sem], recv_sem=ssem.at[1, sem],
                device_id={"dp": to[0], "mp": to[1]}, device_id_type=MESH_ID,
            )

        sbuf[6] = jnp.zeros_like(sbuf[6])
        sbuf[6, 0:1] = bsum_up[0:1]
        sbuf[6, 1:2, : 3 * width] = bsum[0:1]
        for n, (line, at) in enumerate(((2, 0), (2, 1), (2, 2), (3, 1), (2, 3), (3, 0))):
            sbuf[6, line : line + 1, at * width : (at + 1) * width] = sums[n : n + 1]
        s0 = small_copy(0, 6, sib, 0)
        s1 = small_copy(1, 7, (index(z, 1 - y, c), m), 1)
        zs = [small_copy(1 + k, 8, beside(k), 1 + k) for k in (1, 2, 3)]
        s2 = small_copy(5, 9, (me, 1 - m), 5)
        s0.start()

        def chunk(i):
            mm = lax.rem(m + 1 + i // 3, 2)
            at = pl.ds(pl.multiple_of(mm * 3 * lw + lax.rem(i, 3) * lw, 128), lw)
            g_qkv[0, :, :, :, at] = dot(n1t[...], dq_all[:, at]).astype(LOW).reshape(Z * Y, C, part, lw)

            @pl.when(i == 0)
            def _():
                s0.wait()
                sbuf[7] = sbuf[6] + sbuf[0]
                s1.start()

            @pl.when(i == 1)
            def _():
                p_x(0)

            @pl.when(lax.rem(i, 3) == 2)
            def _():
                q_sib(0, 1 - i // 3)

            @pl.when(i == 2)
            def _():
                s1.wait()
                sbuf[8] = sbuf[7] + sbuf[1]
                for copy in zs:
                    copy.start()

            @pl.when(i == 3)
            def _():
                loop(4, lambda k: q_y(0, 1, k))

            @pl.when(i == 4)
            def _():
                for copy in zs:
                    copy.wait()
                sbuf[9] = sbuf[8] + sbuf[2] + sbuf[3] + sbuf[4]
                s2.start()

        loop(6, chunk)
        ff_final(0)
        loop(4, lambda i: q_y(0, 0, i))
        loop(3, lambda i: q_z(0, 1, i))
        ff_final(1)
        s2.wait()
        sbuf[6] = sbuf[9] + sbuf[5]
        o_up[...] = sbuf[6, 0:1, pl.ds(pl.multiple_of(m * fw, 128), fw)].reshape(fw)
        for n in range(2):
            o_qv[n : n + 1] = sbuf[6, 1:2, pl.ds(pl.multiple_of((3 * m + 2 * n) * lw, 128), lw)]
        dp = lax.axis_index("dp")
        for n, (line, at) in enumerate(((2, 0), (2, 1), (2, 2), (3, 1), (2, 3), (3, 0))):
            row = sbuf[6, line : line + 1, at * width : (at + 1) * width]
            pick = row[:, :part]
            for d in range(1, Z * Y * C):
                pick = jnp.where(dp == d, row[:, d * part : (d + 1) * part], pick)
            o_vec[n : n + 1] = pick
        p_final(0)
        q_x(0)
        loop(3, lambda i: q_z(0, 0, i))
        q_final(0)

        def finish(p):
            for copy in tok_copies(p):
                copy.wait()

        loop(pairs, finish)

        def finish_out(q):
            for copy in out_copies(q):
                copy.wait()

        loop(pairs, finish_out)

    pl.run_scoped(
        attention,
        pltpu.VMEM(w_one_in.shape, LOW), pltpu.VMEM((2, rows, 3 * width), LOW), pltpu.VMEM((2, HEADS, rows, rows), LOW),
        pltpu.VMEM((2, rows, width), LOW), pltpu.VMEM((pairs, rows, width), LOW),
        pltpu.VMEM((high, width), LOW), pltpu.VMEM((width, high), LOW), pltpu.VMEM((high, 3 * width), LOW),
    )


def backward_reduce(counts, tokens, cotangent, hid, n2, att, n1, qkv, prob, w_one, w_two, bias, vec):
    pairs, rows, width = n1.shape
    flat = pairs * rows
    part = width // (Z * Y * C)
    fw = w_two.shape[2] // 2
    hbm = pl.BlockSpec(memory_space=pl.ANY)
    vm = pl.BlockSpec(memory_space=pltpu.VMEM)
    kinds = ((2, fw), (1, width // 2), (1, 3 * width // 2))
    scratch = [pltpu.VMEM((n, Z * Y, C, part, 2 * w), LOW) for n, w in kinds]
    for n, w in kinds:
        scratch += [pltpu.VMEM((n * k, part, w), LOW) for k in (16, 8, 6, 1)]
    scratch += [
        pltpu.VMEM((flat, width), F32), pltpu.VMEM((pairs, rows, width), LOW), pltpu.VMEM((8, width), F32),
        pltpu.VMEM((8, 3 * width), F32), pltpu.VMEM((8, 2 * fw), F32), pltpu.VMEM((10, 8, 2 * fw), F32),
        pltpu.SemaphoreType.DMA((4, BLOCKS)), pltpu.SemaphoreType.DMA((4, BLOCKS)), pltpu.SemaphoreType.DMA((9,)),
        pltpu.SemaphoreType.DMA((3, pairs)), pltpu.SemaphoreType.DMA((3, pairs)), pltpu.SemaphoreType.DMA((2, 6)),
        pltpu.SemaphoreType.DMA((pairs,)),
    ]
    plane = lambda a: a.reshape(-1, width)
    return pl.pallas_call(
        back_kernel,
        in_specs=[pl.BlockSpec(memory_space=pltpu.SMEM)] + [hbm] * 10 + [vm] * 2,
        out_specs=[hbm] * 2 + [vm] * 7,
        out_shape=[
            jax.ShapeDtypeStruct((2 * pairs, rows, width), LOW), jax.ShapeDtypeStruct((2 * pairs, rows, width), LOW),
            jax.ShapeDtypeStruct((part, fw), F32), jax.ShapeDtypeStruct((part, fw), F32),
            jax.ShapeDtypeStruct((1, part, width // 2), F32),
            jax.ShapeDtypeStruct((3, part, width // 2), F32), jax.ShapeDtypeStruct((fw,), F32),
            jax.ShapeDtypeStruct((2, width // 2), F32), jax.ShapeDtypeStruct((6, part), F32),
        ],
        scratch_shapes=scratch,
        compiler_params=pltpu.CompilerParams(collective_id=1, has_side_effects=True, vmem_limit_bytes=63 * 2**20),
        name="backward_reduce",
    )(counts, plane(cotangent), plane(hid), plane(n2), plane(att), n1, qkv, prob, tokens, w_one, w_two, bias, vec)


def per_device(
    patch_counts, tokens, cotangent, attn_gain, attn_shift, w_qkv, b_qv, w_proj, b_proj,
    ffn_gain, ffn_shift, w_up, b_up, w_down, b_down,
):
    pairs_all, rows, width = tokens.shape
    n_mp = lax.axis_size("mp")
    n_dp = lax.axis_size("dp")
    pairs = pairs_all // n_mp
    direct = n_dp == Z * Y * C and n_mp == 2 and pairs == 4
    part = w_qkv.shape[0]
    lw = w_qkv.shape[2]
    fw = w_up.shape[1]
    mine = lax.axis_index("mp")
    vectors = [attn_gain, attn_shift, b_proj, ffn_gain, ffn_shift, b_down]
    if direct:
        w_one, w_two, bias, qkv, att, prob, hid, n1, n2, vec = gather_attention(
            patch_counts, tokens, w_qkv, w_proj, w_up, w_down, b_qv, b_up, vectors)
        block_out, tokens_grad, r_down, r_up, r_proj, r_qkv, o_b_up, o_b_qv, o_vec = backward_reduce(
            patch_counts, tokens, cotangent, hid, n2, att, n1, qkv, prob, w_one, w_two, bias, vec)
        o_gain, o_shift, o_b_proj, o_b_down, o_ffn_gain, o_ffn_shift = [o_vec[i] for i in range(6)]
        return (
            block_out, tokens_grad, o_gain, o_shift, r_qkv.transpose(1, 0, 2), o_b_qv,
            r_proj[0].T, o_b_proj, o_ffn_gain, o_ffn_shift, r_up, o_b_up, r_down.T, o_b_down,
        )

    off = jnp.reshape(mine * pairs, (1,)).astype(jnp.int32)
    lens = TEXT + lax.dynamic_slice_in_dim(patch_counts, mine * pairs, pairs, 0)
    first = jnp.concatenate(
        [w_qkv.reshape(part, 3 * lw), w_proj.T, jnp.stack(vectors, axis=1), jnp.zeros((part, EXTRA - 6), F32)], axis=1
    ).astype(LOW)
    second = jnp.concatenate([w_up, w_down.T], axis=1).astype(LOW)
    bias = jnp.concatenate([b_qv.reshape(-1), b_up]).astype(LOW).astype(F32)
    bias = jnp.broadcast_to(bias, (8,) + bias.shape)
    both_axes = ("mp", "dp")
    w_one = lax.all_gather(first, both_axes, axis=0, tiled=True).reshape(n_mp, width, -1)
    w_two = lax.all_gather(second, both_axes, axis=0, tiled=True).reshape(n_mp, width, -1)
    bias = lax.all_gather(bias, "mp", axis=0)
    qkv, att, prob, hid, n1, n2, vec = attention_forward(lens, off, tokens, w_one, bias)

    def grad(left, right):
        return jnp.einsum(
            "rd,rf->df", left.reshape(pairs * rows, width), right.reshape(pairs * rows, -1),
            preferred_element_type=F32,
        )

    def reduce(grads, small):
        axes = ("mp", "dp")
        done = [
            lax.psum_scatter(
                g.reshape(width, n_mp, -1).swapaxes(0, 1).reshape(n_mp * width, -1), axes,
                scatter_dimension=0, tiled=True,
            )
            for g in grads
        ]
        return done + [lax.psum(small, axes)]

    def both(array):
        other = lax.ppermute(array, "mp", [(0, 1), (1, 0)])
        return jnp.where(mine == 0, jnp.concatenate([array, other]), jnp.concatenate([other, array]))

    out_here, act, dpre, dhid, dlow, upl, sums_two, bsum_up = ffn(lens, off, n2, hid, cotangent, w_two, bias, vec)
    block_out = both(out_here)
    tok_here, dqkv, sums_one, bsum_qkv = attention_backward(lens, off, tokens, dhid, qkv, prob, w_one, vec)
    tokens_grad = both(tok_here)
    flat = bsum_qkv[0].reshape(n_mp, 3, lw)
    small = jnp.concatenate([
        sums_one[0], sums_one[1], sums_two[2], sums_two[0], sums_two[1], sums_two[3],
        flat[:, 0].reshape(-1), flat[:, 2].reshape(-1), bsum_up[0]])
    r_up, r_down, r_proj, r_qkv, small = reduce(
        [grad(n2, dpre), grad(upl, act), grad(dlow, att), grad(n1, dqkv)], small)
    place_dp = lax.axis_index("dp") * part

    def piece(i):
        return lax.dynamic_slice_in_dim(small, i * width + place_dp, part, 0)

    rest = small[6 * width :]
    o_b_q = lax.dynamic_slice_in_dim(rest, mine * lw, lw, 0)
    o_b_v = lax.dynamic_slice_in_dim(rest, (n_mp + mine) * lw, lw, 0)
    o_b_up = lax.dynamic_slice_in_dim(rest, 2 * n_mp * lw + mine * fw, fw, 0)
    return (
        block_out, tokens_grad, piece(0), piece(1),
        r_qkv.reshape(part, 3, lw), jnp.stack([o_b_q, o_b_v]),
        r_proj.T, piece(2), piece(3), piece(4), r_up, o_b_up, r_down.T, piece(5),
    )


def solution(mesh):
    vec, mat = P("dp"), P("dp", "mp")
    tok = P("dp", None, None)
    in_specs = (
        vec, tok, tok, vec, vec, P("dp", None, "mp"), P(None, "mp"), P("mp", "dp"), vec, vec, vec,
        mat, P("mp"), P("mp", "dp"), vec,
    )
    out_specs = (
        tok, tok, vec, vec, P("dp", None, "mp"), P(None, "mp"), P("mp", "dp"), vec, vec, vec,
        mat, P("mp"), P("mp", "dp"), vec,
    )
    return jax.shard_map(per_device, mesh=mesh, in_specs=in_specs, out_specs=out_specs, check_vma=False)
```

```python
import functools

import jax
import jax.numpy as jnp
from jax import lax
from jax.experimental import pallas as pl
from jax.experimental.pallas import tpu as pltpu
from jax.sharding import PartitionSpec as P

HEADS = 12
HEAD_DIM = 64
TEXT = 40
LOW = jnp.bfloat16
F32 = jnp.float32
EXTRA = 128
NT = (((1,), (1,)), ((), ()))
NN = (((1,), (0,)), ((), ()))


def dot(a, b, dims=NN):
    return lax.dot_general(a, b, dims, preferred_element_type=F32)


def moments(v):
    center = v - jnp.mean(v, axis=-1, keepdims=True)
    spread = jnp.mean(center * center, axis=-1, keepdims=True)
    r = lax.rsqrt(spread + 1e-06)
    return center * r, r


def row_ids(rows):
    return lax.broadcasted_iota(jnp.int32, (rows, 1), 0)


def attn_body(p, count, x, w_ref, bias_ref, vec_ref, qkv_ref, att_ref, prob_ref, hid_ref, n1_ref, n2_ref, hook):
    rows, width = x.shape
    groups = w_ref.shape[0]
    lw = width // groups
    tiles = lw // 128
    x = x.astype(F32)
    xhat, _ = moments(x)
    n1 = (xhat * vec_ref[0:1] + vec_ref[1:2]).astype(LOW)
    n1_ref[0] = n1
    for m in range(groups):
        y = dot(n1, w_ref[m, :, : 3 * lw])
        base = m * 3 * lw
        qkv_ref[0, :, base : base + lw] = (y[:, :lw] + bias_ref[m, 0:1, :lw]).astype(LOW)
        qkv_ref[0, :, base + lw : base + 2 * lw] = y[:, lw : 2 * lw].astype(LOW)
        qkv_ref[0, :, base + 2 * lw : base + 3 * lw] = (
            y[:, 2 * lw :] + bias_ref[m, 0:1, lw : 2 * lw]
        ).astype(LOW)
    keep = row_ids(rows) < count
    first = lax.broadcasted_iota(jnp.int32, (1, 128), 1) < HEAD_DIM

    def pair(hp, carry):
        base = (hp // tiles) * 3 * lw + lax.rem(hp, tiles) * 128

        def cols(t):
            return pl.ds(pl.multiple_of(base + t * lw, 128), 128)

        q2 = qkv_ref[0, :, cols(0)] * 0.125
        k2 = qkv_ref[0, :, cols(1)]
        v2t = qkv_ref[0, :, cols(2)].T
        outs = []
        for h in range(2):
            qh = jnp.where(first if h == 0 else ~first, q2, 0)
            st = dot(k2, qh, NT)
            st = jnp.where(keep, st, -1e30)
            e = jnp.exp(st - jnp.max(st, axis=0, keepdims=True))
            pt = (e * (1.0 / jnp.sum(e, axis=0, keepdims=True))).astype(LOW)
            prob_ref[0, hp * 2 + h] = pt
            outs.append(dot(v2t[h * HEAD_DIM : (h + 1) * HEAD_DIM], pt))
        att_ref[0, :, pl.ds(pl.multiple_of(hp * 128, 128), 128)] = jnp.concatenate(outs, axis=0).T.astype(LOW)
        hook(hp)
        return carry

    lax.fori_loop(0, groups * tiles, pair, 0)
    proj = sum(dot(att_ref[0, :, m * lw : (m + 1) * lw], w_ref[m, :, 3 * lw : 4 * lw], NT) for m in range(groups))
    hid = x + proj + vec_ref[2:3]
    hid_ref[0] = hid
    xhat2, _ = moments(hid)
    n2_ref[0] = (xhat2 * vec_ref[3:4] + vec_ref[4:5]).astype(LOW)


def attn_kernel(lens, off, x_ref, w_ref, bias_ref, qkv_ref, att_ref, prob_ref, hid_ref, n1_ref, n2_ref, vec_ref):
    p = pl.program_id(0)
    lw = x_ref.shape[2] // w_ref.shape[0]

    @pl.when(p == 0)
    def _():
        vec_ref[...] = w_ref[0, :, 4 * lw :].astype(F32).T[:8]

    attn_body(p, lens[p], x_ref[0], w_ref, bias_ref, vec_ref, qkv_ref, att_ref, prob_ref, hid_ref, n1_ref, n2_ref,
              lambda hp: None)


def const_spec(shape):
    return pl.BlockSpec(shape, lambda *_: (0,) * len(shape), pipeline_mode=pl.Buffered(1))


def pair_spec(*shape):
    return pl.BlockSpec((1,) + shape, lambda p, *_: (p,) + (0,) * len(shape))


def attention_forward(lens, off, tokens, w_one, bias):
    pairs = lens.shape[0]
    _, rows, width = tokens.shape
    out = lambda dt, *s: jax.ShapeDtypeStruct((pairs,) + s, dt)
    return pl.pallas_call(
        attn_kernel,
        grid_spec=pltpu.PrefetchScalarGridSpec(
            num_scalar_prefetch=2,
            grid=(pairs,),
            in_specs=[
                pl.BlockSpec((1, rows, width), lambda p, lens, off: (off[0] + p, 0, 0)),
                const_spec(w_one.shape),
                const_spec(bias.shape),
            ],
            out_specs=[
                pair_spec(rows, 3 * width), pair_spec(rows, width), pair_spec(HEADS, rows, rows),
                pair_spec(rows, width), pair_spec(rows, width), pair_spec(rows, width),
                pl.BlockSpec((8, width), lambda *_: (0, 0)),
            ],
        ),
        out_shape=[
            out(LOW, rows, 3 * width), out(LOW, rows, width), out(LOW, HEADS, rows, rows),
            out(F32, rows, width), out(LOW, rows, width), out(LOW, rows, width),
            jax.ShapeDtypeStruct((8, width), F32),
        ],
        compiler_params=pltpu.CompilerParams(vmem_limit_bytes=60 * 2**20),
        name="attention_forward",
    )(lens, off, tokens, w_one, bias)


def ffn_kernel(lens, off, n2_ref, hid_ref, cot_ref, w_ref, bias_ref, vec_ref,
               out_ref, act_ref, dpre_ref, dhid_ref, dlow_ref, upl_ref, sums_ref, bsum_ref):
    p = pl.program_id(0)
    rows, width = n2_ref.shape[1], n2_ref.shape[2]
    groups = w_ref.shape[0]
    fw = w_ref.shape[2] // 2
    lw = width // groups
    step = 512
    keep = row_ids(rows) < lens[p]
    n2 = n2_ref[0]
    upl = jnp.where(keep, cot_ref[0], 0)
    upl_ref[0] = upl

    @pl.when(p == 0)
    def _():
        sums_ref[...] = jnp.zeros_like(sums_ref)
        bsum_ref[...] = jnp.zeros_like(bsum_ref)

    for m in range(groups):
        for c in range(0, fw, step):
            pre = dot(n2, w_ref[m, :, c : c + step]) + bias_ref[m, 0:1, 2 * lw + c : 2 * lw + c + step]
            cdf = 0.5 * (1.0 + lax.erf(pre * (2.0 ** -0.5)))
            at = m * fw + c
            act_ref[0, :, at : at + step] = (pre * cdf).astype(LOW)
            slope = cdf + pre * (0.3989422804014327 * jnp.exp(-0.5 * pre * pre))
            dpre = slope * dot(upl, w_ref[m, :, fw + c : fw + c + step])
            dpre_ref[0, :, at : at + step] = dpre.astype(LOW)
            bsum_ref[0:1, at : at + step] += jnp.sum(dpre, axis=0, keepdims=True)
    hid = hid_ref[0]
    down = sum(dot(act_ref[0, :, m * fw : (m + 1) * fw], w_ref[m, :, fw:], NT) for m in range(groups))
    out_ref[0] = jnp.where(keep, hid + down + vec_ref[5:6], 0.0).astype(LOW)
    dtwo = sum(dot(dpre_ref[0, :, m * fw : (m + 1) * fw], w_ref[m, :, :fw], NT) for m in range(groups))
    xhat, r = moments(hid)
    dg = dtwo * vec_ref[3:4]
    dn = r * (dg - jnp.mean(dg, axis=-1, keepdims=True) - xhat * jnp.mean(dg * xhat, axis=-1, keepdims=True))
    upf = upl.astype(F32)
    dhid = upf + dn
    dhid_ref[0] = dhid
    dlow_ref[0] = dhid.astype(LOW)
    sums_ref[0:1] += jnp.sum(dtwo * xhat, axis=0, keepdims=True)
    sums_ref[1:2] += jnp.sum(dtwo, axis=0, keepdims=True)
    sums_ref[2:3] += jnp.sum(dhid, axis=0, keepdims=True)
    sums_ref[3:4] += jnp.sum(upf, axis=0, keepdims=True)


def ffn(lens, off, n2, hid, cotangent, w_two, bias, vec):
    pairs, rows, width = n2.shape
    ff = w_two.shape[0] * w_two.shape[2] // 2
    out = lambda dt, *s: jax.ShapeDtypeStruct((pairs,) + s, dt)
    return pl.pallas_call(
        ffn_kernel,
        grid_spec=pltpu.PrefetchScalarGridSpec(
            num_scalar_prefetch=2,
            grid=(pairs,),
            in_specs=[
                pair_spec(rows, width), pair_spec(rows, width),
                pl.BlockSpec((1, rows, width), lambda p, lens, off: (off[0] + p, 0, 0)),
                const_spec(w_two.shape), const_spec(bias.shape), const_spec(vec.shape),
            ],
            out_specs=[
                pair_spec(rows, width), pair_spec(rows, ff), pair_spec(rows, ff), pair_spec(rows, width),
                pair_spec(rows, width), pair_spec(rows, width),
                pl.BlockSpec((8, width), lambda *_: (0, 0)), pl.BlockSpec((8, ff), lambda *_: (0, 0)),
            ],
        ),
        out_shape=[
            out(LOW, rows, width), out(LOW, rows, ff), out(LOW, rows, ff), out(F32, rows, width),
            out(LOW, rows, width), out(LOW, rows, width),
            jax.ShapeDtypeStruct((8, width), F32), jax.ShapeDtypeStruct((8, ff), F32),
        ],
        compiler_params=pltpu.CompilerParams(vmem_limit_bytes=60 * 2**20),
        name="feed_forward",
    )(lens, off, n2, hid, cotangent, w_two, bias, vec)


def plain_back_kernel(lens, off, x_ref, dhid_ref, qkv_ref, prob_ref, w_ref, vec_ref,
                tok_ref, dqkv_ref, sums_ref, bsum_ref, do_ref):
    p = pl.program_id(0)
    rows, width = x_ref.shape[1], x_ref.shape[2]
    groups = w_ref.shape[0]
    lw = width // groups
    tiles = lw // 128

    @pl.when(p == 0)
    def _():
        sums_ref[...] = jnp.zeros_like(sums_ref)
        bsum_ref[...] = jnp.zeros_like(bsum_ref)

    dhid = dhid_ref[0]
    dlow = dhid.astype(LOW)
    for m in range(groups):
        do_ref[:, m * lw : (m + 1) * lw] = dot(dlow, w_ref[m, :, 3 * lw : 4 * lw]).astype(LOW)
    first = lax.broadcasted_iota(jnp.int32, (1, 128), 1) < HEAD_DIM

    def pair(hp, carry):
        base = (hp // tiles) * 3 * lw + (hp % tiles) * 128

        def cols(t):
            return pl.ds(pl.multiple_of(base + t * lw, 128), 128)

        q2 = qkv_ref[0, :, cols(0)] * 0.125
        k2t = qkv_ref[0, :, cols(1)].T
        v2 = qkv_ref[0, :, cols(2)]
        do2 = do_ref[:, pl.ds(pl.multiple_of(hp * 128, 128), 128)]
        dq_t = []
        dk = dv = 0.0
        for h in range(2):
            mine = first if h == 0 else ~first
            doh = jnp.where(mine, do2, 0)
            qh = jnp.where(mine, q2, 0)
            dpt = dot(v2, doh, NT)
            plow = prob_ref[0, hp * 2 + h]
            pt = plow.astype(F32)
            inner = jnp.sum(pt * dpt, axis=0, keepdims=True)
            dst = (pt * (dpt - inner)).astype(LOW)
            dv = dv + dot(plow, doh)
            dk = dk + dot(dst, qh)
            dq_t.append(dot(k2t[h * HEAD_DIM : (h + 1) * HEAD_DIM], dst))
        dq = (jnp.concatenate(dq_t, axis=0) * 0.125).T
        dqkv_ref[0, :, cols(0)] = dq.astype(LOW)
        dqkv_ref[0, :, cols(1)] = dk.astype(LOW)
        dqkv_ref[0, :, cols(2)] = dv.astype(LOW)
        bsum_ref[0:1, cols(0)] += jnp.sum(dq, axis=0, keepdims=True)
        bsum_ref[0:1, cols(2)] += jnp.sum(dv, axis=0, keepdims=True)
        return carry

    lax.fori_loop(0, groups * tiles, pair, 0)
    done = sum(dot(dqkv_ref[0, :, m * 3 * lw : (m + 1) * 3 * lw], w_ref[m, :, : 3 * lw], NT) for m in range(groups))
    xhat, r = moments(x_ref[0].astype(F32))
    dg = done * vec_ref[0:1]
    dn = r * (dg - jnp.mean(dg, axis=-1, keepdims=True) - xhat * jnp.mean(dg * xhat, axis=-1, keepdims=True))
    tok_ref[0] = (dhid + dn).astype(LOW)
    sums_ref[0:1] += jnp.sum(done * xhat, axis=0, keepdims=True)
    sums_ref[1:2] += jnp.sum(done, axis=0, keepdims=True)


def attention_backward(lens, off, tokens, dhid, qkv, prob, w_one, vec):
    pairs, rows, width = dhid.shape
    out = lambda dt, *s: jax.ShapeDtypeStruct((pairs,) + s, dt)
    return pl.pallas_call(
        plain_back_kernel,
        grid_spec=pltpu.PrefetchScalarGridSpec(
            num_scalar_prefetch=2,
            grid=(pairs,),
            in_specs=[
                pl.BlockSpec((1, rows, width), lambda p, lens, off: (off[0] + p, 0, 0)),
                pair_spec(rows, width), pair_spec(rows, 3 * width), pair_spec(HEADS, rows, rows),
                const_spec(w_one.shape), const_spec(vec.shape),
            ],
            out_specs=[
                pair_spec(rows, width), pair_spec(rows, 3 * width),
                pl.BlockSpec((8, width), lambda *_: (0, 0)), pl.BlockSpec((8, 3 * width), lambda *_: (0, 0)),
            ],
            scratch_shapes=[pltpu.VMEM((rows, width), LOW)],
        ),
        out_shape=[
            out(LOW, rows, width), out(LOW, rows, 3 * width),
            jax.ShapeDtypeStruct((8, width), F32), jax.ShapeDtypeStruct((8, 3 * width), F32),
        ],
        compiler_params=pltpu.CompilerParams(vmem_limit_bytes=60 * 2**20),
        name="attention_backward",
    )(lens, off, tokens, dhid, qkv, prob, w_one, vec)
MESH_ID = pl.DeviceIdType.MESH
Z, Y, C = 4, 2, 2


def place():
    dp = lax.axis_index("dp")
    m = lax.axis_index("mp")
    c = lax.rem(dp, 2)
    y = lax.rem(dp // 2, 2)
    z = dp // 4
    return z, y, c, m


def index(z, y, c):
    return (z * Y + y) * C + c


def flips(y, c, m):
    one = (y + c * (1 - 2 * y), m + (1 - c) * (1 - 2 * m))
    two = (y + (1 - c) * (1 - 2 * y), m + c * (1 - 2 * m))
    return one, two


def greet(z, y, c, m):
    barrier = pltpu.get_barrier_semaphore()
    (y1, m1), (y2, m2) = flips(y, c, m)
    peers = [(index(lax.rem(z + k, Z), y, c), m) for k in (1, 2, 3)]
    peers += [(index(z, y1, c), m1), (index(z, y2, c), m2), (index(z, y, 1 - c), m)]
    for dp, mp in peers:
        pl.semaphore_signal(barrier, inc=1, device_id={"dp": dp, "mp": mp}, device_id_type=MESH_ID)
    pl.semaphore_wait(barrier, len(peers))
    return peers


def gather_attn_kernel(counts, tok_all, wq_in, wp_in, wu_in, wd_in, bq_in, bu_in, v0, v1, v2, v3, v4, v5,
                       w_one_out, w_two, b_out, qkv_ref, att_ref, prob_ref, hid_ref, n1_ref, n2_ref, vec_ref,
                       w_one, bias, xbuf, first_ref, second_ref, b_in, vbuf, send, recv, bsem, local):
    p = pl.program_id(0)
    z, y, c, m = place()
    (y1, m1), (y2, m2) = flips(y, c, m)
    pairs, rows, width = xbuf.shape
    part = first_ref.shape[0]
    cols = second_ref.shape[1] // 2
    lw = width // 2
    per_pair = width // 128
    me = index(z, y, c)
    one, two, sib = (index(z, y1, c), m1), (index(z, y2, c), m2), (index(z, y, 1 - c), m)

    def spot(g, dp, mp):
        at = pl.ds(pl.multiple_of(dp * part, part), part)
        if g is None:
            return w_one.at[mp, at]
        return w_two.at[mp, at, pl.ds(pl.multiple_of(g * cols, 128), cols)]

    def shard(g):
        return first_ref if g is None else second_ref.at[:, pl.ds(pl.multiple_of(g * cols, 128), cols)]

    def row(g):
        return 0 if g is None else g + 1

    def copy_of(g, src, dst, out_sem, in_sem, to):
        return pltpu.make_async_remote_copy(
            src_ref=src, dst_ref=dst, send_sem=send.at[row(g), out_sem], recv_sem=recv.at[row(g), in_sem],
            device_id={"dp": to[0], "mp": to[1]}, device_id_type=MESH_ID,
        )

    def push(g, src, dp, mp, to, sem):
        copy_of(g, src, spot(g, dp, mp), sem, mp * (Z * Y * C) + dp, to).start()

    def arrived(g, dp, mp):
        at = spot(g, dp, mp)
        copy_of(g, at, at, 0, mp * (Z * Y * C) + dp, sib).wait_recv()
        return at

    def own_z(g):
        for k in (1, 3, 2):
            push(g, shard(g), me, m, (index(lax.rem(z + k, Z), y, c), m), k - 1)

    def own_near(g):
        for n, to in enumerate((one, two, sib)):
            push(g, shard(g), me, m, to, 3 + n)

    def event_z(g, i):
        dp = index(lax.rem(z + 1 + lax.rem(2 * i, 3), Z), y, c)
        at = arrived(g, dp, m)
        for n, to in enumerate((one, two, sib)):
            push(g, at, dp, m, to, 6 + 3 * i + n)

    def event_one(g, i):
        dp = index(lax.rem(z + i, Z), y1, c)
        at = arrived(g, dp, m1)
        for n, to in enumerate((two, sib)):
            push(g, at, dp, m1, to, 15 + 2 * i + n)

    def event_two(g, i):
        far = lax.rem(i, 2)
        yy = y2 + far * (1 - y - y2)
        mm = m2 + far * (1 - m - m2)
        dp = index(lax.rem(z + i // 2, Z), yy, c)
        push(g, arrived(g, dp, mm), dp, mm, sib, 23 + i)

    def event_core(g, i):
        arrived(g, index(i // 4, lax.rem(i // 2, 2), 1 - c), lax.rem(i, 2))

    def loop(n, event, g):
        def run(i, carry):
            event(g, i)
            return carry

        lax.fori_loop(0, n, run, 0)

    bias_copy = pltpu.make_async_remote_copy(
        src_ref=b_in, dst_ref=bias.at[m], send_sem=bsem.at[0], recv_sem=bsem.at[1],
        device_id={"dp": me, "mp": 1 - m}, device_id_type=MESH_ID,
    )
    x_copy = pltpu.make_async_copy(tok_all.at[pl.ds(m * pairs, pairs)], xbuf, local.at[0])
    mine = [
        pltpu.make_async_copy(b_in, bias.at[m], local.at[1]),
        pltpu.make_async_copy(first_ref, spot(None, me, m), local.at[2]),
    ]
    mine_two = [pltpu.make_async_copy(shard(g), spot(g, me, m), local.at[3 + g]) for g in range(2)]
    keep_one = pltpu.make_async_copy(w_one, w_one_out, local.at[5])
    keep_bias = pltpu.make_async_copy(bias, b_out, local.at[6])

    @pl.when(p == 0)
    def _():
        x_copy.start()
        for t in range(3):
            first_ref[:, t * lw : (t + 1) * lw] = wq_in[t].astype(LOW)
        first_ref[:, 3 * lw : 4 * lw] = wp_in[...].astype(LOW)
        vbuf[...] = jnp.zeros_like(vbuf)
        for n, v in enumerate((v0, v1, v2, v3, v4, v5)):
            vbuf[n : n + 1, :part] = v[...]
        first_ref[:, 4 * lw :] = vbuf[...].T[:part].astype(LOW)
        second_ref[:, :cols] = wu_in[...].astype(LOW)
        second_ref[:, cols:] = wd_in[...].astype(LOW)
        b_in[...] = jnp.zeros_like(b_in)
        b_in[0:1, :lw] = bq_in[0:1].astype(LOW).astype(F32)
        b_in[0:1, lw : 2 * lw] = bq_in[1:2].astype(LOW).astype(F32)
        b_in[0:1, 2 * lw :] = bu_in[...].reshape(1, cols).astype(LOW).astype(F32)
        greet(z, y, c, m)
        own_z(None)
        own_near(None)
        bias_copy.start()
        for copy in mine + mine_two:
            copy.start()
        loop(3, event_z, None)
        own_z(0)
        own_z(1)
        loop(4, event_one, None)
        own_near(0)
        loop(3, event_z, 0)
        loop(8, event_two, None)
        for copy in mine + [x_copy, bias_copy]:
            copy.wait()
        loop(16, event_core, None)
        keep_one.start()
        keep_bias.start()
        vec_ref[...] = w_one[0, :, 4 * lw :].astype(F32).T[:8]

    def hook(hp):
        step = p * per_pair + hp

        def event(e, carry):
            @pl.when(e == 0)
            def _():
                own_near(1)

            @pl.when(((e >= 1) & (e < 5)) | ((e >= 16) & (e < 20)))
            def _():
                g = e // 16
                event_one(g, e - 1 - 15 * g)

            @pl.when((e >= 5) & (e < 8))
            def _():
                event_z(1, e - 5)

            @pl.when(((e >= 8) & (e < 16)) | (e >= 20))
            def _():
                g = e // 20
                event_two(g, e - 8 - 12 * g)

            return carry

        total = pairs * per_pair
        lax.fori_loop(step * 28 // total, (step + 1) * 28 // total, event, 0)

    attn_body(p, TEXT + counts[m * pairs + p], xbuf[p], w_one, bias, vec_ref, qkv_ref, att_ref, prob_ref, hid_ref, n1_ref, n2_ref, hook)

    @pl.when(p == pairs - 1)
    def _():
        for g in range(2):
            loop(16, event_core, g)
        for copy in mine_two + [keep_one, keep_bias]:
            copy.wait()
        for g in (None, 0, 1):
            def sent(i, carry):
                copy_of(g, shard(g), shard(g), i, 0, sib).wait_send()
                return carry

            lax.fori_loop(0, 31, sent, 0)


def gather_attention(counts, tokens, w_qkv, w_proj, w_up, w_down, b_qv, b_up, vectors):
    pairs = counts.shape[0] // 2
    _, rows, width = tokens.shape
    part, fw = w_up.shape
    lw = width // 2
    total = Z * Y * C
    hbm = pl.BlockSpec(memory_space=pl.ANY)
    out = lambda dt, *s: jax.ShapeDtypeStruct((pairs,) + s, dt)
    small = [w_qkv.transpose(1, 0, 2), w_proj.T, w_up, w_down.T, b_qv, b_up]
    small += [v.reshape(1, part) for v in vectors]
    one, two, bias = 4 * lw + EXTRA, 2 * fw, (8, 2 * lw + fw)
    return pl.pallas_call(
        gather_attn_kernel,
        grid_spec=pltpu.PrefetchScalarGridSpec(
            num_scalar_prefetch=1,
            grid=(pairs,),
            in_specs=[hbm] + [const_spec(a.shape) for a in small],
            out_specs=[
                hbm, hbm, hbm,
                pair_spec(rows, 3 * width), pair_spec(rows, width), pair_spec(HEADS, rows, rows),
                pair_spec(rows, width), pair_spec(rows, width), pair_spec(rows, width),
                pl.BlockSpec((8, width), lambda *_: (0, 0)),
            ],
            scratch_shapes=[
                pltpu.VMEM((2, width, one), LOW), pltpu.VMEM((2,) + bias, F32), pltpu.VMEM((pairs, rows, width), LOW),
                pltpu.VMEM((part, one), LOW), pltpu.VMEM((part, two), LOW), pltpu.VMEM(bias, F32),
                pltpu.VMEM((EXTRA, EXTRA), F32),
                pltpu.SemaphoreType.DMA((3, 31)), pltpu.SemaphoreType.DMA((3, 32)),
                pltpu.SemaphoreType.DMA((2,)), pltpu.SemaphoreType.DMA((7,)),
            ],
        ),
        out_shape=[
            jax.ShapeDtypeStruct((2, width, one), LOW),
            jax.ShapeDtypeStruct((2, width, two), LOW),
            jax.ShapeDtypeStruct((2,) + bias, F32),
            out(LOW, rows, 3 * width), out(LOW, rows, width), out(LOW, HEADS, rows, rows),
            out(F32, rows, width), out(LOW, rows, width), out(LOW, rows, width),
            jax.ShapeDtypeStruct((8, width), F32),
        ],
        compiler_params=pltpu.CompilerParams(collective_id=0, has_side_effects=True, vmem_limit_bytes=60 * 2**20),
        name="gather_attention",
    )(counts, tokens, *small)


BLOCKS = 31


def back_kernel(counts, cot, hid_in, n2_in, att_in, n1_all, qkv_all, prob_all, tok_all, w_one_in, w_two, bias_ref, vec_ref,
                block_out, tok_out, r_down, r_up, r_proj, r_qkv, o_up, o_qv, o_vec,
                g_ff, g_proj, g_qkv, rc_ff, rs_ff, rz_ff, rx_ff, rc_p, rs_p, rz_p, rx_p, rc_q, rs_q, rz_q, rx_q,
                dhid_ref, outbuf, sums, bsum, bsum_up, sbuf, send, recv, local, osem, tsem, ssem, n1_sem):
    flat, width = dhid_ref.shape
    pairs, rows = qkv_all.shape[0], qkv_all.shape[1]
    groups = w_two.shape[0]
    fw = w_two.shape[2] // 2
    fc = fw // 3
    lw = width // groups
    tiles = lw // 128
    half = flat // 2
    part = r_proj.shape[1]
    high = pairs * (rows + (-rows) % 16)
    z, y, c, m = place()
    me = index(z, y, c)
    sib = (index(z, y, 1 - c), m)

    def beside(k):
        return (index(lax.rem(z + k, Z), y, c), m)

    def loop(n, event):
        def one(i, carry):
            event(i)
            return carry

        lax.fori_loop(0, n, one, 0)

    def family(grad, rc, rs, rz, rx, out, row0, split):
        cols = rc.shape[2]
        fx = c * split
        near = (index(z, y + (1 - fx) * (1 - 2 * y), c), m + fx * (1 - 2 * m))
        far = (index(z, y + fx * (1 - 2 * y), c), m + (1 - fx) * (1 - 2 * m))

        def copy_of(u, src, dst, out_sem, in_sem, to):
            return pltpu.make_async_remote_copy(
                src_ref=src, dst_ref=dst, send_sem=send.at[row0 + u, out_sem], recv_sem=recv.at[row0 + u, in_sem],
                device_id={"dp": to[0], "mp": to[1]}, device_id_type=MESH_ID,
            )

        def swap(ra, rb, cc):
            f = cc * split
            return f * rb + (1 - f) * ra, f * ra + (1 - f) * rb

        def block(u, ra, rb, k, cc):
            dy, dm = swap(ra, rb, cc)
            yy = y + dy * (1 - 2 * y)
            mm = m + dm * (1 - 2 * m)
            return u, lax.rem(z + k, Z) * Y + yy, cc, slice(None), pl.ds(pl.multiple_of(mm * cols, 128), cols)

        def to_sibling(u, dm):
            def one(i):
                ra, rb = swap(1 - i // 4, dm, 1 - c)
                k = lax.rem(i + 1, 4)
                slot = (ra * 2 + rb) * 4 + k
                copy_of(u, grad.at[block(u, ra, rb, k, 1 - c)], rc.at[u * 16 + slot], slot, slot, sib).start()

            loop(8, one)

        def arrived(u, ref, sem):
            copy_of(u, ref, ref, 0, sem, sib).wait_recv()

        def base(u, ra, rb, k):
            slot = (ra * 2 + rb) * 4 + k
            arrived(u, rc.at[u * 16 + slot], slot)
            return grad[block(u, ra, rb, k, c)].astype(F32) + rc[u * 16 + slot].astype(F32)

        def level(u, rb, k):
            at = rb * 4 + k
            value = base(u, 0, rb, k)
            arrived(u, rs.at[u * 8 + at], 16 + at)
            return value + rs[u * 8 + at].astype(F32)

        def lined(u, rb):
            value = level(u, rb, 0)
            for k in (1, 2, 3):
                at = (k - 1) * 2 + rb
                arrived(u, rz.at[u * 6 + at], 24 + at)
                value = value + rz[u * 6 + at].astype(F32)
            return value

        def event_y(u, rb, i):
            k = lax.rem(i + 1, 4)
            slot = u * 16 + (2 + rb) * 4 + k
            at = rb * 4 + k
            rc[slot] = base(u, 1, rb, k).astype(LOW)
            copy_of(u, rc.at[slot], rs.at[u * 8 + at], 16 + at, 16 + at, near).start()

        def event_z(u, rb, i):
            k = 1 + i
            slot = u * 16 + rb * 4 + k
            at = (k - 1) * 2 + rb
            rc[slot] = level(u, rb, k).astype(LOW)
            copy_of(u, rc.at[slot], rz.at[u * 6 + at], 24 + at, 24 + at, beside(k)).start()

        def event_x(u):
            rc[u * 16 + 4] = lined(u, 1).astype(LOW)
            copy_of(u, rc.at[u * 16 + 4], rx.at[u], 30, 30, far).start()

        def final(u):
            value = lined(u, 0)
            arrived(u, rx.at[u], 30)
            out(u, value + rx[u].astype(F32))

            def one(i):
                copy_of(u, rc.at[0], rc.at[0], i, 0, sib).wait_send()

            loop(BLOCKS, one)

        return to_sibling, event_y, event_z, event_x, final

    def put(ref):
        def store(u, value):
            ref[u] = value

        return store

    def put_ff(u, value):
        (r_down, r_up)[u][...] = value

    def put_qkv(u, value):
        for t in range(3):
            r_qkv[t] = value[:, t * lw : (t + 1) * lw]

    ff_sib, ff_y, ff_z, ff_x, ff_final = family(g_ff, rc_ff, rs_ff, rz_ff, rx_ff, put_ff, 0, 0)
    p_sib, p_y, p_z, p_x, p_final = family(g_proj, rc_p, rs_p, rz_p, rx_p, put(r_proj), 2, 0)
    q_sib, q_y, q_z, q_x, q_final = family(g_qkv, rc_q, rs_q, rz_q, rx_q, put_qkv, 3, 0)

    def out_copies(q):
        src = outbuf.at[q]
        dst = block_out.at[m * pairs + q]
        return pltpu.make_async_copy(src, dst, osem.at[0, q]), pltpu.make_async_remote_copy(
            src_ref=src, dst_ref=dst, send_sem=osem.at[1, q], recv_sem=osem.at[2, q],
            device_id={"dp": me, "mp": 1 - m}, device_id_type=MESH_ID,
        )

    def keep_of(r):
        ids = row_ids(half)
        here = m * pairs + 2 * r
        return ids < TEXT + jnp.where(ids < rows, counts[here], counts[here + 1] + rows)

    def span(r):
        return pl.ds(pl.multiple_of(r * half, 16), half)

    sums[...] = jnp.zeros_like(sums)
    bsum[...] = jnp.zeros_like(bsum)
    bsum_up[...] = jnp.zeros_like(bsum_up)

    def feed_forward(n2, n2t, upl, uplt, hid, acc, slope, chunk, wbuf):
        def place_of(f):
            i = lax.rem(f, 6)
            return lax.rem(m + 1 + i // 3, 2), lax.rem(i, 3) * fc

        def weights(f):
            mm, at = place_of(f)
            slot = lax.rem(f, 2)
            return [
                pltpu.make_async_copy(
                    w_two.at[mm, :, pl.ds(pl.multiple_of(t * fw + at, 128), fc)], wbuf.at[slot, t], local.at[slot * 2 + t])
                for t in range(2)
            ]

        n2_copy = pltpu.make_async_copy(n2_in, n2, local.at[4])
        up_copy = pltpu.make_async_copy(cot.at[pl.ds(pl.multiple_of(m * flat, 16), flat)], upl, local.at[5])
        hid_copy = pltpu.make_async_copy(hid_in, hid, local.at[6])
        att_copy = pltpu.make_async_copy(att_in, slope.at[:, pl.ds(0, width)], local.at[7])
        n2_copy.start()
        up_copy.start()
        for copy in weights(0):
            copy.start()
        hid_copy.start()
        greet(z, y, c, m)
        up_copy.wait()

        def prepare(r):
            value = jnp.where(keep_of(r), upl[span(r)], 0)
            upl[span(r)] = value
            sums[3:4] += jnp.sum(value.astype(F32), axis=0, keepdims=True)
            acc[span(r)] = jnp.zeros((half, width), F32)

        loop(2, prepare)
        uplt[...] = upl[...].T
        n2_copy.wait()
        n2t[...] = n2[...].T

        def traffic(f):
            @pl.when(lax.rem(f, 3) == 2)
            def _():
                n = f // 3
                ff_sib(n // 2, 1 - lax.rem(n, 2))

            @pl.when((lax.rem(f, 3) == 0) & (f > 0))
            def _():
                n = f // 3 - 1
                loop(4, lambda i: ff_y(n // 2, 1 - lax.rem(n, 2), i))

            @pl.when((lax.rem(f, 3) == 1) & (f > 4))
            def _():
                n = (f - 7) // 3
                loop(3, lambda i: ff_z(n // 2, 1 - lax.rem(n, 2), i))

        def store(u, at, value):
            g_ff[u, :, :, :, at] = value.astype(LOW).reshape(Z * Y, C, part, fc)

        def forward(f):
            slot = lax.rem(f, 2)
            for copy in weights(f + 1):
                copy.start()
            for copy in weights(f):
                copy.wait()
            mm, off = place_of(f)
            at = pl.ds(pl.multiple_of(mm * fw + off, 128), fc)
            shift = bias_ref[mm, 0:1, pl.ds(pl.multiple_of(2 * lw + off, 128), fc)]

            def block(r):
                pre = dot(n2[span(r)], wbuf[slot, 0]) + shift
                cdf = 0.5 * (1.0 + lax.erf(pre * (2.0 ** -0.5)))
                chunk[span(r)] = (pre * cdf).astype(LOW)
                slope[span(r), at] = (cdf + pre * (0.3989422804014327 * jnp.exp(-0.5 * pre * pre))).astype(LOW)
                acc[span(r)] += dot(chunk[span(r)], wbuf[slot, 1], NT)

            loop(2, block)
            store(0, at, dot(uplt[...], chunk[...]))
            traffic(f)

        loop(6, forward)
        hid_copy.wait()

        def leave(r):
            value = jnp.where(keep_of(r), hid[span(r)] + acc[span(r)] + vec_ref[5:6], 0.0)
            acc[span(r)] = jnp.zeros((half, width), F32)
            for n in range(2):
                outbuf[2 * r + n] = value[n * rows : (n + 1) * rows].astype(LOW)
                for copy in out_copies(2 * r + n):
                    copy.start()

        loop(2, leave)

        def backward(i):
            f = 6 + i
            slot = lax.rem(f, 2)

            @pl.when(f < 11)
            def _():
                for copy in weights(f + 1):
                    copy.start()

            for copy in weights(f):
                copy.wait()
            mm, off = place_of(f)
            at = pl.ds(pl.multiple_of(mm * fw + off, 128), fc)

            def block(r):
                dpre = slope[span(r), at].astype(F32) * dot(upl[span(r)], wbuf[slot, 1])
                chunk[span(r)] = dpre.astype(LOW)
                bsum_up[0:1, at] += jnp.sum(dpre, axis=0, keepdims=True)
                acc[span(r)] += dot(chunk[span(r)], wbuf[slot, 0], NT)

            loop(2, block)
            store(1, at, dot(n2t[...], chunk[...]))
            traffic(f)

        loop(6, backward)
        att_copy.start()

        def norm_back(r):
            dtwo = acc[span(r)]
            xhat, rr = moments(hid[span(r)])
            dg = dtwo * vec_ref[3:4]
            dn = rr * (dg - jnp.mean(dg, axis=-1, keepdims=True) - xhat * jnp.mean(dg * xhat, axis=-1, keepdims=True))
            dhid = upl[span(r)].astype(F32) + dn
            dhid_ref[span(r)] = dhid
            n2[span(r)] = dhid.astype(LOW)
            sums[4:5] += jnp.sum(dtwo * xhat, axis=0, keepdims=True)
            sums[5:6] += jnp.sum(dtwo, axis=0, keepdims=True)
            sums[2:3] += jnp.sum(dhid, axis=0, keepdims=True)

        loop(2, norm_back)
        att_copy.wait()
        n2t[...] = n2[...].T
        for mm in range(groups):
            at = slice(mm * lw, (mm + 1) * lw)
            g_proj[0, :, :, :, at] = dot(n2t[...], slope[:, at]).astype(LOW).reshape(Z * Y, C, part, lw)
        p_sib(0, 1)
        p_sib(0, 0)

    pl.run_scoped(
        feed_forward,
        pltpu.VMEM((flat, width), LOW), pltpu.VMEM((width, flat), LOW),
        pltpu.VMEM((flat, width), LOW), pltpu.VMEM((width, flat), LOW),
        pltpu.VMEM((flat, width), F32), pltpu.VMEM((flat, width), F32),
        pltpu.VMEM((flat, groups * fw), LOW), pltpu.VMEM((flat, fc), LOW), pltpu.VMEM((2, 2, width, fc), LOW),
    )

    def attention(w_ref, qkv_buf, prob_buf, x_buf, do_ref, n1, n1t, dq_all):
        high = n1.shape[0] // pairs
        proj_cols = pl.ds(3 * lw, lw)
        qkv_cols = pl.ds(0, 3 * lw)
        w_copy = pltpu.make_async_copy(w_one_in.at[:, :, proj_cols], w_ref.at[:, :, proj_cols], local.at[8])
        w_qkv_copy = pltpu.make_async_copy(w_one_in.at[:, :, qkv_cols], w_ref.at[:, :, qkv_cols], local.at[6])

        def loads(p):
            slot = lax.rem(p, 2)
            pieces = [
                (qkv_all.at[p], qkv_buf), (prob_all.at[p], prob_buf), (tok_all.at[m * pairs + p], x_buf),
            ]
            return [
                pltpu.make_async_copy(src, dst.at[slot], local.at[slot * 3 + t])
                for t, (src, dst) in enumerate(pieces)
            ]

        def tok_copies(p):
            src, dst = n1.at[pl.ds(pl.multiple_of(p * high, 16), rows)], tok_out.at[m * pairs + p]
            return pltpu.make_async_copy(src, dst, tsem.at[0, p]), pltpu.make_async_remote_copy(
                src_ref=src, dst_ref=dst, send_sem=tsem.at[1, p], recv_sem=tsem.at[2, p],
                device_id={"dp": me, "mp": 1 - m}, device_id_type=MESH_ID,
            )

        w_copy.start()
        for copy in loads(0):
            copy.start()
        n1_copies = [
            pltpu.make_async_copy(n1_all.at[p], n1.at[pl.ds(p * high, rows)], n1_sem.at[p]) for p in range(pairs)
        ]
        for copy in n1_copies:
            copy.start()
        w_qkv_copy.start()
        w_copy.wait()

        def attended_back(r):
            dlow = dhid_ref[span(r)].astype(LOW)
            for mm in range(groups):
                value = dot(dlow, w_ref[mm, :, 3 * lw : 4 * lw])
                for n in range(2):
                    do_ref[2 * r + n, :, mm * lw : (mm + 1) * lw] = value[n * rows : (n + 1) * rows].astype(LOW)

        loop(2, attended_back)
        for p, copy in enumerate(n1_copies):
            copy.wait()
            n1[p * high + rows : (p + 1) * high] = jnp.zeros((high - rows, width), LOW)
            dq_all[p * high + rows : (p + 1) * high] = jnp.zeros((high - rows, 3 * width), LOW)
        n1t[...] = n1[...].T
        first = lax.broadcasted_iota(jnp.int32, (1, 128), 1) < HEAD_DIM

        def finish_pair(p):
            slot = lax.rem(p, 2)
            here = pl.ds(pl.multiple_of(p * high, 16), rows)
            dhid = dhid_ref[pl.ds(pl.multiple_of(p * rows, 8), rows)]
            done = sum(
                dot(dq_all[here, mm * 3 * lw : (mm + 1) * 3 * lw], w_ref[mm, :, : 3 * lw], NT) for mm in range(groups))
            xhat, r = moments(x_buf[slot].astype(F32))
            dg = done * vec_ref[0:1]
            dn = r * (dg - jnp.mean(dg, axis=-1, keepdims=True) - xhat * jnp.mean(dg * xhat, axis=-1, keepdims=True))
            n1[here] = (dhid + dn).astype(LOW)
            for copy in tok_copies(p):
                copy.start()
            sums[0:1] += jnp.sum(done * xhat, axis=0, keepdims=True)
            sums[1:2] += jnp.sum(done, axis=0, keepdims=True)

        def one_pair(p):
            slot = lax.rem(p, 2)

            @pl.when(p < pairs - 1)
            def _():
                for copy in loads(p + 1):
                    copy.start()

            here = pl.ds(pl.multiple_of(p * high, 16), rows)
            for copy in loads(p):
                copy.wait()

            def heads(hp):
                lane = (hp // tiles) * 3 * lw + lax.rem(hp, tiles) * 128

                def cols(t):
                    return pl.ds(pl.multiple_of(lane + t * lw, 128), 128)

                q2 = qkv_buf[slot, :, cols(0)] * 0.125
                k2t = qkv_buf[slot, :, cols(1)].T
                v2 = qkv_buf[slot, :, cols(2)]
                do2 = do_ref[p, :, pl.ds(pl.multiple_of(hp * 128, 128), 128)]
                dq_t = []
                dk = dv = 0.0
                for h in range(2):
                    mine = first if h == 0 else ~first
                    doh = jnp.where(mine, do2, 0)
                    qh = jnp.where(mine, q2, 0)
                    dpt = dot(v2, doh, NT)
                    plow = prob_buf[slot, hp * 2 + h]
                    pt = plow.astype(F32)
                    inner = jnp.sum(pt * dpt, axis=0, keepdims=True)
                    dst = (pt * (dpt - inner)).astype(LOW)
                    dv = dv + dot(plow, doh)
                    dk = dk + dot(dst, qh)
                    dq_t.append(dot(k2t[h * HEAD_DIM : (h + 1) * HEAD_DIM], dst))
                dq = (jnp.concatenate(dq_t, axis=0) * 0.125).T
                dq_all[here, cols(0)] = dq.astype(LOW)
                dq_all[here, cols(1)] = dk.astype(LOW)
                dq_all[here, cols(2)] = dv.astype(LOW)
                bsum[0:1, cols(0)] += jnp.sum(dq, axis=0, keepdims=True)
                bsum[0:1, cols(2)] += jnp.sum(dv, axis=0, keepdims=True)
                step = p * (groups * tiles) + hp

                @pl.when(step == 0)
                def _():
                    loop(4, lambda i: ff_y(1, 0, i))

                @pl.when((step == 2) | (step == 13))
                def _():
                    loop(3, lambda i: ff_z(1, 1 - step // 13, i))

                @pl.when((step >= 3) & (step < 7))
                def _():
                    loop(2, lambda i: p_y(0, 1 - (step - 3) // 2, 2 * lax.rem(step - 3, 2) + i))

                @pl.when((step == 18) | (step == 19))
                def _():
                    loop(3, lambda i: p_z(0, 19 - step, i))

                @pl.when((step == 16) | (step == 21))
                def _():
                    ff_x((step - 16) // 5)

            loop(groups * tiles, heads)

            @pl.when(p == 0)
            def _():
                w_qkv_copy.wait()

            @pl.when(p < pairs - 1)
            def _():
                finish_pair(p)

        loop(pairs, one_pair)

        def small_copy(slot, src, to, sem):
            return pltpu.make_async_remote_copy(
                src_ref=sbuf.at[src], dst_ref=sbuf.at[slot], send_sem=ssem.at[0, sem], recv_sem=ssem.at[1, sem],
                device_id={"dp": to[0], "mp": to[1]}, device_id_type=MESH_ID,
            )

        s0 = small_copy(0, 6, sib, 0)
        s1 = small_copy(1, 7, (index(z, 1 - y, c), m), 1)
        zs = [small_copy(1 + k, 8, beside(k), 1 + k) for k in (1, 2, 3)]
        s2 = small_copy(5, 9, (me, 1 - m), 5)

        def chunk(i):
            mm = lax.rem(m + 1 + i // 3, 2)
            at = pl.ds(pl.multiple_of(mm * 3 * lw + lax.rem(i, 3) * lw, 128), lw)
            g_qkv[0, :, :, :, at] = dot(n1t[...], dq_all[:, at]).astype(LOW).reshape(Z * Y, C, part, lw)

            @pl.when(i == 1)
            def _():
                p_x(0)

            @pl.when(lax.rem(i, 3) == 2)
            def _():
                q_sib(0, 1 - i // 3)

            @pl.when(i == 3)
            def _():
                loop(4, lambda k: q_y(0, 1, k))

        loop(6, chunk)
        finish_pair(pairs - 1)
        sbuf[6] = jnp.zeros_like(sbuf[6])
        sbuf[6, 0:1] = bsum_up[0:1]
        sbuf[6, 1:2, : 3 * width] = bsum[0:1]
        for n, (line, at) in enumerate(((2, 0), (2, 1), (2, 2), (3, 1), (2, 3), (3, 0))):
            sbuf[6, line : line + 1, at * width : (at + 1) * width] = sums[n : n + 1]
        s0.start()
        ff_final(0)
        s0.wait()
        sbuf[7] = sbuf[6] + sbuf[0]
        s1.start()
        loop(4, lambda i: q_y(0, 0, i))
        loop(3, lambda i: q_z(0, 1, i))
        s1.wait()
        sbuf[8] = sbuf[7] + sbuf[1]
        for copy in zs:
            copy.start()
        ff_final(1)
        p_final(0)
        q_x(0)
        for copy in zs:
            copy.wait()
        sbuf[9] = sbuf[8] + sbuf[2] + sbuf[3] + sbuf[4]
        s2.start()
        loop(3, lambda i: q_z(0, 0, i))
        s2.wait()
        sbuf[6] = sbuf[9] + sbuf[5]
        o_up[...] = sbuf[6, 0:1, pl.ds(pl.multiple_of(m * fw, 128), fw)].reshape(fw)
        for n in range(2):
            o_qv[n : n + 1] = sbuf[6, 1:2, pl.ds(pl.multiple_of((3 * m + 2 * n) * lw, 128), lw)]
        dp = lax.axis_index("dp")
        for n, (line, at) in enumerate(((2, 0), (2, 1), (2, 2), (3, 1), (2, 3), (3, 0))):
            row = sbuf[6, line : line + 1, at * width : (at + 1) * width]
            pick = row[:, :part]
            for d in range(1, Z * Y * C):
                pick = jnp.where(dp == d, row[:, d * part : (d + 1) * part], pick)
            o_vec[n : n + 1] = pick
        q_final(0)

        def finish(p):
            for copy in tok_copies(p):
                copy.wait()

        loop(pairs, finish)

        def finish_out(q):
            for copy in out_copies(q):
                copy.wait()

        loop(pairs, finish_out)

    pl.run_scoped(
        attention,
        pltpu.VMEM(w_one_in.shape, LOW), pltpu.VMEM((2, rows, 3 * width), LOW), pltpu.VMEM((2, HEADS, rows, rows), LOW),
        pltpu.VMEM((2, rows, width), LOW), pltpu.VMEM((pairs, rows, width), LOW),
        pltpu.VMEM((high, width), LOW), pltpu.VMEM((width, high), LOW), pltpu.VMEM((high, 3 * width), LOW),
    )


def backward_reduce(counts, tokens, cotangent, hid, n2, att, n1, qkv, prob, w_one, w_two, bias, vec):
    pairs, rows, width = n1.shape
    flat = pairs * rows
    part = width // (Z * Y * C)
    fw = w_two.shape[2] // 2
    hbm = pl.BlockSpec(memory_space=pl.ANY)
    vm = pl.BlockSpec(memory_space=pltpu.VMEM)
    kinds = ((2, fw), (1, width // 2), (1, 3 * width // 2))
    scratch = [pltpu.VMEM((n, Z * Y, C, part, 2 * w), LOW) for n, w in kinds]
    for n, w in kinds:
        scratch += [pltpu.VMEM((n * k, part, w), LOW) for k in (16, 8, 6, 1)]
    scratch += [
        pltpu.VMEM((flat, width), F32), pltpu.VMEM((pairs, rows, width), LOW), pltpu.VMEM((8, width), F32),
        pltpu.VMEM((8, 3 * width), F32), pltpu.VMEM((8, 2 * fw), F32), pltpu.VMEM((10, 8, 2 * fw), F32),
        pltpu.SemaphoreType.DMA((4, BLOCKS)), pltpu.SemaphoreType.DMA((4, BLOCKS)), pltpu.SemaphoreType.DMA((9,)),
        pltpu.SemaphoreType.DMA((3, pairs)), pltpu.SemaphoreType.DMA((3, pairs)), pltpu.SemaphoreType.DMA((2, 6)),
        pltpu.SemaphoreType.DMA((pairs,)),
    ]
    plane = lambda a: a.reshape(-1, width)
    return pl.pallas_call(
        back_kernel,
        in_specs=[pl.BlockSpec(memory_space=pltpu.SMEM)] + [hbm] * 10 + [vm] * 2,
        out_specs=[hbm] * 2 + [vm] * 7,
        out_shape=[
            jax.ShapeDtypeStruct((2 * pairs, rows, width), LOW), jax.ShapeDtypeStruct((2 * pairs, rows, width), LOW),
            jax.ShapeDtypeStruct((part, fw), F32), jax.ShapeDtypeStruct((part, fw), F32),
            jax.ShapeDtypeStruct((1, part, width // 2), F32),
            jax.ShapeDtypeStruct((3, part, width // 2), F32), jax.ShapeDtypeStruct((fw,), F32),
            jax.ShapeDtypeStruct((2, width // 2), F32), jax.ShapeDtypeStruct((6, part), F32),
        ],
        scratch_shapes=scratch,
        compiler_params=pltpu.CompilerParams(collective_id=1, has_side_effects=True, vmem_limit_bytes=63 * 2**20),
        name="backward_reduce",
    )(counts, plane(cotangent), plane(hid), plane(n2), plane(att), n1, qkv, prob, tokens, w_one, w_two, bias, vec)


def per_device(
    patch_counts, tokens, cotangent, attn_gain, attn_shift, w_qkv, b_qv, w_proj, b_proj,
    ffn_gain, ffn_shift, w_up, b_up, w_down, b_down,
):
    pairs_all, rows, width = tokens.shape
    n_mp = lax.axis_size("mp")
    n_dp = lax.axis_size("dp")
    pairs = pairs_all // n_mp
    direct = n_dp == Z * Y * C and n_mp == 2 and pairs == 4
    part = w_qkv.shape[0]
    lw = w_qkv.shape[2]
    fw = w_up.shape[1]
    mine = lax.axis_index("mp")
    vectors = [attn_gain, attn_shift, b_proj, ffn_gain, ffn_shift, b_down]
    if direct:
        w_one, w_two, bias, qkv, att, prob, hid, n1, n2, vec = gather_attention(
            patch_counts, tokens, w_qkv, w_proj, w_up, w_down, b_qv, b_up, vectors)
        block_out, tokens_grad, r_down, r_up, r_proj, r_qkv, o_b_up, o_b_qv, o_vec = backward_reduce(
            patch_counts, tokens, cotangent, hid, n2, att, n1, qkv, prob, w_one, w_two, bias, vec)
        o_gain, o_shift, o_b_proj, o_b_down, o_ffn_gain, o_ffn_shift = [o_vec[i] for i in range(6)]
        return (
            block_out, tokens_grad, o_gain, o_shift, r_qkv.transpose(1, 0, 2), o_b_qv,
            r_proj[0].T, o_b_proj, o_ffn_gain, o_ffn_shift, r_up, o_b_up, r_down.T, o_b_down,
        )

    off = jnp.reshape(mine * pairs, (1,)).astype(jnp.int32)
    lens = TEXT + lax.dynamic_slice_in_dim(patch_counts, mine * pairs, pairs, 0)
    first = jnp.concatenate(
        [w_qkv.reshape(part, 3 * lw), w_proj.T, jnp.stack(vectors, axis=1), jnp.zeros((part, EXTRA - 6), F32)], axis=1
    ).astype(LOW)
    second = jnp.concatenate([w_up, w_down.T], axis=1).astype(LOW)
    bias = jnp.concatenate([b_qv.reshape(-1), b_up]).astype(LOW).astype(F32)
    bias = jnp.broadcast_to(bias, (8,) + bias.shape)
    both_axes = ("mp", "dp")
    w_one = lax.all_gather(first, both_axes, axis=0, tiled=True).reshape(n_mp, width, -1)
    w_two = lax.all_gather(second, both_axes, axis=0, tiled=True).reshape(n_mp, width, -1)
    bias = lax.all_gather(bias, "mp", axis=0)
    qkv, att, prob, hid, n1, n2, vec = attention_forward(lens, off, tokens, w_one, bias)

    def grad(left, right):
        return jnp.einsum(
            "rd,rf->df", left.reshape(pairs * rows, width), right.reshape(pairs * rows, -1),
            preferred_element_type=F32,
        )

    def reduce(grads, small):
        axes = ("mp", "dp")
        done = [
            lax.psum_scatter(
                g.reshape(width, n_mp, -1).swapaxes(0, 1).reshape(n_mp * width, -1), axes,
                scatter_dimension=0, tiled=True,
            )
            for g in grads
        ]
        return done + [lax.psum(small, axes)]

    def both(array):
        other = lax.ppermute(array, "mp", [(0, 1), (1, 0)])
        return jnp.where(mine == 0, jnp.concatenate([array, other]), jnp.concatenate([other, array]))

    out_here, act, dpre, dhid, dlow, upl, sums_two, bsum_up = ffn(lens, off, n2, hid, cotangent, w_two, bias, vec)
    block_out = both(out_here)
    tok_here, dqkv, sums_one, bsum_qkv = attention_backward(lens, off, tokens, dhid, qkv, prob, w_one, vec)
    tokens_grad = both(tok_here)
    flat = bsum_qkv[0].reshape(n_mp, 3, lw)
    small = jnp.concatenate([
        sums_one[0], sums_one[1], sums_two[2], sums_two[0], sums_two[1], sums_two[3],
        flat[:, 0].reshape(-1), flat[:, 2].reshape(-1), bsum_up[0]])
    r_up, r_down, r_proj, r_qkv, small = reduce(
        [grad(n2, dpre), grad(upl, act), grad(dlow, att), grad(n1, dqkv)], small)
    place_dp = lax.axis_index("dp") * part

    def piece(i):
        return lax.dynamic_slice_in_dim(small, i * width + place_dp, part, 0)

    rest = small[6 * width :]
    o_b_q = lax.dynamic_slice_in_dim(rest, mine * lw, lw, 0)
    o_b_v = lax.dynamic_slice_in_dim(rest, (n_mp + mine) * lw, lw, 0)
    o_b_up = lax.dynamic_slice_in_dim(rest, 2 * n_mp * lw + mine * fw, fw, 0)
    return (
        block_out, tokens_grad, piece(0), piece(1),
        r_qkv.reshape(part, 3, lw), jnp.stack([o_b_q, o_b_v]),
        r_proj.T, piece(2), piece(3), piece(4), r_up, o_b_up, r_down.T, piece(5),
    )


def solution(mesh):
    vec, mat = P("dp"), P("dp", "mp")
    tok = P("dp", None, None)
    in_specs = (
        vec, tok, tok, vec, vec, P("dp", None, "mp"), P(None, "mp"), P("mp", "dp"), vec, vec, vec,
        mat, P("mp"), P("mp", "dp"), vec,
    )
    out_specs = (
        tok, tok, vec, vec, P("dp", None, "mp"), P(None, "mp"), P("mp", "dp"), vec, vec, vec,
        mat, P("mp"), P("mp", "dp"), vec,
    )
    return jax.shard_map(per_device, mesh=mesh, in_specs=in_specs, out_specs=out_specs, check_vma=False)
```
